32 devices in a mesh: row: 4 (over z), col: 8 (over y, x, core).
Axes of the slice: x: 2, y: 2, z: 4, core: 2. Of those that a mesh axis runs over, the one named last changes fastest.
Arguments:
- map_logits: float32 [4096, 4096], P(('row', 'col')), may hold values from -8 to 8
- filter_logits: bfloat16 [4096], P(('row', 'col')), may hold values from -6 to 6
- cell_expr: bfloat16 [4096, 2048], P(('row', 'col')), may hold values from 0.099609375 to 10
- spot_expr: float32 [4096, 2048], P(('row', 'col')), may hold values from 0.1 to 10
- cell_slide: int32 [4096], replicated, may hold values from 0 to 7, as said below
- spot_slide: int32 [4096], P(('row', 'col')), may hold values from 0 to 7, as said below
- density_bins: int32 [4096], P(('row', 'col')), may hold values from 1 to 16
Outputs:
- losses: float32 [4], replicated
- predicted: float32 [4096, 2048], P(('row', 'col'))
- map_grad: float32 [4096, 4096], P(('row', 'col'))
- expr_grad: float32 [4096, 2048], P(('row', 'col'))
- filter_grad: float32 [4096], P(('row', 'col'))
The draws below stay inside these ranges and needn't reach their ends.
Inputs may be any that keep to these rules, and one draw needn't show every extreme that they name: `cell_slide`: every slide number is held by at least one cell; slides differ much in size. `spot_slide`: every slide number is held by at least one spot; slides differ much in size.
All inputs are finite; a program needn't handle non-finite values.
Results may differ from the reference program's by a relative error of at most 0.0057.
Values may be sent and summed in bfloat16 or wider, within the bound.
A program may use at most 320 MiB of HBM per device.

```python
import math
import jax
import jax.numpy as jnp
from jax import lax

GENES = 2048
SLIDES = 8
CELLS = 4096
SPOTS = 4096


def slide_labels(key, amount):
    levels = jax.random.randint(jax.random.fold_in(key, 1), (amount,), 0, SLIDES * SLIDES)
    labels = jnp.zeros((amount,), jnp.int32)
    for border in range(1, SLIDES):
        labels = labels + (levels >= border * border).astype(jnp.int32)
    places = jax.random.permutation(jax.random.fold_in(key, 2), amount)
    return labels.at[places[:SLIDES]].set(jnp.arange(SLIDES, dtype=jnp.int32))


def draw_cell_slide(key, part):
    return slide_labels(jax.random.fold_in(key, 11), CELLS)


def draw_spot_slide(key, part):
    return slide_labels(jax.random.fold_in(key, 12), SPOTS)


def place_ends(array, key, low, top_value):
    shape = array.shape
    place = [jax.random.randint(jax.random.fold_in(key, axis), (), 0, shape[axis]) for axis in range(len(shape))]
    array = array.at[tuple(place)].set(low)
    longest = shape.index(max(shape))
    place[longest] = (place[longest] + 1) % shape[longest]
    return array.at[tuple(place)].set(top_value)


def block_levels(rng, shape, shards, low, largest):
    level = 1.0
    for dim, parts in shards:
        draws = jax.random.uniform(jax.random.fold_in(jax.random.fold_in(rng, 6), dim), (parts,), jnp.float32, low / len(shards), largest / len(shards))
        level = level * jnp.repeat(jnp.exp(draws), shape[dim] // parts).reshape((-1,) + (1,) * (len(shape) - 1 - dim))
    return level


def centred(stream_key, shape, deviation, bound, cuts=(), kind=jnp.bfloat16):
    array = deviation * jax.random.normal(stream_key, shape, jnp.float32)
    if cuts:
        array = array * block_levels(stream_key, shape, cuts, -0.22, 0.18)
    return jnp.clip(array, -bound, bound).astype(kind)


def setup_inputs(seed: int = 0) -> dict:
    arg_keys = jax.random.split(jax.random.key(seed), 8)
    map_logits = centred(arg_keys[0], (SPOTS, CELLS), 2.0, 8.0, ((0, 32),), jnp.float32)
    filter_logits = centred(arg_keys[1], (CELLS,), 1.5, 6.0, ((0, 32),))
    cell_expr = jnp.clip(jnp.exp(math.log(10.0) - 4.609084 * jax.random.uniform(arg_keys[2], (CELLS, GENES), jnp.float32) ** block_levels(arg_keys[2], (CELLS, GENES), ((0, 32),), -0.2, 0.2)), 0.099609375, 10.0).astype(jnp.bfloat16)
    spot_expr = jnp.clip(jnp.exp(math.log(10.0) - 4.6051702 * jax.random.uniform(arg_keys[3], (SPOTS, GENES), jnp.float32) ** block_levels(arg_keys[3], (SPOTS, GENES), ((0, 32),), -0.2, 0.2)), 0.1, 10.0)
    cell_slide = draw_cell_slide(jax.random.fold_in(arg_keys[7], 71), 0)
    spot_slide = draw_spot_slide(jax.random.fold_in(arg_keys[7], 71), 0)
    density_bins = place_ends(jax.random.randint(arg_keys[6], (SPOTS,), 1, 17), jax.random.fold_in(arg_keys[6], 1), 1, 16).astype(jnp.int32)
    return dict(map_logits=map_logits, filter_logits=filter_logits, cell_expr=cell_expr, spot_expr=spot_expr, cell_slide=cell_slide, spot_slide=spot_slide, density_bins=density_bins)


@jax.custom_vjp
def low(v):
    return lax.optimization_barrier(v.astype(jnp.bfloat16)).astype(jnp.float32)

@jax.custom_vjp
def low_back(v):
    return v

def low_keep(v):
    return (low(v), None)

def low_pass(kept, grad):
    return (grad,)

def back_keep(v):
    return (v, None)

def back_low(kept, grad):
    return (low(grad),)
low.defvjp(low_keep, low_pass)
low_back.defvjp(back_keep, back_low)

def slide_onehot(labels):
    return (labels[:, None] == jnp.arange(SLIDES, dtype=jnp.int32)[None, :]).astype(jnp.float32)

def reference(map_logits, filter_logits, cell_expr, spot_expr, cell_slide, spot_slide, density_bins):
    highest = lax.Precision.HIGHEST
    block_rows = math.gcd(SPOTS, 512)
    bin_values = density_bins.astype(jnp.float32)
    onehot = slide_onehot(spot_slide)

    def total_fn(logits, filt_logits, expr):
        keep_rate = jax.nn.sigmoid(filt_logits)
        scaled = low(keep_rate[:, None] * expr)

        def one_block(pieces):
            logit_rows, labels = pieces
            allowed = labels[:, None] == cell_slide[None, :]
            shifted = jnp.where(allowed, logit_rows, -1e+30)
            row_peak = lax.optimization_barrier(jnp.max(shifted, axis=1, keepdims=True))
            raised = jnp.exp(shifted - row_peak)
            chances = raised / lax.optimization_barrier(jnp.sum(raised, axis=1, keepdims=True))
            used_map = low(low_back(chances))
            pred_rows = jnp.dot(used_map, scaled, precision=highest)
            mass_rows = jnp.dot(used_map, keep_rate, precision=highest)
            return (low_back(pred_rows), low_back(mass_rows))
        pred_blocks, mass_blocks = lax.map(jax.checkpoint(one_block), (logits.reshape(-1, block_rows, CELLS), spot_slide.reshape(-1, block_rows)))
        predicted = pred_blocks.reshape(SPOTS, GENES)
        mass = mass_blocks.reshape(SPOTS)
        cross_term = predicted * spot_expr
        gene_cross = jnp.dot(onehot.T, cross_term, precision=highest)
        gene_pred = jnp.dot(onehot.T, predicted * predicted, precision=highest)
        gene_obs = jnp.dot(onehot.T, spot_expr * spot_expr, precision=highest)
        gene_loss = 1.0 - jnp.mean(gene_cross / jnp.sqrt(gene_pred * gene_obs))
        spot_cos = lax.optimization_barrier(jnp.sum(cross_term, axis=1)) / jnp.sqrt(lax.optimization_barrier(jnp.sum(predicted * predicted, axis=1)) * lax.optimization_barrier(jnp.sum(spot_expr * spot_expr, axis=1)))
        spot_loss = 1.0 - jnp.mean(spot_cos)
        slide_mass = jnp.dot(onehot.T, mass, precision=highest)
        slide_bins = jnp.dot(onehot.T, bin_values, precision=highest)
        slide_log = jnp.dot(onehot.T, bin_values * (jnp.log(bin_values) - jnp.log(mass)), precision=highest)
        kl_loss = jnp.mean(slide_log / slide_bins - jnp.log(slide_bins) + jnp.log(slide_mass))
        total_loss = gene_loss + spot_loss + kl_loss
        losses = jnp.stack([total_loss, gene_loss, spot_loss, kl_loss])
        return (total_loss, (losses, predicted))
    total_loss, pullback, extra = jax.vjp(total_fn, map_logits, filter_logits.astype(jnp.float32), cell_expr.astype(jnp.float32), has_aux=True)
    map_grad, filter_grad, expr_grad = pullback(jnp.ones_like(total_loss))
    losses, predicted = extra
    return (losses, predicted, map_grad, expr_grad, filter_grad)
```

```python
import jax
import jax.numpy as jnp
from jax import lax
from jax.sharding import PartitionSpec as P

SLIDES = 8


def shards(map_logits, filter_logits, cell_expr, spot_expr, cell_slide, spot_slide, density_bins):
    highest = lax.Precision.HIGHEST
    both = ("row", "col")
    rows_count = lax.axis_size("row")
    cols_count = lax.axis_size("col")
    spot_dev, cell_total = map_logits.shape
    cell_dev = filter_logits.shape[0]
    spot_total = spot_dev * rows_count * cols_count
    gene_count = cell_expr.shape[1]
    keep_rate = jax.nn.sigmoid(filter_logits.astype(jnp.float32))
    scaled = (keep_rate[:, None] * cell_expr.astype(jnp.float32)).astype(jnp.bfloat16)
    scaled_col = lax.all_gather(scaled, "row", axis=0, tiled=True)
    allowed = spot_slide[:, None] == cell_slide[None, :]
    shifted = jnp.where(allowed, map_logits, -1e30)
    row_peak = jnp.max(shifted, axis=1, keepdims=True)
    raised = jnp.exp(shifted - row_peak)
    chances = raised / jnp.sum(raised, axis=1, keepdims=True)
    chance_low = chances.astype(jnp.bfloat16)
    by_col = chance_low.reshape(spot_dev, rows_count, cols_count, cell_dev)
    mapped = lax.all_to_all(by_col, "col", split_axis=2, concat_axis=0, tiled=True)
    mapped = mapped.reshape(spot_dev * cols_count, rows_count * cell_dev)
    keep_col = lax.all_gather(keep_rate, "row", axis=0, tiled=True)
    part_pred = jnp.dot(mapped, scaled_col, preferred_element_type=jnp.float32)
    part_mass = jnp.dot(mapped, keep_col, precision=highest, preferred_element_type=jnp.float32)
    predicted = lax.psum_scatter(part_pred, "col", scatter_dimension=0, tiled=True)
    mass = lax.psum_scatter(part_mass, "col", scatter_dimension=0, tiled=True)
    onehot = (spot_slide[:, None] == jnp.arange(SLIDES, dtype=jnp.int32)[None, :]).astype(
        jnp.float32
    )
    cross_term = predicted * spot_expr
    pred_sq = predicted * predicted
    obs_sq = spot_expr * spot_expr
    spot_cross = jnp.sum(cross_term, axis=1)
    spot_pred = jnp.sum(pred_sq, axis=1)
    spot_root = jnp.sqrt(spot_pred * jnp.sum(obs_sq, axis=1))
    spot_cos = spot_cross / spot_root
    bin_values = density_bins.astype(jnp.float32)
    log_term = bin_values * (jnp.log(bin_values) - jnp.log(mass))
    all_cross, all_pred, all_obs, slide_mass, slide_bins, slide_log, cos_total = lax.psum(
        (
            jnp.dot(onehot.T, cross_term, precision=highest),
            jnp.dot(onehot.T, pred_sq, precision=highest),
            jnp.dot(onehot.T, obs_sq, precision=highest),
            jnp.dot(onehot.T, mass, precision=highest),
            jnp.dot(onehot.T, bin_values, precision=highest),
            jnp.dot(onehot.T, log_term, precision=highest),
            jnp.sum(spot_cos),
        ),
        both,
    )
    gene_root = jnp.sqrt(all_pred * all_obs)
    gene_loss = 1.0 - jnp.mean(all_cross / gene_root)
    spot_loss = 1.0 - cos_total / spot_total
    kl_loss = jnp.mean(slide_log / slide_bins - jnp.log(slide_bins) + jnp.log(slide_mass))
    total_loss = gene_loss + spot_loss + kl_loss
    losses = jnp.stack([total_loss, gene_loss, spot_loss, kl_loss])
    gene_scale = 1.0 / (SLIDES * gene_count)
    coef_obs = jnp.dot(onehot, 1.0 / gene_root, precision=highest)
    coef_pred = jnp.dot(onehot, all_cross / (all_pred * gene_root), precision=highest)
    pred_grad = -gene_scale * (spot_expr * coef_obs - predicted * coef_pred)
    pred_grad = (
        pred_grad
        - (
            spot_expr / spot_root[:, None]
            - predicted * (spot_cross / (spot_pred * spot_root))[:, None]
        )
        / spot_total
    )
    mass_each = jnp.dot(onehot, slide_mass, precision=highest)
    bins_each = jnp.dot(onehot, slide_bins, precision=highest)
    mass_grad = (1.0 / mass_each - bin_values / (bins_each * mass)) / SLIDES
    grad_low = pred_grad.astype(jnp.bfloat16)
    mass_low = mass_grad.astype(jnp.bfloat16)
    grad_block = lax.all_gather(grad_low, "col", axis=0, tiled=True)
    mass_block = lax.all_gather(mass_low, "col", axis=0, tiled=True)
    back_map = lax.dot_general(
        grad_block, scaled_col, (((1,), (1,)), ((), ())), preferred_element_type=jnp.float32
    )
    back_map = back_map + mass_block.astype(jnp.float32)[:, None] * keep_col[None, :]
    back_low = back_map.astype(jnp.bfloat16)
    returned = lax.all_to_all(
        back_low.reshape(spot_dev * cols_count, rows_count, 1, cell_dev),
        "col",
        split_axis=0,
        concat_axis=2,
        tiled=True,
    ).reshape(spot_dev, cell_total)
    expr_part = lax.dot_general(
        mapped, grad_block, (((0,), (0,)), ((), ())), preferred_element_type=jnp.float32
    )
    mass_reach = lax.dot_general(
        mapped, mass_block, (((0,), (0,)), ((), ())), preferred_element_type=jnp.float32
    )
    expr_sum = lax.psum_scatter(expr_part, "row", scatter_dimension=0, tiled=True)
    mass_sum = lax.psum_scatter(mass_reach, "row", scatter_dimension=0, tiled=True)
    filter_grad = (
        keep_rate
        * (1.0 - keep_rate)
        * (jnp.sum(cell_expr.astype(jnp.float32) * expr_sum, axis=1) + mass_sum)
    )
    expr_grad = keep_rate[:, None] * expr_sum
    chance_grad = returned.astype(jnp.float32)
    inner_sum = jnp.sum(chances * chance_grad, axis=1, keepdims=True)
    map_grad = chances * (chance_grad - inner_sum)
    return (losses, predicted, map_grad, expr_grad, filter_grad)


def solution(mesh):
    both = P(("row", "col"))
    rows = P(("row", "col"), None)
    in_specs = (rows, both, rows, rows, P(), both, both)
    out_specs = (P(), rows, rows, rows, both)
    return jax.shard_map(shards, mesh=mesh, in_specs=in_specs, out_specs=out_specs, check_vma=False)
```

```python
import functools

import jax
import jax.numpy as jnp
from jax import lax
from jax.experimental import pallas as pl
from jax.experimental.pallas import tpu as pltpu
from jax.sharding import PartitionSpec as P

SLIDES = 8
ROWS, PLANE, CORES = 4, 4, 2
WIDTH = 256
MESH = pl.DeviceIdType.MESH


def shards(map_logits, filter_logits, cell_expr, spot_expr, cell_slide, spot_slide, density_bins):
    highest = lax.Precision.HIGHEST
    both = ("row", "col")
    rows_count = lax.axis_size("row")
    cols_count = lax.axis_size("col")
    spot_dev, cell_total = map_logits.shape
    cell_dev = filter_logits.shape[0]
    spot_total = spot_dev * rows_count * cols_count
    gene_count = cell_expr.shape[1]
    keep_rate = jax.nn.sigmoid(filter_logits.astype(jnp.float32))
    scaled = (keep_rate[:, None] * cell_expr.astype(jnp.float32)).astype(jnp.bfloat16)
    scaled_col = lax.all_gather(scaled, "row", axis=0, tiled=True)
    allowed = spot_slide[:, None] == cell_slide[None, :]
    shifted = jnp.where(allowed, map_logits, -1e30)
    row_peak = jnp.max(shifted, axis=1, keepdims=True)
    raised = jnp.exp(shifted - row_peak)
    chances = raised / jnp.sum(raised, axis=1, keepdims=True)
    chance_low = chances.astype(jnp.bfloat16)
    by_col = chance_low.reshape(spot_dev, rows_count, cols_count, cell_dev)
    mapped = lax.all_to_all(by_col, "col", split_axis=2, concat_axis=0, tiled=True)
    mapped = mapped.reshape(spot_dev * cols_count, rows_count * cell_dev)
    keep_col = lax.all_gather(keep_rate, "row", axis=0, tiled=True)
    part_pred = jnp.dot(mapped, scaled_col, preferred_element_type=jnp.float32)
    part_mass = jnp.dot(mapped, keep_col, precision=highest, preferred_element_type=jnp.float32)
    predicted = lax.psum_scatter(part_pred, "col", scatter_dimension=0, tiled=True)
    mass = lax.psum_scatter(part_mass, "col", scatter_dimension=0, tiled=True)
    onehot = (spot_slide[:, None] == jnp.arange(SLIDES, dtype=jnp.int32)[None, :]).astype(
        jnp.float32
    )
    cross_term = predicted * spot_expr
    pred_sq = predicted * predicted
    obs_sq = spot_expr * spot_expr
    spot_cross = jnp.sum(cross_term, axis=1)
    spot_pred = jnp.sum(pred_sq, axis=1)
    spot_root = jnp.sqrt(spot_pred * jnp.sum(obs_sq, axis=1))
    spot_cos = spot_cross / spot_root
    bin_values = density_bins.astype(jnp.float32)
    log_term = bin_values * (jnp.log(bin_values) - jnp.log(mass))
    all_cross, all_pred, all_obs, slide_mass, slide_bins, slide_log, cos_total = lax.psum(
        (
            jnp.dot(onehot.T, cross_term, precision=highest),
            jnp.dot(onehot.T, pred_sq, precision=highest),
            jnp.dot(onehot.T, obs_sq, precision=highest),
            jnp.dot(onehot.T, mass, precision=highest),
            jnp.dot(onehot.T, bin_values, precision=highest),
            jnp.dot(onehot.T, log_term, precision=highest),
            jnp.sum(spot_cos),
        ),
        both,
    )
    gene_root = jnp.sqrt(all_pred * all_obs)
    gene_loss = 1.0 - jnp.mean(all_cross / gene_root)
    spot_loss = 1.0 - cos_total / spot_total
    kl_loss = jnp.mean(slide_log / slide_bins - jnp.log(slide_bins) + jnp.log(slide_mass))
    total_loss = gene_loss + spot_loss + kl_loss
    losses = jnp.stack([total_loss, gene_loss, spot_loss, kl_loss])
    gene_scale = 1.0 / (SLIDES * gene_count)
    coef_obs = jnp.dot(onehot, 1.0 / gene_root, precision=highest)
    coef_pred = jnp.dot(onehot, all_cross / (all_pred * gene_root), precision=highest)
    pred_grad = -gene_scale * (spot_expr * coef_obs - predicted * coef_pred)
    pred_grad = (
        pred_grad
        - (
            spot_expr / spot_root[:, None]
            - predicted * (spot_cross / (spot_pred * spot_root))[:, None]
        )
        / spot_total
    )
    mass_each = jnp.dot(onehot, slide_mass, precision=highest)
    bins_each = jnp.dot(onehot, slide_bins, precision=highest)
    mass_grad = (1.0 / mass_each - bin_values / (bins_each * mass)) / SLIDES
    grad_low = pred_grad.astype(jnp.bfloat16)
    mass_low = mass_grad.astype(jnp.bfloat16)
    grad_block = lax.all_gather(grad_low, "col", axis=0, tiled=True)
    mass_block = lax.all_gather(mass_low, "col", axis=0, tiled=True)
    back_map = lax.dot_general(
        grad_block, scaled_col, (((1,), (1,)), ((), ())), preferred_element_type=jnp.float32
    )
    back_map = back_map + mass_block.astype(jnp.float32)[:, None] * keep_col[None, :]
    back_low = back_map.astype(jnp.bfloat16)
    returned = lax.all_to_all(
        back_low.reshape(spot_dev * cols_count, rows_count, 1, cell_dev),
        "col",
        split_axis=0,
        concat_axis=2,
        tiled=True,
    ).reshape(spot_dev, cell_total)
    expr_part = lax.dot_general(
        mapped, grad_block, (((0,), (0,)), ((), ())), preferred_element_type=jnp.float32
    )
    mass_reach = lax.dot_general(
        mapped, mass_block, (((0,), (0,)), ((), ())), preferred_element_type=jnp.float32
    )
    expr_sum = lax.psum_scatter(expr_part, "row", scatter_dimension=0, tiled=True)
    mass_sum = lax.psum_scatter(mass_reach, "row", scatter_dimension=0, tiled=True)
    filter_grad = (
        keep_rate
        * (1.0 - keep_rate)
        * (jnp.sum(cell_expr.astype(jnp.float32) * expr_sum, axis=1) + mass_sum)
    )
    expr_grad = keep_rate[:, None] * expr_sum
    chance_grad = returned.astype(jnp.float32)
    inner_sum = jnp.sum(chances * chance_grad, axis=1, keepdims=True)
    map_grad = chances * (chance_grad - inner_sum)
    return (losses, predicted, map_grad, expr_grad, filter_grad)


def fused_kernel(
    total_spots, total_genes,
    logit_in, filt_in, cell_in, spot_in, cslide_in, sslide_in, bins_in,
    pred_out, map_out, expr_out, filt_out, loss_out,
    chance, own_low, plane_low, plane_turn, cell_v, hand, col, part, near1, far1, got1, near2,
    got2, pred_h, spot_v, spot_h, stat, st_sum, st1, st2, st3, spacc, spgot, coef, grad,
    sums_up, sums_dn, pass_on, back, back_got, back_low, back_ret, other, other_got, expr_v, map_v,
    small_src, small, reach_src, keep_all,
    load_sem, out_sem, hand_s, hand_r, up_s, dn_s, col_r, low_s, low_r, p_s, p_r, pred_s, pred_r,
    spot_s, spot_r, st_s, st_r, spx_s, spx_r, g_s, g_r, ru_s, rd_s, ru_r, rd_r, back_s, back_r,
    ret_s, ret_r, oth_s, oth_r, sm_s, sm_r,
):
    f32, b16 = jnp.float32, jnp.bfloat16
    chunks = col.shape[0]
    half = chunks * WIDTH
    z = lax.axis_index("row")
    c = lax.axis_index("col")
    j = lax.div(c, 2)
    k = lax.rem(c, 2)
    y = lax.div(j, 2)
    x = lax.rem(j, 2)
    me = z * 8 + c
    mate = 1 - k

    def dev(zz, jj, kk):
        return (zz, jj * 2 + kk)

    jx = y * 2 + (1 - x)
    jy = (1 - y) * 2 + x
    jd = (1 - y) * 2 + (1 - x)
    dev_mate = dev(z, j, mate)
    dev_x = dev(z, jx, k)
    dev_y = dev(z, jy, k)

    def rc(src, dst, ss, rs, to):
        return pltpu.make_async_remote_copy(
            src_ref=src, dst_ref=dst, send_sem=ss, recv_sem=rs, device_id=to, device_id_type=MESH
        )

    def rows(i, size):
        return pl.ds(pl.multiple_of(i * size, size), size)

    load_cell = pltpu.make_async_copy(cell_in, cell_v, load_sem.at[0])
    load_logit = pltpu.make_async_copy(logit_in, chance, load_sem.at[1])
    load_spot = pltpu.make_async_copy(spot_in, spot_v, load_sem.at[2])
    load_cell.start()
    load_logit.start()
    load_spot.start()
    barrier = pltpu.get_barrier_semaphore()

    @pl.loop(1, 32)
    def _(p):
        t = lax.rem(me + p, 32)
        pl.semaphore_signal(
            barrier, inc=1, device_id=(lax.div(t, 8), lax.rem(t, 8)), device_id_type=MESH
        )

    eye = lax.broadcasted_iota(jnp.int32, (128, 128), 0) == lax.broadcasted_iota(
        jnp.int32, (128, 128), 1
    )
    lane = lax.broadcasted_iota(jnp.int32, (128, 128), 1)

    def stand(row):
        return jnp.sum(jnp.where(eye, jnp.broadcast_to(row, (128, 128)), 0.0), 1, keepdims=True)

    def lie(column):
        return jnp.sum(jnp.where(eye, jnp.broadcast_to(column, (128, 128)), 0.0), 0, keepdims=True)

    filt_row = filt_in[...].astype(f32)
    keep_col = stand(jax.nn.sigmoid(filt_row))
    slide_col = stand(sslide_in[...].astype(f32))
    bins_col = stand(bins_in[...].astype(f32))

    load_cell.wait()

    @pl.loop(0, chunks)
    def _(q):
        mine = cell_v[:, pl.ds(pl.multiple_of(k * half + q * WIDTH, WIDTH), WIDTH)]
        col[q, z, rows(k, 128), :] = (keep_col * mine.astype(f32)).astype(b16)
        theirs = cell_v[:, pl.ds(pl.multiple_of(mate * half + q * WIDTH, WIDTH), WIDTH)]
        hand[q] = (keep_col * theirs.astype(f32)).astype(b16)

    pl.semaphore_wait(barrier, 31)

    def hand_copy(q):
        return rc(hand.at[q], col.at[q, z, rows(k, 128)], hand_s.at[q], hand_r.at[q], dev_mate)

    def hand_recv(q):
        return rc(hand.at[q], col.at[q, z, rows(mate, 128)], hand_s.at[q], hand_r.at[q], dev_mate)

    def col_up(q, b):
        return rc(col.at[q, b], col.at[q, b], up_s.at[q, b], col_r.at[q, b], dev(lax.rem(z + 1, 4), j, k))

    def col_dn(q, b):
        return rc(col.at[q, b], col.at[q, b], dn_s.at[q, b], col_r.at[q, b], dev(lax.rem(z + 3, 4), j, k))

    @pl.loop(0, chunks)
    def _(q):
        hand_copy(q).start()

    def col_own(q):
        hand_recv(q).wait_recv()

        @pl.when(z < 3)
        def _():
            col_up(q, z).start()

        @pl.when(z > 0)
        def _():
            col_dn(q, z).start()

    col_own(0)

    def small_start(r, source):
        small[r, me] = source(me)[...]

        @pl.loop(1, 32)
        def _(p):
            t = lax.rem(me + p, 32)
            rc(
                source(t), small.at[r, me], sm_s.at[r, t], sm_r.at[r, me],
                (lax.div(t, 8), lax.rem(t, 8)),
            ).start()

    def small_wait(r, source):
        @pl.loop(1, 32)
        def _(p):
            t = lax.rem(me + p, 32)
            rc(
                source(t), small.at[r, t], sm_s.at[r, t], sm_r.at[r, t],
                (lax.div(t, 8), lax.rem(t, 8)),
            ).wait()

    small_src[0] = filt_row
    small_start(0, lambda t: small_src.at[0])

    load_spot.wait()

    @pl.loop(0, chunks)
    def _(q):
        spot_h[q, rows(k, 128), :] = spot_v[
            :, pl.ds(pl.multiple_of(k * half + q * WIDTH, WIDTH), WIDTH)
        ]

    def spot_copy(q, row):
        return rc(
            spot_v.at[:, pl.ds(pl.multiple_of(mate * half + q * WIDTH, WIDTH), WIDTH)],
            spot_h.at[q, rows(row, 128)], spot_s.at[q], spot_r.at[q], dev_mate,
        )

    @pl.loop(0, chunks)
    def _(q):
        spot_copy(q, k).start()

    load_logit.wait()

    @pl.loop(0, 8)
    def _(g):
        at = rows(g, 16)
        logits = chance[at, :]
        pick = lax.broadcasted_iota(jnp.int32, (16, 128), 0) + g * 16
        here = lax.broadcasted_iota(jnp.int32, (16, 128), 1)
        slide = jnp.sum(
            jnp.where(pick == here, jnp.broadcast_to(sslide_in[...].astype(f32), (16, 128)), 0.0),
            1, keepdims=True,
        )
        allowed = slide == cslide_in[...].astype(f32)
        shifted = jnp.where(allowed, logits, -1e30)
        raised = jnp.exp(shifted - jnp.max(shifted, axis=1, keepdims=True))
        part_sum = jnp.sum(raised, axis=1, keepdims=True)
        value = raised / part_sum
        chance[at, :] = value
        low = value.astype(b16)
        for b in range(4):
            for jj in range(4):
                own_low[jj, at, b * 256 : b * 256 + 256] = low[
                    :, b * 1024 + jj * 256 : b * 1024 + jj * 256 + 256
                ]

    def low_copy(jj):
        return rc(own_low.at[jj], plane_low.at[j * 2 + k], low_s.at[jj], low_r.at[j * 2 + k], dev(z, jj, k))

    def low_pass(jj):
        return rc(plane_low.at[jj * 2 + k], plane_low.at[jj * 2 + k], low_s.at[4 + jj], low_r.at[jj * 2 + k], dev_mate)

    def low_recv(jj, kk):
        at = plane_low.at[jj * 2 + kk]
        return rc(at, at, low_s.at[jj], low_r.at[jj * 2 + kk], dev_mate)

    low_copy(jd).start()
    low_copy(jx).start()
    low_copy(jy).start()
    plane_low[j * 2 + k] = own_low[j]
    low_pass(j).start()

    small_wait(0, lambda t: small_src.at[0])
    keep_all[...] = jax.nn.sigmoid(small[0])

    def of_cells(d):
        b = lax.div(d, 8)
        jj = lax.div(lax.rem(d, 8), 2)
        kk = lax.rem(d, 2)
        return own_low[jj, :, pl.ds(pl.multiple_of(b * 256 + kk * 128, 128), 128)].astype(f32)

    mass_parts = lax.fori_loop(
        0, 32, lambda d, acc: acc + of_cells(d) * keep_all[d], jnp.zeros((128, 128), f32)
    )
    mass = jnp.sum(mass_parts, axis=1, keepdims=True)
    log_term = bins_col * (jnp.log(bins_col) - jnp.log(mass))
    kind = lax.div(lane, 8)
    of_slide = lax.rem(lane, 8) == slide_col.astype(jnp.int32)
    values = jnp.where(
        kind == 0, mass, jnp.where(kind == 1, bins_col, jnp.where(kind == 2, log_term, 0.0))
    )
    small_src[1] = jnp.sum(jnp.where(of_slide, values, 0.0), axis=0, keepdims=True)
    small_start(1, lambda t: small_src.at[1])

    for jj in (jx, jy, jd):
        low_recv(jj, k).wait_recv()
        low_pass(jj).start()
    for jj in range(4):
        low_recv(jj, mate).wait_recv()

    small_wait(1, lambda t: small_src.at[1])
    sums_row = jnp.sum(small[1], axis=0)
    each = jnp.broadcast_to(sums_row, (128, 128))
    mass_each = jnp.sum(jnp.where(of_slide & (kind == 0), each, 0.0), 1, keepdims=True)
    bins_each = jnp.sum(jnp.where(of_slide & (kind == 1), each, 0.0), 1, keepdims=True)
    mass_grad = (1.0 / mass_each - bins_col / (bins_each * mass)) / SLIDES
    mass_grad = mass_grad.astype(b16).astype(f32)

    @pl.loop(0, 32)
    def _(d):
        reach_src[d] = jnp.sum(of_cells(d) * mass_grad, axis=0, keepdims=True)

    small_start(2, lambda t: reach_src.at[t])

    @pl.loop(0, 8)
    def _(i):
        plane_turn[:, rows(i, 128)] = plane_low[i].astype(f32).T.astype(b16)

    slide8 = lax.broadcasted_iota(jnp.int32, (8, 128), 0)
    lane8 = lax.broadcasted_iota(jnp.int32, (8, 128), 1)

    def by_slide(first):
        return jnp.sum(
            jnp.where(lane8 == slide8 + first, jnp.broadcast_to(sums_row, (8, 128)), 0.0), 1, keepdims=True
        )

    mass_s, bins_s, log_s = by_slide(0), by_slide(8), by_slide(16)
    kl_loss = jnp.sum(log_s / bins_s - jnp.log(bins_s) + jnp.log(mass_s), axis=0, keepdims=True) / SLIDES

    small_src[4] = sslide_in[...].astype(f32)
    slide_swap = rc(small_src.at[4], small_src.at[5], spx_s.at[1], spx_r.at[1], dev_mate)
    slide_swap.start()
    slide_swap.wait()
    first = jnp.where(k == 0, small_src[4], small_src[5])
    second = jnp.where(k == 0, small_src[5], small_src[4])
    slides_row = jnp.concatenate([first, second], axis=1)
    hot_lie = (
        lax.broadcasted_iota(jnp.int32, (8, 256), 0).astype(f32) == jnp.broadcast_to(slides_row, (8, 256))
    ).astype(b16)
    slides_col = jnp.concatenate([stand(first), stand(second)], axis=0)
    lane2 = lax.broadcasted_iota(jnp.int32, (256, 128), 1)
    hot_stand = (
        (lax.rem(lane2, 8) == slides_col.astype(jnp.int32)) & (lane2 < 24)
    ).astype(b16)

    def split_dot(a, v):
        high = v.astype(b16)
        rest = (v - high.astype(f32)).astype(b16)
        return jnp.dot(a, high, preferred_element_type=f32) + jnp.dot(a, rest, preferred_element_type=f32)

    def p_copy(q, m):
        src = (near1.at[q], far1.at[q], near2.at[q, 0], near2.at[q, 1])[m]
        dst = (got1.at[q, 0], got1.at[q, 1], got2.at[q, 0], got2.at[q, 1])[m]
        to = (dev_x, dev_y, dev_y, dev_x)[m]
        return rc(src, dst, p_s.at[q, m], p_r.at[q, m], to)

    def pred_copy(q):
        return rc(
            pred_h.at[q, rows(mate, 128)],
            pred_out.at[:, pl.ds(pl.multiple_of(k * half + q * WIDTH, WIDTH), WIDTH)],
            pred_s.at[q], pred_r.at[q], dev_mate,
        )

    def pred_got(q):
        return rc(
            pred_h.at[q, rows(mate, 128)],
            pred_out.at[:, pl.ds(pl.multiple_of(mate * half + q * WIDTH, WIDTH), WIDTH)],
            pred_s.at[q], pred_r.at[q], dev_mate,
        )

    def pred_own(q):
        return pltpu.make_async_copy(
            pred_h.at[q, rows(k, 128)],
            pred_out.at[:, pl.ds(pl.multiple_of(k * half + q * WIDTH, WIDTH), WIDTH)],
            out_sem.at[q],
        )

    spacc[...] = jnp.zeros_like(spacc)

    def gather_step(q):
        @pl.when(q + 1 < chunks)
        def _():
            col_own(q + 1)

        for s in range(3):
            @pl.when(z - 1 - s >= 0)
            def _():
                b = z - 1 - s
                col_up(q, b).wait_recv()

                @pl.when(z < 3)
                def _():
                    col_up(q, b).start()

            @pl.when(z + 1 + s <= 3)
            def _():
                b = z + 1 + s
                col_dn(q, b).wait_recv()

                @pl.when(z > 0)
                def _():
                    col_dn(q, b).start()

    def product(q, left):
        right = (col if left is plane_low else grad)[q].reshape(1024, WIDTH)

        @pl.loop(0, 2)
        def _(h):
            if left is plane_low:
                block = plane_low[pl.ds(h * 4, 4)].reshape(512, 1024)
            else:
                block = plane_turn[rows(h, 512), :]
            part[q, pl.ds(h * 2, 2)] = jnp.dot(block, right, preferred_element_type=f32).reshape(2, 256, WIDTH)

    def reduce_first(q):
        for e in range(2):
            near1[q, e] = part[q, e * 2 + (1 - x), :, :128].astype(b16)
            far1[q, e] = part[q, (1 - y) * 2 + e, :, 128:].astype(b16)
        p_copy(q, 0).start()
        p_copy(q, 1).start()

    def reduce_second(q):
        p_copy(q, 0).wait_recv()
        near2[q, 0] = (part[q, jy, :, :128] + got1[q, 0, 1 - y].astype(f32)).astype(b16)
        p_copy(q, 2).start()
        p_copy(q, 1).wait_recv()
        near2[q, 1] = (part[q, jx, :, 128:] + got1[q, 1, 1 - x].astype(f32)).astype(b16)
        p_copy(q, 3).start()
        part[q, j, :, :128] = part[q, j, :, :128] + got1[q, 0, y].astype(f32)
        part[q, j, :, 128:] = part[q, j, :, 128:] + got1[q, 1, x].astype(f32)

    def reduce_last(q):
        p_copy(q, 2).wait_recv()
        p_copy(q, 3).wait_recv()
        spot_copy(q, mate).wait_recv()
        pred_h[q, :, :128] = part[q, j, :, :128] + got2[q, 0].astype(f32)
        pred_h[q, :, 128:] = part[q, j, :, 128:] + got2[q, 1].astype(f32)
        pred_copy(q).start()
        pred_own(q).start()
        g = lax.div(q, 2)
        inside = lax.rem(q, 2) * 2
        for e in range(2):
            at = slice(e * 128, e * 128 + 128)
            pr = pred_h[q, :, at]
            sp = spot_h[q, :, at]
            for i, v in enumerate((pr * sp, pr * pr, sp * sp)):
                spacc[i] = spacc[i] + v
                stat[g, inside + e, i * 8 : i * 8 + 8] = split_dot(hot_lie, v)

    def st_copy(g, kind_, o):
        if kind_ == 0:
            return rc(stat.at[g, o], st1.at[g, j], st_s.at[g, 0, o], st_r.at[g, 0, j], dev(z, o, k))
        if kind_ == 1:
            return rc(st_sum.at[g, 0], st2.at[g, z], st_s.at[g, 1, o], st_r.at[g, 1, z], dev(o, j, k))
        return rc(st_sum.at[g, 1], st3.at[g, j], st_s.at[g, 2, o], st_r.at[g, 2, j], dev(z, o, k))

    def st_got(g, kind_, o):
        ref = (st1, st2, st3)[kind_].at[g, o]
        return rc(ref, ref, st_s.at[g, kind_, o], st_r.at[g, kind_, o], dev_mate)

    def others(kind_):
        mine = z if kind_ == 1 else j
        return [lax.rem(mine + i, 4) for i in (1, 2, 3)]

    def st_start(g, kind_):
        for o in others(kind_):
            st_copy(g, kind_, o).start()

    def st_finish(g, kind_):
        for o in others(kind_):
            st_got(g, kind_, o).wait_recv()

    def st_send(g, kind_):
        if kind_ == 0:
            st1[g, j] = stat[g, j]
        elif kind_ == 1:
            st_finish(g, 0)
            total = st1[g, 0] + st1[g, 1] + st1[g, 2] + st1[g, 3]
            st_sum[g, 0] = total
            st2[g, z] = total
        else:
            st_finish(g, 1)
            total = st2[g, 0] + st2[g, 1] + st2[g, 2] + st2[g, 3]
            st_sum[g, 1] = total
            st3[g, j] = total
        st_start(g, kind_)

    @pl.loop(0, chunks + 2)
    def _(t):
        @pl.when(t < chunks)
        def _():
            gather_step(t)
            product(t, plane_low)
            reduce_first(t)

        @pl.when((t >= 1) & (t <= chunks))
        def _():
            reduce_second(t - 1)

        @pl.when(t >= 2)
        def _():
            reduce_last(t - 2)

        @pl.when(t == 3)
        def _():
            st_send(0, 0)

        @pl.when(t == 4)
        def _():
            st_send(0, 1)

        @pl.when(t == 5)
        def _():
            st_send(0, 2)

    spx = rc(spacc, spgot, spx_s.at[0], spx_r.at[0], dev_mate)
    spx.start()
    st_send(1, 0)
    st_finish(0, 2)
    spx.wait_recv()
    cross_c, pred_c, obs_c = [
        jnp.sum(spacc[i] + spgot[i], axis=1, keepdims=True) for i in range(3)
    ]
    root_c = jnp.sqrt(pred_c * obs_c)
    cos_c = cross_c / root_c
    spot_obs = (1.0 / root_c) / total_spots
    spot_prd = (cross_c / (pred_c * root_c)) / total_spots
    own_cos = jnp.sum(
        jnp.where(lax.div(lax.broadcasted_iota(jnp.int32, (256, 1), 0), 128) == k, cos_c, 0.0),
        axis=0, keepdims=True,
    )
    coef[...] = jnp.zeros_like(coef)

    def grad_make(q):
        g = lax.div(q, 2)
        inside = lax.rem(q, 2) * 2
        scale = 1.0 / (SLIDES * total_genes)
        for e in range(2):
            sums = st3[g, inside + e]
            cross, prd, obs = sums[:8], sums[8:16], sums[16:]
            root = jnp.sqrt(prd * obs)
            for i, v in enumerate((scale / root, scale * cross / (prd * root))):
                high = v.astype(b16).astype(f32)
                mid = (v - high).astype(b16).astype(f32)
                low = v - high - mid
                stack = jnp.concatenate([high, mid, low, jnp.zeros((8, 128), f32)], axis=0)
                coef[:32, (i * 2 + e) * 128 : (i * 2 + e) * 128 + 128] = stack.astype(b16)
        spread = jnp.dot(hot_stand, coef[...], preferred_element_type=f32)
        value = pred_h[q] * (spread[:, 256:] + spot_prd) - spot_h[q] * (spread[:, :256] + spot_obs)
        grad[q, j] = value.astype(b16)

    def gene_cos(g):
        total = jnp.zeros((8, 128), f32)
        for e in range(4):
            sums = st3[g, e]
            total = total + sums[:8] / jnp.sqrt(sums[8:16] * sums[16:])
        return jnp.sum(jnp.sum(total, axis=0, keepdims=True), axis=1, keepdims=True)

    def g_copy(q, m):
        if m == 0:
            return rc(grad.at[q, j], grad.at[q, j], g_s.at[q, 0], g_r.at[q, 0], dev_x)
        if m == 1:
            return rc(grad.at[q, j], grad.at[q, j], g_s.at[q, 1], g_r.at[q, 1], dev_y)
        if m == 2:
            at = grad.at[q, jx, pl.ds(0, 128)]
            return rc(at, at, g_s.at[q, 2], g_r.at[q, 2], dev_y)
        at = grad.at[q, jy, pl.ds(128, 128)]
        return rc(at, at, g_s.at[q, 3], g_r.at[q, 3], dev_x)

    def g_got(q, m):
        at = (
            grad.at[q, jx], grad.at[q, jy], grad.at[q, jd, pl.ds(0, 128)], grad.at[q, jd, pl.ds(128, 128)],
        )[m]
        return rc(at, at, g_s.at[q, m], g_r.at[q, m], dev_mate)

    def grad_send(q):
        grad_make(q)
        g_copy(q, 0).start()
        g_copy(q, 1).start()

    def grad_pass(q):
        g_got(q, 0).wait_recv()
        g_copy(q, 2).start()
        g_got(q, 1).wait_recv()
        g_copy(q, 3).start()

    def run_up(q, b):
        return rc(pass_on.at[q, b], sums_up.at[q, b], ru_s.at[q, b], ru_r.at[q, b], dev(lax.rem(z + 1, 4), j, k))

    def run_dn(q, b):
        return rc(pass_on.at[q, b], sums_dn.at[q, b], rd_s.at[q, b], rd_r.at[q, b], dev(lax.rem(z + 3, 4), j, k))

    def sums_first(q):
        g_got(q, 2).wait_recv()
        g_got(q, 3).wait_recv()
        product(q, plane_turn)

        @pl.when(z == 0)
        def _():
            for b in (3, 2, 1):
                pass_on[q, b] = part[q, b].astype(b16)
                run_up(q, b).start()

        @pl.when(z == 3)
        def _():
            for b in (0, 1, 2):
                pass_on[q, b] = part[q, b].astype(b16)
                run_dn(q, b).start()

    def sums_pass(q):
        def up(b):
            run_up(q, b).wait_recv()
            pass_on[q, b] = (part[q, b] + sums_up[q, b].astype(f32)).astype(b16)
            run_up(q, b).start()

        def dn(b):
            run_dn(q, b).wait_recv()
            pass_on[q, b] = (part[q, b] + sums_dn[q, b].astype(f32)).astype(b16)
            run_dn(q, b).start()

        @pl.when(z == 1)
        def _():
            up(3)
            up(2)
            dn(0)

        @pl.when(z == 2)
        def _():
            dn(0)
            dn(1)
            up(3)

    def other_copy(q):
        return rc(other.at[q], other_got.at[q], oth_s.at[q], oth_r.at[q], dev_mate)

    def expr_copy(q, kk):
        at = pl.ds(pl.multiple_of(kk * half + q * WIDTH, WIDTH), WIDTH)
        return pltpu.make_async_copy(expr_v.at[:, at], expr_out.at[:, at], out_sem.at[4 + q + 4 * (0 if kk is k else 1)])

    def use_sums(q, kk, sums):
        at = pl.ds(pl.multiple_of(kk * half + q * WIDTH, WIDTH), WIDTH)
        expr_v[:, at] = keep_col * sums
        expr_copy(q, kk).start()
        weighed = cell_v[:, at].astype(f32) * sums
        map_v[:, :128] = map_v[:, :128] + weighed[:, :128] + weighed[:, 128:]

    def sums_last(q):
        @pl.when(z > 0)
        def _():
            run_up(q, z).wait_recv()
            part[q, z] = part[q, z] + sums_up[q, z].astype(f32)

        @pl.when(z < 3)
        def _():
            run_dn(q, z).wait_recv()
            part[q, z] = part[q, z] + sums_dn[q, z].astype(f32)

        other[q] = part[q, z, rows(mate, 128), :]
        other_copy(q).start()
        use_sums(q, k, part[q, z, rows(k, 128), :])

    def sums_other(q):
        other_copy(q).wait_recv()
        use_sums(q, mate, other_got[q])

    map_v[:, :128] = jnp.zeros((128, 128), f32)

    grad_send(0)
    grad_send(1)
    st_send(1, 1)
    grad_pass(0)
    sums_first(0)
    grad_pass(1)
    st_send(1, 2)
    st_finish(1, 2)
    grad_send(2)
    grad_send(3)
    sums_first(1)
    sums_pass(0)
    grad_pass(2)
    grad_pass(3)
    loss_lane = lax.broadcasted_iota(jnp.int32, (1, 128), 1)
    gene_part = gene_cos(0) + gene_cos(1)
    small_src[2] = jnp.where(
        loss_lane == 0, own_cos, jnp.where(loss_lane == 1, gene_part, 0.0)
    )
    small_start(3, lambda t: small_src.at[2])
    sums_first(2)
    sums_first(3)
    sums_pass(1)

    @pl.loop(0, 4)
    def _(b):
        def add(q, acc):
            return acc + lax.dot_general(
                grad[q].reshape(1024, WIDTH), col[q, b], (((1,), (1,)), ((), ())), preferred_element_type=f32
            )

        back[b] = lax.fori_loop(0, chunks, add, jnp.zeros((1024, 256), f32)).reshape(4, 2, 128, 256)
        rc(back.at[b, :, mate], back_got.at[b], back_s.at[b], back_r.at[b], dev_mate).start()

    sums_last(0)
    sums_pass(2)
    sums_other(0)

    @pl.loop(0, 4)
    def _(b):
        rc(back.at[b, :, mate], back_got.at[b], back_s.at[b], back_r.at[b], dev_mate).wait_recv()
        for jj in range(4):
            back_low[jj, :, rows(b, 256)] = (back[b, jj, k] + back_got[b, jj]).astype(b16)

    def ret_copy(jj):
        return rc(back_low.at[jj], back_ret.at[j], ret_s.at[jj], ret_r.at[j], dev(z, jj, k))

    def ret_got(jj):
        return rc(back_low.at[jj], back_ret.at[jj], ret_s.at[jj], ret_r.at[jj], dev(z, jj, k))

    ret_copy(jd).start()
    ret_copy(jx).start()
    ret_copy(jy).start()
    back_ret[j] = back_low[j]

    sums_last(1)
    sums_pass(3)
    sums_other(1)
    sums_last(2)
    sums_other(2)
    small_wait(2, lambda t: reach_src.at[t])
    small_wait(3, lambda t: small_src.at[2])
    reach_row = jnp.sum(small[2], axis=0)
    sums3 = jnp.sum(small[3], axis=0)
    cos_total = jnp.sum(jnp.where(loss_lane == 0, sums3, 0.0), axis=1, keepdims=True)
    gene_total = jnp.sum(jnp.where(loss_lane == 1, sums3, 0.0), axis=1, keepdims=True) / 16.0
    gene_loss = 1.0 - gene_total / (SLIDES * total_genes)
    spot_loss = 1.0 - cos_total / total_spots
    total_loss = gene_loss + spot_loss + kl_loss
    loss_out[...] = jnp.where(
        loss_lane == 0, total_loss,
        jnp.where(loss_lane == 1, gene_loss, jnp.where(loss_lane == 2, spot_loss, jnp.where(loss_lane == 3, kl_loss, 0.0))),
    )
    sums_last(3)
    sums_other(3)
    filt_sum = jnp.sum(map_v[:, :128], axis=1, keepdims=True)
    keep_row = jax.nn.sigmoid(filt_in[...].astype(f32))
    filt_out[...] = keep_row * (1.0 - keep_row) * (lie(filt_sum) + reach_row)

    for jj in (jx, jy, jd):
        ret_got(jj).wait_recv()

    def map_rows(g, _):
        at = rows(g, 16)
        pick = lax.broadcasted_iota(jnp.int32, (16, 128), 0) + g * 16
        here = lax.broadcasted_iota(jnp.int32, (16, 128), 1)
        mg = jnp.sum(jnp.where(pick == here, jnp.broadcast_to(mass_row, (16, 128)), 0.0), 1, keepdims=True)
        inner = jnp.zeros((16, 128), f32)
        for d in range(32):
            b, jj, kk = d // 8, (d % 8) // 2, d % 2
            used = back_ret[jj, at, b * 256 + kk * 128 : b * 256 + kk * 128 + 128].astype(f32) + mg * keep_all[d]
            inner = inner + chance[at, d * 128 : d * 128 + 128] * used
            map_v[at, d * 128 : d * 128 + 128] = used
        inner = jnp.sum(inner, axis=1, keepdims=True)
        map_v[at, :] = chance[at, :] * (map_v[at, :] - inner)
        return 0

    mass_row = lie(mass_grad)
    lax.fori_loop(0, 8, map_rows, 0)
    map_copy = pltpu.make_async_copy(map_v, map_out, load_sem.at[3])
    map_copy.start()

    @pl.loop(0, chunks)
    def _(q):
        hand_copy(q).wait_send()
        spot_copy(q, k).wait_send()
        for m in range(4):
            p_copy(q, m).wait_send()
            g_copy(q, m).wait_send()
        pred_copy(q).wait_send()
        pred_got(q).wait_recv()
        pred_own(q).wait()
        other_copy(q).wait_send()
        expr_copy(q, k).wait()
        expr_copy(q, mate).wait()
        for b in range(4):
            @pl.when((z < 3) & (b <= z))
            def _():
                col_up(q, b).wait_send()

            @pl.when((z > 0) & (b >= z))
            def _():
                col_dn(q, b).wait_send()

            @pl.when(b > z)
            def _():
                run_up(q, b).wait_send()

            @pl.when(b < z)
            def _():
                run_dn(q, b).wait_send()

    for jj in (jx, jy, jd):
        low_copy(jj).wait_send()
        low_pass(jj).wait_send()
        ret_copy(jj).wait_send()
    low_pass(j).wait_send()
    for g in range(2):
        for kind_ in range(3):
            for o in others(kind_):
                st_copy(g, kind_, o).wait_send()
    spx.wait_send()
    for b in range(4):
        rc(back.at[b, :, mate], back_got.at[b], back_s.at[b], back_r.at[b], dev_mate).wait_send()
    map_copy.wait()


def fused_shards(map_logits, filter_logits, cell_expr, spot_expr, cell_slide, spot_slide, density_bins):
    f32, b16 = jnp.float32, jnp.bfloat16
    spots, cells = map_logits.shape
    genes = cell_expr.shape[1]
    chunks = genes // (2 * WIDTH)
    n = chunks
    V, S = pltpu.VMEM, pltpu.SemaphoreType.DMA
    any_, vmem = pl.BlockSpec(memory_space=pl.ANY), pl.BlockSpec(memory_space=pltpu.VMEM)
    scratch = [
        V((128, cells), f32),
        V((4, 128, 1024), b16),
        V((8, 128, 1024), b16),
        V((1024, 1024), b16),
        V((128, genes), b16),
        V((n, 128, WIDTH), b16),
        V((n, 4, 256, WIDTH), b16),
        V((n, 4, 256, WIDTH), f32),
        V((n, 2, 256, 128), b16),
        V((n, 2, 256, 128), b16),
        V((n, 2, 2, 256, 128), b16),
        V((n, 2, 256, 128), b16),
        V((n, 2, 256, 128), b16),
        V((n, 256, WIDTH), f32),
        V((128, genes), f32),
        V((n, 256, WIDTH), f32),
        V((2, 4, 24, 128), f32),
        V((2, 2, 24, 128), f32),
        V((2, 4, 24, 128), f32),
        V((2, 4, 24, 128), f32),
        V((2, 4, 24, 128), f32),
        V((3, 256, 128), f32),
        V((3, 256, 128), f32),
        V((128, 512), b16),
        V((n, 4, 256, WIDTH), b16),
        V((n, 4, 256, WIDTH), b16),
        V((n, 4, 256, WIDTH), b16),
        V((n, 4, 256, WIDTH), b16),
        V((4, 4, 2, 128, 256), f32),
        V((4, 4, 128, 256), f32),
        V((4, 128, 1024), b16),
        V((4, 128, 1024), b16),
        V((n, 128, WIDTH), f32),
        V((n, 128, WIDTH), f32),
        V((128, genes), f32),
        V((128, cells), f32),
        V((6, 1, 128), f32),
        V((4, 32, 1, 128), f32),
        V((32, 1, 128), f32),
        V((32, 1, 128), f32),
        S((4,)), S((12,)), S((n,)), S((n,)),
        S((n, 4)), S((n, 4)), S((n, 4)),
        S((8,)), S((8,)),
        S((n, 4)), S((n, 4)),
        S((n,)), S((n,)), S((n,)), S((n,)),
        S((2, 3, 4)), S((2, 3, 4)),
        S((2,)), S((2,)),
        S((n, 4)), S((n, 4)),
        S((n, 4)), S((n, 4)), S((n, 4)), S((n, 4)),
        S((4,)), S((4,)), S((4,)), S((4,)),
        S((n,)), S((n,)),
        S((4, 32)), S((4, 32)),
    ]
    predicted, map_grad, expr_grad, filt, loss = pl.pallas_call(
        functools.partial(fused_kernel, float(spots * 32), float(genes)),
        out_shape=(
            jax.ShapeDtypeStruct((spots, genes), f32),
            jax.ShapeDtypeStruct((spots, cells), f32),
            jax.ShapeDtypeStruct((spots, genes), f32),
            jax.ShapeDtypeStruct((1, 128), f32),
            jax.ShapeDtypeStruct((1, 128), f32),
        ),
        in_specs=[any_, vmem, any_, any_, vmem, vmem, vmem],
        out_specs=(any_, any_, any_, vmem, vmem),
        scratch_shapes=scratch,
        compiler_params=pltpu.CompilerParams(
            collective_id=0, has_side_effects=True, vmem_limit_bytes=60 * 2**20
        ),
        name="mapping_step",
    )(
        map_logits,
        filter_logits.reshape(1, 128),
        cell_expr,
        spot_expr,
        cell_slide.reshape(1, cells),
        spot_slide.reshape(1, 128),
        density_bins.reshape(1, 128),
    )
    return loss[0, :4], predicted, map_grad, expr_grad, filt.reshape(128)


def solution(mesh):
    both = P(("row", "col"))
    rows = P(("row", "col"), None)
    in_specs = (rows, both, rows, rows, P(), both, both)
    out_specs = (P(), rows, rows, rows, both)
    step = fused_shards if (mesh.shape["row"], mesh.shape["col"]) == (4, 8) else shards
    return jax.shard_map(step, mesh=mesh, in_specs=in_specs, out_specs=out_specs, check_vma=False)
```

```python
import functools

import jax
import jax.numpy as jnp
from jax import lax
from jax.experimental import pallas as pl
from jax.experimental.pallas import tpu as pltpu
from jax.sharding import PartitionSpec as P

SLIDES = 8
ROWS, PLANE, CORES = 4, 4, 2
WIDTH = 256
MESH = pl.DeviceIdType.MESH
FORWARD = (
    "h a0 h "
    "a1 p0 f0 "
    "h c3 s0 "
    "p1 f1 h "
    "l0 q0 q1 "
    "q2 q3 h "
    "s1 h p2 "
    "f2 l1 t0 "
    "h s2 h "
    "t1 l2 h "
    "p3 f3 t2 "
    "s3 l3 "
)
BACKWARD = (
    "gs0 gs1 st1 "
    "gp0 st2 sf0 "
    "gp1 st3 gs2 "
    "re0 gs3 sf1 "
    "sp0 gp2 re1 "
    "sf2 gp3 sf3 "
    "re2 sp1 bd0 "
    "bd1 bd2 bd3 "
    "lo0 sl0 ba0 "
    "ba1 ba2 ba3 "
    "rt so0 sp2 "
    "lo1 sl1 so1 "
    "sl2 lo2 sp3 "
    "so2 mp sl3 "
    "so3 "
)


def shards(map_logits, filter_logits, cell_expr, spot_expr, cell_slide, spot_slide, density_bins):
    highest = lax.Precision.HIGHEST
    both = ("row", "col")
    rows_count = lax.axis_size("row")
    cols_count = lax.axis_size("col")
    spot_dev, cell_total = map_logits.shape
    cell_dev = filter_logits.shape[0]
    spot_total = spot_dev * rows_count * cols_count
    gene_count = cell_expr.shape[1]
    keep_rate = jax.nn.sigmoid(filter_logits.astype(jnp.float32))
    scaled = (keep_rate[:, None] * cell_expr.astype(jnp.float32)).astype(jnp.bfloat16)
    scaled_col = lax.all_gather(scaled, "row", axis=0, tiled=True)
    allowed = spot_slide[:, None] == cell_slide[None, :]
    shifted = jnp.where(allowed, map_logits, -1e30)
    row_peak = jnp.max(shifted, axis=1, keepdims=True)
    raised = jnp.exp(shifted - row_peak)
    chances = raised / jnp.sum(raised, axis=1, keepdims=True)
    chance_low = chances.astype(jnp.bfloat16)
    by_col = chance_low.reshape(spot_dev, rows_count, cols_count, cell_dev)
    mapped = lax.all_to_all(by_col, "col", split_axis=2, concat_axis=0, tiled=True)
    mapped = mapped.reshape(spot_dev * cols_count, rows_count * cell_dev)
    keep_col = lax.all_gather(keep_rate, "row", axis=0, tiled=True)
    part_pred = jnp.dot(mapped, scaled_col, preferred_element_type=jnp.float32)
    part_mass = jnp.dot(mapped, keep_col, precision=highest, preferred_element_type=jnp.float32)
    predicted = lax.psum_scatter(part_pred, "col", scatter_dimension=0, tiled=True)
    mass = lax.psum_scatter(part_mass, "col", scatter_dimension=0, tiled=True)
    onehot = (spot_slide[:, None] == jnp.arange(SLIDES, dtype=jnp.int32)[None, :]).astype(
        jnp.float32
    )
    cross_term = predicted * spot_expr
    pred_sq = predicted * predicted
    obs_sq = spot_expr * spot_expr
    spot_cross = jnp.sum(cross_term, axis=1)
    spot_pred = jnp.sum(pred_sq, axis=1)
    spot_root = jnp.sqrt(spot_pred * jnp.sum(obs_sq, axis=1))
    spot_cos = spot_cross / spot_root
    bin_values = density_bins.astype(jnp.float32)
    log_term = bin_values * (jnp.log(bin_values) - jnp.log(mass))
    all_cross, all_pred, all_obs, slide_mass, slide_bins, slide_log, cos_total = lax.psum(
        (
            jnp.dot(onehot.T, cross_term, precision=highest),
            jnp.dot(onehot.T, pred_sq, precision=highest),
            jnp.dot(onehot.T, obs_sq, precision=highest),
            jnp.dot(onehot.T, mass, precision=highest),
            jnp.dot(onehot.T, bin_values, precision=highest),
            jnp.dot(onehot.T, log_term, precision=highest),
            jnp.sum(spot_cos),
        ),
        both,
    )
    gene_root = jnp.sqrt(all_pred * all_obs)
    gene_loss = 1.0 - jnp.mean(all_cross / gene_root)
    spot_loss = 1.0 - cos_total / spot_total
    kl_loss = jnp.mean(slide_log / slide_bins - jnp.log(slide_bins) + jnp.log(slide_mass))
    total_loss = gene_loss + spot_loss + kl_loss
    losses = jnp.stack([total_loss, gene_loss, spot_loss, kl_loss])
    gene_scale = 1.0 / (SLIDES * gene_count)
    coef_obs = jnp.dot(onehot, 1.0 / gene_root, precision=highest)
    coef_pred = jnp.dot(onehot, all_cross / (all_pred * gene_root), precision=highest)
    pred_grad = -gene_scale * (spot_expr * coef_obs - predicted * coef_pred)
    pred_grad = (
        pred_grad
        - (
            spot_expr / spot_root[:, None]
            - predicted * (spot_cross / (spot_pred * spot_root))[:, None]
        )
        / spot_total
    )
    mass_each = jnp.dot(onehot, slide_mass, precision=highest)
    bins_each = jnp.dot(onehot, slide_bins, precision=highest)
    mass_grad = (1.0 / mass_each - bin_values / (bins_each * mass)) / SLIDES
    grad_low = pred_grad.astype(jnp.bfloat16)
    mass_low = mass_grad.astype(jnp.bfloat16)
    grad_block = lax.all_gather(grad_low, "col", axis=0, tiled=True)
    mass_block = lax.all_gather(mass_low, "col", axis=0, tiled=True)
    back_map = lax.dot_general(
        grad_block, scaled_col, (((1,), (1,)), ((), ())), preferred_element_type=jnp.float32
    )
    back_map = back_map + mass_block.astype(jnp.float32)[:, None] * keep_col[None, :]
    back_low = back_map.astype(jnp.bfloat16)
    returned = lax.all_to_all(
        back_low.reshape(spot_dev * cols_count, rows_count, 1, cell_dev),
        "col",
        split_axis=0,
        concat_axis=2,
        tiled=True,
    ).reshape(spot_dev, cell_total)
    expr_part = lax.dot_general(
        mapped, grad_block, (((0,), (0,)), ((), ())), preferred_element_type=jnp.float32
    )
    mass_reach = lax.dot_general(
        mapped, mass_block, (((0,), (0,)), ((), ())), preferred_element_type=jnp.float32
    )
    expr_sum = lax.psum_scatter(expr_part, "row", scatter_dimension=0, tiled=True)
    mass_sum = lax.psum_scatter(mass_reach, "row", scatter_dimension=0, tiled=True)
    filter_grad = (
        keep_rate
        * (1.0 - keep_rate)
        * (jnp.sum(cell_expr.astype(jnp.float32) * expr_sum, axis=1) + mass_sum)
    )
    expr_grad = keep_rate[:, None] * expr_sum
    chance_grad = returned.astype(jnp.float32)
    inner_sum = jnp.sum(chances * chance_grad, axis=1, keepdims=True)
    map_grad = chances * (chance_grad - inner_sum)
    return (losses, predicted, map_grad, expr_grad, filter_grad)


def fused_kernel(
    total_spots, total_genes,
    logit_in, filt_in, cell_in, spot_in, cslide_in, sslide_in, bins_in,
    pred_out, map_out, expr_out, filt_out, loss_out,
    chance, own_low, plane_low, plane_turn, cell_v, hand, col, part, send1, early, send2, late,
    pred_h, spot_h, stat, st_sum, st1, st2, st3, spacc, spgot, coef, grad,
    sums_up, sums_dn, pass_on, back, back_got, back_low, back_ret, other, other_got,
    f_line, f_pair, f_all, keep_all, m_src, m_got, r_src, r_mate, r_plane_src, r_plane, r_line_src, r_line,
    l_src, l_mate, l_plane, l_line_src, l_line, filt_acc,
    load_sem, own_sem, hand_s, hand_r, up_s, dn_s, col_r, low_s, low_r, send1_s, send2_s, early_r, late_r,
    pred_s, pred_r, spot_s, spot_r, st_s, st_r, spx_s, spx_r, g_s, g_r, rs_s, rs_r, back_s, back_r,
    ret_s, ret_r, oth_s, oth_r, sm_s, sm_r,
):
    f32, b16 = jnp.float32, jnp.bfloat16
    chunks = col.shape[0]
    half = chunks * WIDTH
    units = WIDTH // 128
    z = lax.axis_index("row")
    c = lax.axis_index("col")
    j = lax.div(c, 2)
    k = lax.rem(c, 2)
    y = lax.div(j, 2)
    x = lax.rem(j, 2)
    mate = 1 - k

    def dev(zz, jj, kk):
        return (zz, jj * 2 + kk)

    jx = y * 2 + (1 - x)
    jy = (1 - y) * 2 + x
    jd = (1 - y) * 2 + (1 - x)
    dev_mate = dev(z, j, mate)
    dev_x = dev(z, jx, k)
    dev_y = dev(z, jy, k)
    dev_up = dev(lax.rem(z + 1, 4), j, k)
    dev_dn = dev(lax.rem(z + 3, 4), j, k)
    plane_others = (jx, jy, jd)
    line_others = [lax.rem(z + i, 4) for i in (1, 2, 3)]

    def rc(src, dst, ss, rs, to):
        return pltpu.make_async_remote_copy(
            src_ref=src, dst_ref=dst, send_sem=ss, recv_sem=rs, device_id=to, device_id_type=MESH
        )

    def got(ref, sem):
        rc(ref, ref, sem, sem, dev_mate).wait_recv()

    def sent(ref, sem):
        rc(ref, ref, sem, sem, dev_mate).wait_send()

    def rows(i, size):
        return pl.ds(pl.multiple_of(i * size, size), size)

    def lanes(kk, q):
        return pl.ds(pl.multiple_of(kk * half + q * WIDTH, WIDTH), WIDTH)

    load_cell = pltpu.make_async_copy(cell_in, cell_v, load_sem.at[0])
    load_logit = pltpu.make_async_copy(logit_in, chance, load_sem.at[1])
    load_spot = pltpu.make_async_copy(
        spot_in.at[:, pl.ds(pl.multiple_of(k * half, half), half)], spot_h.at[rows(k, 128)], load_sem.at[2]
    )
    barrier = pltpu.get_barrier_semaphore()
    for to in (
        dev_mate, dev_x, dev_y, dev(z, jd, k),
        dev(line_others[0], j, k), dev(line_others[1], j, k), dev(line_others[2], j, k),
    ):
        pl.semaphore_signal(barrier, inc=1, device_id=to, device_id_type=MESH)
    load_cell.start()
    load_logit.start()
    load_spot.start()

    eye = lax.broadcasted_iota(jnp.int32, (128, 128), 0) == lax.broadcasted_iota(
        jnp.int32, (128, 128), 1
    )
    lane = lax.broadcasted_iota(jnp.int32, (128, 128), 1)

    def stand(row):
        return jnp.sum(jnp.where(eye, jnp.broadcast_to(row, (128, 128)), 0.0), 1, keepdims=True)

    def lie(column):
        return jnp.sum(jnp.where(eye, jnp.broadcast_to(column, (128, 128)), 0.0), 0, keepdims=True)

    filt_row = filt_in[...].astype(f32)
    keep_col = stand(jax.nn.sigmoid(filt_row))
    slide_col = stand(sslide_in[...].astype(f32))
    bins_col = stand(bins_in[...].astype(f32))

    def hand_copy(q):
        return rc(hand.at[q], col.at[q, z, rows(k, 128)], hand_s, hand_r.at[q], dev_mate)

    def col_up(q, b):
        return rc(col.at[q, b], col.at[q, b], up_s, col_r.at[q, b], dev_up)

    def col_dn(q, b):
        return rc(col.at[q, b], col.at[q, b], dn_s, col_r.at[q, b], dev_dn)

    def scale_cells(q):
        hand[q] = (keep_col * cell_v[:, lanes(mate, q)].astype(f32)).astype(b16)
        col[q, z, rows(k, 128), :] = (keep_col * cell_v[:, lanes(k, q)].astype(f32)).astype(b16)

    def col_own(q):
        got(hand.at[q], hand_r.at[q])

        @pl.when(z < 3)
        def _():
            col_up(q, z).start()

        @pl.when(z > 0)
        def _():
            col_dn(q, z).start()

    hops = [(q, s) for q in range(chunks) for s in range(3)]

    def hop():
        q, s = hops.pop(0)

        @pl.when(z - 1 - s >= 0)
        def _():
            b = z - 1 - s
            got(col.at[q, b], col_r.at[q, b])

            @pl.when(z < 3)
            def _():
                col_up(q, b).start()

        @pl.when(z + 1 + s <= 3)
        def _():
            b = z + 1 + s
            got(col.at[q, b], col_r.at[q, b])

            @pl.when(z > 0)
            def _():
                col_dn(q, b).start()

    load_cell.wait()
    scale_cells(0)
    pl.semaphore_wait(barrier, 7)
    hand_copy(0).start()

    @pl.loop(1, chunks)
    def _(q):
        scale_cells(q)
        hand_copy(q).start()

    def spread(source, slots, which, i):
        for o in plane_others if which == "plane" else line_others:
            to = dev(z, o, k) if which == "plane" else dev(o, j, k)
            rc(source(o), slots.at[j if which == "plane" else z], sm_s.at[i], sm_r.at[i], to).start()

    def hand_over(source, slot, i):
        rc(source, slot, sm_s.at[i], sm_r.at[i], dev_mate).start()

    f_line[z] = filt_row
    spread(lambda o: f_line.at[z], f_line, "line", 0)

    load_logit.wait()

    def softmax_rows(g):
        at = rows(g, 16)
        logits = chance[at, :]
        pick = lax.broadcasted_iota(jnp.int32, (16, 128), 0) + g * 16
        here = lax.broadcasted_iota(jnp.int32, (16, 128), 1)
        slide = jnp.sum(
            jnp.where(pick == here, jnp.broadcast_to(sslide_in[...].astype(f32), (16, 128)), 0.0),
            1, keepdims=True,
        )
        allowed = slide == cslide_in[...].astype(f32)
        shifted = jnp.where(allowed, logits, -1e30)
        raised = jnp.exp(shifted - jnp.max(shifted, axis=1, keepdims=True))
        value = raised / jnp.sum(raised, axis=1, keepdims=True)
        chance[at, :] = value
        low = value.astype(b16)
        for b in range(4):
            for jj in range(4):
                own_low[jj, at, b * 256 : b * 256 + 256] = low[
                    :, b * 1024 + jj * 256 : b * 1024 + jj * 256 + 256
                ]

    def low_copy(jj):
        return rc(own_low.at[jj], plane_low.at[k, j], low_s.at[0], low_r.at[j], dev(z, jj, k))

    def low_pass(jj):
        return rc(plane_low.at[k, jj], plane_low.at[k, jj], low_s.at[1], low_r.at[4], dev_mate)

    pl.loop(0, 2)(softmax_rows)
    col_own(0)
    pl.loop(2, 8)(softmax_rows)
    low_copy(jd).start()
    low_copy(jx).start()
    low_copy(jy).start()
    for q in range(1, 2 * 256 // WIDTH):
        col_own(q)
    plane_low[k, j] = own_low[j]
    low_pass(j).start()
    spot_give = rc(
        spot_in.at[:, pl.ds(pl.multiple_of(mate * half, half), half)], spot_h.at[rows(k, 128)], spot_s, spot_r, dev_mate
    )
    spot_give.start()
    got(f_line.at[pl.ds(0, 3)], sm_r.at[0])
    f_pair[k] = f_line[...]
    hand_over(f_line, f_pair.at[k], 1)
    hop()
    got(f_line, sm_r.at[1])
    f_all[j] = f_pair[...]
    spread(lambda o: f_pair, f_all, "plane", 2)
    hop()

    got(f_all.at[pl.ds(0, 3)], sm_r.at[2])
    keep_all[...] = jax.nn.sigmoid(f_all[...])

    def of_cells(jj, kk, b):
        return own_low[jj, :, pl.ds(pl.multiple_of(b * 256 + kk * 128, 128), 128)].astype(f32)

    def split(d):
        return lax.div(d, 8), lax.rem(lax.div(d, 4), 2), lax.rem(d, 4)

    def add_mass(d, acc):
        jj, kk, b = split(d)
        return acc + of_cells(jj, kk, b) * keep_all[jj, kk, b]

    mass = jnp.sum(lax.fori_loop(0, 32, add_mass, jnp.zeros((128, 128), f32)), axis=1, keepdims=True)
    log_term = bins_col * (jnp.log(bins_col) - jnp.log(mass))
    kind = lax.div(lane, 8)
    of_slide = lax.rem(lane, 8) == slide_col.astype(jnp.int32)
    values = jnp.where(
        kind == 0, mass, jnp.where(kind == 1, bins_col, jnp.where(kind == 2, log_term, 0.0))
    )
    m_src[0] = jnp.sum(jnp.where(of_slide, values, 0.0), axis=0, keepdims=True)
    m_src[1] = sslide_in[...].astype(f32)
    hand_over(m_src, m_got, 3)
    hop()
    col_own(2 * 256 // WIDTH)
    got(m_src, sm_r.at[3])
    load_spot.wait()
    got(spot_h.at[rows(mate, 128)], spot_r)
    stat[...] = jnp.zeros_like(stat)
    chip_row = m_src[0] + m_got[0]
    for o in range(4):
        stat[0, o, 24:25, :] = chip_row

    first = jnp.where(k == 0, m_src[1], m_got[1])
    second = jnp.where(k == 0, m_got[1], m_src[1])
    hot_lie = (
        lax.broadcasted_iota(jnp.int32, (8, 256), 0).astype(f32)
        == jnp.broadcast_to(jnp.concatenate([first, second], axis=1), (8, 256))
    ).astype(b16)
    slides_col = jnp.concatenate([stand(first), stand(second)], axis=0)
    lane2 = lax.broadcasted_iota(jnp.int32, (256, 128), 1)
    hot_stand = ((lax.rem(lane2, 8) == slides_col.astype(jnp.int32)) & (lane2 < 24)).astype(b16)
    spacc[...] = jnp.zeros_like(spacc)
    coef[...] = jnp.zeros_like(coef)
    filt_acc[...] = jnp.zeros_like(filt_acc)

    def split_dot(a, v):
        high = v.astype(b16)
        rest = (v - high.astype(f32)).astype(b16)
        return jnp.dot(a, high, preferred_element_type=f32) + jnp.dot(a, rest, preferred_element_type=f32)

    def low_arrive():
        for jj in (jx, jy, jd):
            got(plane_low.at[k, jj], low_r.at[jj])
            low_pass(jj).start()

    def low_all():
        got(plane_low.at[mate], low_r.at[4])

    def product(q, left):
        right = (col if left is plane_low else grad)[q].reshape(1024, WIDTH)

        @pl.loop(0, 2)
        def _(h):
            if left is plane_low:
                block = left[h].reshape(512, 1024)
                part[q, h] = jnp.dot(block, right, preferred_element_type=f32).reshape(4, 128, WIDTH)
            else:
                block = left[rows(h, 512), :]
                part[q, h] = jnp.dot(block, right, preferred_element_type=f32).reshape(4, 128, WIDTH)

    def reduce_first(q):
        for i, (core, owner, to, sem, slot) in enumerate((
            (0, jd, dev_x, early_r.at[q, 0], early.at[q, 0]),
            (1, jd, dev_y, early_r.at[q, 1], early.at[q, 1]),
            (0, jx, dev_x, late_r.at[q], late.at[q, 0]),
            (1, jy, dev_y, late_r.at[q], late.at[q, 1]),
        )):
            send1[q, i] = part[q, core, owner].astype(b16)
            rc(send1.at[q, i], slot, send1_s, sem, to).start()

    def reduce_second(q):
        for i, (owner, to) in enumerate(((jy, dev_y), (jx, dev_x))):
            got(early.at[q, i], early_r.at[q, i])
            send2[q, i] = (part[q, i, owner] + early[q, i].astype(f32)).astype(b16)
            rc(send2.at[q, i], late.at[q, 2 + i], send2_s, late_r.at[q], to).start()

    def pred_give(q):
        return rc(
            pred_h.at[rows(mate, 128), pl.ds(q * WIDTH, WIDTH)], pred_out.at[:, lanes(k, q)], pred_s, pred_r, dev_mate
        )

    def pred_own(q):
        return pltpu.make_async_copy(
            pred_h.at[rows(k, 128), pl.ds(q * WIDTH, WIDTH)], pred_out.at[:, lanes(k, q)], own_sem
        )

    def reduce_last(q):
        got(late.at[q], late_r.at[q])
        for i in range(2):
            pred_h[i * 128 : i * 128 + 128, q * WIDTH : q * WIDTH + WIDTH] = part[q, i, j] + (
                late[q, i].astype(f32) + late[q, 2 + i].astype(f32)
            )
        pred_give(q).start()
        pred_own(q).start()
        for e in range(units):
            at = slice(q * WIDTH + e * 128, q * WIDTH + e * 128 + 128)
            g, o = divmod(q * units + e, 4)
            pr = pred_h[:, at]
            sp = spot_h[:, at]
            for i, v in enumerate((pr * sp, pr * pr, sp * sp)):
                spacc[i] = spacc[i] + v
                stat[g, o, i * 8 : i * 8 + 8] = split_dot(hot_lie, v)

    def st_send(g, i):
        slots = (st1, st2, st3)[i]
        if i == 0:
            st1[g, j] = stat[g, j]
        else:
            prior = (st1, st2)[i - 1]
            got(prior.at[g, pl.ds(0, 3)], st_r.at[g, i - 1])
            total = prior[g, 0] + prior[g, 1] + prior[g, 2] + prior[g, 3]
            st_sum[g, i - 1] = total
            if i == 1:
                st2[g, z] = total
            else:
                st3[g, j] = total
        for o in line_others if i == 1 else plane_others:
            src = stat.at[g, o] if i == 0 else st_sum.at[g, i - 1]
            to = dev(o, j, k) if i == 1 else dev(z, o, k)
            rc(src, slots.at[g, z if i == 1 else j], st_s.at[g, i], st_r.at[g, i], to).start()

    def st_finish(g):
        got(st3.at[g, pl.ds(0, 3)], st_r.at[g, 2])

    steps = {
        "c": lambda q: col_own(q), "h": lambda q: hop(), "p": lambda q: product(q, plane_low),
        "f": reduce_first, "s": reduce_second, "l": reduce_last,
        "t": lambda i: st_send(0, i), "a": lambda i: low_arrive() if i == 0 else low_all(),
        "q": lambda i: turn(i),
    }

    def turn(i):
        for kk in range(2):
            plane_turn[:, (kk * 4 + i) * 128 : (kk * 4 + i) * 128 + 128] = plane_low[kk, i].astype(f32).T.astype(b16)

    for word in FORWARD.split():
        steps[word[0]](int(word[1:]) if len(word) > 1 else 0)

    spx = rc(spacc, spgot, spx_s, spx_r, dev_mate)
    spx.start()
    st_send(1, 0)

    sums_row = st_sum[0, 1, 24:25, :]
    each = jnp.broadcast_to(sums_row, (128, 128))
    mass_each = jnp.sum(jnp.where(of_slide & (kind == 0), each, 0.0), 1, keepdims=True)
    bins_each = jnp.sum(jnp.where(of_slide & (kind == 1), each, 0.0), 1, keepdims=True)
    mass_grad = (1.0 / mass_each - bins_col / (bins_each * mass)) / SLIDES
    mass_grad = mass_grad.astype(b16).astype(f32)
    slide8 = lax.broadcasted_iota(jnp.int32, (8, 128), 0)
    lane8 = lax.broadcasted_iota(jnp.int32, (8, 128), 1)

    def by_slide(begin):
        return jnp.sum(
            jnp.where(lane8 == slide8 + begin, jnp.broadcast_to(sums_row, (8, 128)), 0.0), 1, keepdims=True
        )

    mass_s, bins_s, log_s = by_slide(0), by_slide(8), by_slide(16)
    kl_loss = jnp.sum(log_s / bins_s - jnp.log(bins_s) + jnp.log(mass_s), axis=0, keepdims=True) / SLIDES

    def reach_make():
        @pl.loop(0, 32)
        def _(d):
            jj, kk, b = split(d)
            r_src[kk, jj, b] = jnp.sum(of_cells(jj, kk, b) * mass_grad, axis=0, keepdims=True)

        hand_over(r_src.at[mate], r_mate, 4)

    def reach_plane():
        got(r_mate, sm_r.at[4])
        r_plane_src[...] = r_src[k] + r_mate[...]
        r_plane[j] = r_plane_src[j]
        spread(lambda o: r_plane_src.at[o], r_plane, "plane", 5)

    def reach_line():
        got(r_plane.at[pl.ds(0, 3)], sm_r.at[5])
        r_line_src[...] = r_plane[0] + r_plane[1] + r_plane[2] + r_plane[3]
        r_line[z] = r_line_src[z]
        spread(lambda o: r_line_src.at[o], r_line, "line", 6)

    st_finish(0)
    got(spgot, spx_r)
    cross_c, pred_c, obs_c = [
        jnp.sum(spacc[i] + spgot[i], axis=1, keepdims=True) for i in range(3)
    ]
    root_c = jnp.sqrt(pred_c * obs_c)
    cos_c = cross_c / root_c
    spot_obs = (1.0 / root_c) / total_spots
    spot_prd = (cross_c / (pred_c * root_c)) / total_spots

    def grad_make(q):
        scale = 1.0 / (SLIDES * total_genes)
        for e in range(units):
            g, o = divmod(q * units + e, 4)
            sums = st3[g, o]
            cross, prd, obs = sums[:8], sums[8:16], sums[16:24]
            root = jnp.sqrt(prd * obs)
            for i, v in enumerate((scale / root, scale * cross / (prd * root))):
                high = v.astype(b16).astype(f32)
                mid = (v - high).astype(b16).astype(f32)
                low = v - high - mid
                stack = jnp.concatenate([high, mid, low, jnp.zeros((8, 128), f32)], axis=0)
                coef[:32, (i * units + e) * 128 : (i * units + e) * 128 + 128] = stack.astype(b16)
        each_spot = jnp.dot(hot_stand, coef[...], preferred_element_type=f32)
        at = slice(q * WIDTH, q * WIDTH + WIDTH)
        value = pred_h[:, at] * (each_spot[:, WIDTH:] + spot_prd) - spot_h[:, at] * (each_spot[:, :WIDTH] + spot_obs)
        value = value.astype(b16)
        grad[q, 0, j] = value[:128]
        grad[q, 1, j] = value[128:]

    def gene_cos():
        total = jnp.zeros((8, 128), f32)
        for g in range(2):
            for e in range(4):
                sums = st3[g, e]
                total = total + sums[:8] / jnp.sqrt(sums[8:16] * sums[16:24])
        return jnp.sum(jnp.sum(total, axis=0, keepdims=True), axis=1, keepdims=True)

    def grad_send(q):
        grad_make(q)
        at = grad.at[q, :, j]
        rc(at, at, g_s.at[0], g_r.at[q, 0], dev_x).start()
        rc(at, at, g_s.at[1], g_r.at[q, 1], dev_y).start()

    def grad_pass(q):
        got(grad.at[q, :, jx], g_r.at[q, 0])
        at = grad.at[q, 0, jx]
        rc(at, at, g_s.at[2], g_r.at[q, 2], dev_y).start()
        got(grad.at[q, :, jy], g_r.at[q, 1])
        at = grad.at[q, 1, jy]
        rc(at, at, g_s.at[3], g_r.at[q, 2], dev_x).start()

    def run_up(q, b):
        return rc(pass_on.at[q, b], sums_up.at[q, b], rs_s, rs_r.at[q, b + 1], dev_up)

    def run_dn(q, b):
        return rc(pass_on.at[q, b], sums_dn.at[q, b], rs_s, rs_r.at[q, b], dev_dn)

    def block(q, b):
        return part[q, lax.div(b, 2) if not isinstance(b, int) else b // 2, pl.ds(2 * (b % 2 if isinstance(b, int) else lax.rem(b, 2)), 2)].reshape(256, WIDTH)

    def sums_first(q):
        got(grad.at[q, :, jd], g_r.at[q, 2])
        product(q, plane_turn)

        @pl.when(z == 0)
        def _():
            for b in (3, 2, 1):
                pass_on[q, b] = block(q, b).astype(b16)
                run_up(q, b).start()

        @pl.when(z == 3)
        def _():
            for b in (0, 1, 2):
                pass_on[q, b] = block(q, b).astype(b16)
                run_dn(q, b).start()

    def sums_pass(q):
        def up(b):
            got(sums_up.at[q, b], rs_r.at[q, b + 1])
            pass_on[q, b] = (block(q, b) + sums_up[q, b].astype(f32)).astype(b16)
            run_up(q, b).start()

        def dn(b):
            got(sums_dn.at[q, b], rs_r.at[q, b])
            pass_on[q, b] = (block(q, b) + sums_dn[q, b].astype(f32)).astype(b16)
            run_dn(q, b).start()

        @pl.when(z == 1)
        def _():
            up(3)
            up(2)
            dn(0)

        @pl.when(z == 2)
        def _():
            dn(0)
            dn(1)
            up(3)

    def other_give(q):
        return rc(other.at[q], other_got.at[q], oth_s, oth_r.at[q], dev_mate)

    def use_sums(q, kk, sums):
        at = lanes(kk, q)
        expr_out[:, at] = keep_col * sums
        weighed = cell_v[:, at].astype(f32) * sums
        for e in range(units):
            filt_acc[...] = filt_acc[...] + weighed[:, e * 128 : e * 128 + 128]

    def sums_last(q):
        other[q] = part[q, lax.div(z, 2), 2 * lax.rem(z, 2) + mate]
        own_at = (q, lax.div(z, 2), 2 * lax.rem(z, 2) + k)

        @pl.when(z > 0)
        def _():
            got(sums_up.at[q, z], rs_r.at[q, z + 1])
            other[q] = other[q] + sums_up[q, z, rows(mate, 128), :].astype(f32)
            part[own_at] = part[own_at] + sums_up[q, z, rows(k, 128), :].astype(f32)

        @pl.when(z < 3)
        def _():
            got(sums_dn.at[q, z], rs_r.at[q, z])
            other[q] = other[q] + sums_dn[q, z, rows(mate, 128), :].astype(f32)
            part[own_at] = part[own_at] + sums_dn[q, z, rows(k, 128), :].astype(f32)

        other_give(q).start()
        use_sums(q, k, part[own_at])

    def sums_other(q):
        got(other_got.at[q], oth_r.at[q])
        use_sums(q, mate, other_got[q])

    def back_dot(b):
        pairs = 256 // WIDTH

        def add(q, acc):
            if pairs == 1:
                left, right = grad[q].reshape(1024, WIDTH), col[q, b]
            else:
                left = jnp.concatenate([grad[2 * q + i].reshape(1024, WIDTH) for i in range(2)], axis=1)
                right = jnp.concatenate([col[2 * q + i, b] for i in range(2)], axis=1)
            return acc + lax.dot_general(left, right, (((1,), (1,)), ((), ())), preferred_element_type=f32)

        total = lax.fori_loop(0, chunks // pairs, add, jnp.zeros((1024, 256), f32))
        back[b] = total.reshape(2, 4, 128, 256)
        rc(back.at[b, mate], back_got.at[b], back_s, back_r.at[b], dev_mate).start()

    def back_add(b):
        got(back_got.at[b], back_r.at[b])
        for jj in range(4):
            back_low[jj, :, rows(b, 256)] = (back[b, k, jj] + back_got[b, jj]).astype(b16)

    def ret_send():
        for jj in (jd, jx, jy):
            rc(back_low.at[jj], back_ret.at[j], ret_s, ret_r, dev(z, jj, k)).start()
        back_ret[j] = back_low[j]

    loss_lane = lax.broadcasted_iota(jnp.int32, (1, 128), 1)

    def loss_mate():
        own_cos = jnp.sum(cos_c, axis=0, keepdims=True)
        l_src[...] = jnp.where(loss_lane == 0, own_cos, jnp.where(loss_lane == 1, gene_cos(), 0.0))
        hand_over(l_src, l_mate, 7)
        l_plane[j] = l_src[...]
        spread(lambda o: l_src, l_plane, "plane", 8)

    def loss_line():
        got(l_plane.at[pl.ds(0, 3)], sm_r.at[8])
        total = l_plane[0] + l_plane[1] + l_plane[2] + l_plane[3]
        l_line_src[...] = total
        l_line[z] = total
        spread(lambda o: l_line_src, l_line, "line", 9)

    def loss_end():
        got(l_line.at[pl.ds(0, 3)], sm_r.at[9])
        got(l_mate, sm_r.at[7])
        cos_row = l_line[0] + l_line[1] + l_line[2] + l_line[3]
        gene_row = l_src[...] + l_mate[...]
        cos_total = jnp.sum(jnp.where(loss_lane == 0, cos_row, 0.0), axis=1, keepdims=True)
        gene_total = jnp.sum(jnp.where(loss_lane == 1, gene_row, 0.0), axis=1, keepdims=True)
        gene_loss = 1.0 - gene_total / (SLIDES * total_genes)
        spot_loss = 1.0 - cos_total / total_spots
        total_loss = gene_loss + spot_loss + kl_loss
        picked = jnp.where(loss_lane == 2, spot_loss, jnp.where(loss_lane == 3, kl_loss, 0.0))
        loss_out[...] = jnp.where(loss_lane == 0, total_loss, jnp.where(loss_lane == 1, gene_loss, picked))

    mass_row = lie(mass_grad)

    def map_rows(g):
        at = rows(g, 16)
        pick = lax.broadcasted_iota(jnp.int32, (16, 128), 0) + g * 16
        here = lax.broadcasted_iota(jnp.int32, (16, 128), 1)
        mg = jnp.sum(jnp.where(pick == here, jnp.broadcast_to(mass_row, (16, 128)), 0.0), 1, keepdims=True)
        inner = jnp.zeros((16, 128), f32)
        for d in range(32):
            b, jj, kk = d // 8, (d % 8) // 2, d % 2
            used = back_ret[jj, at, b * 256 + kk * 128 : b * 256 + kk * 128 + 128].astype(f32) + mg * keep_all[jj, kk, b]
            inner = inner + chance[at, d * 128 : d * 128 + 128] * used
            map_out[at, d * 128 : d * 128 + 128] = used
        inner = jnp.sum(inner, axis=1, keepdims=True)
        map_out[at, :] = chance[at, :] * (map_out[at, :] - inner)

    def map_all():
        got(back_ret.at[pl.ds(0, 3)], ret_r)
        pl.loop(0, 8)(map_rows)

    back_steps = {
        "gs": grad_send, "gp": grad_pass, "sf": sums_first, "sp": sums_pass, "sl": sums_last, "so": sums_other,
        "st": lambda i: st_send(1, i) if i < 3 else st_finish(1), "bd": back_dot, "ba": back_add,
        "rt": lambda i: ret_send(), "mp": lambda i: map_all(),
        "re": lambda i: (reach_make, reach_plane, reach_line)[i](),
        "lo": lambda i: (loss_mate, loss_line, loss_end)[i](),
    }
    for word in BACKWARD.split():
        back_steps[word[:2]](int(word[2:]) if len(word) > 2 else 0)

    got(r_line.at[pl.ds(0, 3)], sm_r.at[6])
    reach_row = r_line[0] + r_line[1] + r_line[2] + r_line[3]
    filt_sum = jnp.sum(filt_acc[...], axis=1, keepdims=True)
    keep_row = jax.nn.sigmoid(filt_in[...].astype(f32))
    filt_out[...] = keep_row * (1.0 - keep_row) * (lie(filt_sum) + reach_row)

    sent(hand, hand_s)
    spot_give.wait_send()
    sent(send1, send1_s)
    sent(send2, send2_s)
    sent(pred_h.at[rows(mate, 128)], pred_s)
    got(pred_out.at[:, pl.ds(pl.multiple_of(mate * half, half), half)], pred_r)
    pltpu.make_async_copy(
        pred_h.at[rows(k, 128)], pred_out.at[:, pl.ds(pl.multiple_of(k * half, half), half)], own_sem
    ).wait()
    for i in range(2):
        sent(grad.at[:, :, j], g_s.at[i])
    sent(grad.at[:, 0, jx], g_s.at[2])
    sent(grad.at[:, 1, jy], g_s.at[3])
    for i in range(3):
        @pl.when(z == i)
        def _():
            sent(col.at[:, pl.ds(0, i + 1)], up_s)

        @pl.when(z == 3 - i)
        def _():
            sent(col.at[:, pl.ds(3 - i, i + 1)], dn_s)
    sent(pass_on.at[:, pl.ds(0, 3)], rs_s)
    sent(plane_low.at[k, pl.ds(0, 3)], low_s.at[0])
    sent(plane_low.at[k], low_s.at[1])
    for g in range(2):
        for i in range(3):
            sent(st1.at[g, pl.ds(0, 3)], st_s.at[g, i])
    spx.wait_send()
    sent(back_got, back_s)
    sent(back_low.at[pl.ds(0, 3)], ret_s)
    sent(other, oth_s)
    for i, ref in enumerate((
        f_line.at[pl.ds(0, 3)], f_line, f_all.at[pl.ds(0, 3)], m_src, r_mate, r_plane.at[pl.ds(0, 3)],
        r_line.at[pl.ds(0, 3)], l_mate, l_plane.at[pl.ds(0, 3)], l_line.at[pl.ds(0, 3)],
    )):
        sent(ref, sm_s.at[i])


def fused_shards(map_logits, filter_logits, cell_expr, spot_expr, cell_slide, spot_slide, density_bins):
    f32, b16 = jnp.float32, jnp.bfloat16
    spots, cells = map_logits.shape
    genes = cell_expr.shape[1]
    n = genes // (2 * WIDTH)
    V, S = pltpu.VMEM, pltpu.SemaphoreType.DMA
    any_, vmem = pl.BlockSpec(memory_space=pl.ANY), pl.BlockSpec(memory_space=pltpu.VMEM)
    one = S(())
    scratch = [
        V((128, cells), f32),
        V((4, 128, 1024), b16),
        V((2, 4, 128, 1024), b16),
        V((1024, 1024), b16),
        V((128, genes), b16),
        V((n, 128, WIDTH), b16),
        V((n, 4, 256, WIDTH), b16),
        V((n, 2, 4, 128, WIDTH), f32),
        V((n, 4, 128, WIDTH), b16),
        V((n, 2, 128, WIDTH), b16),
        V((n, 2, 128, WIDTH), b16),
        V((n, 4, 128, WIDTH), b16),
        V((256, genes // 2), f32),
        V((256, genes // 2), f32),
        V((2, 4, 32, 128), f32),
        V((2, 2, 32, 128), f32),
        V((2, 4, 32, 128), f32),
        V((2, 4, 32, 128), f32),
        V((2, 4, 32, 128), f32),
        V((3, 256, 128), f32),
        V((3, 256, 128), f32),
        V((128, 2 * WIDTH), b16),
        V((n, 2, 4, 128, WIDTH), b16),
        V((n, 4, 256, WIDTH), b16),
        V((n, 4, 256, WIDTH), b16),
        V((n, 4, 256, WIDTH), b16),
        V((4, 2, 4, 128, 256), f32),
        V((4, 4, 128, 256), f32),
        V((4, 128, 1024), b16),
        V((4, 128, 1024), b16),
        V((n, 128, WIDTH), f32),
        V((n, 128, WIDTH), f32),
        V((4, 1, 128), f32),
        V((2, 4, 1, 128), f32),
        V((4, 2, 4, 1, 128), f32),
        V((4, 2, 4, 1, 128), f32),
        V((2, 1, 128), f32),
        V((2, 1, 128), f32),
        V((2, 4, 4, 1, 128), f32),
        V((4, 4, 1, 128), f32),
        V((4, 4, 1, 128), f32),
        V((4, 4, 1, 128), f32),
        V((4, 1, 128), f32),
        V((4, 1, 128), f32),
        V((1, 128), f32),
        V((1, 128), f32),
        V((4, 1, 128), f32),
        V((1, 128), f32),
        V((4, 1, 128), f32),
        V((128, 128), f32),
        S((3,)), one, one, S((n,)), one, one, S((n, 4)), S((2,)), S((5,)),
        one, one, S((n, 2)), S((n,)),
        one, one, one, one, S((2, 3)), S((2, 3)), one, one,
        S((4,)), S((n, 3)), one, S((n, 5)), one, S((4,)),
        one, one, one, S((n,)), S((10,)), S((10,)),
    ]
    predicted, map_grad, expr_grad, filt, loss = pl.pallas_call(
        functools.partial(fused_kernel, float(spots * 32), float(genes)),
        out_shape=(
            pltpu.VMEM((spots, genes), f32),
            pltpu.VMEM((spots, cells), f32),
            pltpu.VMEM((spots, genes), f32),
            jax.ShapeDtypeStruct((1, 128), f32),
            jax.ShapeDtypeStruct((1, 128), f32),
        ),
        in_specs=[any_, vmem, any_, any_, vmem, vmem, vmem],
        out_specs=(vmem, vmem, vmem, vmem, vmem),
        scratch_shapes=scratch,
        compiler_params=pltpu.CompilerParams(
            collective_id=0, has_side_effects=True, vmem_limit_bytes=52 * 2**20
        ),
        name="mapping_step",
    )(
        map_logits,
        filter_logits.reshape(1, 128),
        cell_expr,
        spot_expr,
        cell_slide.reshape(1, cells),
        spot_slide.reshape(1, 128),
        density_bins.reshape(1, 128),
    )
    return loss[0, :4], predicted, map_grad, expr_grad, filt.reshape(128)


def solution(mesh):
    both = P(("row", "col"))
    rows = P(("row", "col"), None)
    in_specs = (rows, both, rows, rows, P(), both, both)
    out_specs = (P(), rows, rows, rows, both)
    step = fused_shards if (mesh.shape["row"], mesh.shape["col"]) == (4, 8) else shards
    return jax.shard_map(step, mesh=mesh, in_specs=in_specs, out_specs=out_specs, check_vma=False)
```

```python
import functools

import jax
import jax.numpy as jnp
from jax import lax
from jax.experimental import pallas as pl
from jax.experimental.pallas import tpu as pltpu
from jax.sharding import PartitionSpec as P

SLIDES = 8
ROWS, PLANE, CORES = 4, 4, 2
WIDTH = 128
MESH = pl.DeviceIdType.MESH
ORDER = (
    "c0 c1 x1 c2",
    "x0 x2 i0 x3",
    "w0 h c3 h",
    "h h c4 h",
    "w1 h h a2",
    "h h h c5",
    "a0 a1 i1 h",
    "c6 a3 P0 f0",
    "h f1 h P2",
    "f3 f2 i2 s0",
    "h S0 h s1",
    "h c7 S1 i3",
    "s3 S2 S3 h",
    "s2 h h P4",
    "f5 l0 f4 l3",
    "l2 k3 h h",
    "h k2 l1 k0",
    "s5 k1 t0 S5",
    "p6 f6 h h",
    "p7 f7 t1 s4",
    "S4 q2 q0 S6",
    "l5 s6 S7 k5",
    "s7 l4 t2 l6",
    "k6 k4 l7 k7",
    "z0 z2 g0 z1",
    "g1 y1 m0 n0",
    "g3 q1 m1 q3",
    "y2 r0 n1 g2",
    "n3 e0 m3 y3",
    "g5 r1 m2 n2",
    "g4 o0 V0 g6",
    "g7 m5 D0 n5",
    "R2 n4 m4 D1",
    "E0 E2 U1 n6",
    "m6 n7 m7 E1",
    "e1 U0 R4 r6",
    "U2 r7 b3 U3",
    "V2 V1 V4 D3",
    "b0 D2 b1 b2",
    "V3 E3 A0 V5",
    "A1 L0 D5 A3",
    "A2 T0 D4 E5",
    "U6 e2 E4 L3",
    "U5 L1 o1 E7",
    "L2 U4 L5 U7",
    "V7 V6 D6 D7",
    "L4 E6 O3 O2",
    "M0 L6 L7 O1",
    "o2 O0 O5 O4",
    "O6 O7",
)


def shards(map_logits, filter_logits, cell_expr, spot_expr, cell_slide, spot_slide, density_bins):
    highest = lax.Precision.HIGHEST
    both = ("row", "col")
    rows_count = lax.axis_size("row")
    cols_count = lax.axis_size("col")
    spot_dev, cell_total = map_logits.shape
    cell_dev = filter_logits.shape[0]
    spot_total = spot_dev * rows_count * cols_count
    gene_count = cell_expr.shape[1]
    keep_rate = jax.nn.sigmoid(filter_logits.astype(jnp.float32))
    scaled = (keep_rate[:, None] * cell_expr.astype(jnp.float32)).astype(jnp.bfloat16)
    scaled_col = lax.all_gather(scaled, "row", axis=0, tiled=True)
    allowed = spot_slide[:, None] == cell_slide[None, :]
    shifted = jnp.where(allowed, map_logits, -1e30)
    row_peak = jnp.max(shifted, axis=1, keepdims=True)
    raised = jnp.exp(shifted - row_peak)
    chances = raised / jnp.sum(raised, axis=1, keepdims=True)
    chance_low = chances.astype(jnp.bfloat16)
    by_col = chance_low.reshape(spot_dev, rows_count, cols_count, cell_dev)
    mapped = lax.all_to_all(by_col, "col", split_axis=2, concat_axis=0, tiled=True)
    mapped = mapped.reshape(spot_dev * cols_count, rows_count * cell_dev)
    keep_col = lax.all_gather(keep_rate, "row", axis=0, tiled=True)
    part_pred = jnp.dot(mapped, scaled_col, preferred_element_type=jnp.float32)
    part_mass = jnp.dot(mapped, keep_col, precision=highest, preferred_element_type=jnp.float32)
    predicted = lax.psum_scatter(part_pred, "col", scatter_dimension=0, tiled=True)
    mass = lax.psum_scatter(part_mass, "col", scatter_dimension=0, tiled=True)
    onehot = (spot_slide[:, None] == jnp.arange(SLIDES, dtype=jnp.int32)[None, :]).astype(
        jnp.float32
    )
    cross_term = predicted * spot_expr
    pred_sq = predicted * predicted
    obs_sq = spot_expr * spot_expr
    spot_cross = jnp.sum(cross_term, axis=1)
    spot_pred = jnp.sum(pred_sq, axis=1)
    spot_root = jnp.sqrt(spot_pred * jnp.sum(obs_sq, axis=1))
    spot_cos = spot_cross / spot_root
    bin_values = density_bins.astype(jnp.float32)
    log_term = bin_values * (jnp.log(bin_values) - jnp.log(mass))
    all_cross, all_pred, all_obs, slide_mass, slide_bins, slide_log, cos_total = lax.psum(
        (
            jnp.dot(onehot.T, cross_term, precision=highest),
            jnp.dot(onehot.T, pred_sq, precision=highest),
            jnp.dot(onehot.T, obs_sq, precision=highest),
            jnp.dot(onehot.T, mass, precision=highest),
            jnp.dot(onehot.T, bin_values, precision=highest),
            jnp.dot(onehot.T, log_term, precision=highest),
            jnp.sum(spot_cos),
        ),
        both,
    )
    gene_root = jnp.sqrt(all_pred * all_obs)
    gene_loss = 1.0 - jnp.mean(all_cross / gene_root)
    spot_loss = 1.0 - cos_total / spot_total
    kl_loss = jnp.mean(slide_log / slide_bins - jnp.log(slide_bins) + jnp.log(slide_mass))
    total_loss = gene_loss + spot_loss + kl_loss
    losses = jnp.stack([total_loss, gene_loss, spot_loss, kl_loss])
    gene_scale = 1.0 / (SLIDES * gene_count)
    coef_obs = jnp.dot(onehot, 1.0 / gene_root, precision=highest)
    coef_pred = jnp.dot(onehot, all_cross / (all_pred * gene_root), precision=highest)
    pred_grad = -gene_scale * (spot_expr * coef_obs - predicted * coef_pred)
    pred_grad = (
        pred_grad
        - (
            spot_expr / spot_root[:, None]
            - predicted * (spot_cross / (spot_pred * spot_root))[:, None]
        )
        / spot_total
    )
    mass_each = jnp.dot(onehot, slide_mass, precision=highest)
    bins_each = jnp.dot(onehot, slide_bins, precision=highest)
    mass_grad = (1.0 / mass_each - bin_values / (bins_each * mass)) / SLIDES
    grad_low = pred_grad.astype(jnp.bfloat16)
    mass_low = mass_grad.astype(jnp.bfloat16)
    grad_block = lax.all_gather(grad_low, "col", axis=0, tiled=True)
    mass_block = lax.all_gather(mass_low, "col", axis=0, tiled=True)
    back_map = lax.dot_general(
        grad_block, scaled_col, (((1,), (1,)), ((), ())), preferred_element_type=jnp.float32
    )
    back_map = back_map + mass_block.astype(jnp.float32)[:, None] * keep_col[None, :]
    back_low = back_map.astype(jnp.bfloat16)
    returned = lax.all_to_all(
        back_low.reshape(spot_dev * cols_count, rows_count, 1, cell_dev),
        "col",
        split_axis=0,
        concat_axis=2,
        tiled=True,
    ).reshape(spot_dev, cell_total)
    expr_part = lax.dot_general(
        mapped, grad_block, (((0,), (0,)), ((), ())), preferred_element_type=jnp.float32
    )
    mass_reach = lax.dot_general(
        mapped, mass_block, (((0,), (0,)), ((), ())), preferred_element_type=jnp.float32
    )
    expr_sum = lax.psum_scatter(expr_part, "row", scatter_dimension=0, tiled=True)
    mass_sum = lax.psum_scatter(mass_reach, "row", scatter_dimension=0, tiled=True)
    filter_grad = (
        keep_rate
        * (1.0 - keep_rate)
        * (jnp.sum(cell_expr.astype(jnp.float32) * expr_sum, axis=1) + mass_sum)
    )
    expr_grad = keep_rate[:, None] * expr_sum
    chance_grad = returned.astype(jnp.float32)
    inner_sum = jnp.sum(chances * chance_grad, axis=1, keepdims=True)
    map_grad = chances * (chance_grad - inner_sum)
    return (losses, predicted, map_grad, expr_grad, filter_grad)


def fused_kernel(
    total_spots, total_genes,
    logit_in, filt_in, cell_in, spot_in, cslide_in, sslide_in, bins_in,
    pred_out, map_out, expr_out, filt_out, loss_out,
    chance, own_low, plane_low, plane_turn, cell_v, hand, col, part, send1, early, send2, late,
    pred_h, spot_h, stat, st_sum, st1, st2, st3, spacc, spgot, coef, grad,
    sums_up, sums_dn, pass_on, back, back_got, back_low, back_ret, other, other_got,
    f_line, f_pair, f_all, keep_all, m_src, m_got, r_src, r_mate, r_plane_src, r_plane, r_line_src, r_line,
    l_src, l_mate, l_plane, l_line_src, l_line, filt_acc, hot_lie, hot_stand, mass_row,
    load_sem, own_sem, hand_s, hand_r, up_s, dn_s, col_r, low_s, low_r, send1_s, send2_s, early_r, late_r,
    pred_s, pred_r, spot_s, spot_r, st_s, st_r, spx_s, spx_r, g_s, g_r, rs_s, rs_r, back_s, back_r,
    ret_s, ret_r, oth_s, oth_r, sm_s, sm_r,
):
    f32, b16 = jnp.float32, jnp.bfloat16
    half = col.shape[2]
    chunks = half // WIDTH
    units = WIDTH // 128
    keep = {}
    z = lax.axis_index("row")
    c = lax.axis_index("col")
    j = lax.div(c, 2)
    k = lax.rem(c, 2)
    y = lax.div(j, 2)
    x = lax.rem(j, 2)
    mate = 1 - k

    def dev(zz, jj, kk):
        return (zz, jj * 2 + kk)

    jx = y * 2 + (1 - x)
    jy = (1 - y) * 2 + x
    jd = (1 - y) * 2 + (1 - x)
    dev_mate = dev(z, j, mate)
    dev_x = dev(z, jx, k)
    dev_y = dev(z, jy, k)
    dev_up = dev(lax.rem(z + 1, 4), j, k)
    dev_dn = dev(lax.rem(z + 3, 4), j, k)
    plane_others = (jx, jy, jd)
    line_others = [lax.rem(z + i, 4) for i in (1, 2, 3)]

    def rc(src, dst, ss, rs, to):
        return pltpu.make_async_remote_copy(
            src_ref=src, dst_ref=dst, send_sem=ss, recv_sem=rs, device_id=to, device_id_type=MESH
        )

    def got(ref, sem):
        rc(ref, ref, sem, sem, dev_mate).wait_recv()

    def sent(ref, sem):
        rc(ref, ref, sem, sem, dev_mate).wait_send()

    def rows(i, size):
        return pl.ds(pl.multiple_of(i * size, size), size)

    def at_chunk(q):
        return pl.ds(q * WIDTH, WIDTH)

    def lanes(kk, q):
        return pl.ds(pl.multiple_of(kk * half + q * WIDTH, WIDTH), WIDTH)

    load_cell = pltpu.make_async_copy(cell_in, cell_v, load_sem.at[0])
    load_logit = pltpu.make_async_copy(logit_in, chance, load_sem.at[1])
    load_spot = pltpu.make_async_copy(
        spot_in.at[:, pl.ds(pl.multiple_of(k * half, half), half)], spot_h.at[rows(k, 128)], load_sem.at[2]
    )
    barrier = pltpu.get_barrier_semaphore()
    for to in (
        dev_mate, dev_x, dev_y, dev(z, jd, k),
        dev(line_others[0], j, k), dev(line_others[1], j, k), dev(line_others[2], j, k),
    ):
        pl.semaphore_signal(barrier, inc=1, device_id=to, device_id_type=MESH)
    load_cell.start()
    load_logit.start()
    load_spot.start()

    eye = lax.broadcasted_iota(jnp.int32, (128, 128), 0) == lax.broadcasted_iota(
        jnp.int32, (128, 128), 1
    )
    lane = lax.broadcasted_iota(jnp.int32, (128, 128), 1)

    def stand(row):
        return jnp.sum(jnp.where(eye, jnp.broadcast_to(row, (128, 128)), 0.0), 1, keepdims=True)

    def lie(column):
        return jnp.sum(jnp.where(eye, jnp.broadcast_to(column, (128, 128)), 0.0), 0, keepdims=True)

    filt_row = filt_in[...].astype(f32)
    keep_col = stand(jax.nn.sigmoid(filt_row))
    slide_col = stand(sslide_in[...].astype(f32))
    bins_col = stand(bins_in[...].astype(f32))

    def hand_copy(q):
        return rc(hand.at[q], col.at[z, rows(k, 128), rows(q, WIDTH)], hand_s, hand_r.at[q], dev_mate)

    def col_up(q, b):
        at = col.at[b, :, at_chunk(q)]
        return rc(at, at, up_s, col_r.at[q, b], dev_up)

    def col_dn(q, b):
        at = col.at[b, :, at_chunk(q)]
        return rc(at, at, dn_s, col_r.at[q, b], dev_dn)

    def scale_cells(q):
        hand[q] = (keep_col * cell_v[:, lanes(mate, q)].astype(f32)).astype(b16)
        col[z, rows(k, 128), rows(q, WIDTH)] = (keep_col * cell_v[:, lanes(k, q)].astype(f32)).astype(b16)

    def col_own(q):
        got(hand.at[q], hand_r.at[q])

        @pl.when(z < 3)
        def _():
            col_up(q, z).start()

        @pl.when(z > 0)
        def _():
            col_dn(q, z).start()

    hops = [(q, s) for q in range(chunks) for s in range(3)]

    def hop():
        q, s = hops.pop(0)

        @pl.when(z - 1 - s >= 0)
        def _():
            b = z - 1 - s
            got(col.at[b, :, at_chunk(q)], col_r.at[q, b])

            @pl.when(z < 3)
            def _():
                col_up(q, b).start()

        @pl.when(z + 1 + s <= 3)
        def _():
            b = z + 1 + s
            got(col.at[b, :, at_chunk(q)], col_r.at[q, b])

            @pl.when(z > 0)
            def _():
                col_dn(q, b).start()

    load_cell.wait()
    scale_cells(0)
    pl.semaphore_wait(barrier, 7)
    hand_copy(0).start()

    @pl.loop(1, chunks)
    def _(q):
        scale_cells(q)
        hand_copy(q).start()

    def spread(source, slots, which, i):
        for o in plane_others if which == "plane" else line_others:
            to = dev(z, o, k) if which == "plane" else dev(o, j, k)
            rc(source(o), slots.at[j if which == "plane" else z], sm_s.at[i], sm_r.at[i], to).start()

    def hand_over(source, slot, i):
        rc(source, slot, sm_s.at[i], sm_r.at[i], dev_mate).start()

    f_line[z] = filt_row
    spread(lambda o: f_line.at[z], f_line, "line", 0)

    load_logit.wait()

    def softmax_rows(g):
        at = rows(g, 16)
        logits = chance[at, :]
        pick = lax.broadcasted_iota(jnp.int32, (16, 128), 0) + g * 16
        here = lax.broadcasted_iota(jnp.int32, (16, 128), 1)
        slide = jnp.sum(
            jnp.where(pick == here, jnp.broadcast_to(sslide_in[...].astype(f32), (16, 128)), 0.0),
            1, keepdims=True,
        )
        allowed = slide == cslide_in[...].astype(f32)
        shifted = jnp.where(allowed, logits, -1e30)
        raised = jnp.exp(shifted - jnp.max(shifted, axis=1, keepdims=True))
        value = raised / jnp.sum(raised, axis=1, keepdims=True)
        chance[at, :] = value
        low = value.astype(b16)
        for b in range(4):
            for jj in range(4):
                own_low[jj, at, b * 256 : b * 256 + 256] = low[
                    :, b * 1024 + jj * 256 : b * 1024 + jj * 256 + 256
                ]

    def low_copy(jj):
        return rc(own_low.at[jj], plane_low.at[k, j], low_s.at[0], low_r.at[j], dev(z, jj, k))

    def low_pass(jj):
        return rc(plane_low.at[k, jj], plane_low.at[k, jj], low_s.at[1], low_r.at[4], dev_mate)

    def low_give():
        low_copy(jd).start()
        low_copy(jx).start()
        low_copy(jy).start()

    spot_give = rc(
        spot_in.at[:, pl.ds(pl.multiple_of(mate * half, half), half)], spot_h.at[rows(k, 128)], spot_s, spot_r, dev_mate
    )

    def low_own():
        plane_low[k, j] = own_low[j]
        low_pass(j).start()
        spot_give.start()

    def filt_pair():
        got(f_line.at[pl.ds(0, 3)], sm_r.at[0])
        f_pair[k] = f_line[...]
        hand_over(f_line, f_pair.at[k], 1)

    def filt_plane():
        got(f_line, sm_r.at[1])
        f_all[j] = f_pair[...]
        spread(lambda o: f_pair, f_all, "plane", 2)

    def of_cells(jj, kk, b):
        return own_low[jj, :, pl.ds(pl.multiple_of(b * 256 + kk * 128, 128), 128)].astype(f32)

    def split(d):
        return lax.div(d, 8), lax.rem(lax.div(d, 4), 2), lax.rem(d, 4)

    kind = lax.div(lane, 8)
    of_slide = lax.rem(lane, 8) == slide_col.astype(jnp.int32)

    def mass_make():
        got(f_all.at[pl.ds(0, 3)], sm_r.at[2])
        keep_all[...] = jax.nn.sigmoid(f_all[...])

        def add_mass(d, acc):
            jj, kk, b = split(d)
            return acc + of_cells(jj, kk, b) * keep_all[jj, kk, b]

        mass = jnp.sum(lax.fori_loop(0, 32, add_mass, jnp.zeros((128, 128), f32)), axis=1, keepdims=True)
        keep["mass"] = mass
        log_term = bins_col * (jnp.log(bins_col) - jnp.log(mass))
        values = jnp.where(
            kind == 0, mass, jnp.where(kind == 1, bins_col, jnp.where(kind == 2, log_term, 0.0))
        )
        m_src[0] = jnp.sum(jnp.where(of_slide, values, 0.0), axis=0, keepdims=True)
        m_src[1] = sslide_in[...].astype(f32)
        hand_over(m_src, m_got, 3)

    lane2 = lax.broadcasted_iota(jnp.int32, (256, 128), 1)

    def mass_chip():
        got(m_src, sm_r.at[3])
        load_spot.wait()
        got(spot_h.at[rows(mate, 128)], spot_r)
        stat[...] = jnp.zeros_like(stat)
        chip_row = m_src[0] + m_got[0]
        for o in range(4):
            stat[0, o, 24:25, :] = chip_row
        first = jnp.where(k == 0, m_src[1], m_got[1])
        second = jnp.where(k == 0, m_got[1], m_src[1])
        hot_lie[...] = (
            lax.broadcasted_iota(jnp.int32, (8, 256), 0).astype(f32)
            == jnp.broadcast_to(jnp.concatenate([first, second], axis=1), (8, 256))
        ).astype(f32)
        slides_col = jnp.concatenate([stand(first), stand(second)], axis=0)
        hot_stand[...] = ((lax.rem(lane2, 8) == slides_col.astype(jnp.int32)) & (lane2 < 24)).astype(b16)
        spacc[...] = jnp.zeros_like(spacc)
        coef[...] = jnp.zeros_like(coef)
        filt_acc[...] = jnp.zeros_like(filt_acc)

    def split_dot(a, v):
        high = v.astype(b16)
        rest = (v - high.astype(f32)).astype(b16)
        return jnp.dot(a, high, preferred_element_type=f32) + jnp.dot(a, rest, preferred_element_type=f32)

    def low_arrive(i):
        if i == 3:
            got(plane_low.at[mate], low_r.at[4])
        else:
            jj = (jx, jy, jd)[i]
            got(plane_low.at[k, jj], low_r.at[jj])
            low_pass(jj).start()

    def product(q, left, count):
        at = pl.ds(q * WIDTH, count * WIDTH)

        @pl.loop(0, 2)
        def _(h):
            if left is plane_low:
                whole = jnp.dot(left[h].reshape(512, 1024), col[:, :, at].reshape(1024, count * WIDTH), preferred_element_type=f32)
            else:
                whole = jnp.dot(left[rows(h, 512), :], grad[:, :, :, at].reshape(1024, count * WIDTH), preferred_element_type=f32)
            for i in range(count):
                part[q + i, h] = whole[:, i * WIDTH : i * WIDTH + WIDTH].reshape(4, 128, WIDTH)

    def reduce_first(q):
        for i, (core, owner, to, sem, slot) in enumerate((
            (0, jd, dev_x, early_r.at[q, 0], early.at[q, 0]),
            (1, jd, dev_y, early_r.at[q, 1], early.at[q, 1]),
            (0, jx, dev_x, late_r.at[q], late.at[q, 0]),
            (1, jy, dev_y, late_r.at[q], late.at[q, 1]),
        )):
            send1[q, i] = part[q, core, owner].astype(b16)
            rc(send1.at[q, i], slot, send1_s, sem, to).start()

    def reduce_second(q, i):
        owner, to = ((jy, dev_y), (jx, dev_x))[i]
        got(early.at[q, i], early_r.at[q, i])
        send2[q, i] = (part[q, i, owner] + early[q, i].astype(f32)).astype(b16)
        rc(send2.at[q, i], late.at[q, 2 + i], send2_s, late_r.at[q], to).start()

    def pred_give(q):
        return rc(
            pred_h.at[rows(mate, 128), pl.ds(q * WIDTH, WIDTH)], pred_out.at[:, lanes(k, q)], pred_s, pred_r, dev_mate
        )

    def pred_own(q):
        return pltpu.make_async_copy(
            pred_h.at[rows(k, 128), pl.ds(q * WIDTH, WIDTH)], pred_out.at[:, lanes(k, q)], own_sem
        )

    def reduce_last(q):
        got(late.at[q], late_r.at[q])
        for i in range(2):
            pred_h[i * 128 : i * 128 + 128, q * WIDTH : q * WIDTH + WIDTH] = part[q, i, j] + (
                late[q, i].astype(f32) + late[q, 2 + i].astype(f32)
            )
        pred_give(q).start()
        pred_own(q).start()

    def reduce_stat(q):
        for e in range(units):
            at = slice(q * WIDTH + e * 128, q * WIDTH + e * 128 + 128)
            g, o = divmod(q * units + e, 4)
            pr = pred_h[:, at]
            sp = spot_h[:, at]
            for i, v in enumerate((pr * sp, pr * pr, sp * sp)):
                spacc[i] = spacc[i] + v
                stat[g, o, i * 8 : i * 8 + 8] = split_dot(hot_lie[...].astype(b16), v)

    def st_send(g, i):
        slots = (st1, st2, st3)[i]
        if i == 0:
            st1[g, j] = stat[g, j]
        else:
            prior = (st1, st2)[i - 1]
            got(prior.at[g, pl.ds(0, 3)], st_r.at[g, i - 1])
            total = prior[g, 0] + prior[g, 1] + prior[g, 2] + prior[g, 3]
            st_sum[g, i - 1] = total
            if i == 1:
                st2[g, z] = total
            else:
                st3[g, j] = total
        for o in line_others if i == 1 else plane_others:
            src = stat.at[g, o] if i == 0 else st_sum.at[g, i - 1]
            to = dev(o, j, k) if i == 1 else dev(z, o, k)
            rc(src, slots.at[g, z if i == 1 else j], st_s.at[g, i], st_r.at[g, i], to).start()

    def st_finish(g):
        got(st3.at[g, pl.ds(0, 3)], st_r.at[g, 2])

    def turn(i):
        for kk in range(2):
            plane_turn[:, (kk * 4 + i) * 128 : (kk * 4 + i) * 128 + 128] = plane_low[kk, i].astype(f32).T.astype(b16)

    spx = rc(spacc, spgot, spx_s, spx_r, dev_mate)

    def spot_half():
        spx.start()
        st_send(1, 0)

    slide8 = lax.broadcasted_iota(jnp.int32, (8, 128), 0)
    lane8 = lax.broadcasted_iota(jnp.int32, (8, 128), 1)

    def mass_end():
        sums_row = st_sum[0, 1, 24:25, :]
        each = jnp.broadcast_to(sums_row, (128, 128))
        mass_each = jnp.sum(jnp.where(of_slide & (kind == 0), each, 0.0), 1, keepdims=True)
        bins_each = jnp.sum(jnp.where(of_slide & (kind == 1), each, 0.0), 1, keepdims=True)
        mass_grad = (1.0 / mass_each - bins_col / (bins_each * keep["mass"])) / SLIDES
        keep["grad"] = mass_grad.astype(b16).astype(f32)

        def by_slide(begin):
            return jnp.sum(
                jnp.where(lane8 == slide8 + begin, jnp.broadcast_to(sums_row, (8, 128)), 0.0), 1, keepdims=True
            )

        mass_s, bins_s, log_s = by_slide(0), by_slide(8), by_slide(16)
        kl = jnp.sum(log_s / bins_s - jnp.log(bins_s) + jnp.log(mass_s), axis=0, keepdims=True)
        keep["kl"] = kl / SLIDES

    def reach_make():
        mass_grad = keep["grad"]

        @pl.loop(0, 32)
        def _(d):
            jj, kk, b = split(d)
            r_src[kk, jj, b] = jnp.sum(of_cells(jj, kk, b) * mass_grad, axis=0, keepdims=True)

        hand_over(r_src.at[mate], r_mate, 4)

    def reach_plane():
        got(r_mate, sm_r.at[4])
        r_plane_src[...] = r_src[k] + r_mate[...]
        r_plane[j] = r_plane_src[j]
        spread(lambda o: r_plane_src.at[o], r_plane, "plane", 5)

    def reach_line():
        got(r_plane.at[pl.ds(0, 3)], sm_r.at[5])
        r_line_src[...] = r_plane[0] + r_plane[1] + r_plane[2] + r_plane[3]
        r_line[z] = r_line_src[z]
        spread(lambda o: r_line_src.at[o], r_line, "line", 6)

    def spot_sums():
        st_finish(0)
        got(spgot, spx_r)
        cross_c, pred_c, obs_c = [
            jnp.sum(spacc[i] + spgot[i], axis=1, keepdims=True) for i in range(3)
        ]
        root_c = jnp.sqrt(pred_c * obs_c)
        keep["cos"] = cross_c / root_c
        keep["obs"] = (1.0 / root_c) / total_spots
        keep["prd"] = (cross_c / (pred_c * root_c)) / total_spots

    def grad_make(q):
        scale = 1.0 / (SLIDES * total_genes)
        for e in range(units):
            g, o = divmod(q * units + e, 4)
            sums = st3[g, o]
            cross, prd, obs = sums[:8], sums[8:16], sums[16:24]
            root = jnp.sqrt(prd * obs)
            for i, v in enumerate((scale / root, scale * cross / (prd * root))):
                high = v.astype(b16).astype(f32)
                mid = (v - high).astype(b16).astype(f32)
                low = v - high - mid
                stack = jnp.concatenate([high, mid, low, jnp.zeros((8, 128), f32)], axis=0)
                coef[:32, (i * units + e) * 128 : (i * units + e) * 128 + 128] = stack.astype(b16)
        each_spot = jnp.dot(hot_stand[...], coef[...], preferred_element_type=f32)
        at = slice(q * WIDTH, q * WIDTH + WIDTH)
        value = pred_h[:, at] * (each_spot[:, WIDTH:] + keep["prd"]) - spot_h[:, at] * (each_spot[:, :WIDTH] + keep["obs"])
        value = value.astype(b16)
        grad[0, j, :, at] = value[:128]
        grad[1, j, :, at] = value[128:]

    def gene_cos():
        total = jnp.zeros((8, 128), f32)
        for g in range(2):
            for e in range(4):
                sums = st3[g, e]
                total = total + sums[:8] / jnp.sqrt(sums[8:16] * sums[16:24])
        return jnp.sum(jnp.sum(total, axis=0, keepdims=True), axis=1, keepdims=True)

    def grad_send(q):
        grad_make(q)
        at = grad.at[:, j, :, at_chunk(q)]
        rc(at, at, g_s.at[0], g_r.at[q, 0], dev_x).start()
        rc(at, at, g_s.at[1], g_r.at[q, 1], dev_y).start()

    def grad_pass(q, i):
        owner, to = ((jx, dev_y), (jy, dev_x))[i]
        got(grad.at[:, owner, :, at_chunk(q)], g_r.at[q, i])
        at = grad.at[i, owner, :, at_chunk(q)]
        rc(at, at, g_s.at[2 + i], g_r.at[q, 2], to).start()

    def run_up(q, b):
        return rc(pass_on.at[q, b], sums_up.at[q, b], rs_s, rs_r.at[q, b + 1], dev_up)

    def run_dn(q, b):
        return rc(pass_on.at[q, b], sums_dn.at[q, b], rs_s, rs_r.at[q, b], dev_dn)

    def block(q, b):
        return part[q, b // 2, pl.ds(2 * (b % 2), 2)].reshape(256, WIDTH)

    def sums_first(q, count):
        for i in range(count):
            got(grad.at[:, jd, :, at_chunk(q + i)], g_r.at[q + i, 2])
        product(q, plane_turn, count)

        @pl.when(z == 0)
        def _():
            for i in range(count):
                for b in (3, 2, 1):
                    pass_on[q + i, b] = block(q + i, b).astype(b16)
                    run_up(q + i, b).start()

        @pl.when(z == 3)
        def _():
            for i in range(count):
                for b in (0, 1, 2):
                    pass_on[q + i, b] = block(q + i, b).astype(b16)
                    run_dn(q + i, b).start()

    def pass_up(q, b):
        @pl.when((z == 1) | (z == b - 1))
        def _():
            got(sums_up.at[q, b], rs_r.at[q, b + 1])
            pass_on[q, b] = (block(q, b) + sums_up[q, b].astype(f32)).astype(b16)
            run_up(q, b).start()

    def pass_dn(q, b):
        @pl.when((z == 2) | (z == b + 1))
        def _():
            got(sums_dn.at[q, b], rs_r.at[q, b])
            pass_on[q, b] = (block(q, b) + sums_dn[q, b].astype(f32)).astype(b16)
            run_dn(q, b).start()

    def other_give(q):
        return rc(other.at[q], other_got.at[q], oth_s, oth_r.at[q], dev_mate)

    def use_sums(q, kk, sums):
        at = lanes(kk, q)
        expr_out[:, at] = keep_col * sums
        weighed = cell_v[:, at].astype(f32) * sums
        for e in range(units):
            filt_acc[...] = filt_acc[...] + weighed[:, e * 128 : e * 128 + 128]

    def sums_last(q):
        other[q] = part[q, lax.div(z, 2), 2 * lax.rem(z, 2) + mate]
        own_at = (q, lax.div(z, 2), 2 * lax.rem(z, 2) + k)

        @pl.when(z > 0)
        def _():
            got(sums_up.at[q, z], rs_r.at[q, z + 1])
            other[q] = other[q] + sums_up[q, z, rows(mate, 128), :].astype(f32)
            part[own_at] = part[own_at] + sums_up[q, z, rows(k, 128), :].astype(f32)

        @pl.when(z < 3)
        def _():
            got(sums_dn.at[q, z], rs_r.at[q, z])
            other[q] = other[q] + sums_dn[q, z, rows(mate, 128), :].astype(f32)
            part[own_at] = part[own_at] + sums_dn[q, z, rows(k, 128), :].astype(f32)

        other_give(q).start()
        use_sums(q, k, part[own_at])

    def sums_other(q):
        got(other_got.at[q], oth_r.at[q])
        use_sums(q, mate, other_got[q])

    def back_dot(b):
        @pl.loop(0, 2)
        def _(h):
            back[b, h] = lax.dot_general(
                grad[h].reshape(512, half), col[b], (((1,), (1,)), ((), ())), preferred_element_type=f32
            ).reshape(4, 128, 256)

        rc(back.at[b, mate], back_got.at[b], back_s, back_r.at[b], dev_mate).start()

    def back_add(b):
        got(back_got.at[b], back_r.at[b])
        for jj in range(4):
            back_low[jj, :, rows(b, 256)] = (back[b, k, jj] + back_got[b, jj]).astype(b16)

    def ret_send():
        for jj in (jd, jx, jy):
            rc(back_low.at[jj], back_ret.at[j], ret_s, ret_r, dev(z, jj, k)).start()
        back_ret[j] = back_low[j]

    loss_lane = lax.broadcasted_iota(jnp.int32, (1, 128), 1)

    def loss_mate():
        own_cos = jnp.sum(keep["cos"], axis=0, keepdims=True)
        l_src[...] = jnp.where(loss_lane == 0, own_cos, jnp.where(loss_lane == 1, gene_cos(), 0.0))
        hand_over(l_src, l_mate, 7)
        l_plane[j] = l_src[...]
        spread(lambda o: l_src, l_plane, "plane", 8)

    def loss_line():
        got(l_plane.at[pl.ds(0, 3)], sm_r.at[8])
        total = l_plane[0] + l_plane[1] + l_plane[2] + l_plane[3]
        l_line_src[...] = total
        l_line[z] = total
        spread(lambda o: l_line_src, l_line, "line", 9)

    def loss_end():
        got(l_line.at[pl.ds(0, 3)], sm_r.at[9])
        got(l_mate, sm_r.at[7])
        cos_row = l_line[0] + l_line[1] + l_line[2] + l_line[3]
        gene_row = l_src[...] + l_mate[...]
        cos_total = jnp.sum(jnp.where(loss_lane == 0, cos_row, 0.0), axis=1, keepdims=True)
        gene_total = jnp.sum(jnp.where(loss_lane == 1, gene_row, 0.0), axis=1, keepdims=True)
        gene_loss = 1.0 - gene_total / (SLIDES * total_genes)
        spot_loss = 1.0 - cos_total / total_spots
        kl_loss = keep["kl"]
        total_loss = gene_loss + spot_loss + kl_loss
        picked = jnp.where(loss_lane == 2, spot_loss, jnp.where(loss_lane == 3, kl_loss, 0.0))
        loss_out[...] = jnp.where(loss_lane == 0, total_loss, jnp.where(loss_lane == 1, gene_loss, picked))

    def map_rows(g):
        at = rows(g, 16)
        pick = lax.broadcasted_iota(jnp.int32, (16, 128), 0) + g * 16
        here = lax.broadcasted_iota(jnp.int32, (16, 128), 1)
        mg = jnp.sum(jnp.where(pick == here, jnp.broadcast_to(mass_row[...], (16, 128)), 0.0), 1, keepdims=True)
        inner = jnp.zeros((16, 128), f32)
        for d in range(32):
            b, jj, kk = d // 8, (d % 8) // 2, d % 2
            used = back_ret[jj, at, b * 256 + kk * 128 : b * 256 + kk * 128 + 128].astype(f32) + mg * keep_all[jj, kk, b]
            inner = inner + chance[at, d * 128 : d * 128 + 128] * used
            map_out[at, d * 128 : d * 128 + 128] = used
        inner = jnp.sum(inner, axis=1, keepdims=True)
        map_out[at, :] = chance[at, :] * (map_out[at, :] - inner)

    def map_all():
        got(back_ret.at[pl.ds(0, 3)], ret_r)
        mass_row[...] = lie(keep["grad"])
        pl.loop(0, 8)(map_rows)

    steps = {
        "x": lambda i: pl.loop(2 * i, 2 * i + 2)(softmax_rows), "w": lambda i: (low_give, low_own)[i](),
        "c": col_own, "h": lambda i: hop(), "i": lambda i: (filt_pair, filt_plane, mass_make, mass_chip)[i](),
        "a": low_arrive, "q": turn, "p": lambda q: product(q, plane_low, 1), "P": lambda q: product(q, plane_low, 2),
        "f": reduce_first, "s": lambda q: reduce_second(q, 0), "S": lambda q: reduce_second(q, 1),
        "l": reduce_last, "k": reduce_stat, "t": lambda i: st_send(0, i), "z": lambda i: (spot_half, mass_end, spot_sums)[i](),
        "g": grad_send, "m": lambda q: grad_pass(q, 0), "n": lambda q: grad_pass(q, 1),
        "y": lambda i: st_send(1, i) if i < 3 else st_finish(1), "r": lambda q: sums_first(q, 1), "R": lambda q: sums_first(q, 2),
        "U": lambda q: pass_up(q, 3), "V": lambda q: pass_up(q, 2), "D": lambda q: pass_dn(q, 0), "E": lambda q: pass_dn(q, 1),
        "L": sums_last, "O": sums_other, "b": back_dot, "A": back_add, "T": lambda i: ret_send(), "M": lambda i: map_all(),
        "e": lambda i: (reach_make, reach_plane, reach_line)[i](), "o": lambda i: (loss_mate, loss_line, loss_end)[i](),
    }
    for group in ORDER:
        for word in group.split():
            steps[word[0]](int(word[1:]) if len(word) > 1 else 0)

    got(r_line.at[pl.ds(0, 3)], sm_r.at[6])
    reach_row = r_line[0] + r_line[1] + r_line[2] + r_line[3]
    filt_sum = jnp.sum(filt_acc[...], axis=1, keepdims=True)
    keep_row = jax.nn.sigmoid(filt_in[...].astype(f32))
    filt_out[...] = keep_row * (1.0 - keep_row) * (lie(filt_sum) + reach_row)

    sent(hand, hand_s)
    spot_give.wait_send()
    sent(send1, send1_s)
    sent(send2, send2_s)
    sent(pred_h.at[rows(mate, 128)], pred_s)
    got(pred_out.at[:, pl.ds(pl.multiple_of(mate * half, half), half)], pred_r)
    pltpu.make_async_copy(
        pred_h.at[rows(k, 128)], pred_out.at[:, pl.ds(pl.multiple_of(k * half, half), half)], own_sem
    ).wait()
    for i in range(2):
        sent(grad.at[:, j], g_s.at[i])
    sent(grad.at[0, jx], g_s.at[2])
    sent(grad.at[1, jy], g_s.at[3])
    for i in range(3):
        @pl.when(z == i)
        def _():
            sent(col.at[pl.ds(0, i + 1)], up_s)

        @pl.when(z == 3 - i)
        def _():
            sent(col.at[pl.ds(3 - i, i + 1)], dn_s)
    sent(pass_on.at[:, pl.ds(0, 3)], rs_s)
    sent(plane_low.at[k, pl.ds(0, 3)], low_s.at[0])
    sent(plane_low.at[k], low_s.at[1])
    for g in range(2):
        for i in range(3):
            sent(st1.at[g, pl.ds(0, 3)], st_s.at[g, i])
    spx.wait_send()
    sent(back_got, back_s)
    sent(back_low.at[pl.ds(0, 3)], ret_s)
    sent(other, oth_s)
    for i, ref in enumerate((
        f_line.at[pl.ds(0, 3)], f_line, f_all.at[pl.ds(0, 3)], m_src, r_mate, r_plane.at[pl.ds(0, 3)],
        r_line.at[pl.ds(0, 3)], l_mate, l_plane.at[pl.ds(0, 3)], l_line.at[pl.ds(0, 3)],
    )):
        sent(ref, sm_s.at[i])


def fused_shards(map_logits, filter_logits, cell_expr, spot_expr, cell_slide, spot_slide, density_bins):
    f32, b16 = jnp.float32, jnp.bfloat16
    spots, cells = map_logits.shape
    genes = cell_expr.shape[1]
    n = genes // (2 * WIDTH)
    V, S = pltpu.VMEM, pltpu.SemaphoreType.DMA
    any_, vmem = pl.BlockSpec(memory_space=pl.ANY), pl.BlockSpec(memory_space=pltpu.VMEM)
    one = S(())
    scratch = [
        V((128, cells), f32),
        V((4, 128, 1024), b16),
        V((2, 4, 128, 1024), b16),
        V((1024, 1024), b16),
        V((128, genes), b16),
        V((n, 128, WIDTH), b16),
        V((4, 256, genes // 2), b16),
        V((n, 2, 4, 128, WIDTH), f32),
        V((n, 4, 128, WIDTH), b16),
        V((n, 2, 128, WIDTH), b16),
        V((n, 2, 128, WIDTH), b16),
        V((n, 4, 128, WIDTH), b16),
        V((256, genes // 2), f32),
        V((256, genes // 2), f32),
        V((2, 4, 32, 128), f32),
        V((2, 2, 32, 128), f32),
        V((2, 4, 32, 128), f32),
        V((2, 4, 32, 128), f32),
        V((2, 4, 32, 128), f32),
        V((3, 256, 128), f32),
        V((3, 256, 128), f32),
        V((128, 2 * WIDTH), b16),
        V((2, 4, 128, genes // 2), b16),
        V((n, 4, 256, WIDTH), b16),
        V((n, 4, 256, WIDTH), b16),
        V((n, 4, 256, WIDTH), b16),
        V((4, 2, 4, 128, 256), f32),
        V((4, 4, 128, 256), f32),
        V((4, 128, 1024), b16),
        V((4, 128, 1024), b16),
        V((n, 128, WIDTH), f32),
        V((n, 128, WIDTH), f32),
        V((4, 1, 128), f32),
        V((2, 4, 1, 128), f32),
        V((4, 2, 4, 1, 128), f32),
        V((4, 2, 4, 1, 128), f32),
        V((2, 1, 128), f32),
        V((2, 1, 128), f32),
        V((2, 4, 4, 1, 128), f32),
        V((4, 4, 1, 128), f32),
        V((4, 4, 1, 128), f32),
        V((4, 4, 1, 128), f32),
        V((4, 1, 128), f32),
        V((4, 1, 128), f32),
        V((1, 128), f32),
        V((1, 128), f32),
        V((4, 1, 128), f32),
        V((1, 128), f32),
        V((4, 1, 128), f32),
        V((128, 128), f32),
        V((8, 256), f32),
        V((256, 128), b16),
        V((1, 128), f32),
        S((3,)), one, one, S((n,)), one, one, S((n, 4)), S((2,)), S((5,)),
        one, one, S((n, 2)), S((n,)),
        one, one, one, one, S((2, 3)), S((2, 3)), one, one,
        S((4,)), S((n, 3)), one, S((n, 5)), one, S((4,)),
        one, one, one, S((n,)), S((10,)), S((10,)),
    ]
    predicted, map_grad, expr_grad, filt, loss = pl.pallas_call(
        functools.partial(fused_kernel, float(spots * 32), float(genes)),
        out_shape=(
            pltpu.VMEM((spots, genes), f32),
            pltpu.VMEM((spots, cells), f32),
            pltpu.VMEM((spots, genes), f32),
            jax.ShapeDtypeStruct((1, 128), f32),
            jax.ShapeDtypeStruct((1, 128), f32),
        ),
        in_specs=[any_, vmem, any_, any_, vmem, vmem, vmem],
        out_specs=(vmem, vmem, vmem, vmem, vmem),
        scratch_shapes=scratch,
        compiler_params=pltpu.CompilerParams(
            collective_id=0, has_side_effects=True, vmem_limit_bytes=52 * 2**20
        ),
        name="mapping_step",
    )(
        map_logits,
        filter_logits.reshape(1, 128),
        cell_expr,
        spot_expr,
        cell_slide.reshape(1, cells),
        spot_slide.reshape(1, 128),
        density_bins.reshape(1, 128),
    )
    return loss[0, :4], predicted, map_grad, expr_grad, filt.reshape(128)


def solution(mesh):
    both = P(("row", "col"))
    rows = P(("row", "col"), None)
    in_specs = (rows, both, rows, rows, P(), both, both)
    out_specs = (P(), rows, rows, rows, both)
    step = fused_shards if (mesh.shape["row"], mesh.shape["col"]) == (4, 8) else shards
    return jax.shard_map(step, mesh=mesh, in_specs=in_specs, out_specs=out_specs, check_vma=False)
```

```python
import functools

import jax
import jax.numpy as jnp
from jax import lax
from jax.experimental import pallas as pl
from jax.experimental.pallas import tpu as pltpu
from jax.sharding import PartitionSpec as P

SLIDES = 8
ROWS, PLANE, CORES = 4, 4, 2
WIDTH = 128
MESH = pl.DeviceIdType.MESH
DIRECT = 0
ORDER = (
    "c0 c1 x0 x1",
    "x2 x3 w0 c2",
    "h c3 c4 w1",
    "h h i0 i1",
    "h c5 a2 h",
    "h h h h",
    "h a0 c6 a1",
    "i2 a3 P0 f1",
    "h h h f0",
    "P2 f3 i3 f2",
    "h h S1 h",
    "c7 s1 p4 S0",
    "s0 s3 B0 S3",
    "f4 s2 h h",
    "h p5 S2 l0",
    "l1 l3 f5 j1",
    "h j0 s4 h",
    "h p6 f6 l2",
    "j2 j3 t0 k0",
    "k3 h s5 S5",
    "q3 s6 S4 h",
    "p7 f7 t1 S6",
    "l5 l4 k4 s7",
    "j4 q2 S7 j5",
    "k1 l6 k5 k6",
    "t2 k2 j6 l7",
    "k7 z0 j7 y0",
    "B1 z2 G0 y1",
    "z1 e0 g3 g2",
    "q1 q0 y2 r0",
    "O0 n3 m3 g1",
    "n2 m2 y3 g6",
    "r3 O3 m1 g7",
    "o0 n1 g5 g4",
    "U0 n6 U3 r2",
    "E3 m6 V3 m7",
    "V0 n5 n7 r1",
    "m4 O2 n4 m5",
    "E2 E0 O1 e1",
    "U2 r6 r7 O7",
    "R4 E1 b3 U1",
    "V1 V6 V2 D2",
    "b0 b1 D6 b2",
    "D1 A0 A1 A3",
    "D3 A2 T0 L0",
    "D7 o1 L1 L3",
    "D0 D4 e2 V5",
    "O5 D5 E5 E6",
    "U5 L2 O6 U6",
    "O4 o2 E7 E4",
    "U7 L5 L6 U4",
    "V7 V4 M0 L7",
    "L4",
)


def shards(map_logits, filter_logits, cell_expr, spot_expr, cell_slide, spot_slide, density_bins):
    highest = lax.Precision.HIGHEST
    both = ("row", "col")
    rows_count = lax.axis_size("row")
    cols_count = lax.axis_size("col")
    spot_dev, cell_total = map_logits.shape
    cell_dev = filter_logits.shape[0]
    spot_total = spot_dev * rows_count * cols_count
    gene_count = cell_expr.shape[1]
    keep_rate = jax.nn.sigmoid(filter_logits.astype(jnp.float32))
    scaled = (keep_rate[:, None] * cell_expr.astype(jnp.float32)).astype(jnp.bfloat16)
    scaled_col = lax.all_gather(scaled, "row", axis=0, tiled=True)
    allowed = spot_slide[:, None] == cell_slide[None, :]
    shifted = jnp.where(allowed, map_logits, -1e30)
    row_peak = jnp.max(shifted, axis=1, keepdims=True)
    raised = jnp.exp(shifted - row_peak)
    chances = raised / jnp.sum(raised, axis=1, keepdims=True)
    chance_low = chances.astype(jnp.bfloat16)
    by_col = chance_low.reshape(spot_dev, rows_count, cols_count, cell_dev)
    mapped = lax.all_to_all(by_col, "col", split_axis=2, concat_axis=0, tiled=True)
    mapped = mapped.reshape(spot_dev * cols_count, rows_count * cell_dev)
    keep_col = lax.all_gather(keep_rate, "row", axis=0, tiled=True)
    part_pred = jnp.dot(mapped, scaled_col, preferred_element_type=jnp.float32)
    part_mass = jnp.dot(mapped, keep_col, precision=highest, preferred_element_type=jnp.float32)
    predicted = lax.psum_scatter(part_pred, "col", scatter_dimension=0, tiled=True)
    mass = lax.psum_scatter(part_mass, "col", scatter_dimension=0, tiled=True)
    onehot = (spot_slide[:, None] == jnp.arange(SLIDES, dtype=jnp.int32)[None, :]).astype(
        jnp.float32
    )
    cross_term = predicted * spot_expr
    pred_sq = predicted * predicted
    obs_sq = spot_expr * spot_expr
    spot_cross = jnp.sum(cross_term, axis=1)
    spot_pred = jnp.sum(pred_sq, axis=1)
    spot_root = jnp.sqrt(spot_pred * jnp.sum(obs_sq, axis=1))
    spot_cos = spot_cross / spot_root
    bin_values = density_bins.astype(jnp.float32)
    log_term = bin_values * (jnp.log(bin_values) - jnp.log(mass))
    all_cross, all_pred, all_obs, slide_mass, slide_bins, slide_log, cos_total = lax.psum(
        (
            jnp.dot(onehot.T, cross_term, precision=highest),
            jnp.dot(onehot.T, pred_sq, precision=highest),
            jnp.dot(onehot.T, obs_sq, precision=highest),
            jnp.dot(onehot.T, mass, precision=highest),
            jnp.dot(onehot.T, bin_values, precision=highest),
            jnp.dot(onehot.T, log_term, precision=highest),
            jnp.sum(spot_cos),
        ),
        both,
    )
    gene_root = jnp.sqrt(all_pred * all_obs)
    gene_loss = 1.0 - jnp.mean(all_cross / gene_root)
    spot_loss = 1.0 - cos_total / spot_total
    kl_loss = jnp.mean(slide_log / slide_bins - jnp.log(slide_bins) + jnp.log(slide_mass))
    total_loss = gene_loss + spot_loss + kl_loss
    losses = jnp.stack([total_loss, gene_loss, spot_loss, kl_loss])
    gene_scale = 1.0 / (SLIDES * gene_count)
    coef_obs = jnp.dot(onehot, 1.0 / gene_root, precision=highest)
    coef_pred = jnp.dot(onehot, all_cross / (all_pred * gene_root), precision=highest)
    pred_grad = -gene_scale * (spot_expr * coef_obs - predicted * coef_pred)
    pred_grad = (
        pred_grad
        - (
            spot_expr / spot_root[:, None]
            - predicted * (spot_cross / (spot_pred * spot_root))[:, None]
        )
        / spot_total
    )
    mass_each = jnp.dot(onehot, slide_mass, precision=highest)
    bins_each = jnp.dot(onehot, slide_bins, precision=highest)
    mass_grad = (1.0 / mass_each - bin_values / (bins_each * mass)) / SLIDES
    grad_low = pred_grad.astype(jnp.bfloat16)
    mass_low = mass_grad.astype(jnp.bfloat16)
    grad_block = lax.all_gather(grad_low, "col", axis=0, tiled=True)
    mass_block = lax.all_gather(mass_low, "col", axis=0, tiled=True)
    back_map = lax.dot_general(
        grad_block, scaled_col, (((1,), (1,)), ((), ())), preferred_element_type=jnp.float32
    )
    back_map = back_map + mass_block.astype(jnp.float32)[:, None] * keep_col[None, :]
    back_low = back_map.astype(jnp.bfloat16)
    returned = lax.all_to_all(
        back_low.reshape(spot_dev * cols_count, rows_count, 1, cell_dev),
        "col",
        split_axis=0,
        concat_axis=2,
        tiled=True,
    ).reshape(spot_dev, cell_total)
    expr_part = lax.dot_general(
        mapped, grad_block, (((0,), (0,)), ((), ())), preferred_element_type=jnp.float32
    )
    mass_reach = lax.dot_general(
        mapped, mass_block, (((0,), (0,)), ((), ())), preferred_element_type=jnp.float32
    )
    expr_sum = lax.psum_scatter(expr_part, "row", scatter_dimension=0, tiled=True)
    mass_sum = lax.psum_scatter(mass_reach, "row", scatter_dimension=0, tiled=True)
    filter_grad = (
        keep_rate
        * (1.0 - keep_rate)
        * (jnp.sum(cell_expr.astype(jnp.float32) * expr_sum, axis=1) + mass_sum)
    )
    expr_grad = keep_rate[:, None] * expr_sum
    chance_grad = returned.astype(jnp.float32)
    inner_sum = jnp.sum(chances * chance_grad, axis=1, keepdims=True)
    map_grad = chances * (chance_grad - inner_sum)
    return (losses, predicted, map_grad, expr_grad, filter_grad)


def fused_kernel(
    total_spots, total_genes,
    logit_in, filt_in, cell_in, spot_in, cslide_in, sslide_in, bins_in,
    pred_out, map_out, expr_out, filt_out, loss_out,
    chance, own_low, plane_low, plane_turn, cell_v, hand, col, part, send1, early, send2, late,
    pred_h, spot_h, stat, st_sum, st1, st2, st3, spacc, spgot, ob_acc, ob_got, coef, grad,
    sums_up, sums_dn, pass_on, fin, back, back_got, back_low, back_ret, other, other_got,
    f_line, f_pair, f_all, keep_all, m_src, m_got, r_src, r_mate, r_plane_src, r_plane, r_line_src, r_line,
    l_src, l_mate, l_plane, l_line_src, l_line, filt_acc, hot_lie, hot_stand, mass_row,
    load_sem, own_sem, hand_s, hand_r, up_s, dn_s, col_r, low_s, low_r, send1_s, send2_s, early_r, late_r,
    pred_s, pred_r, spot_s, spot_r, st_s, st_r, spx_s, spx_r, ob_s, ob_r, g_s, g_r, rs_s, rs_r, fin_r, back_s, back_r,
    ret_s, ret_r, oth_s, oth_r, sm_s, sm_r,
):
    f32, b16 = jnp.float32, jnp.bfloat16
    half = col.shape[2]
    chunks = half // WIDTH
    units = WIDTH // 128
    keep = {}
    z = lax.axis_index("row")
    c = lax.axis_index("col")
    j = lax.div(c, 2)
    k = lax.rem(c, 2)
    y = lax.div(j, 2)
    x = lax.rem(j, 2)
    mate = 1 - k

    def dev(zz, jj, kk):
        return (zz, jj * 2 + kk)

    jx = y * 2 + (1 - x)
    jy = (1 - y) * 2 + x
    jd = (1 - y) * 2 + (1 - x)
    dev_mate = dev(z, j, mate)
    dev_x = dev(z, jx, k)
    dev_y = dev(z, jy, k)
    dev_up = dev(lax.rem(z + 1, 4), j, k)
    dev_dn = dev(lax.rem(z + 3, 4), j, k)
    cross_up = dev(lax.rem(z + 1, 4), j, mate)
    cross_dn = dev(lax.rem(z + 3, 4), j, mate)
    plane_others = (jx, jy, jd)
    line_others = [lax.rem(z + i, 4) for i in (1, 2, 3)]

    def rc(src, dst, ss, rs, to):
        return pltpu.make_async_remote_copy(
            src_ref=src, dst_ref=dst, send_sem=ss, recv_sem=rs, device_id=to, device_id_type=MESH
        )

    def got(ref, sem):
        rc(ref, ref, sem, sem, dev_mate).wait_recv()

    def sent(ref, sem):
        rc(ref, ref, sem, sem, dev_mate).wait_send()

    def rows(i, size):
        return pl.ds(pl.multiple_of(i * size, size), size)

    def at_chunk(q):
        return pl.ds(q * WIDTH, WIDTH)

    def lanes(kk, q):
        return pl.ds(pl.multiple_of(kk * half + q * WIDTH, WIDTH), WIDTH)

    load_cell = pltpu.make_async_copy(cell_in, cell_v, load_sem.at[0])
    load_logit = pltpu.make_async_copy(logit_in, chance, load_sem.at[1])
    load_spot = pltpu.make_async_copy(
        spot_in.at[:, pl.ds(pl.multiple_of(k * half, half), half)], spot_h.at[rows(k, 128)], load_sem.at[2]
    )
    barrier = pltpu.get_barrier_semaphore()
    for to in (
        dev_mate, dev_x, dev_y, dev(z, jd, k),
        dev(line_others[0], j, k), dev(line_others[1], j, k), dev(line_others[2], j, k),
        cross_up, cross_dn,
    ):
        pl.semaphore_signal(barrier, inc=1, device_id=to, device_id_type=MESH)
    load_cell.start()
    load_logit.start()
    load_spot.start()

    eye = lax.broadcasted_iota(jnp.int32, (128, 128), 0) == lax.broadcasted_iota(
        jnp.int32, (128, 128), 1
    )
    lane = lax.broadcasted_iota(jnp.int32, (128, 128), 1)

    def stand(row):
        return jnp.sum(jnp.where(eye, jnp.broadcast_to(row, (128, 128)), 0.0), 1, keepdims=True)

    def lie(column):
        return jnp.sum(jnp.where(eye, jnp.broadcast_to(column, (128, 128)), 0.0), 0, keepdims=True)

    filt_row = filt_in[...].astype(f32)
    keep_col = stand(jax.nn.sigmoid(filt_row))
    slide_col = stand(sslide_in[...].astype(f32))
    bins_col = stand(bins_in[...].astype(f32))

    def hand_copy(q):
        return rc(hand.at[q], col.at[z, rows(k, 128), rows(q, WIDTH)], hand_s, hand_r, dev_mate)

    def col_up(q, b):
        at = col.at[b, :, at_chunk(q)]
        return rc(at, at, up_s, col_r.at[q, b], dev_up)

    def col_dn(q, b):
        at = col.at[b, :, at_chunk(q)]
        return rc(at, at, dn_s, col_r.at[q, b], dev_dn)

    def scale_cells(q):
        hand[q] = (keep_col * cell_v[:, lanes(mate, q)].astype(f32)).astype(b16)
        col[z, rows(k, 128), rows(q, WIDTH)] = (keep_col * cell_v[:, lanes(k, q)].astype(f32)).astype(b16)

    def col_own(q):
        own = col.at[z, rows(k, 128), at_chunk(q)]

        @pl.when(z < 3)
        def _():
            rc(own, own, up_s, col_r.at[q, z], dev_up).start()
            rc(hand.at[q], own, up_s, col_r.at[q, z], cross_up).start()

        @pl.when(z > 0)
        def _():
            rc(own, own, dn_s, col_r.at[q, z], dev_dn).start()
            rc(hand.at[q], own, dn_s, col_r.at[q, z], cross_dn).start()

    hops = [(q, s) for q in range(chunks) for s in range(3)]

    def hop():
        q, s = hops.pop(0)

        @pl.when(z - 1 - s >= 0)
        def _():
            b = z - 1 - s
            got(col.at[b, :, at_chunk(q)], col_r.at[q, b])

            @pl.when(z < 3)
            def _():
                col_up(q, b).start()

        @pl.when(z + 1 + s <= 3)
        def _():
            b = z + 1 + s
            got(col.at[b, :, at_chunk(q)], col_r.at[q, b])

            @pl.when(z > 0)
            def _():
                col_dn(q, b).start()

    load_cell.wait()
    scale_cells(0)
    pl.semaphore_wait(barrier, 9)
    hand_copy(0).start()

    @pl.loop(1, chunks)
    def _(q):
        scale_cells(q)
        hand_copy(q).start()

    def spread(source, slots, which, i):
        for o in plane_others if which == "plane" else line_others:
            to = dev(z, o, k) if which == "plane" else dev(o, j, k)
            rc(source(o), slots.at[j if which == "plane" else z], sm_s.at[i], sm_r.at[i], to).start()

    def hand_over(source, slot, i):
        rc(source, slot, sm_s.at[i], sm_r.at[i], dev_mate).start()

    f_line[z] = filt_row
    spread(lambda o: f_line.at[z], f_line, "line", 0)

    load_logit.wait()

    def softmax_rows(g):
        at = rows(g, 16)
        logits = chance[at, :]
        pick = lax.broadcasted_iota(jnp.int32, (16, 128), 0) + g * 16
        here = lax.broadcasted_iota(jnp.int32, (16, 128), 1)
        slide = jnp.sum(
            jnp.where(pick == here, jnp.broadcast_to(sslide_in[...].astype(f32), (16, 128)), 0.0),
            1, keepdims=True,
        )
        allowed = slide == cslide_in[...].astype(f32)
        shifted = jnp.where(allowed, logits, -1e30)
        raised = jnp.exp(shifted - jnp.max(shifted, axis=1, keepdims=True))
        value = raised / jnp.sum(raised, axis=1, keepdims=True)
        chance[at, :] = value
        low = value.astype(b16)
        for b in range(4):
            for jj in range(4):
                own_low[jj, at, b * 256 : b * 256 + 256] = low[
                    :, b * 1024 + jj * 256 : b * 1024 + jj * 256 + 256
                ]

    def low_copy(jj):
        return rc(own_low.at[jj], plane_low.at[k, j], low_s.at[0], low_r.at[j], dev(z, jj, k))

    def low_pass(jj):
        return rc(plane_low.at[k, jj], plane_low.at[k, jj], low_s.at[1], low_r.at[4], dev_mate)

    def low_give():
        low_copy(jd).start()
        low_copy(jx).start()
        low_copy(jy).start()

    spot_give = rc(
        spot_in.at[:, pl.ds(pl.multiple_of(mate * half, half), half)], spot_h.at[rows(k, 128)], spot_s, spot_r, dev_mate
    )

    def low_own():
        plane_low[k, j] = own_low[j]
        low_pass(j).start()
        spot_give.start()

    def filt_pair():
        got(f_line.at[pl.ds(0, 3)], sm_r.at[0])
        f_pair[k] = f_line[...]
        hand_over(f_line, f_pair.at[k], 1)

    def filt_plane():
        got(f_line, sm_r.at[1])
        f_all[j] = f_pair[...]
        spread(lambda o: f_pair, f_all, "plane", 2)

    def of_cells(jj, kk, b):
        return own_low[jj, :, pl.ds(pl.multiple_of(b * 256 + kk * 128, 128), 128)].astype(f32)

    def split(d):
        return lax.div(d, 8), lax.rem(lax.div(d, 4), 2), lax.rem(d, 4)

    kind = lax.div(lane, 8)
    of_slide = lax.rem(lane, 8) == slide_col.astype(jnp.int32)

    def mass_make():
        got(f_all.at[pl.ds(0, 3)], sm_r.at[2])
        keep_all[...] = jax.nn.sigmoid(f_all[...])

        def add_mass(d, acc):
            jj, kk, b = split(d)
            return acc + of_cells(jj, kk, b) * keep_all[jj, kk, b]

        mass = jnp.sum(lax.fori_loop(0, 32, add_mass, jnp.zeros((128, 128), f32)), axis=1, keepdims=True)
        keep["mass"] = mass
        log_term = bins_col * (jnp.log(bins_col) - jnp.log(mass))
        values = jnp.where(
            kind == 0, mass, jnp.where(kind == 1, bins_col, jnp.where(kind == 2, log_term, 0.0))
        )
        m_src[0] = jnp.sum(jnp.where(of_slide, values, 0.0), axis=0, keepdims=True)
        m_src[1] = sslide_in[...].astype(f32)
        hand_over(m_src, m_got, 3)

    lane2 = lax.broadcasted_iota(jnp.int32, (256, 128), 1)

    def mass_chip():
        got(m_src, sm_r.at[3])
        load_spot.wait()
        got(spot_h.at[rows(mate, 128)], spot_r)
        stat[...] = jnp.zeros_like(stat)
        chip_row = m_src[0] + m_got[0]
        for o in range(4):
            stat[0, o, 24:25, :] = chip_row
        first = jnp.where(k == 0, m_src[1], m_got[1])
        second = jnp.where(k == 0, m_got[1], m_src[1])
        hot_lie[...] = (
            lax.broadcasted_iota(jnp.int32, (8, 256), 0).astype(f32)
            == jnp.broadcast_to(jnp.concatenate([first, second], axis=1), (8, 256))
        ).astype(f32)
        slides_col = jnp.concatenate([stand(first), stand(second)], axis=0)
        hot_stand[...] = ((lax.rem(lane2, 8) == slides_col.astype(jnp.int32)) & (lane2 < 24)).astype(b16)
        coef[...] = jnp.zeros_like(coef)
        filt_acc[...] = jnp.zeros_like(filt_acc)

    def split_dot(a, v):
        high = v.astype(b16)
        rest = (v - high.astype(f32)).astype(b16)
        return jnp.dot(a, high, preferred_element_type=f32) + jnp.dot(a, rest, preferred_element_type=f32)

    def low_arrive(i):
        if i == 3:
            got(plane_low.at[mate], low_r.at[4])
            got(hand, hand_r)
        else:
            jj = (jx, jy, jd)[i]
            got(plane_low.at[k, jj], low_r.at[jj])
            low_pass(jj).start()

    def product(q, left, count):
        at = pl.ds(q * WIDTH, count * WIDTH)

        @pl.loop(0, 2)
        def _(h):
            if left is plane_low:
                whole = jnp.dot(left[h].reshape(512, 1024), col[:, :, at].reshape(1024, count * WIDTH), preferred_element_type=f32)
            else:
                whole = jnp.dot(left[rows(h, 512), :], grad[:, :, :, at].reshape(1024, count * WIDTH), preferred_element_type=f32)
            for i in range(count):
                part[q + i, h] = whole[:, i * WIDTH : i * WIDTH + WIDTH].reshape(4, 128, WIDTH)

    def reduce_first(q):
        for i, (core, owner, to, sem, slot) in enumerate((
            (0, jd, dev_x, early_r.at[q, 0], early.at[q, 0]),
            (1, jd, dev_y, early_r.at[q, 1], early.at[q, 1]),
            (0, jx, dev_x, late_r.at[q], late.at[q, 0]),
            (1, jy, dev_y, late_r.at[q], late.at[q, 1]),
        )):
            send1[q, i] = part[q, core, owner].astype(b16)
            rc(send1.at[q, i], slot, send1_s, sem, to).start()

    def reduce_second(q, i):
        owner, to = ((jy, dev_y), (jx, dev_x))[i]
        got(early.at[q, i], early_r.at[q, i])
        send2[q, i] = (part[q, i, owner] + early[q, i].astype(f32)).astype(b16)
        rc(send2.at[q, i], late.at[q, 2 + i], send2_s, late_r.at[q], to).start()

    def pred_give(q):
        return rc(
            pred_h.at[rows(mate, 128), pl.ds(q * WIDTH, WIDTH)], pred_out.at[:, lanes(k, q)], pred_s, pred_r, dev_mate
        )

    def pred_own(q):
        return pltpu.make_async_copy(
            pred_h.at[rows(k, 128), pl.ds(q * WIDTH, WIDTH)], pred_out.at[:, lanes(k, q)], own_sem
        )

    def reduce_last(q):
        got(late.at[q], late_r.at[q])
        for i in range(2):
            pred_h[i * 128 : i * 128 + 128, q * WIDTH : q * WIDTH + WIDTH] = part[q, i, j] + (
                late[q, i].astype(f32) + late[q, 2 + i].astype(f32)
            )
        pred_give(q).start()
        pred_own(q).start()

    def reduce_stat(q):
        pr = pred_h[:, q * WIDTH : q * WIDTH + WIDTH]
        sp = spot_h[:, q * WIDTH : q * WIDTH + WIDTH]
        for i, v in enumerate((pr * sp, pr * pr)):
            spacc[i] = v if q == 0 else spacc[i] + v

    def reduce_slides(q):
        pr = pred_h[:, q * WIDTH : q * WIDTH + WIDTH]
        sp = spot_h[:, q * WIDTH : q * WIDTH + WIDTH]
        for i, v in enumerate((pr * sp, pr * pr)):
            stat[q // 4, q % 4, i * 8 : i * 8 + 8] = split_dot(hot_lie[...].astype(b16), v)

    def obs_sums():
        for q in range(chunks):
            sp = spot_h[:, q * WIDTH : q * WIDTH + WIDTH]
            v = sp * sp
            ob_acc[...] = v if q == 0 else ob_acc[...] + v
            stat[q // 4, q % 4, 16:24] = split_dot(hot_lie[...].astype(b16), v)
        rc(ob_acc, ob_got, ob_s, ob_r, dev_mate).start()

    def st_send(g, i):
        slots = (st1, st2, st3)[i]
        if i == 0:
            st1[g, j] = stat[g, j]
        else:
            prior = (st1, st2)[i - 1]
            got(prior.at[g, pl.ds(0, 3)], st_r.at[g, i - 1])
            total = prior[g, 0] + prior[g, 1] + prior[g, 2] + prior[g, 3]
            st_sum[g, i - 1] = total
            if i == 1:
                st2[g, z] = total
            else:
                st3[g, j] = total
        for o in line_others if i == 1 else plane_others:
            src = stat.at[g, o] if i == 0 else st_sum.at[g, i - 1]
            to = dev(o, j, k) if i == 1 else dev(z, o, k)
            rc(src, slots.at[g, z if i == 1 else j], st_s.at[g, i], st_r.at[g, i], to).start()

    def st_finish(g):
        got(st3.at[g, pl.ds(0, 3)], st_r.at[g, 2])

    def turn(i):
        for kk in range(2):
            plane_turn[:, (kk * 4 + i) * 128 : (kk * 4 + i) * 128 + 128] = plane_low[kk, i].astype(f32).T.astype(b16)

    spx = rc(spacc, spgot, spx_s, spx_r, dev_mate)

    def spot_half():
        spx.start()

    slide8 = lax.broadcasted_iota(jnp.int32, (8, 128), 0)
    lane8 = lax.broadcasted_iota(jnp.int32, (8, 128), 1)

    def mass_end():
        sums_row = st_sum[0, 1, 24:25, :]
        each = jnp.broadcast_to(sums_row, (128, 128))
        mass_each = jnp.sum(jnp.where(of_slide & (kind == 0), each, 0.0), 1, keepdims=True)
        bins_each = jnp.sum(jnp.where(of_slide & (kind == 1), each, 0.0), 1, keepdims=True)
        mass_grad = (1.0 / mass_each - bins_col / (bins_each * keep["mass"])) / SLIDES
        keep["grad"] = mass_grad.astype(b16).astype(f32)

        def by_slide(begin):
            return jnp.sum(
                jnp.where(lane8 == slide8 + begin, jnp.broadcast_to(sums_row, (8, 128)), 0.0), 1, keepdims=True
            )

        mass_s, bins_s, log_s = by_slide(0), by_slide(8), by_slide(16)
        kl = jnp.sum(log_s / bins_s - jnp.log(bins_s) + jnp.log(mass_s), axis=0, keepdims=True)
        keep["kl"] = kl / SLIDES

    def reach_make():
        mass_grad = keep["grad"]

        @pl.loop(0, 32)
        def _(d):
            jj, kk, b = split(d)
            r_src[kk, jj, b] = jnp.sum(of_cells(jj, kk, b) * mass_grad, axis=0, keepdims=True)

        hand_over(r_src.at[mate], r_mate, 4)

    def reach_plane():
        got(r_mate, sm_r.at[4])
        r_plane_src[...] = r_src[k] + r_mate[...]
        r_plane[j] = r_plane_src[j]
        spread(lambda o: r_plane_src.at[o], r_plane, "plane", 5)

    def reach_line():
        got(r_plane.at[pl.ds(0, 3)], sm_r.at[5])
        r_line_src[...] = r_plane[0] + r_plane[1] + r_plane[2] + r_plane[3]
        r_line[z] = r_line_src[z]
        spread(lambda o: r_line_src.at[o], r_line, "line", 6)

    def obs_end():
        got(ob_got, ob_r)
        keep["obs_c"] = jnp.sum(ob_acc[...] + ob_got[...], axis=1, keepdims=True)

    def spot_sums():
        st_finish(0)
        got(spgot, spx_r)
        cross_c, pred_c = [jnp.sum(spacc[i] + spgot[i], axis=1, keepdims=True) for i in range(2)]
        obs_c = keep["obs_c"]
        root_c = jnp.sqrt(pred_c * obs_c)
        keep["cos"] = cross_c / root_c
        keep["obs"] = (1.0 / root_c) / total_spots
        keep["prd"] = (cross_c / (pred_c * root_c)) / total_spots

    def grad_make(q):
        scale = 1.0 / (SLIDES * total_genes)
        for e in range(units):
            g, o = divmod(q * units + e, 4)
            sums = st3[g, o]
            cross, prd, obs = sums[:8], sums[8:16], sums[16:24]
            root = jnp.sqrt(prd * obs)
            for i, v in enumerate((scale / root, scale * cross / (prd * root))):
                high = v.astype(b16).astype(f32)
                mid = (v - high).astype(b16).astype(f32)
                low = v - high - mid
                stack = jnp.concatenate([high, mid, low, jnp.zeros((8, 128), f32)], axis=0)
                coef[:32, (i * units + e) * 128 : (i * units + e) * 128 + 128] = stack.astype(b16)
        each_spot = jnp.dot(hot_stand[...], coef[...], preferred_element_type=f32)
        at = slice(q * WIDTH, q * WIDTH + WIDTH)
        value = pred_h[:, at] * (each_spot[:, WIDTH:] + keep["prd"]) - spot_h[:, at] * (each_spot[:, :WIDTH] + keep["obs"])
        value = value.astype(b16)
        grad[0, j, :, at] = value[:128]
        grad[1, j, :, at] = value[128:]

    def gene_cos():
        total = jnp.zeros((8, 128), f32)
        for g in range(2):
            for e in range(4):
                sums = st3[g, e]
                total = total + sums[:8] / jnp.sqrt(sums[8:16] * sums[16:24])
        return jnp.sum(jnp.sum(total, axis=0, keepdims=True), axis=1, keepdims=True)

    def grad_send(q):
        grad_make(q)
        at = grad.at[:, j, :, at_chunk(q)]
        rc(at, at, g_s.at[0], g_r.at[q, 0], dev_x).start()
        rc(at, at, g_s.at[1], g_r.at[q, 1], dev_y).start()

    def grad_direct(q):
        grad_make(q)
        at = grad.at[:, j, :, at_chunk(q)]
        rc(at, at, g_s.at[4], g_r.at[q, 2], dev(z, jd, k)).start()
        rc(at, at, g_s.at[0], g_r.at[q, 0], dev_x).start()
        rc(at, at, g_s.at[1], g_r.at[q, 1], dev_y).start()

    def grad_pass(q, i):
        owner, to = ((jx, dev_y), (jy, dev_x))[i]
        got(grad.at[:, owner, :, at_chunk(q)], g_r.at[q, i])
        at = grad.at[i, owner, :, at_chunk(q)]
        rc(at, at, g_s.at[2 + i], g_r.at[q, 2], to).start()

    def run_up(q, b):
        return rc(pass_on.at[q, b], sums_up.at[q, b], rs_s, rs_r.at[q, b], dev_up)

    def run_dn(q, b):
        return rc(pass_on.at[q, b], sums_dn.at[q, b], rs_s, rs_r.at[q, b], dev_dn)

    def block(q, b):
        return part[q, b // 2, pl.ds(2 * (b % 2), 2)].reshape(256, WIDTH)

    def run_last(q, b, up):
        i = 0 if up else 1
        to, cross = (dev_up, cross_up) if up else (dev_dn, cross_dn)
        rc(pass_on.at[q, b, rows(k, 128)], fin.at[q, i, k], rs_s, fin_r.at[q], to).start()
        rc(pass_on.at[q, b, rows(mate, 128)], fin.at[q, i, k], rs_s, fin_r.at[q], cross).start()

    def sums_half(q, h):
        whole = jnp.dot(
            plane_turn[rows(h, 512), :], grad[:, :, :, at_chunk(q)].reshape(1024, WIDTH), preferred_element_type=f32
        )
        part[q, h] = whole.reshape(4, 128, WIDTH)

    def sums_give(q, b):
        pass_on[q, b] = block(q, b).astype(b16)

    def sums_first(q, count):
        for i in range(count):
            if DIRECT == q + i:
                got(grad.at[:, jx, :, at_chunk(q + i)], g_r.at[q + i, 0])
                got(grad.at[:, jy, :, at_chunk(q + i)], g_r.at[q + i, 1])
            got(grad.at[:, jd, :, at_chunk(q + i)], g_r.at[q + i, 2])
        if count == 2:
            product(q, plane_turn, count)
        for step in range(2):
            if count == 1:
                sums_half(q, jnp.where(z < 2, 1 - step, step))

            @pl.when(z == 0)
            def _():
                for i in range(count):
                    for b in ((3, 2), (1,))[step]:
                        sums_give(q + i, b)
                        run_last(q + i, b, True) if b == 1 else run_up(q + i, b).start()

            @pl.when(z == 3)
            def _():
                for i in range(count):
                    for b in ((0, 1), (2,))[step]:
                        sums_give(q + i, b)
                        run_last(q + i, b, False) if b == 2 else run_dn(q + i, b).start()

    def pass_up(q, b):
        def add():
            got(sums_up.at[q, b], rs_r.at[q, b])
            pass_on[q, b] = (block(q, b) + sums_up[q, b].astype(f32)).astype(b16)

        if b == 3:
            @pl.when(z == 1)
            def _():
                add()
                run_up(q, b).start()

        @pl.when(z == b - 1)
        def _():
            add()
            run_last(q, b, True)

    def pass_dn(q, b):
        def add():
            got(sums_dn.at[q, b], rs_r.at[q, b])
            pass_on[q, b] = (block(q, b) + sums_dn[q, b].astype(f32)).astype(b16)

        if b == 0:
            @pl.when(z == 2)
            def _():
                add()
                run_dn(q, b).start()

        @pl.when(z == b + 1)
        def _():
            add()
            run_last(q, b, False)

    def other_give(q):
        return rc(other.at[q], other_got.at[q], oth_s, oth_r.at[q], dev_mate)

    def use_sums(q, kk, sums):
        at = lanes(kk, q)
        expr_out[:, at] = keep_col * sums
        weighed = cell_v[:, at].astype(f32) * sums
        for e in range(units):
            filt_acc[...] = filt_acc[...] + weighed[:, e * 128 : e * 128 + 128]

    def sums_other(q):
        other[q] = part[q, lax.div(z, 2), 2 * lax.rem(z, 2) + mate]
        other_give(q).start()

    def sums_last(q):
        @pl.when(z == 0)
        def _():
            got(fin.at[q, 1], fin_r.at[q])

        @pl.when(z == 3)
        def _():
            got(fin.at[q, 0], fin_r.at[q])

        @pl.when((z > 0) & (z < 3))
        def _():
            got(fin.at[q], fin_r.at[q])

        got(other_got.at[q], oth_r.at[q])
        own_at = (q, lax.div(z, 2), 2 * lax.rem(z, 2) + k)
        for kk, base in ((k, part[own_at]), (mate, other_got[q])):
            up = jnp.where(z > 0, fin[q, 0, kk].astype(f32), 0.0)
            dn = jnp.where(z < 3, fin[q, 1, kk].astype(f32), 0.0)
            use_sums(q, kk, base + (up + dn))

    def back_dot(b):
        @pl.loop(0, 2)
        def _(h):
            back[b, h] = lax.dot_general(
                grad[h].reshape(512, half), col[b], (((1,), (1,)), ((), ())), preferred_element_type=f32
            ).reshape(4, 128, 256)

        rc(back.at[b, mate], back_got.at[b], back_s, back_r.at[b], dev_mate).start()

    def back_add(b):
        got(back_got.at[b], back_r.at[b])
        for jj in range(4):
            back_low[jj, :, rows(b, 256)] = (back[b, k, jj] + back_got[b, jj]).astype(b16)

    def ret_send():
        for jj in (jd, jx, jy):
            rc(back_low.at[jj], back_ret.at[j], ret_s, ret_r, dev(z, jj, k)).start()
        back_ret[j] = back_low[j]

    loss_lane = lax.broadcasted_iota(jnp.int32, (1, 128), 1)

    def loss_mate():
        own_cos = jnp.sum(keep["cos"], axis=0, keepdims=True)
        l_src[...] = jnp.where(loss_lane == 0, own_cos, jnp.where(loss_lane == 1, gene_cos(), 0.0))
        hand_over(l_src, l_mate, 7)
        l_plane[j] = l_src[...]
        spread(lambda o: l_src, l_plane, "plane", 8)

    def loss_line():
        got(l_plane.at[pl.ds(0, 3)], sm_r.at[8])
        total = l_plane[0] + l_plane[1] + l_plane[2] + l_plane[3]
        l_line_src[...] = total
        l_line[z] = total
        spread(lambda o: l_line_src, l_line, "line", 9)

    def loss_end():
        got(l_line.at[pl.ds(0, 3)], sm_r.at[9])
        got(l_mate, sm_r.at[7])
        cos_row = l_line[0] + l_line[1] + l_line[2] + l_line[3]
        gene_row = l_src[...] + l_mate[...]
        cos_total = jnp.sum(jnp.where(loss_lane == 0, cos_row, 0.0), axis=1, keepdims=True)
        gene_total = jnp.sum(jnp.where(loss_lane == 1, gene_row, 0.0), axis=1, keepdims=True)
        gene_loss = 1.0 - gene_total / (SLIDES * total_genes)
        spot_loss = 1.0 - cos_total / total_spots
        kl_loss = keep["kl"]
        total_loss = gene_loss + spot_loss + kl_loss
        picked = jnp.where(loss_lane == 2, spot_loss, jnp.where(loss_lane == 3, kl_loss, 0.0))
        loss_out[...] = jnp.where(loss_lane == 0, total_loss, jnp.where(loss_lane == 1, gene_loss, picked))

    def map_rows(g):
        at = rows(g, 16)
        pick = lax.broadcasted_iota(jnp.int32, (16, 128), 0) + g * 16
        here = lax.broadcasted_iota(jnp.int32, (16, 128), 1)
        mg = jnp.sum(jnp.where(pick == here, jnp.broadcast_to(mass_row[...], (16, 128)), 0.0), 1, keepdims=True)
        inner = jnp.zeros((16, 128), f32)
        for d in range(32):
            b, jj, kk = d // 8, (d % 8) // 2, d % 2
            used = back_ret[jj, at, b * 256 + kk * 128 : b * 256 + kk * 128 + 128].astype(f32) + mg * keep_all[jj, kk, b]
            inner = inner + chance[at, d * 128 : d * 128 + 128] * used
            map_out[at, d * 128 : d * 128 + 128] = used
        inner = jnp.sum(inner, axis=1, keepdims=True)
        map_out[at, :] = chance[at, :] * (map_out[at, :] - inner)

    def map_all():
        got(back_ret.at[pl.ds(0, 3)], ret_r)
        mass_row[...] = lie(keep["grad"])
        pl.loop(0, 8)(map_rows)

    steps = {
        "x": lambda i: pl.loop(2 * i, 2 * i + 2)(softmax_rows), "w": lambda i: (low_give, low_own)[i](),
        "c": col_own, "h": lambda i: hop(), "i": lambda i: (filt_pair, filt_plane, mass_make, mass_chip)[i](),
        "a": low_arrive, "q": turn, "p": lambda q: product(q, plane_low, 1), "P": lambda q: product(q, plane_low, 2),
        "f": reduce_first, "s": lambda q: reduce_second(q, 0), "S": lambda q: reduce_second(q, 1),
        "l": reduce_last, "k": reduce_stat, "j": reduce_slides, "B": lambda i: (obs_sums, obs_end)[i](), "t": lambda i: st_send(0, i), "z": lambda i: (spot_half, mass_end, spot_sums)[i](),
        "g": grad_send, "G": grad_direct, "m": lambda q: grad_pass(q, 0), "n": lambda q: grad_pass(q, 1),
        "y": lambda i: st_send(1, i) if i < 3 else st_finish(1), "r": lambda q: sums_first(q, 1), "R": lambda q: sums_first(q, 2),
        "U": lambda q: pass_up(q, 3), "V": lambda q: pass_up(q, 2), "D": lambda q: pass_dn(q, 0), "E": lambda q: pass_dn(q, 1),
        "L": sums_last, "O": sums_other, "b": back_dot, "A": back_add, "T": lambda i: ret_send(), "M": lambda i: map_all(),
        "e": lambda i: (reach_make, reach_plane, reach_line)[i](), "o": lambda i: (loss_mate, loss_line, loss_end)[i](),
    }
    for group in ORDER:
        for word in group.split():
            steps[word[0]](int(word[1:]) if len(word) > 1 else 0)

    got(r_line.at[pl.ds(0, 3)], sm_r.at[6])
    reach_row = r_line[0] + r_line[1] + r_line[2] + r_line[3]
    filt_sum = jnp.sum(filt_acc[...], axis=1, keepdims=True)
    keep_row = jax.nn.sigmoid(filt_in[...].astype(f32))
    filt_out[...] = keep_row * (1.0 - keep_row) * (lie(filt_sum) + reach_row)

    sent(hand, hand_s)
    spot_give.wait_send()
    sent(send1, send1_s)
    sent(send2, send2_s)
    sent(pred_h.at[rows(mate, 128)], pred_s)
    got(pred_out.at[:, pl.ds(pl.multiple_of(mate * half, half), half)], pred_r)
    pltpu.make_async_copy(
        pred_h.at[rows(k, 128)], pred_out.at[:, pl.ds(pl.multiple_of(k * half, half), half)], own_sem
    ).wait()
    for i in range(2):
        sent(grad.at[:, j], g_s.at[i])
    others = [q for q in range(chunks) if q != DIRECT]
    sent(grad.at[0, jx, :, pl.ds(0, len(others) * WIDTH)], g_s.at[2])
    sent(grad.at[1, jy, :, pl.ds(0, len(others) * WIDTH)], g_s.at[3])
    if DIRECT is not None:
        sent(grad.at[:, j, :, at_chunk(DIRECT)], g_s.at[4])
    sent(ob_acc, ob_s)
    for i in range(3):
        @pl.when(z == i)
        def _():
            sent(col.at[pl.ds(0, i + 1)], up_s)

        @pl.when(z == 3 - i)
        def _():
            sent(col.at[pl.ds(3 - i, i + 1)], dn_s)
    sent(pass_on.at[:, pl.ds(0, 3)], rs_s)
    sent(plane_low.at[k, pl.ds(0, 3)], low_s.at[0])
    sent(plane_low.at[k], low_s.at[1])
    for g in range(2):
        for i in range(3):
            sent(st1.at[g, pl.ds(0, 3)], st_s.at[g, i])
    spx.wait_send()
    sent(back_got, back_s)
    sent(back_low.at[pl.ds(0, 3)], ret_s)
    sent(other, oth_s)
    for i, ref in enumerate((
        f_line.at[pl.ds(0, 3)], f_line, f_all.at[pl.ds(0, 3)], m_src, r_mate, r_plane.at[pl.ds(0, 3)],
        r_line.at[pl.ds(0, 3)], l_mate, l_plane.at[pl.ds(0, 3)], l_line.at[pl.ds(0, 3)],
    )):
        sent(ref, sm_s.at[i])


def hand_out(pred_in, map_in, expr_in, filt_in, loss_in, pred_out, map_out, expr_out, filt_out, loss_out, sems):
    pairs = ((map_in, map_out), (pred_in, pred_out), (expr_in, expr_out))
    copies = [pltpu.make_async_copy(src, dst, sems.at[i]) for i, (src, dst) in enumerate(pairs)]
    for copy in copies:
        copy.start()
    filt_out[...] = filt_in[...]
    loss_out[...] = loss_in[:, :4]
    for copy in copies:
        copy.wait()


def fused_shards(map_logits, filter_logits, cell_expr, spot_expr, cell_slide, spot_slide, density_bins):
    f32, b16 = jnp.float32, jnp.bfloat16
    spots, cells = map_logits.shape
    genes = cell_expr.shape[1]
    n = genes // (2 * WIDTH)
    V, S = pltpu.VMEM, pltpu.SemaphoreType.DMA
    any_, vmem = pl.BlockSpec(memory_space=pl.ANY), pl.BlockSpec(memory_space=pltpu.VMEM)
    one = S(())
    scratch = [
        V((128, cells), f32),
        V((4, 128, 1024), b16),
        V((2, 4, 128, 1024), b16),
        V((1024, 1024), b16),
        V((128, genes), b16),
        V((n, 128, WIDTH), b16),
        V((4, 256, genes // 2), b16),
        V((n, 2, 4, 128, WIDTH), f32),
        V((n, 4, 128, WIDTH), b16),
        V((n, 2, 128, WIDTH), b16),
        V((n, 2, 128, WIDTH), b16),
        V((n, 4, 128, WIDTH), b16),
        V((256, genes // 2), f32),
        V((256, genes // 2), f32),
        V((2, 4, 32, 128), f32),
        V((2, 2, 32, 128), f32),
        V((2, 4, 32, 128), f32),
        V((2, 4, 32, 128), f32),
        V((2, 4, 32, 128), f32),
        V((2, 256, 128), f32),
        V((2, 256, 128), f32),
        V((256, 128), f32),
        V((256, 128), f32),
        V((128, 2 * WIDTH), b16),
        V((2, 4, 128, genes // 2), b16),
        V((n, 4, 256, WIDTH), b16),
        V((n, 4, 256, WIDTH), b16),
        V((n, 4, 256, WIDTH), b16),
        V((n, 2, 2, 128, WIDTH), b16),
        V((4, 2, 4, 128, 256), f32),
        V((4, 4, 128, 256), f32),
        V((4, 128, 1024), b16),
        V((4, 128, 1024), b16),
        V((n, 128, WIDTH), f32),
        V((n, 128, WIDTH), f32),
        V((4, 1, 128), f32),
        V((2, 4, 1, 128), f32),
        V((4, 2, 4, 1, 128), f32),
        V((4, 2, 4, 1, 128), f32),
        V((2, 1, 128), f32),
        V((2, 1, 128), f32),
        V((2, 4, 4, 1, 128), f32),
        V((4, 4, 1, 128), f32),
        V((4, 4, 1, 128), f32),
        V((4, 4, 1, 128), f32),
        V((4, 1, 128), f32),
        V((4, 1, 128), f32),
        V((1, 128), f32),
        V((1, 128), f32),
        V((4, 1, 128), f32),
        V((1, 128), f32),
        V((4, 1, 128), f32),
        V((128, 128), f32),
        V((8, 256), f32),
        V((256, 128), b16),
        V((1, 128), f32),
        S((3,)), one, one, one, one, one, S((n, 4)), S((2,)), S((5,)),
        one, one, S((n, 2)), S((n,)),
        one, one, one, one, S((2, 3)), S((2, 3)), one, one, one, one,
        S((5,)), S((n, 3)), one, S((n, 4)), S((n,)), one, S((4,)),
        one, one, one, S((n,)), S((10,)), S((10,)),
    ]
    predicted, map_grad, expr_grad, filt, loss = pl.pallas_call(
        functools.partial(fused_kernel, float(spots * 32), float(genes)),
        out_shape=(
            pltpu.VMEM((spots, genes), f32),
            pltpu.VMEM((spots, cells), f32),
            pltpu.VMEM((spots, genes), f32),
            V((1, 128), f32),
            V((1, 128), f32),
        ),
        in_specs=[any_, vmem, any_, any_, vmem, vmem, vmem],
        out_specs=(vmem, vmem, vmem, vmem, vmem),
        scratch_shapes=scratch,
        compiler_params=pltpu.CompilerParams(
            collective_id=0, has_side_effects=True, vmem_limit_bytes=58 * 2**20
        ),
        name="mapping_step",
    )(
        map_logits,
        filter_logits.reshape(1, 128),
        cell_expr,
        spot_expr,
        cell_slide.reshape(1, cells),
        spot_slide.reshape(1, 128),
        density_bins.reshape(1, 128),
    )
    predicted, map_grad, expr_grad, filt, loss = pl.pallas_call(
        hand_out,
        out_shape=(
            jax.ShapeDtypeStruct((spots, genes), f32),
            jax.ShapeDtypeStruct((spots, cells), f32),
            jax.ShapeDtypeStruct((spots, genes), f32),
            jax.ShapeDtypeStruct((1, 128), f32),
            jax.ShapeDtypeStruct((1, 4), f32),
        ),
        in_specs=[vmem] * 5,
        out_specs=(any_, any_, any_, vmem, vmem),
        scratch_shapes=[S((3,))],
        compiler_params=pltpu.CompilerParams(vmem_limit_bytes=2**20),
        name="hand_out",
    )(*[pltpu.with_memory_space_constraint(v, pltpu.VMEM) for v in (predicted, map_grad, expr_grad, filt, loss)])
    return loss.reshape(4), predicted, map_grad, expr_grad, filt.reshape(128)


def solution(mesh):
    both = P(("row", "col"))
    rows = P(("row", "col"), None)
    in_specs = (rows, both, rows, rows, P(), both, both)
    out_specs = (P(), rows, rows, rows, both)
    step = fused_shards if (mesh.shape["row"], mesh.shape["col"]) == (4, 8) else shards
    return jax.shard_map(step, mesh=mesh, in_specs=in_specs, out_specs=out_specs, check_vma=False)
```

```python
import functools

import jax
import jax.numpy as jnp
from jax import lax
from jax.experimental import pallas as pl
from jax.experimental.pallas import tpu as pltpu
from jax.sharding import PartitionSpec as P

SLIDES = 8
ROWS, PLANE, CORES = 4, 4, 2
WIDTH = 128
MESH = pl.DeviceIdType.MESH
DIRECT = 0
ORDER = (
    "c0 c1 c2 x1",
    "x3 i0 x0 x2",
    "i1 w0 h w1",
    "c3 c4 i2 h",
    "i3 h h c5",
    "B0 h h h",
    "a2 h h h",
    "a0 a1 c6 h",
    "a3 P0 f1 h",
    "h f0 c7 P2",
    "f3 f2 h h",
    "h p4 s1 S0",
    "s0 S1 S3 s3",
    "f4 s2 h h",
    "h p5 S2 f5",
    "l1 l0 l3 j0",
    "h j1 h h",
    "p6 f6 l2 j2",
    "j3 t0 s4 k0",
    "h S4 S5 h",
    "p7 f7 q1 s6",
    "t1 S6 s5 l4",
    "k4 q3 k1 s7",
    "S7 k2 j4 q2",
    "l6 t2 l5 k5",
    "k6 l7 k7 k3",
    "z0 j5 j6 j7",
    "y0 B1 z2 G0",
    "q0 g1 g2 y1",
    "y2 W0 r0 m1",
    "n1 g3 y3 g6",
    "n2 m2 W1 r1",
    "V0 m3 n3 g7",
    "O0 z1 g5 o0",
    "O1 g4 n6 W2",
    "r2 e0 n7 m7",
    "W3 n5 r3 U1",
    "m6 m5 m4 n4",
    "o1 U0 V2 W7",
    "r7 U2 W6 r6",
    "W5 W4 b0 R4",
    "V1 b2 e1 U3",
    "A0 T0 D1 O7",
    "V3 D0 O2 b1",
    "A2 T2 U7 b3",
    "V7 A1 O4 U6",
    "T1 O5 A3 e2",
    "D7 V6 O3 T3",
    "D3 O6 L1 U4",
    "L3 D2 L7 V4",
    "o2 D6 L2 U5",
    "L6 L0 D4 V5",
    "M0 M2 D5 L4",
    "M1 M3 L5",
)


def shards(map_logits, filter_logits, cell_expr, spot_expr, cell_slide, spot_slide, density_bins):
    highest = lax.Precision.HIGHEST
    both = ("row", "col")
    rows_count = lax.axis_size("row")
    cols_count = lax.axis_size("col")
    spot_dev, cell_total = map_logits.shape
    cell_dev = filter_logits.shape[0]
    spot_total = spot_dev * rows_count * cols_count
    gene_count = cell_expr.shape[1]
    keep_rate = jax.nn.sigmoid(filter_logits.astype(jnp.float32))
    scaled = (keep_rate[:, None] * cell_expr.astype(jnp.float32)).astype(jnp.bfloat16)
    scaled_col = lax.all_gather(scaled, "row", axis=0, tiled=True)
    allowed = spot_slide[:, None] == cell_slide[None, :]
    shifted = jnp.where(allowed, map_logits, -1e30)
    row_peak = jnp.max(shifted, axis=1, keepdims=True)
    raised = jnp.exp(shifted - row_peak)
    chances = raised / jnp.sum(raised, axis=1, keepdims=True)
    chance_low = chances.astype(jnp.bfloat16)
    by_col = chance_low.reshape(spot_dev, rows_count, cols_count, cell_dev)
    mapped = lax.all_to_all(by_col, "col", split_axis=2, concat_axis=0, tiled=True)
    mapped = mapped.reshape(spot_dev * cols_count, rows_count * cell_dev)
    keep_col = lax.all_gather(keep_rate, "row", axis=0, tiled=True)
    part_pred = jnp.dot(mapped, scaled_col, preferred_element_type=jnp.float32)
    part_mass = jnp.dot(mapped, keep_col, precision=highest, preferred_element_type=jnp.float32)
    predicted = lax.psum_scatter(part_pred, "col", scatter_dimension=0, tiled=True)
    mass = lax.psum_scatter(part_mass, "col", scatter_dimension=0, tiled=True)
    onehot = (spot_slide[:, None] == jnp.arange(SLIDES, dtype=jnp.int32)[None, :]).astype(
        jnp.float32
    )
    cross_term = predicted * spot_expr
    pred_sq = predicted * predicted
    obs_sq = spot_expr * spot_expr
    spot_cross = jnp.sum(cross_term, axis=1)
    spot_pred = jnp.sum(pred_sq, axis=1)
    spot_root = jnp.sqrt(spot_pred * jnp.sum(obs_sq, axis=1))
    spot_cos = spot_cross / spot_root
    bin_values = density_bins.astype(jnp.float32)
    log_term = bin_values * (jnp.log(bin_values) - jnp.log(mass))
    all_cross, all_pred, all_obs, slide_mass, slide_bins, slide_log, cos_total = lax.psum(
        (
            jnp.dot(onehot.T, cross_term, precision=highest),
            jnp.dot(onehot.T, pred_sq, precision=highest),
            jnp.dot(onehot.T, obs_sq, precision=highest),
            jnp.dot(onehot.T, mass, precision=highest),
            jnp.dot(onehot.T, bin_values, precision=highest),
            jnp.dot(onehot.T, log_term, precision=highest),
            jnp.sum(spot_cos),
        ),
        both,
    )
    gene_root = jnp.sqrt(all_pred * all_obs)
    gene_loss = 1.0 - jnp.mean(all_cross / gene_root)
    spot_loss = 1.0 - cos_total / spot_total
    kl_loss = jnp.mean(slide_log / slide_bins - jnp.log(slide_bins) + jnp.log(slide_mass))
    total_loss = gene_loss + spot_loss + kl_loss
    losses = jnp.stack([total_loss, gene_loss, spot_loss, kl_loss])
    gene_scale = 1.0 / (SLIDES * gene_count)
    coef_obs = jnp.dot(onehot, 1.0 / gene_root, precision=highest)
    coef_pred = jnp.dot(onehot, all_cross / (all_pred * gene_root), precision=highest)
    pred_grad = -gene_scale * (spot_expr * coef_obs - predicted * coef_pred)
    pred_grad = (
        pred_grad
        - (
            spot_expr / spot_root[:, None]
            - predicted * (spot_cross / (spot_pred * spot_root))[:, None]
        )
        / spot_total
    )
    mass_each = jnp.dot(onehot, slide_mass, precision=highest)
    bins_each = jnp.dot(onehot, slide_bins, precision=highest)
    mass_grad = (1.0 / mass_each - bin_values / (bins_each * mass)) / SLIDES
    grad_low = pred_grad.astype(jnp.bfloat16)
    mass_low = mass_grad.astype(jnp.bfloat16)
    grad_block = lax.all_gather(grad_low, "col", axis=0, tiled=True)
    mass_block = lax.all_gather(mass_low, "col", axis=0, tiled=True)
    back_map = lax.dot_general(
        grad_block, scaled_col, (((1,), (1,)), ((), ())), preferred_element_type=jnp.float32
    )
    back_map = back_map + mass_block.astype(jnp.float32)[:, None] * keep_col[None, :]
    back_low = back_map.astype(jnp.bfloat16)
    returned = lax.all_to_all(
        back_low.reshape(spot_dev * cols_count, rows_count, 1, cell_dev),
        "col",
        split_axis=0,
        concat_axis=2,
        tiled=True,
    ).reshape(spot_dev, cell_total)
    expr_part = lax.dot_general(
        mapped, grad_block, (((0,), (0,)), ((), ())), preferred_element_type=jnp.float32
    )
    mass_reach = lax.dot_general(
        mapped, mass_block, (((0,), (0,)), ((), ())), preferred_element_type=jnp.float32
    )
    expr_sum = lax.psum_scatter(expr_part, "row", scatter_dimension=0, tiled=True)
    mass_sum = lax.psum_scatter(mass_reach, "row", scatter_dimension=0, tiled=True)
    filter_grad = (
        keep_rate
        * (1.0 - keep_rate)
        * (jnp.sum(cell_expr.astype(jnp.float32) * expr_sum, axis=1) + mass_sum)
    )
    expr_grad = keep_rate[:, None] * expr_sum
    chance_grad = returned.astype(jnp.float32)
    inner_sum = jnp.sum(chances * chance_grad, axis=1, keepdims=True)
    map_grad = chances * (chance_grad - inner_sum)
    return (losses, predicted, map_grad, expr_grad, filter_grad)


def fused_kernel(
    total_spots, total_genes,
    logit_in, filt_in, cell_in, spot_in, cslide_in, sslide_in, bins_in,
    pred_out, map_out, expr_out, filt_out, loss_out,
    chance, own_low, plane_low, plane_turn, cell_v, hand, col, part, send1, early, send2, late,
    pred_h, spot_h, stat, st_sum, st1, st2, st3, spacc, spgot, ob_acc, ob_got, coef, grad,
    sums_up, sums_dn, pass_on, fin, back, back_got, back_low, back_ret, other, other_got,
    f_line, f_pair, f_all, keep_all, m_src, m_got, r_src, r_mate, r_plane_src, r_plane, r_line_src, r_line,
    l_src, l_mate, l_plane, l_line_src, l_line, filt_acc, hot_lie, hot_stand, mass_row,
    load_sem, own_sem, hand_s, hand_r, up_s, dn_s, col_r, low_s, low_r, send1_s, send2_s, early_r, late_r,
    pred_s, pred_r, spot_s, spot_r, st_s, st_r, spx_s, spx_r, ob_s, ob_r, g_s, g_r, rs_s, rs_r, fin_r, back_s, back_r,
    ret_s, ret_r, oth_s, oth_r, sm_s, sm_r,
):
    f32, b16 = jnp.float32, jnp.bfloat16
    half = col.shape[2]
    chunks = half // WIDTH
    units = WIDTH // 128
    keep = {}
    z = lax.axis_index("row")
    c = lax.axis_index("col")
    j = lax.div(c, 2)
    k = lax.rem(c, 2)
    y = lax.div(j, 2)
    x = lax.rem(j, 2)
    mate = 1 - k

    def dev(zz, jj, kk):
        return (zz, jj * 2 + kk)

    jx = y * 2 + (1 - x)
    jy = (1 - y) * 2 + x
    jd = (1 - y) * 2 + (1 - x)
    dev_mate = dev(z, j, mate)
    dev_x = dev(z, jx, k)
    dev_y = dev(z, jy, k)
    dev_up = dev(lax.rem(z + 1, 4), j, k)
    dev_dn = dev(lax.rem(z + 3, 4), j, k)
    cross_up = dev(lax.rem(z + 1, 4), j, mate)
    cross_dn = dev(lax.rem(z + 3, 4), j, mate)
    plane_others = (jx, jy, jd)
    line_others = [lax.rem(z + i, 4) for i in (1, 2, 3)]

    def rc(src, dst, ss, rs, to):
        return pltpu.make_async_remote_copy(
            src_ref=src, dst_ref=dst, send_sem=ss, recv_sem=rs, device_id=to, device_id_type=MESH
        )

    def got(ref, sem):
        rc(ref, ref, sem, sem, dev_mate).wait_recv()

    def sent(ref, sem):
        rc(ref, ref, sem, sem, dev_mate).wait_send()

    def rows(i, size):
        return pl.ds(pl.multiple_of(i * size, size), size)

    def at_chunk(q):
        return pl.ds(q * WIDTH, WIDTH)

    def lanes(kk, q):
        return pl.ds(pl.multiple_of(kk * half + q * WIDTH, WIDTH), WIDTH)

    load_cell = pltpu.make_async_copy(cell_in, cell_v, load_sem.at[0])
    load_logit = pltpu.make_async_copy(logit_in, chance, load_sem.at[1])
    load_spot = pltpu.make_async_copy(
        spot_in.at[:, pl.ds(pl.multiple_of(k * half, half), half)], spot_h.at[rows(k, 128)], load_sem.at[2]
    )
    barrier = pltpu.get_barrier_semaphore()
    for to in (
        dev_mate, dev_x, dev_y, dev(z, jd, k),
        dev(line_others[0], j, k), dev(line_others[1], j, k), dev(line_others[2], j, k),
        cross_up, cross_dn,
    ):
        pl.semaphore_signal(barrier, inc=1, device_id=to, device_id_type=MESH)
    load_cell.start()
    load_logit.start()
    load_spot.start()

    eye = lax.broadcasted_iota(jnp.int32, (128, 128), 0) == lax.broadcasted_iota(
        jnp.int32, (128, 128), 1
    )
    lane = lax.broadcasted_iota(jnp.int32, (128, 128), 1)

    def stand(row):
        return jnp.sum(jnp.where(eye, jnp.broadcast_to(row, (128, 128)), 0.0), 1, keepdims=True)

    def lie(column):
        return jnp.sum(jnp.where(eye, jnp.broadcast_to(column, (128, 128)), 0.0), 0, keepdims=True)

    filt_row = filt_in[...].astype(f32)
    keep_col = stand(jax.nn.sigmoid(filt_row))
    slide_col = stand(sslide_in[...].astype(f32))
    bins_col = stand(bins_in[...].astype(f32))

    def hand_copy(q):
        return rc(hand.at[q], col.at[z, rows(k, 128), rows(q, WIDTH)], hand_s, hand_r, dev_mate)

    def col_up(q, b):
        at = col.at[b, :, at_chunk(q)]
        return rc(at, at, up_s, col_r.at[q, b], dev_up)

    def col_dn(q, b):
        at = col.at[b, :, at_chunk(q)]
        return rc(at, at, dn_s, col_r.at[q, b], dev_dn)

    def scale_cells(q):
        hand[q] = (keep_col * cell_v[:, lanes(mate, q)].astype(f32)).astype(b16)
        col[z, rows(k, 128), rows(q, WIDTH)] = (keep_col * cell_v[:, lanes(k, q)].astype(f32)).astype(b16)

    def col_own(q):
        own = col.at[z, rows(k, 128), at_chunk(q)]

        @pl.when(z < 3)
        def _():
            rc(own, own, up_s, col_r.at[q, z], dev_up).start()
            rc(hand.at[q], own, up_s, col_r.at[q, z], cross_up).start()

        @pl.when(z > 0)
        def _():
            rc(own, own, dn_s, col_r.at[q, z], dev_dn).start()
            rc(hand.at[q], own, dn_s, col_r.at[q, z], cross_dn).start()

    hops = [(q, s) for q in range(chunks) for s in range(3)]

    def hop():
        q, s = hops.pop(0)

        @pl.when(z - 1 - s >= 0)
        def _():
            b = z - 1 - s
            got(col.at[b, :, at_chunk(q)], col_r.at[q, b])

            @pl.when(z < 3)
            def _():
                col_up(q, b).start()

        @pl.when(z + 1 + s <= 3)
        def _():
            b = z + 1 + s
            got(col.at[b, :, at_chunk(q)], col_r.at[q, b])

            @pl.when(z > 0)
            def _():
                col_dn(q, b).start()

    load_cell.wait()
    scale_cells(0)
    pl.semaphore_wait(barrier, 9)
    hand_copy(0).start()

    @pl.loop(1, chunks)
    def _(q):
        scale_cells(q)
        hand_copy(q).start()

    def spread(source, slots, which, i):
        for o in plane_others if which == "plane" else line_others:
            to = dev(z, o, k) if which == "plane" else dev(o, j, k)
            rc(source(o), slots.at[j if which == "plane" else z], sm_s.at[i], sm_r.at[i], to).start()

    def hand_over(source, slot, i):
        rc(source, slot, sm_s.at[i], sm_r.at[i], dev_mate).start()

    f_line[z] = filt_row
    spread(lambda o: f_line.at[z], f_line, "line", 0)

    load_logit.wait()

    def softmax_rows(g):
        at = rows(g, 16)
        logits = chance[at, :]
        pick = lax.broadcasted_iota(jnp.int32, (16, 128), 0) + g * 16
        here = lax.broadcasted_iota(jnp.int32, (16, 128), 1)
        slide = jnp.sum(
            jnp.where(pick == here, jnp.broadcast_to(sslide_in[...].astype(f32), (16, 128)), 0.0),
            1, keepdims=True,
        )
        allowed = slide == cslide_in[...].astype(f32)
        shifted = jnp.where(allowed, logits, -1e30)
        raised = jnp.exp(shifted - jnp.max(shifted, axis=1, keepdims=True))
        value = raised / jnp.sum(raised, axis=1, keepdims=True)
        chance[at, :] = value
        low = value.astype(b16)
        for b in range(4):
            for jj in range(4):
                own_low[jj, at, b * 256 : b * 256 + 256] = low[
                    :, b * 1024 + jj * 256 : b * 1024 + jj * 256 + 256
                ]

    def low_copy(jj):
        return rc(own_low.at[jj], plane_low.at[k, j], low_s.at[0], low_r.at[j], dev(z, jj, k))

    def low_pass(jj):
        return rc(plane_low.at[k, jj], plane_low.at[k, jj], low_s.at[1], low_r.at[4], dev_mate)

    def low_give():
        low_copy(jd).start()
        low_copy(jx).start()
        low_copy(jy).start()

    spot_give = rc(
        spot_in.at[:, pl.ds(pl.multiple_of(mate * half, half), half)], spot_h.at[rows(k, 128)], spot_s, spot_r, dev_mate
    )

    def low_own():
        plane_low[k, j] = own_low[j]
        low_pass(j).start()
        spot_give.start()

    def filt_pair():
        got(f_line.at[pl.ds(0, 3)], sm_r.at[0])
        f_pair[k] = f_line[...]
        hand_over(f_line, f_pair.at[k], 1)

    def filt_plane():
        got(f_line, sm_r.at[1])
        f_all[j] = f_pair[...]
        spread(lambda o: f_pair, f_all, "plane", 2)

    def of_cells(jj, kk, b):
        return own_low[jj, :, pl.ds(pl.multiple_of(b * 256 + kk * 128, 128), 128)].astype(f32)

    def split(d):
        return lax.div(d, 8), lax.rem(lax.div(d, 4), 2), lax.rem(d, 4)

    kind = lax.div(lane, 8)
    of_slide = lax.rem(lane, 8) == slide_col.astype(jnp.int32)

    def mass_make():
        got(f_all.at[pl.ds(0, 3)], sm_r.at[2])
        keep_all[...] = jax.nn.sigmoid(f_all[...])

        def add_mass(d, acc):
            jj, kk, b = split(d)
            return acc + of_cells(jj, kk, b) * keep_all[jj, kk, b]

        mass = jnp.sum(lax.fori_loop(0, 32, add_mass, jnp.zeros((128, 128), f32)), axis=1, keepdims=True)
        keep["mass"] = mass
        log_term = bins_col * (jnp.log(bins_col) - jnp.log(mass))
        values = jnp.where(
            kind == 0, mass, jnp.where(kind == 1, bins_col, jnp.where(kind == 2, log_term, 0.0))
        )
        m_src[0] = jnp.sum(jnp.where(of_slide, values, 0.0), axis=0, keepdims=True)
        m_src[1] = sslide_in[...].astype(f32)
        hand_over(m_src, m_got, 3)

    lane2 = lax.broadcasted_iota(jnp.int32, (256, 128), 1)

    def mass_chip():
        got(m_src, sm_r.at[3])
        load_spot.wait()
        got(spot_h.at[rows(mate, 128)], spot_r)
        stat[...] = jnp.zeros_like(stat)
        chip_row = m_src[0] + m_got[0]
        for o in range(4):
            stat[0, o, 24:25, :] = chip_row
        first = jnp.where(k == 0, m_src[1], m_got[1])
        second = jnp.where(k == 0, m_got[1], m_src[1])
        hot_lie[...] = (
            lax.broadcasted_iota(jnp.int32, (8, 256), 0).astype(f32)
            == jnp.broadcast_to(jnp.concatenate([first, second], axis=1), (8, 256))
        ).astype(f32)
        slides_col = jnp.concatenate([stand(first), stand(second)], axis=0)
        hot_stand[...] = ((lax.rem(lane2, 8) == slides_col.astype(jnp.int32)) & (lane2 < 24)).astype(b16)
        coef[...] = jnp.zeros_like(coef)
        filt_acc[...] = jnp.zeros_like(filt_acc)

    def split_dot(a, v):
        high = v.astype(b16)
        rest = (v - high.astype(f32)).astype(b16)
        return jnp.dot(a, high, preferred_element_type=f32) + jnp.dot(a, rest, preferred_element_type=f32)

    def low_arrive(i):
        if i == 3:
            got(plane_low.at[mate], low_r.at[4])
            got(hand, hand_r)
        else:
            jj = (jx, jy, jd)[i]
            got(plane_low.at[k, jj], low_r.at[jj])
            low_pass(jj).start()

    def product(q, left, count):
        at = pl.ds(q * WIDTH, count * WIDTH)

        @pl.loop(0, 2)
        def _(h):
            if left is plane_low:
                whole = jnp.dot(left[h].reshape(512, 1024), col[:, :, at].reshape(1024, count * WIDTH), preferred_element_type=f32)
            else:
                whole = jnp.dot(left[rows(h, 512), :], grad[:, :, :, at].reshape(1024, count * WIDTH), preferred_element_type=f32)
            for i in range(count):
                part[q + i, h] = whole[:, i * WIDTH : i * WIDTH + WIDTH].reshape(4, 128, WIDTH)

    def reduce_first(q):
        for i, (core, owner, to, sem, slot) in enumerate((
            (0, jd, dev_x, early_r.at[q, 0], early.at[q, 0]),
            (1, jd, dev_y, early_r.at[q, 1], early.at[q, 1]),
            (0, jx, dev_x, late_r.at[q], late.at[q, 0]),
            (1, jy, dev_y, late_r.at[q], late.at[q, 1]),
        )):
            send1[q, i] = part[q, core, owner].astype(b16)
            rc(send1.at[q, i], slot, send1_s, sem, to).start()

    def reduce_second(q, i):
        owner, to = ((jy, dev_y), (jx, dev_x))[i]
        got(early.at[q, i], early_r.at[q, i])
        send2[q, i] = (part[q, i, owner] + early[q, i].astype(f32)).astype(b16)
        rc(send2.at[q, i], late.at[q, 2 + i], send2_s, late_r.at[q], to).start()

    def pred_give(q):
        return rc(
            pred_h.at[rows(mate, 128), pl.ds(q * WIDTH, WIDTH)], pred_out.at[:, lanes(k, q)], pred_s, pred_r, dev_mate
        )

    def pred_own(q):
        return pltpu.make_async_copy(
            pred_h.at[rows(k, 128), pl.ds(q * WIDTH, WIDTH)], pred_out.at[:, lanes(k, q)], own_sem
        )

    def reduce_last(q):
        got(late.at[q], late_r.at[q])
        for i in range(2):
            pred_h[i * 128 : i * 128 + 128, q * WIDTH : q * WIDTH + WIDTH] = part[q, i, j] + (
                late[q, i].astype(f32) + late[q, 2 + i].astype(f32)
            )
        pred_give(q).start()
        pred_own(q).start()

    def reduce_stat(q):
        pr = pred_h[:, q * WIDTH : q * WIDTH + WIDTH]
        sp = spot_h[:, q * WIDTH : q * WIDTH + WIDTH]
        for i, v in enumerate((pr * sp, pr * pr)):
            spacc[i] = v if q == 0 else spacc[i] + v

    def reduce_slides(q):
        pr = pred_h[:, q * WIDTH : q * WIDTH + WIDTH]
        sp = spot_h[:, q * WIDTH : q * WIDTH + WIDTH]
        for i, v in enumerate((pr * sp, pr * pr)):
            stat[q // 4, q % 4, i * 8 : i * 8 + 8] = split_dot(hot_lie[...].astype(b16), v)

    def obs_sums():
        for q in range(chunks):
            sp = spot_h[:, q * WIDTH : q * WIDTH + WIDTH]
            v = sp * sp
            ob_acc[...] = v if q == 0 else ob_acc[...] + v
            stat[q // 4, q % 4, 16:24] = split_dot(hot_lie[...].astype(b16), v)
        rc(ob_acc, ob_got, ob_s, ob_r, dev_mate).start()

    def st_send(g, i):
        slots = (st1, st2, st3)[i]
        if i == 0:
            st1[g, j] = stat[g, j]
        else:
            prior = (st1, st2)[i - 1]
            got(prior.at[g, pl.ds(0, 3)], st_r.at[g, i - 1])
            total = prior[g, 0] + prior[g, 1] + prior[g, 2] + prior[g, 3]
            st_sum[g, i - 1] = total
            if i == 1:
                st2[g, z] = total
            else:
                st3[g, j] = total
        for o in line_others if i == 1 else plane_others:
            src = stat.at[g, o] if i == 0 else st_sum.at[g, i - 1]
            to = dev(o, j, k) if i == 1 else dev(z, o, k)
            rc(src, slots.at[g, z if i == 1 else j], st_s.at[g, i], st_r.at[g, i], to).start()

    def st_finish(g):
        got(st3.at[g, pl.ds(0, 3)], st_r.at[g, 2])

    def turn(i):
        for kk in range(2):
            plane_turn[:, (kk * 4 + i) * 128 : (kk * 4 + i) * 128 + 128] = plane_low[kk, i].astype(f32).T.astype(b16)

    spx = rc(spacc, spgot, spx_s, spx_r, dev_mate)

    def spot_half():
        spx.start()

    slide8 = lax.broadcasted_iota(jnp.int32, (8, 128), 0)
    lane8 = lax.broadcasted_iota(jnp.int32, (8, 128), 1)

    def mass_end():
        sums_row = st_sum[0, 1, 24:25, :]
        each = jnp.broadcast_to(sums_row, (128, 128))
        mass_each = jnp.sum(jnp.where(of_slide & (kind == 0), each, 0.0), 1, keepdims=True)
        bins_each = jnp.sum(jnp.where(of_slide & (kind == 1), each, 0.0), 1, keepdims=True)
        mass_grad = (1.0 / mass_each - bins_col / (bins_each * keep["mass"])) / SLIDES
        keep["grad"] = mass_grad.astype(b16).astype(f32)

        def by_slide(begin):
            return jnp.sum(
                jnp.where(lane8 == slide8 + begin, jnp.broadcast_to(sums_row, (8, 128)), 0.0), 1, keepdims=True
            )

        mass_s, bins_s, log_s = by_slide(0), by_slide(8), by_slide(16)
        kl = jnp.sum(log_s / bins_s - jnp.log(bins_s) + jnp.log(mass_s), axis=0, keepdims=True)
        keep["kl"] = kl / SLIDES

    def reach_make():
        mass_grad = keep["grad"]

        @pl.loop(0, 32)
        def _(d):
            jj, kk, b = split(d)
            r_src[kk, jj, b] = jnp.sum(of_cells(jj, kk, b) * mass_grad, axis=0, keepdims=True)

        hand_over(r_src.at[mate], r_mate, 4)

    def reach_plane():
        got(r_mate, sm_r.at[4])
        r_plane_src[...] = r_src[k] + r_mate[...]
        r_plane[j] = r_plane_src[j]
        spread(lambda o: r_plane_src.at[o], r_plane, "plane", 5)

    def reach_line():
        got(r_plane.at[pl.ds(0, 3)], sm_r.at[5])
        r_line_src[...] = r_plane[0] + r_plane[1] + r_plane[2] + r_plane[3]
        r_line[z] = r_line_src[z]
        spread(lambda o: r_line_src.at[o], r_line, "line", 6)

    def obs_end():
        got(ob_got, ob_r)
        keep["obs_c"] = jnp.sum(ob_acc[...] + ob_got[...], axis=1, keepdims=True)

    def spot_sums():
        st_finish(0)
        got(spgot, spx_r)
        cross_c, pred_c = [jnp.sum(spacc[i] + spgot[i], axis=1, keepdims=True) for i in range(2)]
        obs_c = keep["obs_c"]
        root_c = jnp.sqrt(pred_c * obs_c)
        keep["cos"] = cross_c / root_c
        keep["obs"] = (1.0 / root_c) / total_spots
        keep["prd"] = (cross_c / (pred_c * root_c)) / total_spots

    def grad_make(q):
        scale = 1.0 / (SLIDES * total_genes)
        for e in range(units):
            g, o = divmod(q * units + e, 4)
            sums = st3[g, o]
            cross, prd, obs = sums[:8], sums[8:16], sums[16:24]
            root = jnp.sqrt(prd * obs)
            for i, v in enumerate((scale / root, scale * cross / (prd * root))):
                high = v.astype(b16).astype(f32)
                mid = (v - high).astype(b16).astype(f32)
                low = v - high - mid
                stack = jnp.concatenate([high, mid, low, jnp.zeros((8, 128), f32)], axis=0)
                coef[:32, (i * units + e) * 128 : (i * units + e) * 128 + 128] = stack.astype(b16)
        each_spot = jnp.dot(hot_stand[...], coef[...], preferred_element_type=f32)
        at = slice(q * WIDTH, q * WIDTH + WIDTH)
        value = pred_h[:, at] * (each_spot[:, WIDTH:] + keep["prd"]) - spot_h[:, at] * (each_spot[:, :WIDTH] + keep["obs"])
        value = value.astype(b16)
        grad[0, j, :, at] = value[:128]
        grad[1, j, :, at] = value[128:]

    def gene_cos():
        total = jnp.zeros((8, 128), f32)
        for g in range(2):
            for e in range(4):
                sums = st3[g, e]
                total = total + sums[:8] / jnp.sqrt(sums[8:16] * sums[16:24])
        return jnp.sum(jnp.sum(total, axis=0, keepdims=True), axis=1, keepdims=True)

    def grad_send(q):
        grad_make(q)
        at = grad.at[:, j, :, at_chunk(q)]
        rc(at, at, g_s.at[0], g_r.at[q, 0], dev_x).start()
        rc(at, at, g_s.at[1], g_r.at[q, 1], dev_y).start()

    def grad_direct(q):
        grad_make(q)
        at = grad.at[:, j, :, at_chunk(q)]
        rc(at, at, g_s.at[4], g_r.at[q, 2], dev(z, jd, k)).start()
        rc(at, at, g_s.at[0], g_r.at[q, 0], dev_x).start()
        rc(at, at, g_s.at[1], g_r.at[q, 1], dev_y).start()

    def grad_pass(q, i):
        owner, to = ((jx, dev_y), (jy, dev_x))[i]
        got(grad.at[:, owner, :, at_chunk(q)], g_r.at[q, i])
        at = grad.at[i, owner, :, at_chunk(q)]
        rc(at, at, g_s.at[2 + i], g_r.at[q, 2], to).start()

    def run_up(q, b):
        return rc(pass_on.at[q, b], sums_up.at[q, b], rs_s, rs_r.at[q, b], dev_up)

    def run_dn(q, b):
        return rc(pass_on.at[q, b], sums_dn.at[q, b], rs_s, rs_r.at[q, b], dev_dn)

    def block(q, b):
        return part[q, b // 2, pl.ds(2 * (b % 2), 2)].reshape(256, WIDTH)

    def run_last(q, b, up):
        i = 0 if up else 1
        to, cross = (dev_up, cross_up) if up else (dev_dn, cross_dn)
        rc(pass_on.at[q, b, rows(k, 128)], fin.at[q, i, k], rs_s, fin_r.at[q], to).start()
        rc(pass_on.at[q, b, rows(mate, 128)], fin.at[q, i, k], rs_s, fin_r.at[q], cross).start()

    def sums_half(q, h):
        whole = jnp.dot(
            plane_turn[rows(h, 512), :], grad[:, :, :, at_chunk(q)].reshape(1024, WIDTH), preferred_element_type=f32
        )
        part[q, h] = whole.reshape(4, 128, WIDTH)

    def sums_give(q, b):
        pass_on[q, b] = block(q, b).astype(b16)

    def grad_wait(q):
        if DIRECT == q:
            got(grad.at[:, jx, :, at_chunk(q)], g_r.at[q, 0])
            got(grad.at[:, jy, :, at_chunk(q)], g_r.at[q, 1])
        got(grad.at[:, jd, :, at_chunk(q)], g_r.at[q, 2])

    def sums_first(q, count):
        if count == 2:
            product(q, plane_turn, count)
        for step in range(2):
            if count == 1:
                sums_half(q, jnp.where(z < 2, 1 - step, step))

            @pl.when(z == 0)
            def _():
                for i in range(count):
                    for b in ((3, 2), (1,))[step]:
                        sums_give(q + i, b)
                        run_last(q + i, b, True) if b == 1 else run_up(q + i, b).start()

            @pl.when(z == 3)
            def _():
                for i in range(count):
                    for b in ((0, 1), (2,))[step]:
                        sums_give(q + i, b)
                        run_last(q + i, b, False) if b == 2 else run_dn(q + i, b).start()

    def pass_add(q, b, slots):
        got(slots.at[q, b], rs_r.at[q, b])
        pass_on[q, b] = (block(q, b) + slots[q, b].astype(f32)).astype(b16)

    def pass_far(q):
        @pl.when(z == 1)
        def _():
            pass_add(q, 3, sums_up)
            run_up(q, 3).start()

        @pl.when(z == 2)
        def _():
            pass_add(q, 0, sums_dn)
            run_dn(q, 0).start()

    def pass_middle(q):
        @pl.when(z == 1)
        def _():
            pass_add(q, 2, sums_up)
            run_last(q, 2, True)

        @pl.when(z == 2)
        def _():
            pass_add(q, 1, sums_dn)
            run_last(q, 1, False)

    def pass_near(q):
        @pl.when(z == 1)
        def _():
            pass_add(q, 0, sums_dn)
            run_last(q, 0, False)

        @pl.when(z == 2)
        def _():
            pass_add(q, 3, sums_up)
            run_last(q, 3, True)

    def other_give(q):
        return rc(other.at[q], other_got.at[q], oth_s, oth_r.at[q], dev_mate)

    def use_sums(q, kk, sums):
        at = lanes(kk, q)
        expr_out[:, at] = keep_col * sums
        weighed = cell_v[:, at].astype(f32) * sums
        for e in range(units):
            filt_acc[...] = filt_acc[...] + weighed[:, e * 128 : e * 128 + 128]

    def sums_other(q):
        other[q] = part[q, lax.div(z, 2), 2 * lax.rem(z, 2) + mate]
        other_give(q).start()

    def sums_last(q):
        @pl.when(z == 0)
        def _():
            got(fin.at[q, 1], fin_r.at[q])

        @pl.when(z == 3)
        def _():
            got(fin.at[q, 0], fin_r.at[q])

        @pl.when((z > 0) & (z < 3))
        def _():
            got(fin.at[q], fin_r.at[q])

        got(other_got.at[q], oth_r.at[q])
        own_at = (q, lax.div(z, 2), 2 * lax.rem(z, 2) + k)
        for kk, base in ((k, part[own_at]), (mate, other_got[q])):
            up = jnp.where(z > 0, fin[q, 0, kk].astype(f32), 0.0)
            dn = jnp.where(z < 3, fin[q, 1, kk].astype(f32), 0.0)
            use_sums(q, kk, base + (up + dn))

    def back_dot(b):
        @pl.loop(0, 2)
        def _(h):
            back[b, h] = lax.dot_general(
                grad[h].reshape(512, half), col[b], (((1,), (1,)), ((), ())), preferred_element_type=f32
            ).reshape(4, 128, 256)

        rc(back.at[b, mate], back_got.at[b], back_s, back_r.at[b], dev_mate).start()

    def back_add(b):
        got(back_got.at[b], back_r.at[b])
        for jj in range(4):
            back_low[jj, :, rows(b, 256)] = (back[b, k, jj] + back_got[b, jj]).astype(b16)

    def ret_send(b):
        at = rows(b, 256)
        for jj in (jd, jx, jy):
            rc(back_low.at[jj, :, at], back_ret.at[j, :, at], ret_s, ret_r, dev(z, jj, k)).start()
        back_ret[j, :, at] = back_low[j, :, at]

    loss_lane = lax.broadcasted_iota(jnp.int32, (1, 128), 1)

    def loss_mate():
        own_cos = jnp.sum(keep["cos"], axis=0, keepdims=True)
        l_src[...] = jnp.where(loss_lane == 0, own_cos, jnp.where(loss_lane == 1, gene_cos(), 0.0))
        hand_over(l_src, l_mate, 7)
        l_plane[j] = l_src[...]
        spread(lambda o: l_src, l_plane, "plane", 8)

    def loss_line():
        got(l_plane.at[pl.ds(0, 3)], sm_r.at[8])
        total = l_plane[0] + l_plane[1] + l_plane[2] + l_plane[3]
        l_line_src[...] = total
        l_line[z] = total
        spread(lambda o: l_line_src, l_line, "line", 9)

    def loss_end():
        got(l_line.at[pl.ds(0, 3)], sm_r.at[9])
        got(l_mate, sm_r.at[7])
        cos_row = l_line[0] + l_line[1] + l_line[2] + l_line[3]
        gene_row = l_src[...] + l_mate[...]
        cos_total = jnp.sum(jnp.where(loss_lane == 0, cos_row, 0.0), axis=1, keepdims=True)
        gene_total = jnp.sum(jnp.where(loss_lane == 1, gene_row, 0.0), axis=1, keepdims=True)
        gene_loss = 1.0 - gene_total / (SLIDES * total_genes)
        spot_loss = 1.0 - cos_total / total_spots
        kl_loss = keep["kl"]
        total_loss = gene_loss + spot_loss + kl_loss
        picked = jnp.where(loss_lane == 2, spot_loss, jnp.where(loss_lane == 3, kl_loss, 0.0))
        loss_out[...] = jnp.where(loss_lane == 0, total_loss, jnp.where(loss_lane == 1, gene_loss, picked))

    def map_rows(g):
        at = rows(g, 16)
        pick = lax.broadcasted_iota(jnp.int32, (16, 128), 0) + g * 16
        here = lax.broadcasted_iota(jnp.int32, (16, 128), 1)
        mg = jnp.sum(jnp.where(pick == here, jnp.broadcast_to(mass_row[...], (16, 128)), 0.0), 1, keepdims=True)
        inner = jnp.zeros((16, 128), f32)
        for d in range(32):
            b, jj, kk = d // 8, (d % 8) // 2, d % 2
            used = back_ret[jj, at, b * 256 + kk * 128 : b * 256 + kk * 128 + 128].astype(f32) + mg * keep_all[jj, kk, b]
            inner = inner + chance[at, d * 128 : d * 128 + 128] * used
            map_out[at, d * 128 : d * 128 + 128] = used
        inner = jnp.sum(inner, axis=1, keepdims=True)
        map_out[at, :] = chance[at, :] * (map_out[at, :] - inner)

    def map_some(i):
        if i == 0:
            got(back_ret.at[pl.ds(0, 3)], ret_r)
            mass_row[...] = lie(keep["grad"])
        pl.loop(2 * i, 2 * i + 2)(map_rows)

    steps = {
        "x": lambda i: pl.loop(2 * i, 2 * i + 2)(softmax_rows), "w": lambda i: (low_give, low_own)[i](),
        "c": col_own, "h": lambda i: hop(), "i": lambda i: (filt_pair, filt_plane, mass_make, mass_chip)[i](),
        "a": low_arrive, "q": turn, "p": lambda q: product(q, plane_low, 1), "P": lambda q: product(q, plane_low, 2),
        "f": reduce_first, "s": lambda q: reduce_second(q, 0), "S": lambda q: reduce_second(q, 1),
        "l": reduce_last, "k": reduce_stat, "j": reduce_slides, "B": lambda i: (obs_sums, obs_end)[i](), "t": lambda i: st_send(0, i), "z": lambda i: (spot_half, mass_end, spot_sums)[i](),
        "g": grad_send, "G": grad_direct, "m": lambda q: grad_pass(q, 0), "n": lambda q: grad_pass(q, 1),
        "y": lambda i: st_send(1, i) if i < 3 else st_finish(1), "r": lambda q: sums_first(q, 1), "R": lambda q: sums_first(q, 2),
        "U": pass_far, "V": pass_middle, "D": pass_near,
        "L": sums_last, "O": sums_other, "b": back_dot, "A": back_add, "T": ret_send, "W": grad_wait, "M": map_some,
        "e": lambda i: (reach_make, reach_plane, reach_line)[i](), "o": lambda i: (loss_mate, loss_line, loss_end)[i](),
    }
    for group in ORDER:
        for word in group.split():
            steps[word[0]](int(word[1:]) if len(word) > 1 else 0)

    got(r_line.at[pl.ds(0, 3)], sm_r.at[6])
    reach_row = r_line[0] + r_line[1] + r_line[2] + r_line[3]
    filt_sum = jnp.sum(filt_acc[...], axis=1, keepdims=True)
    keep_row = jax.nn.sigmoid(filt_in[...].astype(f32))
    filt_out[...] = keep_row * (1.0 - keep_row) * (lie(filt_sum) + reach_row)

    sent(hand, hand_s)
    spot_give.wait_send()
    sent(send1, send1_s)
    sent(send2, send2_s)
    sent(pred_h.at[rows(mate, 128)], pred_s)
    got(pred_out.at[:, pl.ds(pl.multiple_of(mate * half, half), half)], pred_r)
    pltpu.make_async_copy(
        pred_h.at[rows(k, 128)], pred_out.at[:, pl.ds(pl.multiple_of(k * half, half), half)], own_sem
    ).wait()
    for i in range(2):
        sent(grad.at[:, j], g_s.at[i])
    others = [q for q in range(chunks) if q != DIRECT]
    sent(grad.at[0, jx, :, pl.ds(0, len(others) * WIDTH)], g_s.at[2])
    sent(grad.at[1, jy, :, pl.ds(0, len(others) * WIDTH)], g_s.at[3])
    if DIRECT is not None:
        sent(grad.at[:, j, :, at_chunk(DIRECT)], g_s.at[4])
    sent(ob_acc, ob_s)
    for i in range(3):
        @pl.when(z == i)
        def _():
            sent(col.at[pl.ds(0, i + 1)], up_s)

        @pl.when(z == 3 - i)
        def _():
            sent(col.at[pl.ds(3 - i, i + 1)], dn_s)
    sent(pass_on.at[:, pl.ds(0, 3)], rs_s)
    sent(plane_low.at[k, pl.ds(0, 3)], low_s.at[0])
    sent(plane_low.at[k], low_s.at[1])
    for g in range(2):
        for i in range(3):
            sent(st1.at[g, pl.ds(0, 3)], st_s.at[g, i])
    spx.wait_send()
    sent(back_got, back_s)
    sent(back_low.at[pl.ds(0, 3)], ret_s)
    sent(other, oth_s)
    for i, ref in enumerate((
        f_line.at[pl.ds(0, 3)], f_line, f_all.at[pl.ds(0, 3)], m_src, r_mate, r_plane.at[pl.ds(0, 3)],
        r_line.at[pl.ds(0, 3)], l_mate, l_plane.at[pl.ds(0, 3)], l_line.at[pl.ds(0, 3)],
    )):
        sent(ref, sm_s.at[i])


def hand_out(pred_in, map_in, expr_in, filt_in, loss_in, pred_out, map_out, expr_out, filt_out, loss_out, sems):
    pairs = ((map_in, map_out), (pred_in, pred_out), (expr_in, expr_out))
    copies = [pltpu.make_async_copy(src, dst, sems.at[i]) for i, (src, dst) in enumerate(pairs)]
    for copy in copies:
        copy.start()
    filt_out[...] = filt_in[...]
    loss_out[...] = loss_in[:, :4]
    for copy in copies:
        copy.wait()


def fused_shards(map_logits, filter_logits, cell_expr, spot_expr, cell_slide, spot_slide, density_bins):
    f32, b16 = jnp.float32, jnp.bfloat16
    spots, cells = map_logits.shape
    genes = cell_expr.shape[1]
    n = genes // (2 * WIDTH)
    V, S = pltpu.VMEM, pltpu.SemaphoreType.DMA
    any_, vmem = pl.BlockSpec(memory_space=pl.ANY), pl.BlockSpec(memory_space=pltpu.VMEM)
    one = S(())
    scratch = [
        V((128, cells), f32),
        V((4, 128, 1024), b16),
        V((2, 4, 128, 1024), b16),
        V((1024, 1024), b16),
        V((128, genes), b16),
        V((n, 128, WIDTH), b16),
        V((4, 256, genes // 2), b16),
        V((n, 2, 4, 128, WIDTH), f32),
        V((n, 4, 128, WIDTH), b16),
        V((n, 2, 128, WIDTH), b16),
        V((n, 2, 128, WIDTH), b16),
        V((n, 4, 128, WIDTH), b16),
        V((256, genes // 2), f32),
        V((256, genes // 2), f32),
        V((2, 4, 32, 128), f32),
        V((2, 2, 32, 128), f32),
        V((2, 4, 32, 128), f32),
        V((2, 4, 32, 128), f32),
        V((2, 4, 32, 128), f32),
        V((2, 256, 128), f32),
        V((2, 256, 128), f32),
        V((256, 128), f32),
        V((256, 128), f32),
        V((128, 2 * WIDTH), b16),
        V((2, 4, 128, genes // 2), b16),
        V((n, 4, 256, WIDTH), b16),
        V((n, 4, 256, WIDTH), b16),
        V((n, 4, 256, WIDTH), b16),
        V((n, 2, 2, 128, WIDTH), b16),
        V((4, 2, 4, 128, 256), f32),
        V((4, 4, 128, 256), f32),
        V((4, 128, 1024), b16),
        V((4, 128, 1024), b16),
        V((n, 128, WIDTH), f32),
        V((n, 128, WIDTH), f32),
        V((4, 1, 128), f32),
        V((2, 4, 1, 128), f32),
        V((4, 2, 4, 1, 128), f32),
        V((4, 2, 4, 1, 128), f32),
        V((2, 1, 128), f32),
        V((2, 1, 128), f32),
        V((2, 4, 4, 1, 128), f32),
        V((4, 4, 1, 128), f32),
        V((4, 4, 1, 128), f32),
        V((4, 4, 1, 128), f32),
        V((4, 1, 128), f32),
        V((4, 1, 128), f32),
        V((1, 128), f32),
        V((1, 128), f32),
        V((4, 1, 128), f32),
        V((1, 128), f32),
        V((4, 1, 128), f32),
        V((128, 128), f32),
        V((8, 256), f32),
        V((256, 128), b16),
        V((1, 128), f32),
        S((3,)), one, one, one, one, one, S((n, 4)), S((2,)), S((5,)),
        one, one, S((n, 2)), S((n,)),
        one, one, one, one, S((2, 3)), S((2, 3)), one, one, one, one,
        S((5,)), S((n, 3)), one, S((n, 4)), S((n,)), one, S((4,)),
        one, one, one, S((n,)), S((10,)), S((10,)),
    ]
    predicted, map_grad, expr_grad, filt, loss = pl.pallas_call(
        functools.partial(fused_kernel, float(spots * 32), float(genes)),
        out_shape=(
            pltpu.VMEM((spots, genes), f32),
            pltpu.VMEM((spots, cells), f32),
            pltpu.VMEM((spots, genes), f32),
            V((1, 128), f32),
            V((1, 128), f32),
        ),
        in_specs=[any_, vmem, any_, any_, vmem, vmem, vmem],
        out_specs=(vmem, vmem, vmem, vmem, vmem),
        scratch_shapes=scratch,
        compiler_params=pltpu.CompilerParams(
            collective_id=0, has_side_effects=True, vmem_limit_bytes=58 * 2**20
        ),
        name="mapping_step",
    )(
        map_logits,
        filter_logits.reshape(1, 128),
        cell_expr,
        spot_expr,
        cell_slide.reshape(1, cells),
        spot_slide.reshape(1, 128),
        density_bins.reshape(1, 128),
    )
    predicted, map_grad, expr_grad, filt, loss = pl.pallas_call(
        hand_out,
        out_shape=(
            jax.ShapeDtypeStruct((spots, genes), f32),
            jax.ShapeDtypeStruct((spots, cells), f32),
            jax.ShapeDtypeStruct((spots, genes), f32),
            jax.ShapeDtypeStruct((1, 128), f32),
            jax.ShapeDtypeStruct((1, 4), f32),
        ),
        in_specs=[vmem] * 5,
        out_specs=(any_, any_, any_, vmem, vmem),
        scratch_shapes=[S((3,))],
        compiler_params=pltpu.CompilerParams(vmem_limit_bytes=2**20),
        name="hand_out",
    )(*[pltpu.with_memory_space_constraint(v, pltpu.VMEM) for v in (predicted, map_grad, expr_grad, filt, loss)])
    return loss.reshape(4), predicted, map_grad, expr_grad, filt.reshape(128)


def solution(mesh):
    both = P(("row", "col"))
    rows = P(("row", "col"), None)
    in_specs = (rows, both, rows, rows, P(), both, both)
    out_specs = (P(), rows, rows, rows, both)
    step = fused_shards if (mesh.shape["row"], mesh.shape["col"]) == (4, 8) else shards
    return jax.shard_map(step, mesh=mesh, in_specs=in_specs, out_specs=out_specs, check_vma=False)
```

```python
import functools

import jax
import jax.numpy as jnp
from jax import lax
from jax.experimental import pallas as pl
from jax.experimental.pallas import tpu as pltpu
from jax.sharding import PartitionSpec as P

SLIDES = 8
ROWS, PLANE, CORES = 4, 4, 2
WIDTH = 128
MESH = pl.DeviceIdType.MESH
DIRECT = 0
ORDER = (
    "c0 H0 x1 H1",
    "x3 c1 x0 x2",
    "w0 F0 h H2",
    "H3 H4 H5 w1",
    "c2 c3 H6 H7",
    "i0 h h h",
    "c4 i1 h h",
    "h a2 c5 h",
    "h h a0 c6",
    "a1 i2 a3 P0",
    "f1 h h h",
    "f0 P2 f2 i3",
    "f3 s1 S1 h",
    "h h c7 S0",
    "B0 s0 p4 f4",
    "S3 s3 h h",
    "h S2 s2 l1",
    "p5 f5 S4 j1",
    "l0 j0 s4 h",
    "h h l3 j3",
    "l2 j2 t0 p6",
    "f6 s5 S5 h",
    "h p7 f7 t1",
    "k0 k3 q2 B1",
    "S6 s6 l4 l5",
    "s7 S7 k4 k1",
    "k2 t2 l6 k6",
    "j6 k5 j5 l7",
    "k7 z0 j7 j4",
    "y0 z2 g2 g1",
    "y1 q3 q0 m2",
    "n2 g3 m1 q1",
    "y2 n1 W2 r2",
    "G0 z1 y3 g7",
    "g5 W1 r1 U2",
    "o0 g6 W0 r0",
    "n7 O2 m7 g4",
    "m3 e0 n3 m5",
    "m6 U1 n6 e1",
    "n5 W7 r7 n4",
    "m4 W3 V2 r3",
    "V1 W6 r6 W5",
    "W4 b0 U7 O3",
    "O0 b2 A0 T0",
    "V0 V7 D1 U0",
    "b3 b1 A2 T2",
    "U3 V3 R4 O4",
    "D2 A3 T3 A1",
    "O1 O7 O6 U6",
    "D7 o1 T1 V6",
    "O5 L2 D0 e2",
    "D3 U4 L0 V4",
    "D6 L3 L7 U5",
    "L6 L1 D4 V5",
    "M0 M1 M2 D5",
    "M3 L4 o2 L5",
)


def shards(map_logits, filter_logits, cell_expr, spot_expr, cell_slide, spot_slide, density_bins):
    highest = lax.Precision.HIGHEST
    both = ("row", "col")
    rows_count = lax.axis_size("row")
    cols_count = lax.axis_size("col")
    spot_dev, cell_total = map_logits.shape
    cell_dev = filter_logits.shape[0]
    spot_total = spot_dev * rows_count * cols_count
    gene_count = cell_expr.shape[1]
    keep_rate = jax.nn.sigmoid(filter_logits.astype(jnp.float32))
    scaled = (keep_rate[:, None] * cell_expr.astype(jnp.float32)).astype(jnp.bfloat16)
    scaled_col = lax.all_gather(scaled, "row", axis=0, tiled=True)
    allowed = spot_slide[:, None] == cell_slide[None, :]
    shifted = jnp.where(allowed, map_logits, -1e30)
    row_peak = jnp.max(shifted, axis=1, keepdims=True)
    raised = jnp.exp(shifted - row_peak)
    chances = raised / jnp.sum(raised, axis=1, keepdims=True)
    chance_low = chances.astype(jnp.bfloat16)
    by_col = chance_low.reshape(spot_dev, rows_count, cols_count, cell_dev)
    mapped = lax.all_to_all(by_col, "col", split_axis=2, concat_axis=0, tiled=True)
    mapped = mapped.reshape(spot_dev * cols_count, rows_count * cell_dev)
    keep_col = lax.all_gather(keep_rate, "row", axis=0, tiled=True)
    part_pred = jnp.dot(mapped, scaled_col, preferred_element_type=jnp.float32)
    part_mass = jnp.dot(mapped, keep_col, precision=highest, preferred_element_type=jnp.float32)
    predicted = lax.psum_scatter(part_pred, "col", scatter_dimension=0, tiled=True)
    mass = lax.psum_scatter(part_mass, "col", scatter_dimension=0, tiled=True)
    onehot = (spot_slide[:, None] == jnp.arange(SLIDES, dtype=jnp.int32)[None, :]).astype(
        jnp.float32
    )
    cross_term = predicted * spot_expr
    pred_sq = predicted * predicted
    obs_sq = spot_expr * spot_expr
    spot_cross = jnp.sum(cross_term, axis=1)
    spot_pred = jnp.sum(pred_sq, axis=1)
    spot_root = jnp.sqrt(spot_pred * jnp.sum(obs_sq, axis=1))
    spot_cos = spot_cross / spot_root
    bin_values = density_bins.astype(jnp.float32)
    log_term = bin_values * (jnp.log(bin_values) - jnp.log(mass))
    all_cross, all_pred, all_obs, slide_mass, slide_bins, slide_log, cos_total = lax.psum(
        (
            jnp.dot(onehot.T, cross_term, precision=highest),
            jnp.dot(onehot.T, pred_sq, precision=highest),
            jnp.dot(onehot.T, obs_sq, precision=highest),
            jnp.dot(onehot.T, mass, precision=highest),
            jnp.dot(onehot.T, bin_values, precision=highest),
            jnp.dot(onehot.T, log_term, precision=highest),
            jnp.sum(spot_cos),
        ),
        both,
    )
    gene_root = jnp.sqrt(all_pred * all_obs)
    gene_loss = 1.0 - jnp.mean(all_cross / gene_root)
    spot_loss = 1.0 - cos_total / spot_total
    kl_loss = jnp.mean(slide_log / slide_bins - jnp.log(slide_bins) + jnp.log(slide_mass))
    total_loss = gene_loss + spot_loss + kl_loss
    losses = jnp.stack([total_loss, gene_loss, spot_loss, kl_loss])
    gene_scale = 1.0 / (SLIDES * gene_count)
    coef_obs = jnp.dot(onehot, 1.0 / gene_root, precision=highest)
    coef_pred = jnp.dot(onehot, all_cross / (all_pred * gene_root), precision=highest)
    pred_grad = -gene_scale * (spot_expr * coef_obs - predicted * coef_pred)
    pred_grad = (
        pred_grad
        - (
            spot_expr / spot_root[:, None]
            - predicted * (spot_cross / (spot_pred * spot_root))[:, None]
        )
        / spot_total
    )
    mass_each = jnp.dot(onehot, slide_mass, precision=highest)
    bins_each = jnp.dot(onehot, slide_bins, precision=highest)
    mass_grad = (1.0 / mass_each - bin_values / (bins_each * mass)) / SLIDES
    grad_low = pred_grad.astype(jnp.bfloat16)
    mass_low = mass_grad.astype(jnp.bfloat16)
    grad_block = lax.all_gather(grad_low, "col", axis=0, tiled=True)
    mass_block = lax.all_gather(mass_low, "col", axis=0, tiled=True)
    back_map = lax.dot_general(
        grad_block, scaled_col, (((1,), (1,)), ((), ())), preferred_element_type=jnp.float32
    )
    back_map = back_map + mass_block.astype(jnp.float32)[:, None] * keep_col[None, :]
    back_low = back_map.astype(jnp.bfloat16)
    returned = lax.all_to_all(
        back_low.reshape(spot_dev * cols_count, rows_count, 1, cell_dev),
        "col",
        split_axis=0,
        concat_axis=2,
        tiled=True,
    ).reshape(spot_dev, cell_total)
    expr_part = lax.dot_general(
        mapped, grad_block, (((0,), (0,)), ((), ())), preferred_element_type=jnp.float32
    )
    mass_reach = lax.dot_general(
        mapped, mass_block, (((0,), (0,)), ((), ())), preferred_element_type=jnp.float32
    )
    expr_sum = lax.psum_scatter(expr_part, "row", scatter_dimension=0, tiled=True)
    mass_sum = lax.psum_scatter(mass_reach, "row", scatter_dimension=0, tiled=True)
    filter_grad = (
        keep_rate
        * (1.0 - keep_rate)
        * (jnp.sum(cell_expr.astype(jnp.float32) * expr_sum, axis=1) + mass_sum)
    )
    expr_grad = keep_rate[:, None] * expr_sum
    chance_grad = returned.astype(jnp.float32)
    inner_sum = jnp.sum(chances * chance_grad, axis=1, keepdims=True)
    map_grad = chances * (chance_grad - inner_sum)
    return (losses, predicted, map_grad, expr_grad, filter_grad)


def fused_kernel(
    total_spots, total_genes,
    logit_in, filt_in, cell_in, spot_in, cslide_in, sslide_in, bins_in,
    pred_out, map_out, expr_out, filt_out, loss_out,
    chance, own_low, plane_low, plane_turn, cell_v, hand, col, part, send1, early, send2, late,
    pred_h, spot_h, stat, st_sum, st1, st2, st3, spacc, spgot, ob_acc, ob_got, coef, grad,
    sums_up, sums_dn, pass_on, fin, back, back_got, back_low, back_ret, other, other_got,
    f_line, f_pair, f_all, keep_all, m_src, m_got, r_src, r_mate, r_plane_src, r_plane, r_line_src, r_line,
    l_src, l_mate, l_plane, l_line_src, l_line, filt_acc, hot_lie, hot_stand, mass_row,
    load_sem, own_sem, hand_s, hand_r, up_s, dn_s, col_r, low_s, low_r, send1_s, send2_s, early_r, late_r,
    pred_s, pred_r, spot_s, spot_r, st_s, st_r, spx_s, spx_r, ob_s, ob_r, g_s, g_r, rs_s, rs_r, fin_r, back_s, back_r,
    ret_s, ret_r, oth_s, oth_r, sm_s, sm_r,
):
    f32, b16 = jnp.float32, jnp.bfloat16
    half = col.shape[2]
    chunks = half // WIDTH
    units = WIDTH // 128
    keep = {}
    z = lax.axis_index("row")
    c = lax.axis_index("col")
    j = lax.div(c, 2)
    k = lax.rem(c, 2)
    y = lax.div(j, 2)
    x = lax.rem(j, 2)
    mate = 1 - k

    def dev(zz, jj, kk):
        return (zz, jj * 2 + kk)

    jx = y * 2 + (1 - x)
    jy = (1 - y) * 2 + x
    jd = (1 - y) * 2 + (1 - x)
    dev_mate = dev(z, j, mate)
    dev_x = dev(z, jx, k)
    dev_y = dev(z, jy, k)
    dev_up = dev(lax.rem(z + 1, 4), j, k)
    dev_dn = dev(lax.rem(z + 3, 4), j, k)
    cross_up = dev(lax.rem(z + 1, 4), j, mate)
    cross_dn = dev(lax.rem(z + 3, 4), j, mate)
    plane_others = (jx, jy, jd)
    line_others = [lax.rem(z + i, 4) for i in (1, 2, 3)]

    def rc(src, dst, ss, rs, to):
        return pltpu.make_async_remote_copy(
            src_ref=src, dst_ref=dst, send_sem=ss, recv_sem=rs, device_id=to, device_id_type=MESH
        )

    def got(ref, sem):
        rc(ref, ref, sem, sem, dev_mate).wait_recv()

    def sent(ref, sem):
        rc(ref, ref, sem, sem, dev_mate).wait_send()

    def rows(i, size):
        return pl.ds(pl.multiple_of(i * size, size), size)

    def at_chunk(q):
        return pl.ds(q * WIDTH, WIDTH)

    def lanes(kk, q):
        return pl.ds(pl.multiple_of(kk * half + q * WIDTH, WIDTH), WIDTH)

    load_cell = pltpu.make_async_copy(cell_in, cell_v, load_sem.at[0])
    load_logit = pltpu.make_async_copy(logit_in, chance, load_sem.at[1])
    load_spot = pltpu.make_async_copy(
        spot_in.at[:, pl.ds(pl.multiple_of(k * half, half), half)], spot_h.at[rows(k, 128)], load_sem.at[2]
    )
    barrier = pltpu.get_barrier_semaphore()
    for to in (
        dev_mate, dev_x, dev_y, dev(z, jd, k),
        dev(line_others[0], j, k), dev(line_others[1], j, k), dev(line_others[2], j, k),
        cross_up, cross_dn,
    ):
        pl.semaphore_signal(barrier, inc=1, device_id=to, device_id_type=MESH)
    load_cell.start()
    load_logit.start()
    load_spot.start()

    eye = lax.broadcasted_iota(jnp.int32, (128, 128), 0) == lax.broadcasted_iota(
        jnp.int32, (128, 128), 1
    )
    lane = lax.broadcasted_iota(jnp.int32, (128, 128), 1)

    def stand(row):
        return jnp.sum(jnp.where(eye, jnp.broadcast_to(row, (128, 128)), 0.0), 1, keepdims=True)

    def lie(column):
        return jnp.sum(jnp.where(eye, jnp.broadcast_to(column, (128, 128)), 0.0), 0, keepdims=True)

    filt_row = filt_in[...].astype(f32)
    keep_col = stand(jax.nn.sigmoid(filt_row))
    slide_col = stand(sslide_in[...].astype(f32))
    bins_col = stand(bins_in[...].astype(f32))

    def hand_copy(q):
        return rc(hand.at[q], col.at[z, rows(k, 128), at_chunk(q)], hand_s, hand_r, dev_mate)

    def col_up(q, b):
        at = col.at[b, :, at_chunk(q)]
        return rc(at, at, up_s, col_r.at[q, b], dev_up)

    def col_dn(q, b):
        at = col.at[b, :, at_chunk(q)]
        return rc(at, at, dn_s, col_r.at[q, b], dev_dn)

    def scale_cells(q):
        hand[q] = (keep_col * cell_v[:, lanes(mate, q)].astype(f32)).astype(b16)
        col[z, rows(k, 128), at_chunk(q)] = (keep_col * cell_v[:, lanes(k, q)].astype(f32)).astype(b16)

    def col_own(q):
        own = col.at[z, rows(k, 128), at_chunk(q)]

        @pl.when(z < 3)
        def _():
            rc(own, own, up_s, col_r.at[q, z], dev_up).start()
            rc(hand.at[q], own, up_s, col_r.at[q, z], cross_up).start()

        @pl.when(z > 0)
        def _():
            rc(own, own, dn_s, col_r.at[q, z], dev_dn).start()
            rc(hand.at[q], own, dn_s, col_r.at[q, z], cross_dn).start()

    hops = [(q, s) for q in range(chunks) for s in range(3)]

    def hop():
        q, s = hops.pop(0)

        @pl.when(z - 1 - s >= 0)
        def _():
            b = z - 1 - s
            got(col.at[b, :, at_chunk(q)], col_r.at[q, b])

            @pl.when(z < 3)
            def _():
                col_up(q, b).start()

        @pl.when(z + 1 + s <= 3)
        def _():
            b = z + 1 + s
            got(col.at[b, :, at_chunk(q)], col_r.at[q, b])

            @pl.when(z > 0)
            def _():
                col_dn(q, b).start()

    load_cell.wait()
    scale_cells(0)
    pl.semaphore_wait(barrier, 9)

    def scale_more(q):
        if q:
            scale_cells(q)
        hand_copy(q).start()

    def spread(source, slots, which, i):
        for o in plane_others if which == "plane" else line_others:
            to = dev(z, o, k) if which == "plane" else dev(o, j, k)
            rc(source(o), slots.at[j if which == "plane" else z], sm_s.at[i], sm_r.at[i], to).start()

    def hand_over(source, slot, i):
        rc(source, slot, sm_s.at[i], sm_r.at[i], dev_mate).start()

    def filt_line():
        f_line[z] = filt_row
        spread(lambda o: f_line.at[z], f_line, "line", 0)

    def softmax_some(i):
        if not keep.get("logits"):
            load_logit.wait()
            keep["logits"] = True
        pl.loop(2 * i, 2 * i + 2)(softmax_rows)

    def softmax_rows(g):
        at = rows(g, 16)
        logits = chance[at, :]
        pick = lax.broadcasted_iota(jnp.int32, (16, 128), 0) + g * 16
        here = lax.broadcasted_iota(jnp.int32, (16, 128), 1)
        slide = jnp.sum(
            jnp.where(pick == here, jnp.broadcast_to(sslide_in[...].astype(f32), (16, 128)), 0.0),
            1, keepdims=True,
        )
        allowed = slide == cslide_in[...].astype(f32)
        shifted = jnp.where(allowed, logits, -1e30)
        raised = jnp.exp(shifted - jnp.max(shifted, axis=1, keepdims=True))
        value = raised / jnp.sum(raised, axis=1, keepdims=True)
        chance[at, :] = value
        low = value.astype(b16)
        for b in range(4):
            for jj in range(4):
                own_low[jj, at, b * 256 : b * 256 + 256] = low[
                    :, b * 1024 + jj * 256 : b * 1024 + jj * 256 + 256
                ]

    def low_copy(jj):
        return rc(own_low.at[jj], plane_low.at[k, j], low_s.at[0], low_r.at[j], dev(z, jj, k))

    def low_pass(jj):
        return rc(plane_low.at[k, jj], plane_low.at[k, jj], low_s.at[1], low_r.at[4], dev_mate)

    def low_give():
        low_copy(jd).start()
        low_copy(jx).start()
        low_copy(jy).start()

    spot_give = rc(
        spot_in.at[:, pl.ds(pl.multiple_of(mate * half, half), half)], spot_h.at[rows(k, 128)], spot_s, spot_r, dev_mate
    )

    def low_own():
        plane_low[k, j] = own_low[j]
        low_pass(j).start()
        spot_give.start()

    def filt_pair():
        got(f_line.at[pl.ds(0, 3)], sm_r.at[0])
        f_pair[k] = f_line[...]
        hand_over(f_line, f_pair.at[k], 1)

    def filt_plane():
        got(f_line, sm_r.at[1])
        f_all[j] = f_pair[...]
        spread(lambda o: f_pair, f_all, "plane", 2)

    def of_cells(jj, kk, b):
        return own_low[jj, :, pl.ds(pl.multiple_of(b * 256 + kk * 128, 128), 128)].astype(f32)

    def split(d):
        return lax.div(d, 8), lax.rem(lax.div(d, 4), 2), lax.rem(d, 4)

    kind = lax.div(lane, 8)
    of_slide = lax.rem(lane, 8) == slide_col.astype(jnp.int32)

    def mass_make():
        got(f_all.at[pl.ds(0, 3)], sm_r.at[2])
        keep_all[...] = jax.nn.sigmoid(f_all[...])

        def add_mass(d, acc):
            jj, kk, b = split(d)
            return acc + of_cells(jj, kk, b) * keep_all[jj, kk, b]

        mass = jnp.sum(lax.fori_loop(0, 32, add_mass, jnp.zeros((128, 128), f32)), axis=1, keepdims=True)
        keep["mass"] = mass
        log_term = bins_col * (jnp.log(bins_col) - jnp.log(mass))
        values = jnp.where(
            kind == 0, mass, jnp.where(kind == 1, bins_col, jnp.where(kind == 2, log_term, 0.0))
        )
        m_src[0] = jnp.sum(jnp.where(of_slide, values, 0.0), axis=0, keepdims=True)
        m_src[1] = sslide_in[...].astype(f32)
        hand_over(m_src, m_got, 3)

    lane2 = lax.broadcasted_iota(jnp.int32, (256, 128), 1)

    def mass_chip():
        got(m_src, sm_r.at[3])
        load_spot.wait()
        got(spot_h.at[rows(mate, 128)], spot_r)
        stat[...] = jnp.zeros_like(stat)
        chip_row = m_src[0] + m_got[0]
        for o in range(4):
            stat[0, o, 24:25, :] = chip_row
        first = jnp.where(k == 0, m_src[1], m_got[1])
        second = jnp.where(k == 0, m_got[1], m_src[1])
        hot_lie[...] = (
            lax.broadcasted_iota(jnp.int32, (8, 256), 0).astype(f32)
            == jnp.broadcast_to(jnp.concatenate([first, second], axis=1), (8, 256))
        ).astype(f32)
        slides_col = jnp.concatenate([stand(first), stand(second)], axis=0)
        hot_stand[...] = ((lax.rem(lane2, 8) == slides_col.astype(jnp.int32)) & (lane2 < 24)).astype(b16)
        coef[...] = jnp.zeros_like(coef)
        filt_acc[...] = jnp.zeros_like(filt_acc)

    def split_dot(a, v):
        high = v.astype(b16)
        rest = (v - high.astype(f32)).astype(b16)
        return jnp.dot(a, high, preferred_element_type=f32) + jnp.dot(a, rest, preferred_element_type=f32)

    def low_arrive(i):
        if i == 3:
            got(plane_low.at[mate], low_r.at[4])
            got(hand, hand_r)
        else:
            jj = (jx, jy, jd)[i]
            got(plane_low.at[k, jj], low_r.at[jj])
            low_pass(jj).start()

    def product(q, left, count):
        at = pl.ds(q * WIDTH, count * WIDTH)

        @pl.loop(0, 2)
        def _(h):
            if left is plane_low:
                whole = jnp.dot(left[h].reshape(512, 1024), col[:, :, at].reshape(1024, count * WIDTH), preferred_element_type=f32)
            else:
                whole = jnp.dot(left[rows(h, 512), :], grad[:, :, :, at].reshape(1024, count * WIDTH), preferred_element_type=f32)
            for i in range(count):
                part[q + i, h] = whole[:, i * WIDTH : i * WIDTH + WIDTH].reshape(4, 128, WIDTH)

    def reduce_first(q):
        for i, (core, owner, to, sem, slot) in enumerate((
            (0, jd, dev_x, early_r.at[q, 0], early.at[q, 0]),
            (1, jd, dev_y, early_r.at[q, 1], early.at[q, 1]),
            (0, jx, dev_x, late_r.at[q], late.at[q, 0]),
            (1, jy, dev_y, late_r.at[q], late.at[q, 1]),
        )):
            send1[q, i] = part[q, core, owner].astype(b16)
            rc(send1.at[q, i], slot, send1_s, sem, to).start()

    def reduce_second(q, i):
        owner, to = ((jy, dev_y), (jx, dev_x))[i]
        got(early.at[q, i], early_r.at[q, i])
        send2[q, i] = (part[q, i, owner] + early[q, i].astype(f32)).astype(b16)
        rc(send2.at[q, i], late.at[q, 2 + i], send2_s, late_r.at[q], to).start()

    def pred_give(q):
        return rc(
            pred_h.at[rows(mate, 128), pl.ds(q * WIDTH, WIDTH)], pred_out.at[:, lanes(k, q)], pred_s, pred_r, dev_mate
        )

    def pred_own(q):
        return pltpu.make_async_copy(
            pred_h.at[rows(k, 128), pl.ds(q * WIDTH, WIDTH)], pred_out.at[:, lanes(k, q)], own_sem
        )

    def reduce_last(q):
        got(late.at[q], late_r.at[q])
        for i in range(2):
            pred_h[i * 128 : i * 128 + 128, q * WIDTH : q * WIDTH + WIDTH] = part[q, i, j] + (
                late[q, i].astype(f32) + late[q, 2 + i].astype(f32)
            )
        pred_give(q).start()
        pred_own(q).start()

    def reduce_stat(q):
        pr = pred_h[:, q * WIDTH : q * WIDTH + WIDTH]
        sp = spot_h[:, q * WIDTH : q * WIDTH + WIDTH]
        for i, v in enumerate((pr * sp, pr * pr)):
            spacc[i] = v if q == 0 else spacc[i] + v

    def reduce_slides(q):
        pr = pred_h[:, q * WIDTH : q * WIDTH + WIDTH]
        sp = spot_h[:, q * WIDTH : q * WIDTH + WIDTH]
        for i, v in enumerate((pr * sp, pr * pr)):
            stat[q // 4, q % 4, i * 8 : i * 8 + 8] = split_dot(hot_lie[...].astype(b16), v)

    def obs_sums():
        for q in range(chunks):
            sp = spot_h[:, q * WIDTH : q * WIDTH + WIDTH]
            v = sp * sp
            ob_acc[...] = v if q == 0 else ob_acc[...] + v
            stat[q // 4, q % 4, 16:24] = split_dot(hot_lie[...].astype(b16), v)
        rc(ob_acc, ob_got, ob_s, ob_r, dev_mate).start()

    def st_send(g, i):
        slots = (st1, st2, st3)[i]
        if i == 0:
            st1[g, j] = stat[g, j]
        else:
            prior = (st1, st2)[i - 1]
            got(prior.at[g, pl.ds(0, 3)], st_r.at[g, i - 1])
            total = prior[g, 0] + prior[g, 1] + prior[g, 2] + prior[g, 3]
            st_sum[g, i - 1] = total
            if i == 1:
                st2[g, z] = total
            else:
                st3[g, j] = total
        for o in line_others if i == 1 else plane_others:
            src = stat.at[g, o] if i == 0 else st_sum.at[g, i - 1]
            to = dev(o, j, k) if i == 1 else dev(z, o, k)
            rc(src, slots.at[g, z if i == 1 else j], st_s.at[g, i], st_r.at[g, i], to).start()

    def st_finish(g):
        got(st3.at[g, pl.ds(0, 3)], st_r.at[g, 2])

    def turn(i):
        for kk in range(2):
            plane_turn[:, (kk * 4 + i) * 128 : (kk * 4 + i) * 128 + 128] = plane_low[kk, i].astype(f32).T.astype(b16)

    spx = rc(spacc, spgot, spx_s, spx_r, dev_mate)

    def spot_half():
        spx.start()

    slide8 = lax.broadcasted_iota(jnp.int32, (8, 128), 0)
    lane8 = lax.broadcasted_iota(jnp.int32, (8, 128), 1)

    def mass_end():
        sums_row = st_sum[0, 1, 24:25, :]
        each = jnp.broadcast_to(sums_row, (128, 128))
        mass_each = jnp.sum(jnp.where(of_slide & (kind == 0), each, 0.0), 1, keepdims=True)
        bins_each = jnp.sum(jnp.where(of_slide & (kind == 1), each, 0.0), 1, keepdims=True)
        mass_grad = (1.0 / mass_each - bins_col / (bins_each * keep["mass"])) / SLIDES
        keep["grad"] = mass_grad.astype(b16).astype(f32)

        def by_slide(begin):
            return jnp.sum(
                jnp.where(lane8 == slide8 + begin, jnp.broadcast_to(sums_row, (8, 128)), 0.0), 1, keepdims=True
            )

        mass_s, bins_s, log_s = by_slide(0), by_slide(8), by_slide(16)
        kl = jnp.sum(log_s / bins_s - jnp.log(bins_s) + jnp.log(mass_s), axis=0, keepdims=True)
        keep["kl"] = kl / SLIDES

    def reach_make():
        mass_grad = keep["grad"]

        @pl.loop(0, 32)
        def _(d):
            jj, kk, b = split(d)
            r_src[kk, jj, b] = jnp.sum(of_cells(jj, kk, b) * mass_grad, axis=0, keepdims=True)

        hand_over(r_src.at[mate], r_mate, 4)

    def reach_plane():
        got(r_mate, sm_r.at[4])
        r_plane_src[...] = r_src[k] + r_mate[...]
        r_plane[j] = r_plane_src[j]
        spread(lambda o: r_plane_src.at[o], r_plane, "plane", 5)

    def reach_line():
        got(r_plane.at[pl.ds(0, 3)], sm_r.at[5])
        r_line_src[...] = r_plane[0] + r_plane[1] + r_plane[2] + r_plane[3]
        r_line[z] = r_line_src[z]
        spread(lambda o: r_line_src.at[o], r_line, "line", 6)

    def obs_end():
        got(ob_got, ob_r)
        keep["obs_c"] = jnp.sum(ob_acc[...] + ob_got[...], axis=1, keepdims=True)

    def spot_sums():
        st_finish(0)
        got(spgot, spx_r)
        cross_c, pred_c = [jnp.sum(spacc[i] + spgot[i], axis=1, keepdims=True) for i in range(2)]
        obs_c = keep["obs_c"]
        root_c = jnp.sqrt(pred_c * obs_c)
        keep["cos"] = cross_c / root_c
        keep["obs"] = (1.0 / root_c) / total_spots
        keep["prd"] = (cross_c / (pred_c * root_c)) / total_spots

    def grad_make(q):
        scale = 1.0 / (SLIDES * total_genes)
        for e in range(units):
            g, o = divmod(q * units + e, 4)
            sums = st3[g, o]
            cross, prd, obs = sums[:8], sums[8:16], sums[16:24]
            root = jnp.sqrt(prd * obs)
            for i, v in enumerate((scale / root, scale * cross / (prd * root))):
                high = v.astype(b16).astype(f32)
                mid = (v - high).astype(b16).astype(f32)
                low = v - high - mid
                stack = jnp.concatenate([high, mid, low, jnp.zeros((8, 128), f32)], axis=0)
                coef[:32, (i * units + e) * 128 : (i * units + e) * 128 + 128] = stack.astype(b16)
        each_spot = jnp.dot(hot_stand[...], coef[...], preferred_element_type=f32)
        at = slice(q * WIDTH, q * WIDTH + WIDTH)
        value = pred_h[:, at] * (each_spot[:, WIDTH:] + keep["prd"]) - spot_h[:, at] * (each_spot[:, :WIDTH] + keep["obs"])
        value = value.astype(b16)
        grad[0, j, :, at] = value[:128]
        grad[1, j, :, at] = value[128:]

    def gene_cos():
        total = jnp.zeros((8, 128), f32)
        for g in range(2):
            for e in range(4):
                sums = st3[g, e]
                total = total + sums[:8] / jnp.sqrt(sums[8:16] * sums[16:24])
        return jnp.sum(jnp.sum(total, axis=0, keepdims=True), axis=1, keepdims=True)

    def grad_send(q):
        grad_make(q)
        at = grad.at[:, j, :, at_chunk(q)]
        rc(at, at, g_s.at[0], g_r.at[q, 0], dev_x).start()
        rc(at, at, g_s.at[1], g_r.at[q, 1], dev_y).start()

    def grad_direct(q):
        grad_make(q)
        at = grad.at[:, j, :, at_chunk(q)]
        rc(at, at, g_s.at[4], g_r.at[q, 2], dev(z, jd, k)).start()
        rc(at, at, g_s.at[0], g_r.at[q, 0], dev_x).start()
        rc(at, at, g_s.at[1], g_r.at[q, 1], dev_y).start()

    def grad_pass(q, i):
        owner, to = ((jx, dev_y), (jy, dev_x))[i]
        got(grad.at[:, owner, :, at_chunk(q)], g_r.at[q, i])
        at = grad.at[i, owner, :, at_chunk(q)]
        rc(at, at, g_s.at[2 + i], g_r.at[q, 2], to).start()

    def run_up(q, b):
        return rc(pass_on.at[q, b], sums_up.at[q, b], rs_s, rs_r.at[q, b], dev_up)

    def run_dn(q, b):
        return rc(pass_on.at[q, b], sums_dn.at[q, b], rs_s, rs_r.at[q, b], dev_dn)

    def block(q, b):
        return part[q, b // 2, pl.ds(2 * (b % 2), 2)].reshape(256, WIDTH)

    def run_last(q, b, up):
        i = 0 if up else 1
        to, cross = (dev_up, cross_up) if up else (dev_dn, cross_dn)
        rc(pass_on.at[q, b, rows(k, 128)], fin.at[q, i, k], rs_s, fin_r.at[q], to).start()
        rc(pass_on.at[q, b, rows(mate, 128)], fin.at[q, i, k], rs_s, fin_r.at[q], cross).start()

    def sums_half(q, h):
        whole = jnp.dot(
            plane_turn[rows(h, 512), :], grad[:, :, :, at_chunk(q)].reshape(1024, WIDTH), preferred_element_type=f32
        )
        part[q, h] = whole.reshape(4, 128, WIDTH)

    def sums_give(q, b):
        pass_on[q, b] = block(q, b).astype(b16)

    def grad_wait(q):
        if DIRECT == q:
            got(grad.at[:, jx, :, at_chunk(q)], g_r.at[q, 0])
            got(grad.at[:, jy, :, at_chunk(q)], g_r.at[q, 1])
        got(grad.at[:, jd, :, at_chunk(q)], g_r.at[q, 2])

    def sums_first(q, count):
        if count == 2:
            product(q, plane_turn, count)
        for step in range(2):
            if count == 1:
                sums_half(q, jnp.where(z < 2, 1 - step, step))

            @pl.when(z == 0)
            def _():
                for i in range(count):
                    for b in ((3, 2), (1,))[step]:
                        sums_give(q + i, b)
                        run_last(q + i, b, True) if b == 1 else run_up(q + i, b).start()

            @pl.when(z == 3)
            def _():
                for i in range(count):
                    for b in ((0, 1), (2,))[step]:
                        sums_give(q + i, b)
                        run_last(q + i, b, False) if b == 2 else run_dn(q + i, b).start()

    def pass_add(q, b, slots):
        got(slots.at[q, b], rs_r.at[q, b])
        pass_on[q, b] = (block(q, b) + slots[q, b].astype(f32)).astype(b16)

    def pass_far(q):
        @pl.when(z == 1)
        def _():
            pass_add(q, 3, sums_up)
            run_up(q, 3).start()

        @pl.when(z == 2)
        def _():
            pass_add(q, 0, sums_dn)
            run_dn(q, 0).start()

    def pass_middle(q):
        @pl.when(z == 1)
        def _():
            pass_add(q, 2, sums_up)
            run_last(q, 2, True)

        @pl.when(z == 2)
        def _():
            pass_add(q, 1, sums_dn)
            run_last(q, 1, False)

    def pass_near(q):
        @pl.when(z == 1)
        def _():
            pass_add(q, 0, sums_dn)
            run_last(q, 0, False)

        @pl.when(z == 2)
        def _():
            pass_add(q, 3, sums_up)
            run_last(q, 3, True)

    def other_give(q):
        return rc(other.at[q], other_got.at[q], oth_s, oth_r.at[q], dev_mate)

    def use_sums(q, kk, sums):
        at = lanes(kk, q)
        expr_out[:, at] = keep_col * sums
        weighed = cell_v[:, at].astype(f32) * sums
        for e in range(units):
            filt_acc[...] = filt_acc[...] + weighed[:, e * 128 : e * 128 + 128]

    def sums_other(q):
        other[q] = part[q, lax.div(z, 2), 2 * lax.rem(z, 2) + mate]
        other_give(q).start()

    def sums_last(q):
        @pl.when(z == 0)
        def _():
            got(fin.at[q, 1], fin_r.at[q])

        @pl.when(z == 3)
        def _():
            got(fin.at[q, 0], fin_r.at[q])

        @pl.when((z > 0) & (z < 3))
        def _():
            got(fin.at[q], fin_r.at[q])

        got(other_got.at[q], oth_r.at[q])
        own_at = (q, lax.div(z, 2), 2 * lax.rem(z, 2) + k)
        for kk, base in ((k, part[own_at]), (mate, other_got[q])):
            up = jnp.where(z > 0, fin[q, 0, kk].astype(f32), 0.0)
            dn = jnp.where(z < 3, fin[q, 1, kk].astype(f32), 0.0)
            use_sums(q, kk, base + (up + dn))

    def back_dot(b):
        @pl.loop(0, 2)
        def _(h):
            back[b, h] = lax.dot_general(
                grad[h].reshape(512, half), col[b], (((1,), (1,)), ((), ())), preferred_element_type=f32
            ).reshape(4, 128, 256)

        rc(back.at[b, mate], back_got.at[b], back_s, back_r.at[b], dev_mate).start()

    def back_add(b):
        got(back_got.at[b], back_r.at[b])
        for jj in range(4):
            back_low[jj, :, rows(b, 256)] = (back[b, k, jj] + back_got[b, jj]).astype(b16)

    def ret_send(b):
        at = rows(b, 256)
        for jj in (jd, jx, jy):
            rc(back_low.at[jj, :, at], back_ret.at[j, :, at], ret_s, ret_r, dev(z, jj, k)).start()
        back_ret[j, :, at] = back_low[j, :, at]

    loss_lane = lax.broadcasted_iota(jnp.int32, (1, 128), 1)

    def loss_mate():
        own_cos = jnp.sum(keep["cos"], axis=0, keepdims=True)
        l_src[...] = jnp.where(loss_lane == 0, own_cos, jnp.where(loss_lane == 1, gene_cos(), 0.0))
        hand_over(l_src, l_mate, 7)
        l_plane[j] = l_src[...]
        spread(lambda o: l_src, l_plane, "plane", 8)

    def loss_line():
        got(l_plane.at[pl.ds(0, 3)], sm_r.at[8])
        total = l_plane[0] + l_plane[1] + l_plane[2] + l_plane[3]
        l_line_src[...] = total
        l_line[z] = total
        spread(lambda o: l_line_src, l_line, "line", 9)

    def loss_end():
        got(l_line.at[pl.ds(0, 3)], sm_r.at[9])
        got(l_mate, sm_r.at[7])
        cos_row = l_line[0] + l_line[1] + l_line[2] + l_line[3]
        gene_row = l_src[...] + l_mate[...]
        cos_total = jnp.sum(jnp.where(loss_lane == 0, cos_row, 0.0), axis=1, keepdims=True)
        gene_total = jnp.sum(jnp.where(loss_lane == 1, gene_row, 0.0), axis=1, keepdims=True)
        gene_loss = 1.0 - gene_total / (SLIDES * total_genes)
        spot_loss = 1.0 - cos_total / total_spots
        kl_loss = keep["kl"]
        total_loss = gene_loss + spot_loss + kl_loss
        picked = jnp.where(loss_lane == 2, spot_loss, jnp.where(loss_lane == 3, kl_loss, 0.0))
        loss_out[...] = jnp.where(loss_lane == 0, total_loss, jnp.where(loss_lane == 1, gene_loss, picked))

    def map_rows(g):
        at = rows(g, 16)
        pick = lax.broadcasted_iota(jnp.int32, (16, 128), 0) + g * 16
        here = lax.broadcasted_iota(jnp.int32, (16, 128), 1)
        mg = jnp.sum(jnp.where(pick == here, jnp.broadcast_to(mass_row[...], (16, 128)), 0.0), 1, keepdims=True)
        inner = jnp.zeros((16, 128), f32)
        for d in range(32):
            b, jj, kk = d // 8, (d % 8) // 2, d % 2
            used = back_ret[jj, at, b * 256 + kk * 128 : b * 256 + kk * 128 + 128].astype(f32) + mg * keep_all[jj, kk, b]
            inner = inner + chance[at, d * 128 : d * 128 + 128] * used
            map_out[at, d * 128 : d * 128 + 128] = used
        inner = jnp.sum(inner, axis=1, keepdims=True)
        map_out[at, :] = chance[at, :] * (map_out[at, :] - inner)

    def map_some(i):
        if i == 0:
            got(back_ret.at[pl.ds(0, 3)], ret_r)
            mass_row[...] = lie(keep["grad"])
        pl.loop(2 * i, 2 * i + 2)(map_rows)

    steps = {
        "x": softmax_some, "H": scale_more, "F": lambda i: filt_line(), "w": lambda i: (low_give, low_own)[i](),
        "c": col_own, "h": lambda i: hop(), "i": lambda i: (filt_pair, filt_plane, mass_make, mass_chip)[i](),
        "a": low_arrive, "q": turn, "p": lambda q: product(q, plane_low, 1), "P": lambda q: product(q, plane_low, 2),
        "f": reduce_first, "s": lambda q: reduce_second(q, 0), "S": lambda q: reduce_second(q, 1),
        "l": reduce_last, "k": reduce_stat, "j": reduce_slides, "B": lambda i: (obs_sums, obs_end)[i](), "t": lambda i: st_send(0, i), "z": lambda i: (spot_half, mass_end, spot_sums)[i](),
        "g": grad_send, "G": grad_direct, "m": lambda q: grad_pass(q, 0), "n": lambda q: grad_pass(q, 1),
        "y": lambda i: st_send(1, i) if i < 3 else st_finish(1), "r": lambda q: sums_first(q, 1), "R": lambda q: sums_first(q, 2),
        "U": pass_far, "V": pass_middle, "D": pass_near,
        "L": sums_last, "O": sums_other, "b": back_dot, "A": back_add, "T": ret_send, "W": grad_wait, "M": map_some,
        "e": lambda i: (reach_make, reach_plane, reach_line)[i](), "o": lambda i: (loss_mate, loss_line, loss_end)[i](),
    }
    for group in ORDER:
        for word in group.split():
            steps[word[0]](int(word[1:]) if len(word) > 1 else 0)

    got(r_line.at[pl.ds(0, 3)], sm_r.at[6])
    reach_row = r_line[0] + r_line[1] + r_line[2] + r_line[3]
    filt_sum = jnp.sum(filt_acc[...], axis=1, keepdims=True)
    keep_row = jax.nn.sigmoid(filt_in[...].astype(f32))
    filt_out[...] = keep_row * (1.0 - keep_row) * (lie(filt_sum) + reach_row)

    sent(hand, hand_s)
    spot_give.wait_send()
    sent(send1, send1_s)
    sent(send2, send2_s)
    sent(pred_h.at[rows(mate, 128)], pred_s)
    got(pred_out.at[:, pl.ds(pl.multiple_of(mate * half, half), half)], pred_r)
    pltpu.make_async_copy(
        pred_h.at[rows(k, 128)], pred_out.at[:, pl.ds(pl.multiple_of(k * half, half), half)], own_sem
    ).wait()
    for i in range(2):
        sent(grad.at[:, j], g_s.at[i])
    others = [q for q in range(chunks) if q != DIRECT]
    sent(grad.at[0, jx, :, pl.ds(0, len(others) * WIDTH)], g_s.at[2])
    sent(grad.at[1, jy, :, pl.ds(0, len(others) * WIDTH)], g_s.at[3])
    if DIRECT is not None:
        sent(grad.at[:, j, :, at_chunk(DIRECT)], g_s.at[4])
    sent(ob_acc, ob_s)
    for i in range(3):
        @pl.when(z == i)
        def _():
            sent(col.at[pl.ds(0, i + 1)], up_s)

        @pl.when(z == 3 - i)
        def _():
            sent(col.at[pl.ds(3 - i, i + 1)], dn_s)
    sent(pass_on.at[:, pl.ds(0, 3)], rs_s)
    sent(plane_low.at[k, pl.ds(0, 3)], low_s.at[0])
    sent(plane_low.at[k], low_s.at[1])
    for g in range(2):
        for i in range(3):
            sent(st1.at[g, pl.ds(0, 3)], st_s.at[g, i])
    spx.wait_send()
    sent(back_got, back_s)
    sent(back_low.at[pl.ds(0, 3)], ret_s)
    sent(other, oth_s)
    for i, ref in enumerate((
        f_line.at[pl.ds(0, 3)], f_line, f_all.at[pl.ds(0, 3)], m_src, r_mate, r_plane.at[pl.ds(0, 3)],
        r_line.at[pl.ds(0, 3)], l_mate, l_plane.at[pl.ds(0, 3)], l_line.at[pl.ds(0, 3)],
    )):
        sent(ref, sm_s.at[i])


def hand_out(pred_in, map_in, expr_in, filt_in, loss_in, pred_out, map_out, expr_out, filt_out, loss_out, sems):
    pairs = ((map_in, map_out), (pred_in, pred_out), (expr_in, expr_out))
    copies = [pltpu.make_async_copy(src, dst, sems.at[i]) for i, (src, dst) in enumerate(pairs)]
    for copy in copies:
        copy.start()
    filt_out[...] = filt_in[...]
    loss_out[...] = loss_in[:, :4]
    for copy in copies:
        copy.wait()


def fused_shards(map_logits, filter_logits, cell_expr, spot_expr, cell_slide, spot_slide, density_bins):
    f32, b16 = jnp.float32, jnp.bfloat16
    spots, cells = map_logits.shape
    genes = cell_expr.shape[1]
    n = genes // (2 * WIDTH)
    V, S = pltpu.VMEM, pltpu.SemaphoreType.DMA
    any_, vmem = pl.BlockSpec(memory_space=pl.ANY), pl.BlockSpec(memory_space=pltpu.VMEM)
    one = S(())
    scratch = [
        V((128, cells), f32),
        V((4, 128, 1024), b16),
        V((2, 4, 128, 1024), b16),
        V((1024, 1024), b16),
        V((128, genes), b16),
        V((n, 128, WIDTH), b16),
        V((4, 256, genes // 2), b16),
        V((n, 2, 4, 128, WIDTH), f32),
        V((n, 4, 128, WIDTH), b16),
        V((n, 2, 128, WIDTH), b16),
        V((n, 2, 128, WIDTH), b16),
        V((n, 4, 128, WIDTH), b16),
        V((256, genes // 2), f32),
        V((256, genes // 2), f32),
        V((2, 4, 32, 128), f32),
        V((2, 2, 32, 128), f32),
        V((2, 4, 32, 128), f32),
        V((2, 4, 32, 128), f32),
        V((2, 4, 32, 128), f32),
        V((2, 256, 128), f32),
        V((2, 256, 128), f32),
        V((256, 128), f32),
        V((256, 128), f32),
        V((128, 2 * WIDTH), b16),
        V((2, 4, 128, genes // 2), b16),
        V((n, 4, 256, WIDTH), b16),
        V((n, 4, 256, WIDTH), b16),
        V((n, 4, 256, WIDTH), b16),
        V((n, 2, 2, 128, WIDTH), b16),
        V((4, 2, 4, 128, 256), f32),
        V((4, 4, 128, 256), f32),
        V((4, 128, 1024), b16),
        V((4, 128, 1024), b16),
        V((n, 128, WIDTH), f32),
        V((n, 128, WIDTH), f32),
        V((4, 1, 128), f32),
        V((2, 4, 1, 128), f32),
        V((4, 2, 4, 1, 128), f32),
        V((4, 2, 4, 1, 128), f32),
        V((2, 1, 128), f32),
        V((2, 1, 128), f32),
        V((2, 4, 4, 1, 128), f32),
        V((4, 4, 1, 128), f32),
        V((4, 4, 1, 128), f32),
        V((4, 4, 1, 128), f32),
        V((4, 1, 128), f32),
        V((4, 1, 128), f32),
        V((1, 128), f32),
        V((1, 128), f32),
        V((4, 1, 128), f32),
        V((1, 128), f32),
        V((4, 1, 128), f32),
        V((128, 128), f32),
        V((8, 256), f32),
        V((256, 128), b16),
        V((1, 128), f32),
        S((3,)), one, one, one, one, one, S((n, 4)), S((2,)), S((5,)),
        one, one, S((n, 2)), S((n,)),
        one, one, one, one, S((2, 3)), S((2, 3)), one, one, one, one,
        S((5,)), S((n, 3)), one, S((n, 4)), S((n,)), one, S((4,)),
        one, one, one, S((n,)), S((10,)), S((10,)),
    ]
    predicted, map_grad, expr_grad, filt, loss = pl.pallas_call(
        functools.partial(fused_kernel, float(spots * 32), float(genes)),
        out_shape=(
            pltpu.VMEM((spots, genes), f32),
            pltpu.VMEM((spots, cells), f32),
            pltpu.VMEM((spots, genes), f32),
            V((1, 128), f32),
            V((1, 128), f32),
        ),
        in_specs=[any_, vmem, any_, any_, vmem, vmem, vmem],
        out_specs=(vmem, vmem, vmem, vmem, vmem),
        scratch_shapes=scratch,
        compiler_params=pltpu.CompilerParams(
            collective_id=0, has_side_effects=True, vmem_limit_bytes=58 * 2**20
        ),
        name="mapping_step",
    )(
        map_logits,
        filter_logits.reshape(1, 128),
        cell_expr,
        spot_expr,
        cell_slide.reshape(1, cells),
        spot_slide.reshape(1, 128),
        density_bins.reshape(1, 128),
    )
    predicted, map_grad, expr_grad, filt, loss = pl.pallas_call(
        hand_out,
        out_shape=(
            jax.ShapeDtypeStruct((spots, genes), f32),
            jax.ShapeDtypeStruct((spots, cells), f32),
            jax.ShapeDtypeStruct((spots, genes), f32),
            jax.ShapeDtypeStruct((1, 128), f32),
            jax.ShapeDtypeStruct((1, 4), f32),
        ),
        in_specs=[vmem] * 5,
        out_specs=(any_, any_, any_, vmem, vmem),
        scratch_shapes=[S((3,))],
        compiler_params=pltpu.CompilerParams(vmem_limit_bytes=2**20),
        name="hand_out",
    )(*[pltpu.with_memory_space_constraint(v, pltpu.VMEM) for v in (predicted, map_grad, expr_grad, filt, loss)])
    return loss.reshape(4), predicted, map_grad, expr_grad, filt.reshape(128)


def solution(mesh):
    both = P(("row", "col"))
    rows = P(("row", "col"), None)
    in_specs = (rows, both, rows, rows, P(), both, both)
    out_specs = (P(), rows, rows, rows, both)
    step = fused_shards if (mesh.shape["row"], mesh.shape["col"]) == (4, 8) else shards
    return jax.shard_map(step, mesh=mesh, in_specs=in_specs, out_specs=out_specs, check_vma=False)
```

```python
import functools

import jax
import jax.numpy as jnp
from jax import lax
from jax.experimental import pallas as pl
from jax.experimental.pallas import tpu as pltpu
from jax.sharding import PartitionSpec as P

SLIDES = 8
ROWS, PLANE, CORES = 4, 4, 2
WIDTH = 128
MESH = pl.DeviceIdType.MESH
DIRECT = 0
ORDER = (
    "c0 N0 H0 H1",
    "x0 w0 c1 N1",
    "F0 H2 c2 H3",
    "H4 x1 w1 H5",
    "h H6 c3 c4",
    "x2 i0 x3 i1",
    "H7 w3 h h",
    "h w2 c5 i2",
    "v0 h h h",
    "i3 B0 a2 a0",
    "a1 h h h",
    "c6 a3 P0 f0",
    "f1 h h h",
    "P2 f2 s0 q1",
    "f3 S1 h h",
    "h c7 s2 s1",
    "S0 p4 S2 s3",
    "f4 S3 h h",
    "h p5 f5 l1",
    "l0 l2 j0 j2",
    "j1 s4 h h",
    "h l3 j3 t0",
    "s5 S4 p6 f6",
    "k0 k2 k1 S5",
    "h h p7 t1",
    "f7 s6 Y2 k3",
    "l4 j4 S6 l5",
    "k5 B1 s7 S7",
    "t2 q0 j5 l6",
    "k6 k4 l7 k7",
    "z0 q3 j6 j7",
    "y0 z2 G0 Y3",
    "q2 g2 g1 y1",
    "W0 r0 m2 n2",
    "z1 y2 Y7 g3",
    "m1 n1 W2 r2",
    "y3 g7 U0 e0",
    "Y0 m3 n3 g4",
    "g6 W1 r1 g5",
    "U2 m7 o0 m4",
    "W3 V0 n7 V2",
    "n4 r3 m6 n6",
    "n5 D2 m5 O1",
    "V1 W7 r7 U1",
    "W6 r6 D0 W4",
    "O2 W5 b2 O6",
    "b0 O0 b1 Y5",
    "A2 T2 U3 U7",
    "e1 A0 T0 V7",
    "A1 o1 R4 O5",
    "V3 T1 Y6 Y1",
    "Y4 L0 b3 U6",
    "O3 D1 e2 V6",
    "O7 D7 A3 T3",
    "U4 D3 L2 L7",
    "O4 D6 o2 L1",
    "U5 V4 L3 L6",
    "V5 D4 M0 D5",
    "M1 M2 L4 M3",
    "L5",
)


def shards(map_logits, filter_logits, cell_expr, spot_expr, cell_slide, spot_slide, density_bins):
    highest = lax.Precision.HIGHEST
    both = ("row", "col")
    rows_count = lax.axis_size("row")
    cols_count = lax.axis_size("col")
    spot_dev, cell_total = map_logits.shape
    cell_dev = filter_logits.shape[0]
    spot_total = spot_dev * rows_count * cols_count
    gene_count = cell_expr.shape[1]
    keep_rate = jax.nn.sigmoid(filter_logits.astype(jnp.float32))
    scaled = (keep_rate[:, None] * cell_expr.astype(jnp.float32)).astype(jnp.bfloat16)
    scaled_col = lax.all_gather(scaled, "row", axis=0, tiled=True)
    allowed = spot_slide[:, None] == cell_slide[None, :]
    shifted = jnp.where(allowed, map_logits, -1e30)
    row_peak = jnp.max(shifted, axis=1, keepdims=True)
    raised = jnp.exp(shifted - row_peak)
    chances = raised / jnp.sum(raised, axis=1, keepdims=True)
    chance_low = chances.astype(jnp.bfloat16)
    by_col = chance_low.reshape(spot_dev, rows_count, cols_count, cell_dev)
    mapped = lax.all_to_all(by_col, "col", split_axis=2, concat_axis=0, tiled=True)
    mapped = mapped.reshape(spot_dev * cols_count, rows_count * cell_dev)
    keep_col = lax.all_gather(keep_rate, "row", axis=0, tiled=True)
    part_pred = jnp.dot(mapped, scaled_col, preferred_element_type=jnp.float32)
    part_mass = jnp.dot(mapped, keep_col, precision=highest, preferred_element_type=jnp.float32)
    predicted = lax.psum_scatter(part_pred, "col", scatter_dimension=0, tiled=True)
    mass = lax.psum_scatter(part_mass, "col", scatter_dimension=0, tiled=True)
    onehot = (spot_slide[:, None] == jnp.arange(SLIDES, dtype=jnp.int32)[None, :]).astype(
        jnp.float32
    )
    cross_term = predicted * spot_expr
    pred_sq = predicted * predicted
    obs_sq = spot_expr * spot_expr
    spot_cross = jnp.sum(cross_term, axis=1)
    spot_pred = jnp.sum(pred_sq, axis=1)
    spot_root = jnp.sqrt(spot_pred * jnp.sum(obs_sq, axis=1))
    spot_cos = spot_cross / spot_root
    bin_values = density_bins.astype(jnp.float32)
    log_term = bin_values * (jnp.log(bin_values) - jnp.log(mass))
    all_cross, all_pred, all_obs, slide_mass, slide_bins, slide_log, cos_total = lax.psum(
        (
            jnp.dot(onehot.T, cross_term, precision=highest),
            jnp.dot(onehot.T, pred_sq, precision=highest),
            jnp.dot(onehot.T, obs_sq, precision=highest),
            jnp.dot(onehot.T, mass, precision=highest),
            jnp.dot(onehot.T, bin_values, precision=highest),
            jnp.dot(onehot.T, log_term, precision=highest),
            jnp.sum(spot_cos),
        ),
        both,
    )
    gene_root = jnp.sqrt(all_pred * all_obs)
    gene_loss = 1.0 - jnp.mean(all_cross / gene_root)
    spot_loss = 1.0 - cos_total / spot_total
    kl_loss = jnp.mean(slide_log / slide_bins - jnp.log(slide_bins) + jnp.log(slide_mass))
    total_loss = gene_loss + spot_loss + kl_loss
    losses = jnp.stack([total_loss, gene_loss, spot_loss, kl_loss])
    gene_scale = 1.0 / (SLIDES * gene_count)
    coef_obs = jnp.dot(onehot, 1.0 / gene_root, precision=highest)
    coef_pred = jnp.dot(onehot, all_cross / (all_pred * gene_root), precision=highest)
    pred_grad = -gene_scale * (spot_expr * coef_obs - predicted * coef_pred)
    pred_grad = (
        pred_grad
        - (
            spot_expr / spot_root[:, None]
            - predicted * (spot_cross / (spot_pred * spot_root))[:, None]
        )
        / spot_total
    )
    mass_each = jnp.dot(onehot, slide_mass, precision=highest)
    bins_each = jnp.dot(onehot, slide_bins, precision=highest)
    mass_grad = (1.0 / mass_each - bin_values / (bins_each * mass)) / SLIDES
    grad_low = pred_grad.astype(jnp.bfloat16)
    mass_low = mass_grad.astype(jnp.bfloat16)
    grad_block = lax.all_gather(grad_low, "col", axis=0, tiled=True)
    mass_block = lax.all_gather(mass_low, "col", axis=0, tiled=True)
    back_map = lax.dot_general(
        grad_block, scaled_col, (((1,), (1,)), ((), ())), preferred_element_type=jnp.float32
    )
    back_map = back_map + mass_block.astype(jnp.float32)[:, None] * keep_col[None, :]
    back_low = back_map.astype(jnp.bfloat16)
    returned = lax.all_to_all(
        back_low.reshape(spot_dev * cols_count, rows_count, 1, cell_dev),
        "col",
        split_axis=0,
        concat_axis=2,
        tiled=True,
    ).reshape(spot_dev, cell_total)
    expr_part = lax.dot_general(
        mapped, grad_block, (((0,), (0,)), ((), ())), preferred_element_type=jnp.float32
    )
    mass_reach = lax.dot_general(
        mapped, mass_block, (((0,), (0,)), ((), ())), preferred_element_type=jnp.float32
    )
    expr_sum = lax.psum_scatter(expr_part, "row", scatter_dimension=0, tiled=True)
    mass_sum = lax.psum_scatter(mass_reach, "row", scatter_dimension=0, tiled=True)
    filter_grad = (
        keep_rate
        * (1.0 - keep_rate)
        * (jnp.sum(cell_expr.astype(jnp.float32) * expr_sum, axis=1) + mass_sum)
    )
    expr_grad = keep_rate[:, None] * expr_sum
    chance_grad = returned.astype(jnp.float32)
    inner_sum = jnp.sum(chances * chance_grad, axis=1, keepdims=True)
    map_grad = chances * (chance_grad - inner_sum)
    return (losses, predicted, map_grad, expr_grad, filter_grad)


def fused_kernel(
    total_spots, total_genes,
    logit_in, filt_in, cell_in, spot_in, cslide_in, sslide_in, bins_in,
    pred_out, map_out, expr_out, filt_out, loss_out,
    chance, own_low, plane_low, plane_turn, cell_v, hand, col, part, send1, early, send2, late,
    pred_h, spot_h, stat, st_sum, st1, st2, st3, spacc, spgot, ob_acc, ob_got, coef, grad,
    sums_up, sums_dn, pass_on, fin, back, back_got, back_low, back_ret, other, other_got,
    f_line, f_pair, f_all, keep_all, m_src, m_got, r_src, r_mate, r_plane_src, r_plane, r_line_src, r_line,
    l_src, l_mate, l_plane, l_line_src, l_line, filt_acc, hot_lie, hot_stand, mass_row,
    load_sem, own_sem, hand_s, hand_r, up_s, dn_s, col_r, low_s, low_r, send1_s, send2_s, early_r, late_r,
    pred_s, pred_r, spot_s, spot_r, st_s, st_r, spx_s, spx_r, ob_s, ob_r, g_s, g_r, rs_s, rs_r, fin_r, back_s, back_r,
    ret_s, ret_r, oth_s, oth_r, sm_s, sm_r, ready,
):
    f32, b16 = jnp.float32, jnp.bfloat16
    half = col.shape[2]
    chunks = half // WIDTH
    units = WIDTH // 128
    keep = {}
    z = lax.axis_index("row")
    c = lax.axis_index("col")
    j = lax.div(c, 2)
    k = lax.rem(c, 2)
    y = lax.div(j, 2)
    x = lax.rem(j, 2)
    mate = 1 - k

    def dev(zz, jj, kk):
        return (zz, jj * 2 + kk)

    jx = y * 2 + (1 - x)
    jy = (1 - y) * 2 + x
    jd = (1 - y) * 2 + (1 - x)
    dev_mate = dev(z, j, mate)
    dev_x = dev(z, jx, k)
    dev_y = dev(z, jy, k)
    dev_up = dev(lax.rem(z + 1, 4), j, k)
    dev_dn = dev(lax.rem(z + 3, 4), j, k)
    cross_up = dev(lax.rem(z + 1, 4), j, mate)
    cross_dn = dev(lax.rem(z + 3, 4), j, mate)
    plane_others = (jx, jy, jd)
    line_others = [lax.rem(z + i, 4) for i in (1, 2, 3)]

    def rc(src, dst, ss, rs, to):
        return pltpu.make_async_remote_copy(
            src_ref=src, dst_ref=dst, send_sem=ss, recv_sem=rs, device_id=to, device_id_type=MESH
        )

    def got(ref, sem):
        rc(ref, ref, sem, sem, dev_mate).wait_recv()

    def sent(ref, sem):
        rc(ref, ref, sem, sem, dev_mate).wait_send()

    def rows(i, size):
        return pl.ds(pl.multiple_of(i * size, size), size)

    def at_chunk(q):
        return pl.ds(q * WIDTH, WIDTH)

    def lanes(kk, q):
        return pl.ds(pl.multiple_of(kk * half + q * WIDTH, WIDTH), WIDTH)

    load_cell = pltpu.make_async_copy(cell_in, cell_v, load_sem.at[0])
    load_logit = pltpu.make_async_copy(logit_in, chance, load_sem.at[1])
    load_spot = pltpu.make_async_copy(
        spot_in.at[:, pl.ds(pl.multiple_of(k * half, half), half)], spot_h.at[rows(k, 128)], load_sem.at[2]
    )
    barrier = pltpu.get_barrier_semaphore()
    for to in (dev_mate, dev_x, dev_y, dev(z, jd, k)):
        pl.semaphore_signal(barrier, inc=1, device_id=to, device_id_type=MESH)
    for i, near in enumerate(((dev_up, cross_up), (dev_dn, cross_dn))):
        @pl.when((z < 3) if i == 0 else (z > 0))
        def _():
            for to in near:
                pl.semaphore_signal(barrier, inc=1, device_id=to, device_id_type=MESH)
    load_cell.start()
    load_logit.start()
    load_spot.start()

    eye = lax.broadcasted_iota(jnp.int32, (128, 128), 0) == lax.broadcasted_iota(
        jnp.int32, (128, 128), 1
    )
    lane = lax.broadcasted_iota(jnp.int32, (128, 128), 1)

    def stand(row):
        return jnp.sum(jnp.where(eye, jnp.broadcast_to(row, (128, 128)), 0.0), 1, keepdims=True)

    def lie(column):
        return jnp.sum(jnp.where(eye, jnp.broadcast_to(column, (128, 128)), 0.0), 0, keepdims=True)

    filt_row = filt_in[...].astype(f32)
    keep_col = stand(jax.nn.sigmoid(filt_row))
    slide_col = stand(sslide_in[...].astype(f32))
    bins_col = stand(bins_in[...].astype(f32))

    def hand_copy(q):
        return rc(hand.at[q], col.at[z, rows(k, 128), at_chunk(q)], hand_s, hand_r, dev_mate)

    def col_up(q, b):
        at = col.at[b, :, at_chunk(q)]
        return rc(at, at, up_s, col_r.at[q, b], dev_up)

    def col_dn(q, b):
        at = col.at[b, :, at_chunk(q)]
        return rc(at, at, dn_s, col_r.at[q, b], dev_dn)

    def scale_cells(q):
        hand[q] = (keep_col * cell_v[:, lanes(mate, q)].astype(f32)).astype(b16)
        col[z, rows(k, 128), at_chunk(q)] = (keep_col * cell_v[:, lanes(k, q)].astype(f32)).astype(b16)

    def col_own(q):
        own = col.at[z, rows(k, 128), at_chunk(q)]

        @pl.when(z < 3)
        def _():
            rc(own, own, up_s, col_r.at[q, z], dev_up).start()
            rc(hand.at[q], own, up_s, col_r.at[q, z], cross_up).start()

        @pl.when(z > 0)
        def _():
            rc(own, own, dn_s, col_r.at[q, z], dev_dn).start()
            rc(hand.at[q], own, dn_s, col_r.at[q, z], cross_dn).start()

    hops = [(q, s) for q in range(chunks) for s in range(3)]

    def hop():
        q, s = hops.pop(0)

        @pl.when(z - 1 - s >= 0)
        def _():
            b = z - 1 - s
            got(col.at[b, :, at_chunk(q)], col_r.at[q, b])

            @pl.when(z < 3)
            def _():
                col_up(q, b).start()

        @pl.when(z + 1 + s <= 3)
        def _():
            b = z + 1 + s
            got(col.at[b, :, at_chunk(q)], col_r.at[q, b])

            @pl.when(z > 0)
            def _():
                col_dn(q, b).start()

    load_cell.wait()
    scale_cells(0)
    pl.semaphore_wait(barrier, jnp.where((z == 0) | (z == 3), 6, 8))

    def far_ready(i):
        if i == 0:
            @pl.when(z == 1)
            def _():
                pl.semaphore_signal(ready, inc=1, device_id=dev_up, device_id_type=MESH)

            @pl.when(z == 2)
            def _():
                pl.semaphore_signal(ready, inc=1, device_id=dev_dn, device_id_type=MESH)
        else:
            pl.semaphore_wait(ready, 1)

            @pl.when(z == 1)
            def _():
                pl.semaphore_signal(ready, inc=1, device_id=dev_dn, device_id_type=MESH)

            @pl.when(z == 2)
            def _():
                pl.semaphore_signal(ready, inc=1, device_id=dev_up, device_id_type=MESH)


    def scale_more(q):
        if q:
            scale_cells(q)
        hand_copy(q).start()

    def spread(source, slots, which, i):
        for o in plane_others if which == "plane" else line_others:
            to = dev(z, o, k) if which == "plane" else dev(o, j, k)
            rc(source(o), slots.at[j if which == "plane" else z], sm_s.at[i], sm_r.at[i], to).start()

    def hand_over(source, slot, i):
        rc(source, slot, sm_s.at[i], sm_r.at[i], dev_mate).start()

    def filt_line():
        f_line[z] = filt_row
        spread(lambda o: f_line.at[z], f_line, "line", 0)

    def softmax_some(i):
        if not keep.get("logits"):
            load_logit.wait()
            keep["logits"] = True
        pl.loop(2 * i, 2 * i + 2)(softmax_rows)

    def softmax_rows(g):
        at = rows(g, 16)
        logits = chance[at, :]
        pick = lax.broadcasted_iota(jnp.int32, (16, 128), 0) + g * 16
        here = lax.broadcasted_iota(jnp.int32, (16, 128), 1)
        slide = jnp.sum(
            jnp.where(pick == here, jnp.broadcast_to(sslide_in[...].astype(f32), (16, 128)), 0.0),
            1, keepdims=True,
        )
        allowed = slide == cslide_in[...].astype(f32)
        shifted = jnp.where(allowed, logits, -1e30)
        raised = jnp.exp(shifted - jnp.max(shifted, axis=1, keepdims=True))
        value = raised / jnp.sum(raised, axis=1, keepdims=True)
        chance[at, :] = value
        low = value.astype(b16)
        for b in range(4):
            for jj in range(4):
                own_low[jj, at, b * 256 : b * 256 + 256] = low[
                    :, b * 1024 + jj * 256 : b * 1024 + jj * 256 + 256
                ]

    def low_copy(jj, i):
        at = pl.ds(i * 32, 32)
        return rc(own_low.at[jj, at], plane_low.at[k, j, at], low_s.at[0], low_r.at[j], dev(z, jj, k))

    def low_pass(jj):
        return rc(plane_low.at[k, jj], plane_low.at[k, jj], low_s.at[1], low_r.at[4], dev_mate)

    def low_give(i):
        for jj in (jd, jx, jy):
            low_copy(jj, i).start()

    spot_give = rc(
        spot_in.at[:, pl.ds(pl.multiple_of(mate * half, half), half)], spot_h.at[rows(k, 128)], spot_s, spot_r, dev_mate
    )

    def low_own():
        plane_low[k, j] = own_low[j]
        low_pass(j).start()
        spot_give.start()

    def filt_pair():
        got(f_line.at[pl.ds(0, 3)], sm_r.at[0])
        f_pair[k] = f_line[...]
        hand_over(f_line, f_pair.at[k], 1)

    def filt_plane():
        got(f_line, sm_r.at[1])
        f_all[j] = f_pair[...]
        spread(lambda o: f_pair, f_all, "plane", 2)

    def of_cells(jj, kk, b):
        return own_low[jj, :, pl.ds(pl.multiple_of(b * 256 + kk * 128, 128), 128)].astype(f32)

    def split(d):
        return lax.div(d, 8), lax.rem(lax.div(d, 4), 2), lax.rem(d, 4)

    kind = lax.div(lane, 8)
    of_slide = lax.rem(lane, 8) == slide_col.astype(jnp.int32)

    def mass_make():
        got(f_all.at[pl.ds(0, 3)], sm_r.at[2])
        keep_all[...] = jax.nn.sigmoid(f_all[...])

        def add_mass(d, acc):
            jj, kk, b = split(d)
            return acc + of_cells(jj, kk, b) * keep_all[jj, kk, b]

        mass = jnp.sum(lax.fori_loop(0, 32, add_mass, jnp.zeros((128, 128), f32)), axis=1, keepdims=True)
        keep["mass"] = mass
        log_term = bins_col * (jnp.log(bins_col) - jnp.log(mass))
        values = jnp.where(
            kind == 0, mass, jnp.where(kind == 1, bins_col, jnp.where(kind == 2, log_term, 0.0))
        )
        m_src[0] = jnp.sum(jnp.where(of_slide, values, 0.0), axis=0, keepdims=True)
        m_src[1] = sslide_in[...].astype(f32)
        hand_over(m_src, m_got, 3)

    lane2 = lax.broadcasted_iota(jnp.int32, (256, 128), 1)

    def mass_chip():
        got(m_src, sm_r.at[3])
        load_spot.wait()
        got(spot_h.at[rows(mate, 128)], spot_r)
        stat[...] = jnp.zeros_like(stat)
        chip_row = m_src[0] + m_got[0]
        for o in range(4):
            stat[0, o, 24:25, :] = chip_row
        first = jnp.where(k == 0, m_src[1], m_got[1])
        second = jnp.where(k == 0, m_got[1], m_src[1])
        hot_lie[...] = (
            lax.broadcasted_iota(jnp.int32, (8, 256), 0).astype(f32)
            == jnp.broadcast_to(jnp.concatenate([first, second], axis=1), (8, 256))
        ).astype(f32)
        slides_col = jnp.concatenate([stand(first), stand(second)], axis=0)
        hot_stand[...] = ((lax.rem(lane2, 8) == slides_col.astype(jnp.int32)) & (lane2 < 24)).astype(b16)
        coef[...] = jnp.zeros_like(coef)
        filt_acc[...] = jnp.zeros_like(filt_acc)

    def split_dot(a, v):
        high = v.astype(b16)
        rest = (v - high.astype(f32)).astype(b16)
        return jnp.dot(a, high, preferred_element_type=f32) + jnp.dot(a, rest, preferred_element_type=f32)

    def low_arrive(i):
        if i == 3:
            got(plane_low.at[mate], low_r.at[4])
            got(hand, hand_r)
        else:
            jj = (jx, jy, jd)[i]
            got(plane_low.at[k, jj], low_r.at[jj])
            low_pass(jj).start()

    def product(q, left, count):
        at = pl.ds(q * WIDTH, count * WIDTH)

        @pl.loop(0, 2)
        def _(h):
            if left is plane_low:
                whole = jnp.dot(left[h].reshape(512, 1024), col[:, :, at].reshape(1024, count * WIDTH), preferred_element_type=f32)
            else:
                whole = jnp.dot(left[rows(h, 512), :], grad[:, :, :, at].reshape(1024, count * WIDTH), preferred_element_type=f32)
            for i in range(count):
                part[q + i, h] = whole[:, i * WIDTH : i * WIDTH + WIDTH].reshape(4, 128, WIDTH)

    def reduce_first(q):
        for i, (core, owner, to, sem, slot) in enumerate((
            (0, jd, dev_x, early_r.at[q, 0], early.at[q, 0]),
            (1, jd, dev_y, early_r.at[q, 1], early.at[q, 1]),
            (0, jx, dev_x, late_r.at[q], late.at[q, 0]),
            (1, jy, dev_y, late_r.at[q], late.at[q, 1]),
        )):
            send1[q, i] = part[q, core, owner].astype(b16)
            rc(send1.at[q, i], slot, send1_s, sem, to).start()

    def reduce_second(q, i):
        owner, to = ((jy, dev_y), (jx, dev_x))[i]
        got(early.at[q, i], early_r.at[q, i])
        send2[q, i] = (part[q, i, owner] + early[q, i].astype(f32)).astype(b16)
        rc(send2.at[q, i], late.at[q, 2 + i], send2_s, late_r.at[q], to).start()

    def pred_give(q):
        return rc(
            pred_h.at[rows(mate, 128), pl.ds(q * WIDTH, WIDTH)], pred_out.at[:, lanes(k, q)], pred_s, pred_r, dev_mate
        )

    def pred_own(q):
        return pltpu.make_async_copy(
            pred_h.at[rows(k, 128), pl.ds(q * WIDTH, WIDTH)], pred_out.at[:, lanes(k, q)], own_sem
        )

    def reduce_last(q):
        got(late.at[q], late_r.at[q])
        for i in range(2):
            pred_h[i * 128 : i * 128 + 128, q * WIDTH : q * WIDTH + WIDTH] = part[q, i, j] + (
                late[q, i].astype(f32) + late[q, 2 + i].astype(f32)
            )

    def pred_move(q):
        pred_give(q).start()
        pred_own(q).start()

    def reduce_stat(q):
        pr = pred_h[:, q * WIDTH : q * WIDTH + WIDTH]
        sp = spot_h[:, q * WIDTH : q * WIDTH + WIDTH]
        for i, v in enumerate((pr * sp, pr * pr)):
            spacc[i] = v if q == 0 else spacc[i] + v

    def reduce_slides(q):
        pr = pred_h[:, q * WIDTH : q * WIDTH + WIDTH]
        sp = spot_h[:, q * WIDTH : q * WIDTH + WIDTH]
        for i, v in enumerate((pr * sp, pr * pr)):
            stat[q // 4, q % 4, i * 8 : i * 8 + 8] = split_dot(hot_lie[...].astype(b16), v)

    def obs_sums():
        for q in range(chunks):
            sp = spot_h[:, q * WIDTH : q * WIDTH + WIDTH]
            v = sp * sp
            ob_acc[...] = v if q == 0 else ob_acc[...] + v
            stat[q // 4, q % 4, 16:24] = split_dot(hot_lie[...].astype(b16), v)
        rc(ob_acc, ob_got, ob_s, ob_r, dev_mate).start()

    def st_send(g, i):
        slots = (st1, st2, st3)[i]
        if i == 0:
            st1[g, j] = stat[g, j]
        else:
            prior = (st1, st2)[i - 1]
            got(prior.at[g, pl.ds(0, 3)], st_r.at[g, i - 1])
            total = prior[g, 0] + prior[g, 1] + prior[g, 2] + prior[g, 3]
            st_sum[g, i - 1] = total
            if i == 1:
                st2[g, z] = total
            else:
                st3[g, j] = total
        for o in line_others if i == 1 else plane_others:
            src = stat.at[g, o] if i == 0 else st_sum.at[g, i - 1]
            to = dev(o, j, k) if i == 1 else dev(z, o, k)
            rc(src, slots.at[g, z if i == 1 else j], st_s.at[g, i], st_r.at[g, i], to).start()

    def st_finish(g):
        got(st3.at[g, pl.ds(0, 3)], st_r.at[g, 2])

    def turn(i):
        for kk in range(2):
            plane_turn[:, (kk * 4 + i) * 128 : (kk * 4 + i) * 128 + 128] = plane_low[kk, i].astype(f32).T.astype(b16)

    spx = rc(spacc, spgot, spx_s, spx_r, dev_mate)

    def spot_half():
        spx.start()

    slide8 = lax.broadcasted_iota(jnp.int32, (8, 128), 0)
    lane8 = lax.broadcasted_iota(jnp.int32, (8, 128), 1)

    def mass_end():
        sums_row = st_sum[0, 1, 24:25, :]
        each = jnp.broadcast_to(sums_row, (128, 128))
        mass_each = jnp.sum(jnp.where(of_slide & (kind == 0), each, 0.0), 1, keepdims=True)
        bins_each = jnp.sum(jnp.where(of_slide & (kind == 1), each, 0.0), 1, keepdims=True)
        mass_grad = (1.0 / mass_each - bins_col / (bins_each * keep["mass"])) / SLIDES
        keep["grad"] = mass_grad.astype(b16).astype(f32)

        def by_slide(begin):
            return jnp.sum(
                jnp.where(lane8 == slide8 + begin, jnp.broadcast_to(sums_row, (8, 128)), 0.0), 1, keepdims=True
            )

        mass_s, bins_s, log_s = by_slide(0), by_slide(8), by_slide(16)
        kl = jnp.sum(log_s / bins_s - jnp.log(bins_s) + jnp.log(mass_s), axis=0, keepdims=True)
        keep["kl"] = kl / SLIDES

    def reach_make():
        mass_grad = keep["grad"]

        @pl.loop(0, 32)
        def _(d):
            jj, kk, b = split(d)
            r_src[kk, jj, b] = jnp.sum(of_cells(jj, kk, b) * mass_grad, axis=0, keepdims=True)

        hand_over(r_src.at[mate], r_mate, 4)

    def reach_plane():
        got(r_mate, sm_r.at[4])
        r_plane_src[...] = r_src[k] + r_mate[...]
        r_plane[j] = r_plane_src[j]
        spread(lambda o: r_plane_src.at[o], r_plane, "plane", 5)

    def reach_line():
        got(r_plane.at[pl.ds(0, 3)], sm_r.at[5])
        r_line_src[...] = r_plane[0] + r_plane[1] + r_plane[2] + r_plane[3]
        r_line[z] = r_line_src[z]
        spread(lambda o: r_line_src.at[o], r_line, "line", 6)

    def obs_end():
        got(ob_got, ob_r)
        keep["obs_c"] = jnp.sum(ob_acc[...] + ob_got[...], axis=1, keepdims=True)

    def spot_sums():
        st_finish(0)
        got(spgot, spx_r)
        cross_c, pred_c = [jnp.sum(spacc[i] + spgot[i], axis=1, keepdims=True) for i in range(2)]
        obs_c = keep["obs_c"]
        root_c = jnp.sqrt(pred_c * obs_c)
        keep["cos"] = cross_c / root_c
        keep["obs"] = (1.0 / root_c) / total_spots
        keep["prd"] = (cross_c / (pred_c * root_c)) / total_spots

    def grad_make(q):
        scale = 1.0 / (SLIDES * total_genes)
        for e in range(units):
            g, o = divmod(q * units + e, 4)
            sums = st3[g, o]
            cross, prd, obs = sums[:8], sums[8:16], sums[16:24]
            root = jnp.sqrt(prd * obs)
            for i, v in enumerate((scale / root, scale * cross / (prd * root))):
                high = v.astype(b16).astype(f32)
                mid = (v - high).astype(b16).astype(f32)
                low = v - high - mid
                stack = jnp.concatenate([high, mid, low, jnp.zeros((8, 128), f32)], axis=0)
                coef[:32, (i * units + e) * 128 : (i * units + e) * 128 + 128] = stack.astype(b16)
        each_spot = jnp.dot(hot_stand[...], coef[...], preferred_element_type=f32)
        at = slice(q * WIDTH, q * WIDTH + WIDTH)
        value = pred_h[:, at] * (each_spot[:, WIDTH:] + keep["prd"]) - spot_h[:, at] * (each_spot[:, :WIDTH] + keep["obs"])
        value = value.astype(b16)
        grad[0, j, :, at] = value[:128]
        grad[1, j, :, at] = value[128:]

    def gene_cos():
        total = jnp.zeros((8, 128), f32)
        for g in range(2):
            for e in range(4):
                sums = st3[g, e]
                total = total + sums[:8] / jnp.sqrt(sums[8:16] * sums[16:24])
        return jnp.sum(jnp.sum(total, axis=0, keepdims=True), axis=1, keepdims=True)

    def grad_send(q):
        grad_make(q)
        at = grad.at[:, j, :, at_chunk(q)]
        rc(at, at, g_s.at[0], g_r.at[q, 0], dev_x).start()
        rc(at, at, g_s.at[1], g_r.at[q, 1], dev_y).start()

    def grad_direct(q):
        grad_make(q)
        at = grad.at[:, j, :, at_chunk(q)]
        rc(at, at, g_s.at[4], g_r.at[q, 2], dev(z, jd, k)).start()
        rc(at, at, g_s.at[0], g_r.at[q, 0], dev_x).start()
        rc(at, at, g_s.at[1], g_r.at[q, 1], dev_y).start()

    def grad_pass(q, i):
        owner, to = ((jx, dev_y), (jy, dev_x))[i]
        got(grad.at[:, owner, :, at_chunk(q)], g_r.at[q, i])
        at = grad.at[i, owner, :, at_chunk(q)]
        rc(at, at, g_s.at[2 + i], g_r.at[q, 2], to).start()

    def run_up(q, b):
        return rc(pass_on.at[q, b], sums_up.at[q, b], rs_s, rs_r.at[q, b], dev_up)

    def run_dn(q, b):
        return rc(pass_on.at[q, b], sums_dn.at[q, b], rs_s, rs_r.at[q, b], dev_dn)

    def block(q, b):
        return part[q, b // 2, pl.ds(2 * (b % 2), 2)].reshape(256, WIDTH)

    def run_last(q, b, up):
        i = 0 if up else 1
        to, cross = (dev_up, cross_up) if up else (dev_dn, cross_dn)
        rc(pass_on.at[q, b, rows(k, 128)], fin.at[q, i, k], rs_s, fin_r.at[q], to).start()
        rc(pass_on.at[q, b, rows(mate, 128)], fin.at[q, i, k], rs_s, fin_r.at[q], cross).start()

    def sums_half(q, h):
        whole = jnp.dot(
            plane_turn[rows(h, 512), :], grad[:, :, :, at_chunk(q)].reshape(1024, WIDTH), preferred_element_type=f32
        )
        part[q, h] = whole.reshape(4, 128, WIDTH)

    def sums_give(q, b):
        pass_on[q, b] = block(q, b).astype(b16)

    def grad_wait(q):
        if DIRECT == q:
            got(grad.at[:, jx, :, at_chunk(q)], g_r.at[q, 0])
            got(grad.at[:, jy, :, at_chunk(q)], g_r.at[q, 1])
        got(grad.at[:, jd, :, at_chunk(q)], g_r.at[q, 2])

    def sums_first(q, count):
        if count == 2:
            product(q, plane_turn, count)
        for step in range(2):
            if count == 1:
                sums_half(q, jnp.where(z < 2, 1 - step, step))

            @pl.when(z == 0)
            def _():
                for i in range(count):
                    for b in ((3, 2), (1,))[step]:
                        sums_give(q + i, b)
                        run_last(q + i, b, True) if b == 1 else run_up(q + i, b).start()

            @pl.when(z == 3)
            def _():
                for i in range(count):
                    for b in ((0, 1), (2,))[step]:
                        sums_give(q + i, b)
                        run_last(q + i, b, False) if b == 2 else run_dn(q + i, b).start()

    def pass_add(q, b, slots):
        got(slots.at[q, b], rs_r.at[q, b])
        pass_on[q, b] = (block(q, b) + slots[q, b].astype(f32)).astype(b16)

    def pass_far(q):
        @pl.when(z == 1)
        def _():
            pass_add(q, 3, sums_up)
            run_up(q, 3).start()

        @pl.when(z == 2)
        def _():
            pass_add(q, 0, sums_dn)
            run_dn(q, 0).start()

    def pass_middle(q):
        @pl.when(z == 1)
        def _():
            pass_add(q, 2, sums_up)
            run_last(q, 2, True)

        @pl.when(z == 2)
        def _():
            pass_add(q, 1, sums_dn)
            run_last(q, 1, False)

    def pass_near(q):
        @pl.when(z == 1)
        def _():
            pass_add(q, 0, sums_dn)
            run_last(q, 0, False)

        @pl.when(z == 2)
        def _():
            pass_add(q, 3, sums_up)
            run_last(q, 3, True)

    def other_give(q):
        return rc(other.at[q], other_got.at[q], oth_s, oth_r.at[q], dev_mate)

    def use_sums(q, kk, sums):
        at = lanes(kk, q)
        expr_out[:, at] = keep_col * sums
        weighed = cell_v[:, at].astype(f32) * sums
        for e in range(units):
            filt_acc[...] = filt_acc[...] + weighed[:, e * 128 : e * 128 + 128]

    def sums_other(q):
        other[q] = part[q, lax.div(z, 2), 2 * lax.rem(z, 2) + mate]
        other_give(q).start()

    def sums_last(q):
        @pl.when(z == 0)
        def _():
            got(fin.at[q, 1], fin_r.at[q])

        @pl.when(z == 3)
        def _():
            got(fin.at[q, 0], fin_r.at[q])

        @pl.when((z > 0) & (z < 3))
        def _():
            got(fin.at[q], fin_r.at[q])

        got(other_got.at[q], oth_r.at[q])
        own_at = (q, lax.div(z, 2), 2 * lax.rem(z, 2) + k)
        for kk, base in ((k, part[own_at]), (mate, other_got[q])):
            up = jnp.where(z > 0, fin[q, 0, kk].astype(f32), 0.0)
            dn = jnp.where(z < 3, fin[q, 1, kk].astype(f32), 0.0)
            use_sums(q, kk, base + (up + dn))

    def back_dot(b):
        @pl.loop(0, 2)
        def _(h):
            back[b, h] = lax.dot_general(
                grad[h].reshape(512, half), col[b], (((1,), (1,)), ((), ())), preferred_element_type=f32
            ).reshape(4, 128, 256)

        rc(back.at[b, mate], back_got.at[b], back_s, back_r.at[b], dev_mate).start()

    def back_add(b):
        got(back_got.at[b], back_r.at[b])
        for jj in range(4):
            back_low[jj, :, rows(b, 256)] = (back[b, k, jj] + back_got[b, jj]).astype(b16)

    def ret_send(b):
        at = rows(b, 256)
        for jj in (jd, jx, jy):
            rc(back_low.at[jj, :, at], back_ret.at[j, :, at], ret_s, ret_r, dev(z, jj, k)).start()
        back_ret[j, :, at] = back_low[j, :, at]

    loss_lane = lax.broadcasted_iota(jnp.int32, (1, 128), 1)

    def loss_mate():
        own_cos = jnp.sum(keep["cos"], axis=0, keepdims=True)
        l_src[...] = jnp.where(loss_lane == 0, own_cos, jnp.where(loss_lane == 1, gene_cos(), 0.0))
        hand_over(l_src, l_mate, 7)
        l_plane[j] = l_src[...]
        spread(lambda o: l_src, l_plane, "plane", 8)

    def loss_line():
        got(l_plane.at[pl.ds(0, 3)], sm_r.at[8])
        total = l_plane[0] + l_plane[1] + l_plane[2] + l_plane[3]
        l_line_src[...] = total
        l_line[z] = total
        spread(lambda o: l_line_src, l_line, "line", 9)

    def loss_end():
        got(l_line.at[pl.ds(0, 3)], sm_r.at[9])
        got(l_mate, sm_r.at[7])
        cos_row = l_line[0] + l_line[1] + l_line[2] + l_line[3]
        gene_row = l_src[...] + l_mate[...]
        cos_total = jnp.sum(jnp.where(loss_lane == 0, cos_row, 0.0), axis=1, keepdims=True)
        gene_total = jnp.sum(jnp.where(loss_lane == 1, gene_row, 0.0), axis=1, keepdims=True)
        gene_loss = 1.0 - gene_total / (SLIDES * total_genes)
        spot_loss = 1.0 - cos_total / total_spots
        kl_loss = keep["kl"]
        total_loss = gene_loss + spot_loss + kl_loss
        picked = jnp.where(loss_lane == 2, spot_loss, jnp.where(loss_lane == 3, kl_loss, 0.0))
        loss_out[...] = jnp.where(loss_lane == 0, total_loss, jnp.where(loss_lane == 1, gene_loss, picked))

    def map_rows(g):
        at = rows(g, 16)
        pick = lax.broadcasted_iota(jnp.int32, (16, 128), 0) + g * 16
        here = lax.broadcasted_iota(jnp.int32, (16, 128), 1)
        mg = jnp.sum(jnp.where(pick == here, jnp.broadcast_to(mass_row[...], (16, 128)), 0.0), 1, keepdims=True)
        inner = jnp.zeros((16, 128), f32)
        for d in range(32):
            b, jj, kk = d // 8, (d % 8) // 2, d % 2
            used = back_ret[jj, at, b * 256 + kk * 128 : b * 256 + kk * 128 + 128].astype(f32) + mg * keep_all[jj, kk, b]
            inner = inner + chance[at, d * 128 : d * 128 + 128] * used
            map_out[at, d * 128 : d * 128 + 128] = used
        inner = jnp.sum(inner, axis=1, keepdims=True)
        map_out[at, :] = chance[at, :] * (map_out[at, :] - inner)

    def map_some(i):
        if i == 0:
            got(back_ret.at[pl.ds(0, 3)], ret_r)
            mass_row[...] = lie(keep["grad"])
        pl.loop(2 * i, 2 * i + 2)(map_rows)

    steps = {
        "x": softmax_some, "H": scale_more, "F": lambda i: filt_line(), "N": far_ready, "Y": pred_move, "w": low_give, "v": lambda i: low_own(),
        "c": col_own, "h": lambda i: hop(), "i": lambda i: (filt_pair, filt_plane, mass_make, mass_chip)[i](),
        "a": low_arrive, "q": turn, "p": lambda q: product(q, plane_low, 1), "P": lambda q: product(q, plane_low, 2),
        "f": reduce_first, "s": lambda q: reduce_second(q, 0), "S": lambda q: reduce_second(q, 1),
        "l": reduce_last, "k": reduce_stat, "j": reduce_slides, "B": lambda i: (obs_sums, obs_end)[i](), "t": lambda i: st_send(0, i), "z": lambda i: (spot_half, mass_end, spot_sums)[i](),
        "g": grad_send, "G": grad_direct, "m": lambda q: grad_pass(q, 0), "n": lambda q: grad_pass(q, 1),
        "y": lambda i: st_send(1, i) if i < 3 else st_finish(1), "r": lambda q: sums_first(q, 1), "R": lambda q: sums_first(q, 2),
        "U": pass_far, "V": pass_middle, "D": pass_near,
        "L": sums_last, "O": sums_other, "b": back_dot, "A": back_add, "T": ret_send, "W": grad_wait, "M": map_some,
        "e": lambda i: (reach_make, reach_plane, reach_line)[i](), "o": lambda i: (loss_mate, loss_line, loss_end)[i](),
    }
    for group in ORDER:
        for word in group.split():
            steps[word[0]](int(word[1:]) if len(word) > 1 else 0)

    got(r_line.at[pl.ds(0, 3)], sm_r.at[6])
    reach_row = r_line[0] + r_line[1] + r_line[2] + r_line[3]
    filt_sum = jnp.sum(filt_acc[...], axis=1, keepdims=True)
    keep_row = jax.nn.sigmoid(filt_in[...].astype(f32))
    filt_out[...] = keep_row * (1.0 - keep_row) * (lie(filt_sum) + reach_row)

    sent(hand, hand_s)
    spot_give.wait_send()
    sent(send1, send1_s)
    sent(send2, send2_s)
    sent(pred_h.at[rows(mate, 128)], pred_s)
    got(pred_out.at[:, pl.ds(pl.multiple_of(mate * half, half), half)], pred_r)
    pltpu.make_async_copy(
        pred_h.at[rows(k, 128)], pred_out.at[:, pl.ds(pl.multiple_of(k * half, half), half)], own_sem
    ).wait()
    for i in range(2):
        sent(grad.at[:, j], g_s.at[i])
    others = [q for q in range(chunks) if q != DIRECT]
    sent(grad.at[0, jx, :, pl.ds(0, len(others) * WIDTH)], g_s.at[2])
    sent(grad.at[1, jy, :, pl.ds(0, len(others) * WIDTH)], g_s.at[3])
    if DIRECT is not None:
        sent(grad.at[:, j, :, at_chunk(DIRECT)], g_s.at[4])
    sent(ob_acc, ob_s)
    for i in range(3):
        @pl.when(z == i)
        def _():
            sent(col.at[pl.ds(0, i + 1)], up_s)

        @pl.when(z == 3 - i)
        def _():
            sent(col.at[pl.ds(3 - i, i + 1)], dn_s)
    sent(pass_on.at[:, pl.ds(0, 3)], rs_s)
    sent(plane_low.at[k, pl.ds(0, 3)], low_s.at[0])
    sent(plane_low.at[k], low_s.at[1])
    for g in range(2):
        for i in range(3):
            sent(st1.at[g, pl.ds(0, 3)], st_s.at[g, i])
    spx.wait_send()
    sent(back_got, back_s)
    sent(back_low.at[pl.ds(0, 3)], ret_s)
    sent(other, oth_s)
    for i, ref in enumerate((
        f_line.at[pl.ds(0, 3)], f_line, f_all.at[pl.ds(0, 3)], m_src, r_mate, r_plane.at[pl.ds(0, 3)],
        r_line.at[pl.ds(0, 3)], l_mate, l_plane.at[pl.ds(0, 3)], l_line.at[pl.ds(0, 3)],
    )):
        sent(ref, sm_s.at[i])


def hand_out(pred_in, map_in, expr_in, filt_in, loss_in, pred_out, map_out, expr_out, filt_out, loss_out, sems):
    pairs = ((map_in, map_out), (pred_in, pred_out), (expr_in, expr_out))
    copies = [pltpu.make_async_copy(src, dst, sems.at[i]) for i, (src, dst) in enumerate(pairs)]
    for copy in copies:
        copy.start()
    filt_out[...] = filt_in[...]
    loss_out[...] = loss_in[:, :4]
    for copy in copies:
        copy.wait()


def fused_shards(map_logits, filter_logits, cell_expr, spot_expr, cell_slide, spot_slide, density_bins):
    f32, b16 = jnp.float32, jnp.bfloat16
    spots, cells = map_logits.shape
    genes = cell_expr.shape[1]
    n = genes // (2 * WIDTH)
    V, S = pltpu.VMEM, pltpu.SemaphoreType.DMA
    any_, vmem = pl.BlockSpec(memory_space=pl.ANY), pl.BlockSpec(memory_space=pltpu.VMEM)
    one = S(())
    scratch = [
        V((128, cells), f32),
        V((4, 128, 1024), b16),
        V((2, 4, 128, 1024), b16),
        V((1024, 1024), b16),
        V((128, genes), b16),
        V((n, 128, WIDTH), b16),
        V((4, 256, genes // 2), b16),
        V((n, 2, 4, 128, WIDTH), f32),
        V((n, 4, 128, WIDTH), b16),
        V((n, 2, 128, WIDTH), b16),
        V((n, 2, 128, WIDTH), b16),
        V((n, 4, 128, WIDTH), b16),
        V((256, genes // 2), f32),
        V((256, genes // 2), f32),
        V((2, 4, 32, 128), f32),
        V((2, 2, 32, 128), f32),
        V((2, 4, 32, 128), f32),
        V((2, 4, 32, 128), f32),
        V((2, 4, 32, 128), f32),
        V((2, 256, 128), f32),
        V((2, 256, 128), f32),
        V((256, 128), f32),
        V((256, 128), f32),
        V((128, 2 * WIDTH), b16),
        V((2, 4, 128, genes // 2), b16),
        V((n, 4, 256, WIDTH), b16),
        V((n, 4, 256, WIDTH), b16),
        V((n, 4, 256, WIDTH), b16),
        V((n, 2, 2, 128, WIDTH), b16),
        V((4, 2, 4, 128, 256), f32),
        V((4, 4, 128, 256), f32),
        V((4, 128, 1024), b16),
        V((4, 128, 1024), b16),
        V((n, 128, WIDTH), f32),
        V((n, 128, WIDTH), f32),
        V((4, 1, 128), f32),
        V((2, 4, 1, 128), f32),
        V((4, 2, 4, 1, 128), f32),
        V((4, 2, 4, 1, 128), f32),
        V((2, 1, 128), f32),
        V((2, 1, 128), f32),
        V((2, 4, 4, 1, 128), f32),
        V((4, 4, 1, 128), f32),
        V((4, 4, 1, 128), f32),
        V((4, 4, 1, 128), f32),
        V((4, 1, 128), f32),
        V((4, 1, 128), f32),
        V((1, 128), f32),
        V((1, 128), f32),
        V((4, 1, 128), f32),
        V((1, 128), f32),
        V((4, 1, 128), f32),
        V((128, 128), f32),
        V((8, 256), f32),
        V((256, 128), b16),
        V((1, 128), f32),
        S((3,)), one, one, one, one, one, S((n, 4)), S((2,)), S((5,)),
        one, one, S((n, 2)), S((n,)),
        one, one, one, one, S((2, 3)), S((2, 3)), one, one, one, one,
        S((5,)), S((n, 3)), one, S((n, 4)), S((n,)), one, S((4,)),
        one, one, one, S((n,)), S((10,)), S((10,)), pltpu.SemaphoreType.REGULAR,
    ]
    predicted, map_grad, expr_grad, filt, loss = pl.pallas_call(
        functools.partial(fused_kernel, float(spots * 32), float(genes)),
        out_shape=(
            pltpu.VMEM((spots, genes), f32),
            pltpu.VMEM((spots, cells), f32),
            pltpu.VMEM((spots, genes), f32),
            V((1, 128), f32),
            V((1, 128), f32),
        ),
        in_specs=[any_, vmem, any_, any_, vmem, vmem, vmem],
        out_specs=(vmem, vmem, vmem, vmem, vmem),
        scratch_shapes=scratch,
        compiler_params=pltpu.CompilerParams(
            collective_id=0, has_side_effects=True, vmem_limit_bytes=58 * 2**20
        ),
        name="mapping_step",
    )(
        map_logits,
        filter_logits.reshape(1, 128),
        cell_expr,
        spot_expr,
        cell_slide.reshape(1, cells),
        spot_slide.reshape(1, 128),
        density_bins.reshape(1, 128),
    )
    predicted, map_grad, expr_grad, filt, loss = pl.pallas_call(
        hand_out,
        out_shape=(
            jax.ShapeDtypeStruct((spots, genes), f32),
            jax.ShapeDtypeStruct((spots, cells), f32),
            jax.ShapeDtypeStruct((spots, genes), f32),
            jax.ShapeDtypeStruct((1, 128), f32),
            jax.ShapeDtypeStruct((1, 4), f32),
        ),
        in_specs=[vmem] * 5,
        out_specs=(any_, any_, any_, vmem, vmem),
        scratch_shapes=[S((3,))],
        compiler_params=pltpu.CompilerParams(vmem_limit_bytes=2**20),
        name="hand_out",
    )(*[pltpu.with_memory_space_constraint(v, pltpu.VMEM) for v in (predicted, map_grad, expr_grad, filt, loss)])
    return loss.reshape(4), predicted, map_grad, expr_grad, filt.reshape(128)


def solution(mesh):
    both = P(("row", "col"))
    rows = P(("row", "col"), None)
    in_specs = (rows, both, rows, rows, P(), both, both)
    out_specs = (P(), rows, rows, rows, both)
    step = fused_shards if (mesh.shape["row"], mesh.shape["col"]) == (4, 8) else shards
    return jax.shard_map(step, mesh=mesh, in_specs=in_specs, out_specs=out_specs, check_vma=False)
```

```python
import functools

import jax
import jax.numpy as jnp
from jax import lax
from jax.experimental import pallas as pl
from jax.experimental.pallas import tpu as pltpu
from jax.sharding import PartitionSpec as P

SLIDES = 8
ROWS, PLANE, CORES = 4, 4, 2
WIDTH = 128
MESH = pl.DeviceIdType.MESH
DIRECT = 0
ORDER = (
    "c0 N0 H0 H1",
    "x0 w0 c1 N1",
    "F0 H2 c2 H3",
    "H4 x1 w1 H5",
    "h H6 c3 c4",
    "x2 i0 x3 i1",
    "H7 w3 h h",
    "h w2 c5 i2",
    "v0 h h h",
    "i3 B0 a2 a0",
    "a1 h h h",
    "c6 a3 P0 f0",
    "f1 h h h",
    "P2 f2 s0 q1",
    "f3 S1 h h",
    "h c7 s2 s1",
    "S0 p4 S2 s3",
    "f4 S3 h h",
    "h p5 f5 l1",
    "l0 l2 j0 j2",
    "j1 s4 h h",
    "h l3 j3 t0",
    "s5 S4 p6 f6",
    "k0 k2 k1 S5",
    "h h p7 t1",
    "f7 s6 Y2 k3",
    "l4 j4 S6 l5",
    "k5 B1 s7 S7",
    "t2 q0 j5 l6",
    "k6 k4 l7 k7",
    "z0 q3 j6 j7",
    "y0 z2 G0 Y3",
    "q2 g2 g1 y1",
    "W0 r0 m2 n2",
    "z1 y2 Y7 g3",
    "m1 n1 W2 r2",
    "y3 g7 U0 e0",
    "Y0 m3 n3 g4",
    "g6 W1 r1 g5",
    "U2 m7 o0 m4",
    "W3 V0 n7 V2",
    "n4 r3 m6 n6",
    "n5 D2 m5 O1",
    "V1 W7 r7 U1",
    "W6 r6 D0 W4",
    "O2 W5 b2 O6",
    "b0 O0 b1 Y5",
    "A2 T2 U3 U7",
    "e1 A0 T0 V7",
    "A1 o1 R4 O5",
    "V3 T1 Y6 Y1",
    "Y4 L0 b3 U6",
    "O3 D1 e2 V6",
    "O7 D7 A3 T3",
    "U4 D3 L2 L7",
    "O4 D6 o2 L1",
    "U5 V4 L3 L6",
    "V5 D4 M0 D5",
    "M1 M2 L4 M3",
    "L5",
)


def shards(map_logits, filter_logits, cell_expr, spot_expr, cell_slide, spot_slide, density_bins):
    highest = lax.Precision.HIGHEST
    both = ("row", "col")
    rows_count = lax.axis_size("row")
    cols_count = lax.axis_size("col")
    spot_dev, cell_total = map_logits.shape
    cell_dev = filter_logits.shape[0]
    spot_total = spot_dev * rows_count * cols_count
    gene_count = cell_expr.shape[1]
    keep_rate = jax.nn.sigmoid(filter_logits.astype(jnp.float32))
    scaled = (keep_rate[:, None] * cell_expr.astype(jnp.float32)).astype(jnp.bfloat16)
    scaled_col = lax.all_gather(scaled, "row", axis=0, tiled=True)
    allowed = spot_slide[:, None] == cell_slide[None, :]
    shifted = jnp.where(allowed, map_logits, -1e30)
    row_peak = jnp.max(shifted, axis=1, keepdims=True)
    raised = jnp.exp(shifted - row_peak)
    chances = raised / jnp.sum(raised, axis=1, keepdims=True)
    chance_low = chances.astype(jnp.bfloat16)
    by_col = chance_low.reshape(spot_dev, rows_count, cols_count, cell_dev)
    mapped = lax.all_to_all(by_col, "col", split_axis=2, concat_axis=0, tiled=True)
    mapped = mapped.reshape(spot_dev * cols_count, rows_count * cell_dev)
    keep_col = lax.all_gather(keep_rate, "row", axis=0, tiled=True)
    part_pred = jnp.dot(mapped, scaled_col, preferred_element_type=jnp.float32)
    part_mass = jnp.dot(mapped, keep_col, precision=highest, preferred_element_type=jnp.float32)
    predicted = lax.psum_scatter(part_pred, "col", scatter_dimension=0, tiled=True)
    mass = lax.psum_scatter(part_mass, "col", scatter_dimension=0, tiled=True)
    onehot = (spot_slide[:, None] == jnp.arange(SLIDES, dtype=jnp.int32)[None, :]).astype(
        jnp.float32
    )
    cross_term = predicted * spot_expr
    pred_sq = predicted * predicted
    obs_sq = spot_expr * spot_expr
    spot_cross = jnp.sum(cross_term, axis=1)
    spot_pred = jnp.sum(pred_sq, axis=1)
    spot_root = jnp.sqrt(spot_pred * jnp.sum(obs_sq, axis=1))
    spot_cos = spot_cross / spot_root
    bin_values = density_bins.astype(jnp.float32)
    log_term = bin_values * (jnp.log(bin_values) - jnp.log(mass))
    all_cross, all_pred, all_obs, slide_mass, slide_bins, slide_log, cos_total = lax.psum(
        (
            jnp.dot(onehot.T, cross_term, precision=highest),
            jnp.dot(onehot.T, pred_sq, precision=highest),
            jnp.dot(onehot.T, obs_sq, precision=highest),
            jnp.dot(onehot.T, mass, precision=highest),
            jnp.dot(onehot.T, bin_values, precision=highest),
            jnp.dot(onehot.T, log_term, precision=highest),
            jnp.sum(spot_cos),
        ),
        both,
    )
    gene_root = jnp.sqrt(all_pred * all_obs)
    gene_loss = 1.0 - jnp.mean(all_cross / gene_root)
    spot_loss = 1.0 - cos_total / spot_total
    kl_loss = jnp.mean(slide_log / slide_bins - jnp.log(slide_bins) + jnp.log(slide_mass))
    total_loss = gene_loss + spot_loss + kl_loss
    losses = jnp.stack([total_loss, gene_loss, spot_loss, kl_loss])
    gene_scale = 1.0 / (SLIDES * gene_count)
    coef_obs = jnp.dot(onehot, 1.0 / gene_root, precision=highest)
    coef_pred = jnp.dot(onehot, all_cross / (all_pred * gene_root), precision=highest)
    pred_grad = -gene_scale * (spot_expr * coef_obs - predicted * coef_pred)
    pred_grad = (
        pred_grad
        - (
            spot_expr / spot_root[:, None]
            - predicted * (spot_cross / (spot_pred * spot_root))[:, None]
        )
        / spot_total
    )
    mass_each = jnp.dot(onehot, slide_mass, precision=highest)
    bins_each = jnp.dot(onehot, slide_bins, precision=highest)
    mass_grad = (1.0 / mass_each - bin_values / (bins_each * mass)) / SLIDES
    grad_low = pred_grad.astype(jnp.bfloat16)
    mass_low = mass_grad.astype(jnp.bfloat16)
    grad_block = lax.all_gather(grad_low, "col", axis=0, tiled=True)
    mass_block = lax.all_gather(mass_low, "col", axis=0, tiled=True)
    back_map = lax.dot_general(
        grad_block, scaled_col, (((1,), (1,)), ((), ())), preferred_element_type=jnp.float32
    )
    back_map = back_map + mass_block.astype(jnp.float32)[:, None] * keep_col[None, :]
    back_low = back_map.astype(jnp.bfloat16)
    returned = lax.all_to_all(
        back_low.reshape(spot_dev * cols_count, rows_count, 1, cell_dev),
        "col",
        split_axis=0,
        concat_axis=2,
        tiled=True,
    ).reshape(spot_dev, cell_total)
    expr_part = lax.dot_general(
        mapped, grad_block, (((0,), (0,)), ((), ())), preferred_element_type=jnp.float32
    )
    mass_reach = lax.dot_general(
        mapped, mass_block, (((0,), (0,)), ((), ())), preferred_element_type=jnp.float32
    )
    expr_sum = lax.psum_scatter(expr_part, "row", scatter_dimension=0, tiled=True)
    mass_sum = lax.psum_scatter(mass_reach, "row", scatter_dimension=0, tiled=True)
    filter_grad = (
        keep_rate
        * (1.0 - keep_rate)
        * (jnp.sum(cell_expr.astype(jnp.float32) * expr_sum, axis=1) + mass_sum)
    )
    expr_grad = keep_rate[:, None] * expr_sum
    chance_grad = returned.astype(jnp.float32)
    inner_sum = jnp.sum(chances * chance_grad, axis=1, keepdims=True)
    map_grad = chances * (chance_grad - inner_sum)
    return (losses, predicted, map_grad, expr_grad, filter_grad)


def fused_kernel(
    total_spots, total_genes,
    logit_in, filt_hbm, cell_in, spot_in, cslide_hbm, sslide_hbm, bins_hbm,
    pred_out, map_out, expr_out, filt_out, loss_out,
    chance, own_low, plane_low, plane_turn, cell_v, hand, col, part, send1, early, send2, late,
    pred_h, spot_h, stat, st_sum, st1, st2, st3, spacc, spgot, ob_acc, ob_got, coef, grad,
    sums_up, sums_dn, pass_on, fin, back, back_got, back_low, back_ret, other, other_got,
    f_line, f_pair, f_all, keep_all, m_src, m_got, r_src, r_mate, r_plane_src, r_plane, r_line_src, r_line,
    l_src, l_mate, l_plane, l_line_src, l_line, filt_acc, hot_lie, hot_stand, mass_row, filt_in, cslide_in, sslide_in, bins_in,
    load_sem, own_sem, hand_s, hand_r, up_s, dn_s, col_r, low_s, low_r, send1_s, send2_s, early_r, late_r,
    pred_s, pred_r, spot_s, spot_r, st_s, st_r, spx_s, spx_r, ob_s, ob_r, g_s, g_r, rs_s, rs_r, fin_r, back_s, back_r,
    ret_s, ret_r, oth_s, oth_r, sm_s, sm_r, ready,
):
    f32, b16 = jnp.float32, jnp.bfloat16
    half = col.shape[2]
    chunks = half // WIDTH
    units = WIDTH // 128
    keep = {}
    z = lax.axis_index("row")
    c = lax.axis_index("col")
    j = lax.div(c, 2)
    k = lax.rem(c, 2)
    y = lax.div(j, 2)
    x = lax.rem(j, 2)
    mate = 1 - k

    def dev(zz, jj, kk):
        return (zz, jj * 2 + kk)

    jx = y * 2 + (1 - x)
    jy = (1 - y) * 2 + x
    jd = (1 - y) * 2 + (1 - x)
    dev_mate = dev(z, j, mate)
    dev_x = dev(z, jx, k)
    dev_y = dev(z, jy, k)
    dev_up = dev(lax.rem(z + 1, 4), j, k)
    dev_dn = dev(lax.rem(z + 3, 4), j, k)
    cross_up = dev(lax.rem(z + 1, 4), j, mate)
    cross_dn = dev(lax.rem(z + 3, 4), j, mate)
    plane_others = (jx, jy, jd)
    line_others = [lax.rem(z + i, 4) for i in (1, 2, 3)]

    def rc(src, dst, ss, rs, to):
        return pltpu.make_async_remote_copy(
            src_ref=src, dst_ref=dst, send_sem=ss, recv_sem=rs, device_id=to, device_id_type=MESH
        )

    def got(ref, sem):
        rc(ref, ref, sem, sem, dev_mate).wait_recv()

    def sent(ref, sem):
        rc(ref, ref, sem, sem, dev_mate).wait_send()

    def rows(i, size):
        return pl.ds(pl.multiple_of(i * size, size), size)

    def at_chunk(q):
        return pl.ds(q * WIDTH, WIDTH)

    def lanes(kk, q):
        return pl.ds(pl.multiple_of(kk * half + q * WIDTH, WIDTH), WIDTH)

    load_cell = pltpu.make_async_copy(cell_in, cell_v, load_sem.at[0])
    load_logit = pltpu.make_async_copy(logit_in, chance, load_sem.at[1])
    load_spot = pltpu.make_async_copy(
        spot_in.at[:, pl.ds(pl.multiple_of(k * half, half), half)], spot_h.at[rows(k, 128)], load_sem.at[2]
    )
    small_loads = [
        pltpu.make_async_copy(src, dst, load_sem.at[3 + i])
        for i, (src, dst) in enumerate((
            (filt_hbm, filt_in), (sslide_hbm, sslide_in), (bins_hbm, bins_in), (cslide_hbm, cslide_in),
        ))
    ]
    barrier = pltpu.get_barrier_semaphore()
    for to in (dev_mate, dev_x, dev_y, dev(z, jd, k)):
        pl.semaphore_signal(barrier, inc=1, device_id=to, device_id_type=MESH)
    for i, near in enumerate(((dev_up, cross_up), (dev_dn, cross_dn))):
        @pl.when((z < 3) if i == 0 else (z > 0))
        def _():
            for to in near:
                pl.semaphore_signal(barrier, inc=1, device_id=to, device_id_type=MESH)
    small_loads[0].start()
    load_cell.start()
    for load in small_loads[1:]:
        load.start()
    load_logit.start()
    load_spot.start()

    eye = lax.broadcasted_iota(jnp.int32, (128, 128), 0) == lax.broadcasted_iota(
        jnp.int32, (128, 128), 1
    )
    lane = lax.broadcasted_iota(jnp.int32, (128, 128), 1)

    def stand(row):
        return jnp.sum(jnp.where(eye, jnp.broadcast_to(row, (128, 128)), 0.0), 1, keepdims=True)

    def lie(column):
        return jnp.sum(jnp.where(eye, jnp.broadcast_to(column, (128, 128)), 0.0), 0, keepdims=True)

    for load in small_loads[:3]:
        load.wait()
    filt_row = filt_in[...].astype(f32)
    keep_col = stand(jax.nn.sigmoid(filt_row))
    slide_col = stand(sslide_in[...].astype(f32))
    bins_col = stand(bins_in[...].astype(f32))

    def hand_copy(q):
        return rc(hand.at[q], col.at[z, rows(k, 128), at_chunk(q)], hand_s, hand_r, dev_mate)

    def col_up(q, b):
        at = col.at[b, :, at_chunk(q)]
        return rc(at, at, up_s, col_r.at[q, b], dev_up)

    def col_dn(q, b):
        at = col.at[b, :, at_chunk(q)]
        return rc(at, at, dn_s, col_r.at[q, b], dev_dn)

    def scale_cells(q):
        hand[q] = (keep_col * cell_v[:, lanes(mate, q)].astype(f32)).astype(b16)
        col[z, rows(k, 128), at_chunk(q)] = (keep_col * cell_v[:, lanes(k, q)].astype(f32)).astype(b16)

    def col_own(q):
        own = col.at[z, rows(k, 128), at_chunk(q)]

        @pl.when(z < 3)
        def _():
            rc(own, own, up_s, col_r.at[q, z], dev_up).start()
            rc(hand.at[q], own, up_s, col_r.at[q, z], cross_up).start()

        @pl.when(z > 0)
        def _():
            rc(own, own, dn_s, col_r.at[q, z], dev_dn).start()
            rc(hand.at[q], own, dn_s, col_r.at[q, z], cross_dn).start()

    hops = [(q, s) for q in range(chunks) for s in range(3)]

    def hop():
        q, s = hops.pop(0)

        @pl.when(z - 1 - s >= 0)
        def _():
            b = z - 1 - s
            got(col.at[b, :, at_chunk(q)], col_r.at[q, b])

            @pl.when(z < 3)
            def _():
                col_up(q, b).start()

        @pl.when(z + 1 + s <= 3)
        def _():
            b = z + 1 + s
            got(col.at[b, :, at_chunk(q)], col_r.at[q, b])

            @pl.when(z > 0)
            def _():
                col_dn(q, b).start()

    load_cell.wait()
    scale_cells(0)
    pl.semaphore_wait(barrier, jnp.where((z == 0) | (z == 3), 6, 8))

    def far_ready(i):
        if i == 0:
            @pl.when(z == 1)
            def _():
                pl.semaphore_signal(ready, inc=1, device_id=dev_up, device_id_type=MESH)

            @pl.when(z == 2)
            def _():
                pl.semaphore_signal(ready, inc=1, device_id=dev_dn, device_id_type=MESH)
        else:
            pl.semaphore_wait(ready, 1)

            @pl.when(z == 1)
            def _():
                pl.semaphore_signal(ready, inc=1, device_id=dev_dn, device_id_type=MESH)

            @pl.when(z == 2)
            def _():
                pl.semaphore_signal(ready, inc=1, device_id=dev_up, device_id_type=MESH)


    def scale_more(q):
        if q:
            scale_cells(q)
        hand_copy(q).start()

    def spread(source, slots, which, i):
        for o in plane_others if which == "plane" else line_others:
            to = dev(z, o, k) if which == "plane" else dev(o, j, k)
            rc(source(o), slots.at[j if which == "plane" else z], sm_s.at[i], sm_r.at[i], to).start()

    def hand_over(source, slot, i):
        rc(source, slot, sm_s.at[i], sm_r.at[i], dev_mate).start()

    def filt_line():
        f_line[z] = filt_row
        spread(lambda o: f_line.at[z], f_line, "line", 0)

    def softmax_some(i):
        if not keep.get("logits"):
            small_loads[3].wait()
            load_logit.wait()
            keep["logits"] = True
        pl.loop(2 * i, 2 * i + 2)(softmax_rows)

    def softmax_rows(g):
        at = rows(g, 16)
        logits = chance[at, :]
        pick = lax.broadcasted_iota(jnp.int32, (16, 128), 0) + g * 16
        here = lax.broadcasted_iota(jnp.int32, (16, 128), 1)
        slide = jnp.sum(
            jnp.where(pick == here, jnp.broadcast_to(sslide_in[...].astype(f32), (16, 128)), 0.0),
            1, keepdims=True,
        )
        allowed = slide == cslide_in[...].astype(f32)
        shifted = jnp.where(allowed, logits, -1e30)
        raised = jnp.exp(shifted - jnp.max(shifted, axis=1, keepdims=True))
        value = raised / jnp.sum(raised, axis=1, keepdims=True)
        chance[at, :] = value
        low = value.astype(b16)
        for b in range(4):
            for jj in range(4):
                own_low[jj, at, b * 256 : b * 256 + 256] = low[
                    :, b * 1024 + jj * 256 : b * 1024 + jj * 256 + 256
                ]

    def low_copy(jj, i):
        at = pl.ds(i * 32, 32)
        return rc(own_low.at[jj, at], plane_low.at[k, j, at], low_s.at[0], low_r.at[j], dev(z, jj, k))

    def low_pass(jj):
        return rc(plane_low.at[k, jj], plane_low.at[k, jj], low_s.at[1], low_r.at[4], dev_mate)

    def low_give(i):
        for jj in (jd, jx, jy):
            low_copy(jj, i).start()

    spot_give = rc(
        spot_in.at[:, pl.ds(pl.multiple_of(mate * half, half), half)], spot_h.at[rows(k, 128)], spot_s, spot_r, dev_mate
    )

    def low_own():
        plane_low[k, j] = own_low[j]
        low_pass(j).start()
        spot_give.start()

    def filt_pair():
        got(f_line.at[pl.ds(0, 3)], sm_r.at[0])
        f_pair[k] = f_line[...]
        hand_over(f_line, f_pair.at[k], 1)

    def filt_plane():
        got(f_line, sm_r.at[1])
        f_all[j] = f_pair[...]
        spread(lambda o: f_pair, f_all, "plane", 2)

    def of_cells(jj, kk, b):
        return own_low[jj, :, pl.ds(pl.multiple_of(b * 256 + kk * 128, 128), 128)].astype(f32)

    def split(d):
        return lax.div(d, 8), lax.rem(lax.div(d, 4), 2), lax.rem(d, 4)

    kind = lax.div(lane, 8)
    of_slide = lax.rem(lane, 8) == slide_col.astype(jnp.int32)

    def mass_make():
        got(f_all.at[pl.ds(0, 3)], sm_r.at[2])
        keep_all[...] = jax.nn.sigmoid(f_all[...])

        def add_mass(d, acc):
            jj, kk, b = split(d)
            return acc + of_cells(jj, kk, b) * keep_all[jj, kk, b]

        mass = jnp.sum(lax.fori_loop(0, 32, add_mass, jnp.zeros((128, 128), f32)), axis=1, keepdims=True)
        keep["mass"] = mass
        log_term = bins_col * (jnp.log(bins_col) - jnp.log(mass))
        values = jnp.where(
            kind == 0, mass, jnp.where(kind == 1, bins_col, jnp.where(kind == 2, log_term, 0.0))
        )
        m_src[0] = jnp.sum(jnp.where(of_slide, values, 0.0), axis=0, keepdims=True)
        m_src[1] = sslide_in[...].astype(f32)
        hand_over(m_src, m_got, 3)

    lane2 = lax.broadcasted_iota(jnp.int32, (256, 128), 1)

    def mass_chip():
        got(m_src, sm_r.at[3])
        load_spot.wait()
        got(spot_h.at[rows(mate, 128)], spot_r)
        stat[...] = jnp.zeros_like(stat)
        chip_row = m_src[0] + m_got[0]
        for o in range(4):
            stat[0, o, 24:25, :] = chip_row
        first = jnp.where(k == 0, m_src[1], m_got[1])
        second = jnp.where(k == 0, m_got[1], m_src[1])
        hot_lie[...] = (
            lax.broadcasted_iota(jnp.int32, (8, 256), 0).astype(f32)
            == jnp.broadcast_to(jnp.concatenate([first, second], axis=1), (8, 256))
        ).astype(f32)
        slides_col = jnp.concatenate([stand(first), stand(second)], axis=0)
        hot_stand[...] = ((lax.rem(lane2, 8) == slides_col.astype(jnp.int32)) & (lane2 < 24)).astype(b16)
        coef[...] = jnp.zeros_like(coef)
        filt_acc[...] = jnp.zeros_like(filt_acc)

    def split_dot(a, v):
        high = v.astype(b16)
        rest = (v - high.astype(f32)).astype(b16)
        return jnp.dot(a, high, preferred_element_type=f32) + jnp.dot(a, rest, preferred_element_type=f32)

    def low_arrive(i):
        if i == 3:
            got(plane_low.at[mate], low_r.at[4])
            got(hand, hand_r)
        else:
            jj = (jx, jy, jd)[i]
            got(plane_low.at[k, jj], low_r.at[jj])
            low_pass(jj).start()

    def product(q, left, count):
        at = pl.ds(q * WIDTH, count * WIDTH)

        @pl.loop(0, 2)
        def _(h):
            if left is plane_low:
                whole = jnp.dot(left[h].reshape(512, 1024), col[:, :, at].reshape(1024, count * WIDTH), preferred_element_type=f32)
            else:
                whole = jnp.dot(left[rows(h, 512), :], grad[:, :, :, at].reshape(1024, count * WIDTH), preferred_element_type=f32)
            for i in range(count):
                part[q + i, h] = whole[:, i * WIDTH : i * WIDTH + WIDTH].reshape(4, 128, WIDTH)

    def reduce_first(q):
        for i, (core, owner, to, sem, slot) in enumerate((
            (0, jd, dev_x, early_r.at[q, 0], early.at[q, 0]),
            (1, jd, dev_y, early_r.at[q, 1], early.at[q, 1]),
            (0, jx, dev_x, late_r.at[q], late.at[q, 0]),
            (1, jy, dev_y, late_r.at[q], late.at[q, 1]),
        )):
            send1[q, i] = part[q, core, owner].astype(b16)
            rc(send1.at[q, i], slot, send1_s, sem, to).start()

    def reduce_second(q, i):
        owner, to = ((jy, dev_y), (jx, dev_x))[i]
        got(early.at[q, i], early_r.at[q, i])
        send2[q, i] = (part[q, i, owner] + early[q, i].astype(f32)).astype(b16)
        rc(send2.at[q, i], late.at[q, 2 + i], send2_s, late_r.at[q], to).start()

    def pred_give(q):
        return rc(
            pred_h.at[rows(mate, 128), pl.ds(q * WIDTH, WIDTH)], pred_out.at[:, lanes(k, q)], pred_s, pred_r, dev_mate
        )

    def pred_own(q):
        return pltpu.make_async_copy(
            pred_h.at[rows(k, 128), pl.ds(q * WIDTH, WIDTH)], pred_out.at[:, lanes(k, q)], own_sem
        )

    def reduce_last(q):
        got(late.at[q], late_r.at[q])
        for i in range(2):
            pred_h[i * 128 : i * 128 + 128, q * WIDTH : q * WIDTH + WIDTH] = part[q, i, j] + (
                late[q, i].astype(f32) + late[q, 2 + i].astype(f32)
            )

    def pred_move(q):
        pred_give(q).start()
        pred_own(q).start()

    def reduce_stat(q):
        pr = pred_h[:, q * WIDTH : q * WIDTH + WIDTH]
        sp = spot_h[:, q * WIDTH : q * WIDTH + WIDTH]
        for i, v in enumerate((pr * sp, pr * pr)):
            spacc[i] = v if q == 0 else spacc[i] + v

    def reduce_slides(q):
        pr = pred_h[:, q * WIDTH : q * WIDTH + WIDTH]
        sp = spot_h[:, q * WIDTH : q * WIDTH + WIDTH]
        for i, v in enumerate((pr * sp, pr * pr)):
            stat[q // 4, q % 4, i * 8 : i * 8 + 8] = split_dot(hot_lie[...].astype(b16), v)

    def obs_sums():
        for q in range(chunks):
            sp = spot_h[:, q * WIDTH : q * WIDTH + WIDTH]
            v = sp * sp
            ob_acc[...] = v if q == 0 else ob_acc[...] + v
            stat[q // 4, q % 4, 16:24] = split_dot(hot_lie[...].astype(b16), v)
        rc(ob_acc, ob_got, ob_s, ob_r, dev_mate).start()

    def st_send(g, i):
        slots = (st1, st2, st3)[i]
        if i == 0:
            st1[g, j] = stat[g, j]
        else:
            prior = (st1, st2)[i - 1]
            got(prior.at[g, pl.ds(0, 3)], st_r.at[g, i - 1])
            total = prior[g, 0] + prior[g, 1] + prior[g, 2] + prior[g, 3]
            st_sum[g, i - 1] = total
            if i == 1:
                st2[g, z] = total
            else:
                st3[g, j] = total
        for o in line_others if i == 1 else plane_others:
            src = stat.at[g, o] if i == 0 else st_sum.at[g, i - 1]
            to = dev(o, j, k) if i == 1 else dev(z, o, k)
            rc(src, slots.at[g, z if i == 1 else j], st_s.at[g, i], st_r.at[g, i], to).start()

    def st_finish(g):
        got(st3.at[g, pl.ds(0, 3)], st_r.at[g, 2])

    def turn(i):
        for kk in range(2):
            plane_turn[:, (kk * 4 + i) * 128 : (kk * 4 + i) * 128 + 128] = plane_low[kk, i].astype(f32).T.astype(b16)

    spx = rc(spacc, spgot, spx_s, spx_r, dev_mate)

    def spot_half():
        spx.start()

    slide8 = lax.broadcasted_iota(jnp.int32, (8, 128), 0)
    lane8 = lax.broadcasted_iota(jnp.int32, (8, 128), 1)

    def mass_end():
        sums_row = st_sum[0, 1, 24:25, :]
        each = jnp.broadcast_to(sums_row, (128, 128))
        mass_each = jnp.sum(jnp.where(of_slide & (kind == 0), each, 0.0), 1, keepdims=True)
        bins_each = jnp.sum(jnp.where(of_slide & (kind == 1), each, 0.0), 1, keepdims=True)
        mass_grad = (1.0 / mass_each - bins_col / (bins_each * keep["mass"])) / SLIDES
        keep["grad"] = mass_grad.astype(b16).astype(f32)

        def by_slide(begin):
            return jnp.sum(
                jnp.where(lane8 == slide8 + begin, jnp.broadcast_to(sums_row, (8, 128)), 0.0), 1, keepdims=True
            )

        mass_s, bins_s, log_s = by_slide(0), by_slide(8), by_slide(16)
        kl = jnp.sum(log_s / bins_s - jnp.log(bins_s) + jnp.log(mass_s), axis=0, keepdims=True)
        keep["kl"] = kl / SLIDES

    def reach_make():
        mass_grad = keep["grad"]

        @pl.loop(0, 32)
        def _(d):
            jj, kk, b = split(d)
            r_src[kk, jj, b] = jnp.sum(of_cells(jj, kk, b) * mass_grad, axis=0, keepdims=True)

        hand_over(r_src.at[mate], r_mate, 4)

    def reach_plane():
        got(r_mate, sm_r.at[4])
        r_plane_src[...] = r_src[k] + r_mate[...]
        r_plane[j] = r_plane_src[j]
        spread(lambda o: r_plane_src.at[o], r_plane, "plane", 5)

    def reach_line():
        got(r_plane.at[pl.ds(0, 3)], sm_r.at[5])
        r_line_src[...] = r_plane[0] + r_plane[1] + r_plane[2] + r_plane[3]
        r_line[z] = r_line_src[z]
        spread(lambda o: r_line_src.at[o], r_line, "line", 6)

    def obs_end():
        got(ob_got, ob_r)
        keep["obs_c"] = jnp.sum(ob_acc[...] + ob_got[...], axis=1, keepdims=True)

    def spot_sums():
        st_finish(0)
        got(spgot, spx_r)
        cross_c, pred_c = [jnp.sum(spacc[i] + spgot[i], axis=1, keepdims=True) for i in range(2)]
        obs_c = keep["obs_c"]
        root_c = jnp.sqrt(pred_c * obs_c)
        keep["cos"] = cross_c / root_c
        keep["obs"] = (1.0 / root_c) / total_spots
        keep["prd"] = (cross_c / (pred_c * root_c)) / total_spots

    def grad_make(q):
        scale = 1.0 / (SLIDES * total_genes)
        for e in range(units):
            g, o = divmod(q * units + e, 4)
            sums = st3[g, o]
            cross, prd, obs = sums[:8], sums[8:16], sums[16:24]
            root = jnp.sqrt(prd * obs)
            for i, v in enumerate((scale / root, scale * cross / (prd * root))):
                high = v.astype(b16).astype(f32)
                mid = (v - high).astype(b16).astype(f32)
                low = v - high - mid
                stack = jnp.concatenate([high, mid, low, jnp.zeros((8, 128), f32)], axis=0)
                coef[:32, (i * units + e) * 128 : (i * units + e) * 128 + 128] = stack.astype(b16)
        each_spot = jnp.dot(hot_stand[...], coef[...], preferred_element_type=f32)
        at = slice(q * WIDTH, q * WIDTH + WIDTH)
        value = pred_h[:, at] * (each_spot[:, WIDTH:] + keep["prd"]) - spot_h[:, at] * (each_spot[:, :WIDTH] + keep["obs"])
        value = value.astype(b16)
        grad[0, j, :, at] = value[:128]
        grad[1, j, :, at] = value[128:]

    def gene_cos():
        total = jnp.zeros((8, 128), f32)
        for g in range(2):
            for e in range(4):
                sums = st3[g, e]
                total = total + sums[:8] / jnp.sqrt(sums[8:16] * sums[16:24])
        return jnp.sum(jnp.sum(total, axis=0, keepdims=True), axis=1, keepdims=True)

    def grad_send(q):
        grad_make(q)
        at = grad.at[:, j, :, at_chunk(q)]
        rc(at, at, g_s.at[0], g_r.at[q, 0], dev_x).start()
        rc(at, at, g_s.at[1], g_r.at[q, 1], dev_y).start()

    def grad_direct(q):
        grad_make(q)
        at = grad.at[:, j, :, at_chunk(q)]
        rc(at, at, g_s.at[4], g_r.at[q, 2], dev(z, jd, k)).start()
        rc(at, at, g_s.at[0], g_r.at[q, 0], dev_x).start()
        rc(at, at, g_s.at[1], g_r.at[q, 1], dev_y).start()

    def grad_pass(q, i):
        owner, to = ((jx, dev_y), (jy, dev_x))[i]
        got(grad.at[:, owner, :, at_chunk(q)], g_r.at[q, i])
        at = grad.at[i, owner, :, at_chunk(q)]
        rc(at, at, g_s.at[2 + i], g_r.at[q, 2], to).start()

    def run_up(q, b):
        return rc(pass_on.at[q, b], sums_up.at[q, b], rs_s, rs_r.at[q, b], dev_up)

    def run_dn(q, b):
        return rc(pass_on.at[q, b], sums_dn.at[q, b], rs_s, rs_r.at[q, b], dev_dn)

    def block(q, b):
        return part[q, b // 2, pl.ds(2 * (b % 2), 2)].reshape(256, WIDTH)

    def run_last(q, b, up):
        i = 0 if up else 1
        to, cross = (dev_up, cross_up) if up else (dev_dn, cross_dn)
        rc(pass_on.at[q, b, rows(k, 128)], fin.at[q, i, k], rs_s, fin_r.at[q], to).start()
        rc(pass_on.at[q, b, rows(mate, 128)], fin.at[q, i, k], rs_s, fin_r.at[q], cross).start()

    def sums_half(q, h):
        whole = jnp.dot(
            plane_turn[rows(h, 512), :], grad[:, :, :, at_chunk(q)].reshape(1024, WIDTH), preferred_element_type=f32
        )
        part[q, h] = whole.reshape(4, 128, WIDTH)

    def sums_give(q, b):
        pass_on[q, b] = block(q, b).astype(b16)

    def grad_wait(q):
        if DIRECT == q:
            got(grad.at[:, jx, :, at_chunk(q)], g_r.at[q, 0])
            got(grad.at[:, jy, :, at_chunk(q)], g_r.at[q, 1])
        got(grad.at[:, jd, :, at_chunk(q)], g_r.at[q, 2])

    def sums_first(q, count):
        if count == 2:
            product(q, plane_turn, count)
        for step in range(2):
            if count == 1:
                sums_half(q, jnp.where(z < 2, 1 - step, step))

            @pl.when(z == 0)
            def _():
                for i in range(count):
                    for b in ((3, 2), (1,))[step]:
                        sums_give(q + i, b)
                        run_last(q + i, b, True) if b == 1 else run_up(q + i, b).start()

            @pl.when(z == 3)
            def _():
                for i in range(count):
                    for b in ((0, 1), (2,))[step]:
                        sums_give(q + i, b)
                        run_last(q + i, b, False) if b == 2 else run_dn(q + i, b).start()

    def pass_add(q, b, slots):
        got(slots.at[q, b], rs_r.at[q, b])
        pass_on[q, b] = (block(q, b) + slots[q, b].astype(f32)).astype(b16)

    def pass_far(q):
        @pl.when(z == 1)
        def _():
            pass_add(q, 3, sums_up)
            run_up(q, 3).start()

        @pl.when(z == 2)
        def _():
            pass_add(q, 0, sums_dn)
            run_dn(q, 0).start()

    def pass_middle(q):
        @pl.when(z == 1)
        def _():
            pass_add(q, 2, sums_up)
            run_last(q, 2, True)

        @pl.when(z == 2)
        def _():
            pass_add(q, 1, sums_dn)
            run_last(q, 1, False)

    def pass_near(q):
        @pl.when(z == 1)
        def _():
            pass_add(q, 0, sums_dn)
            run_last(q, 0, False)

        @pl.when(z == 2)
        def _():
            pass_add(q, 3, sums_up)
            run_last(q, 3, True)

    def other_give(q):
        return rc(other.at[q], other_got.at[q], oth_s, oth_r.at[q], dev_mate)

    def use_sums(q, kk, sums):
        at = lanes(kk, q)
        expr_out[:, at] = keep_col * sums
        weighed = cell_v[:, at].astype(f32) * sums
        for e in range(units):
            filt_acc[...] = filt_acc[...] + weighed[:, e * 128 : e * 128 + 128]

    def sums_other(q):
        other[q] = part[q, lax.div(z, 2), 2 * lax.rem(z, 2) + mate]
        other_give(q).start()

    def sums_last(q):
        @pl.when(z == 0)
        def _():
            got(fin.at[q, 1], fin_r.at[q])

        @pl.when(z == 3)
        def _():
            got(fin.at[q, 0], fin_r.at[q])

        @pl.when((z > 0) & (z < 3))
        def _():
            got(fin.at[q], fin_r.at[q])

        got(other_got.at[q], oth_r.at[q])
        own_at = (q, lax.div(z, 2), 2 * lax.rem(z, 2) + k)
        for kk, base in ((k, part[own_at]), (mate, other_got[q])):
            up = jnp.where(z > 0, fin[q, 0, kk].astype(f32), 0.0)
            dn = jnp.where(z < 3, fin[q, 1, kk].astype(f32), 0.0)
            use_sums(q, kk, base + (up + dn))

    def back_dot(b):
        @pl.loop(0, 2)
        def _(h):
            back[b, h] = lax.dot_general(
                grad[h].reshape(512, half), col[b], (((1,), (1,)), ((), ())), preferred_element_type=f32
            ).reshape(4, 128, 256)

        rc(back.at[b, mate], back_got.at[b], back_s, back_r.at[b], dev_mate).start()

    def back_add(b):
        got(back_got.at[b], back_r.at[b])
        for jj in range(4):
            back_low[jj, :, rows(b, 256)] = (back[b, k, jj] + back_got[b, jj]).astype(b16)

    def ret_send(b):
        at = rows(b, 256)
        for jj in (jd, jx, jy):
            rc(back_low.at[jj, :, at], back_ret.at[j, :, at], ret_s, ret_r, dev(z, jj, k)).start()
        back_ret[j, :, at] = back_low[j, :, at]

    loss_lane = lax.broadcasted_iota(jnp.int32, (1, 128), 1)

    def loss_mate():
        own_cos = jnp.sum(keep["cos"], axis=0, keepdims=True)
        l_src[...] = jnp.where(loss_lane == 0, own_cos, jnp.where(loss_lane == 1, gene_cos(), 0.0))
        hand_over(l_src, l_mate, 7)
        l_plane[j] = l_src[...]
        spread(lambda o: l_src, l_plane, "plane", 8)

    def loss_line():
        got(l_plane.at[pl.ds(0, 3)], sm_r.at[8])
        total = l_plane[0] + l_plane[1] + l_plane[2] + l_plane[3]
        l_line_src[...] = total
        l_line[z] = total
        spread(lambda o: l_line_src, l_line, "line", 9)

    def loss_end():
        got(l_line.at[pl.ds(0, 3)], sm_r.at[9])
        got(l_mate, sm_r.at[7])
        cos_row = l_line[0] + l_line[1] + l_line[2] + l_line[3]
        gene_row = l_src[...] + l_mate[...]
        cos_total = jnp.sum(jnp.where(loss_lane == 0, cos_row, 0.0), axis=1, keepdims=True)
        gene_total = jnp.sum(jnp.where(loss_lane == 1, gene_row, 0.0), axis=1, keepdims=True)
        gene_loss = 1.0 - gene_total / (SLIDES * total_genes)
        spot_loss = 1.0 - cos_total / total_spots
        kl_loss = keep["kl"]
        total_loss = gene_loss + spot_loss + kl_loss
        picked = jnp.where(loss_lane == 2, spot_loss, jnp.where(loss_lane == 3, kl_loss, 0.0))
        loss_out[...] = jnp.where(loss_lane == 0, total_loss, jnp.where(loss_lane == 1, gene_loss, picked))

    def map_rows(g):
        at = rows(g, 16)
        pick = lax.broadcasted_iota(jnp.int32, (16, 128), 0) + g * 16
        here = lax.broadcasted_iota(jnp.int32, (16, 128), 1)
        mg = jnp.sum(jnp.where(pick == here, jnp.broadcast_to(mass_row[...], (16, 128)), 0.0), 1, keepdims=True)
        inner = jnp.zeros((16, 128), f32)
        for d in range(32):
            b, jj, kk = d // 8, (d % 8) // 2, d % 2
            used = back_ret[jj, at, b * 256 + kk * 128 : b * 256 + kk * 128 + 128].astype(f32) + mg * keep_all[jj, kk, b]
            inner = inner + chance[at, d * 128 : d * 128 + 128] * used
            map_out[at, d * 128 : d * 128 + 128] = used
        inner = jnp.sum(inner, axis=1, keepdims=True)
        map_out[at, :] = chance[at, :] * (map_out[at, :] - inner)

    def map_some(i):
        if i == 0:
            got(back_ret.at[pl.ds(0, 3)], ret_r)
            mass_row[...] = lie(keep["grad"])
        pl.loop(2 * i, 2 * i + 2)(map_rows)

    steps = {
        "x": softmax_some, "H": scale_more, "F": lambda i: filt_line(), "N": far_ready, "Y": pred_move, "w": low_give, "v": lambda i: low_own(),
        "c": col_own, "h": lambda i: hop(), "i": lambda i: (filt_pair, filt_plane, mass_make, mass_chip)[i](),
        "a": low_arrive, "q": turn, "p": lambda q: product(q, plane_low, 1), "P": lambda q: product(q, plane_low, 2),
        "f": reduce_first, "s": lambda q: reduce_second(q, 0), "S": lambda q: reduce_second(q, 1),
        "l": reduce_last, "k": reduce_stat, "j": reduce_slides, "B": lambda i: (obs_sums, obs_end)[i](), "t": lambda i: st_send(0, i), "z": lambda i: (spot_half, mass_end, spot_sums)[i](),
        "g": grad_send, "G": grad_direct, "m": lambda q: grad_pass(q, 0), "n": lambda q: grad_pass(q, 1),
        "y": lambda i: st_send(1, i) if i < 3 else st_finish(1), "r": lambda q: sums_first(q, 1), "R": lambda q: sums_first(q, 2),
        "U": pass_far, "V": pass_middle, "D": pass_near,
        "L": sums_last, "O": sums_other, "b": back_dot, "A": back_add, "T": ret_send, "W": grad_wait, "M": map_some,
        "e": lambda i: (reach_make, reach_plane, reach_line)[i](), "o": lambda i: (loss_mate, loss_line, loss_end)[i](),
    }
    for group in ORDER:
        for word in group.split():
            steps[word[0]](int(word[1:]) if len(word) > 1 else 0)

    got(r_line.at[pl.ds(0, 3)], sm_r.at[6])
    reach_row = r_line[0] + r_line[1] + r_line[2] + r_line[3]
    filt_sum = jnp.sum(filt_acc[...], axis=1, keepdims=True)
    keep_row = jax.nn.sigmoid(filt_in[...].astype(f32))
    filt_out[...] = keep_row * (1.0 - keep_row) * (lie(filt_sum) + reach_row)

    sent(hand, hand_s)
    spot_give.wait_send()
    sent(send1, send1_s)
    sent(send2, send2_s)
    sent(pred_h.at[rows(mate, 128)], pred_s)
    got(pred_out.at[:, pl.ds(pl.multiple_of(mate * half, half), half)], pred_r)
    pltpu.make_async_copy(
        pred_h.at[rows(k, 128)], pred_out.at[:, pl.ds(pl.multiple_of(k * half, half), half)], own_sem
    ).wait()
    for i in range(2):
        sent(grad.at[:, j], g_s.at[i])
    others = [q for q in range(chunks) if q != DIRECT]
    sent(grad.at[0, jx, :, pl.ds(0, len(others) * WIDTH)], g_s.at[2])
    sent(grad.at[1, jy, :, pl.ds(0, len(others) * WIDTH)], g_s.at[3])
    if DIRECT is not None:
        sent(grad.at[:, j, :, at_chunk(DIRECT)], g_s.at[4])
    sent(ob_acc, ob_s)
    for i in range(3):
        @pl.when(z == i)
        def _():
            sent(col.at[pl.ds(0, i + 1)], up_s)

        @pl.when(z == 3 - i)
        def _():
            sent(col.at[pl.ds(3 - i, i + 1)], dn_s)
    sent(pass_on.at[:, pl.ds(0, 3)], rs_s)
    sent(plane_low.at[k, pl.ds(0, 3)], low_s.at[0])
    sent(plane_low.at[k], low_s.at[1])
    for g in range(2):
        for i in range(3):
            sent(st1.at[g, pl.ds(0, 3)], st_s.at[g, i])
    spx.wait_send()
    sent(back_got, back_s)
    sent(back_low.at[pl.ds(0, 3)], ret_s)
    sent(other, oth_s)
    for i, ref in enumerate((
        f_line.at[pl.ds(0, 3)], f_line, f_all.at[pl.ds(0, 3)], m_src, r_mate, r_plane.at[pl.ds(0, 3)],
        r_line.at[pl.ds(0, 3)], l_mate, l_plane.at[pl.ds(0, 3)], l_line.at[pl.ds(0, 3)],
    )):
        sent(ref, sm_s.at[i])


def hand_out(pred_in, map_in, expr_in, filt_in, loss_in, pred_out, map_out, expr_out, filt_out, loss_out, sems):
    pairs = ((map_in, map_out), (pred_in, pred_out), (expr_in, expr_out))
    size = 128 // 2
    copies = [
        pltpu.make_async_copy(src.at[pl.ds(p * size, size)], dst.at[pl.ds(p * size, size)], sems.at[i, p])
        for p in range(2)
        for i, (src, dst) in enumerate(pairs)
    ]
    for copy in copies:
        copy.start()
    filt_out[...] = filt_in[...]
    loss_out[...] = loss_in[:, :4]
    for copy in copies:
        copy.wait()


def fused_shards(map_logits, filter_logits, cell_expr, spot_expr, cell_slide, spot_slide, density_bins):
    f32, b16 = jnp.float32, jnp.bfloat16
    spots, cells = map_logits.shape
    genes = cell_expr.shape[1]
    n = genes // (2 * WIDTH)
    V, S = pltpu.VMEM, pltpu.SemaphoreType.DMA
    any_, vmem = pl.BlockSpec(memory_space=pl.ANY), pl.BlockSpec(memory_space=pltpu.VMEM)
    one = S(())
    scratch = [
        V((128, cells), f32),
        V((4, 128, 1024), b16),
        V((2, 4, 128, 1024), b16),
        V((1024, 1024), b16),
        V((128, genes), b16),
        V((n, 128, WIDTH), b16),
        V((4, 256, genes // 2), b16),
        V((n, 2, 4, 128, WIDTH), f32),
        V((n, 4, 128, WIDTH), b16),
        V((n, 2, 128, WIDTH), b16),
        V((n, 2, 128, WIDTH), b16),
        V((n, 4, 128, WIDTH), b16),
        V((256, genes // 2), f32),
        V((256, genes // 2), f32),
        V((2, 4, 32, 128), f32),
        V((2, 2, 32, 128), f32),
        V((2, 4, 32, 128), f32),
        V((2, 4, 32, 128), f32),
        V((2, 4, 32, 128), f32),
        V((2, 256, 128), f32),
        V((2, 256, 128), f32),
        V((256, 128), f32),
        V((256, 128), f32),
        V((128, 2 * WIDTH), b16),
        V((2, 4, 128, genes // 2), b16),
        V((n, 4, 256, WIDTH), b16),
        V((n, 4, 256, WIDTH), b16),
        V((n, 4, 256, WIDTH), b16),
        V((n, 2, 2, 128, WIDTH), b16),
        V((4, 2, 4, 128, 256), f32),
        V((4, 4, 128, 256), f32),
        V((4, 128, 1024), b16),
        V((4, 128, 1024), b16),
        V((n, 128, WIDTH), f32),
        V((n, 128, WIDTH), f32),
        V((4, 1, 128), f32),
        V((2, 4, 1, 128), f32),
        V((4, 2, 4, 1, 128), f32),
        V((4, 2, 4, 1, 128), f32),
        V((2, 1, 128), f32),
        V((2, 1, 128), f32),
        V((2, 4, 4, 1, 128), f32),
        V((4, 4, 1, 128), f32),
        V((4, 4, 1, 128), f32),
        V((4, 4, 1, 128), f32),
        V((4, 1, 128), f32),
        V((4, 1, 128), f32),
        V((1, 128), f32),
        V((1, 128), f32),
        V((4, 1, 128), f32),
        V((1, 128), f32),
        V((4, 1, 128), f32),
        V((128, 128), f32),
        V((8, 256), f32),
        V((256, 128), b16),
        V((1, 128), f32),
        V((1, 128), b16),
        V((1, cells), jnp.int32),
        V((1, 128), jnp.int32),
        V((1, 128), jnp.int32),
        S((7,)), one, one, one, one, one, S((n, 4)), S((2,)), S((5,)),
        one, one, S((n, 2)), S((n,)),
        one, one, one, one, S((2, 3)), S((2, 3)), one, one, one, one,
        S((5,)), S((n, 3)), one, S((n, 4)), S((n,)), one, S((4,)),
        one, one, one, S((n,)), S((10,)), S((10,)), pltpu.SemaphoreType.REGULAR,
    ]
    predicted, map_grad, expr_grad, filt, loss = pl.pallas_call(
        functools.partial(fused_kernel, float(spots * 32), float(genes)),
        out_shape=(
            pltpu.VMEM((spots, genes), f32),
            pltpu.VMEM((spots, cells), f32),
            pltpu.VMEM((spots, genes), f32),
            V((1, 128), f32),
            V((1, 128), f32),
        ),
        in_specs=[any_] * 7,
        out_specs=(vmem, vmem, vmem, vmem, vmem),
        scratch_shapes=scratch,
        compiler_params=pltpu.CompilerParams(
            collective_id=0, has_side_effects=True, vmem_limit_bytes=58 * 2**20
        ),
        name="mapping_step",
    )(
        map_logits,
        filter_logits.reshape(1, 128),
        cell_expr,
        spot_expr,
        cell_slide.reshape(1, cells),
        spot_slide.reshape(1, 128),
        density_bins.reshape(1, 128),
    )
    predicted, map_grad, expr_grad, filt, loss = pl.pallas_call(
        hand_out,
        out_shape=(
            jax.ShapeDtypeStruct((spots, genes), f32),
            jax.ShapeDtypeStruct((spots, cells), f32),
            jax.ShapeDtypeStruct((spots, genes), f32),
            jax.ShapeDtypeStruct((1, 128), f32),
            jax.ShapeDtypeStruct((1, 4), f32),
        ),
        in_specs=[vmem] * 5,
        out_specs=(any_, any_, any_, vmem, vmem),
        scratch_shapes=[S((3, 2))],
        compiler_params=pltpu.CompilerParams(vmem_limit_bytes=2**20),
        name="hand_out",
    )(*[pltpu.with_memory_space_constraint(v, pltpu.VMEM) for v in (predicted, map_grad, expr_grad, filt, loss)])
    return loss.reshape(4), predicted, map_grad, expr_grad, filt.reshape(128)


def solution(mesh):
    both = P(("row", "col"))
    rows = P(("row", "col"), None)
    in_specs = (rows, both, rows, rows, P(), both, both)
    out_specs = (P(), rows, rows, rows, both)
    step = fused_shards if (mesh.shape["row"], mesh.shape["col"]) == (4, 8) else shards
    return jax.shard_map(step, mesh=mesh, in_specs=in_specs, out_specs=out_specs, check_vma=False)
```

```python
import functools

import jax
import jax.numpy as jnp
from jax import lax
from jax.experimental import pallas as pl
from jax.experimental.pallas import tpu as pltpu
from jax.sharding import PartitionSpec as P

SLIDES = 8
ROWS, PLANE, CORES = 4, 4, 2
WIDTH = 128
MESH = pl.DeviceIdType.MESH
DIRECT = 0
ORDER = (
    "c0 N0 H0 H1",
    "x0 w0 c1 N1",
    "F0 H2 c2 H3",
    "H4 x1 w1 H5",
    "h H6 c3 c4",
    "x2 i0 x3 v0",
    "i1 H7 w3 h",
    "h h w2 i2",
    "c5 h h h",
    "i3 B0 a2 a0",
    "a1 h h h",
    "c6 a3 P0 f0",
    "f1 h h h",
    "P2 f2 s0 q1",
    "f3 S1 h h",
    "h c7 s2 s1",
    "S0 p4 S2 s3",
    "f4 S3 h h",
    "h p5 f5 l1",
    "l0 l2 j0 j2",
    "j1 s4 h h",
    "h l3 j3 t0",
    "S4 p6 f6 k0",
    "k2 k1 s5 S5",
    "h h p7 t1",
    "f7 s6 Y2 k3",
    "l4 j4 S6 l5",
    "k5 B1 s7 S7",
    "t2 q0 j5 l6",
    "k6 k4 l7 k7",
    "z0 q3 j6 j7",
    "y0 z2 G0 Y3",
    "q2 g2 g1 y1",
    "W0 r0 m2 n2",
    "z1 y2 Y7 g3",
    "m1 n1 W2 r2",
    "y3 g7 U0 e0",
    "Y0 m3 g4 n3",
    "g6 W1 r1 g5",
    "U2 m7 o0 m4",
    "W3 V0 n7 V2",
    "n4 r3 m6 n6",
    "n5 D2 m5 O1",
    "U1 V1 W7 r7",
    "W4 W6 r6 D0",
    "O2 W5 b2 O6",
    "b0 O0 b1 Y5",
    "A2 T2 U3 U7",
    "e1 A0 T0 V7",
    "A1 o1 R4 O5",
    "V3 T1 Y6 Y1",
    "Y4 L0 b3 U6",
    "O3 D1 e2 V6",
    "O7 D7 A3 T3",
    "U4 D3 L2 L7",
    "O4 D6 o2 L1",
    "U5 V4 L3 L6",
    "V5 D4 M0 D5",
    "M1 M2 L4 M3",
    "L5",
)


def shards(map_logits, filter_logits, cell_expr, spot_expr, cell_slide, spot_slide, density_bins):
    highest = lax.Precision.HIGHEST
    both = ("row", "col")
    rows_count = lax.axis_size("row")
    cols_count = lax.axis_size("col")
    spot_dev, cell_total = map_logits.shape
    cell_dev = filter_logits.shape[0]
    spot_total = spot_dev * rows_count * cols_count
    gene_count = cell_expr.shape[1]
    keep_rate = jax.nn.sigmoid(filter_logits.astype(jnp.float32))
    scaled = (keep_rate[:, None] * cell_expr.astype(jnp.float32)).astype(jnp.bfloat16)
    scaled_col = lax.all_gather(scaled, "row", axis=0, tiled=True)
    allowed = spot_slide[:, None] == cell_slide[None, :]
    shifted = jnp.where(allowed, map_logits, -1e30)
    row_peak = jnp.max(shifted, axis=1, keepdims=True)
    raised = jnp.exp(shifted - row_peak)
    chances = raised / jnp.sum(raised, axis=1, keepdims=True)
    chance_low = chances.astype(jnp.bfloat16)
    by_col = chance_low.reshape(spot_dev, rows_count, cols_count, cell_dev)
    mapped = lax.all_to_all(by_col, "col", split_axis=2, concat_axis=0, tiled=True)
    mapped = mapped.reshape(spot_dev * cols_count, rows_count * cell_dev)
    keep_col = lax.all_gather(keep_rate, "row", axis=0, tiled=True)
    part_pred = jnp.dot(mapped, scaled_col, preferred_element_type=jnp.float32)
    part_mass = jnp.dot(mapped, keep_col, precision=highest, preferred_element_type=jnp.float32)
    predicted = lax.psum_scatter(part_pred, "col", scatter_dimension=0, tiled=True)
    mass = lax.psum_scatter(part_mass, "col", scatter_dimension=0, tiled=True)
    onehot = (spot_slide[:, None] == jnp.arange(SLIDES, dtype=jnp.int32)[None, :]).astype(
        jnp.float32
    )
    cross_term = predicted * spot_expr
    pred_sq = predicted * predicted
    obs_sq = spot_expr * spot_expr
    spot_cross = jnp.sum(cross_term, axis=1)
    spot_pred = jnp.sum(pred_sq, axis=1)
    spot_root = jnp.sqrt(spot_pred * jnp.sum(obs_sq, axis=1))
    spot_cos = spot_cross / spot_root
    bin_values = density_bins.astype(jnp.float32)
    log_term = bin_values * (jnp.log(bin_values) - jnp.log(mass))
    all_cross, all_pred, all_obs, slide_mass, slide_bins, slide_log, cos_total = lax.psum(
        (
            jnp.dot(onehot.T, cross_term, precision=highest),
            jnp.dot(onehot.T, pred_sq, precision=highest),
            jnp.dot(onehot.T, obs_sq, precision=highest),
            jnp.dot(onehot.T, mass, precision=highest),
            jnp.dot(onehot.T, bin_values, precision=highest),
            jnp.dot(onehot.T, log_term, precision=highest),
            jnp.sum(spot_cos),
        ),
        both,
    )
    gene_root = jnp.sqrt(all_pred * all_obs)
    gene_loss = 1.0 - jnp.mean(all_cross / gene_root)
    spot_loss = 1.0 - cos_total / spot_total
    kl_loss = jnp.mean(slide_log / slide_bins - jnp.log(slide_bins) + jnp.log(slide_mass))
    total_loss = gene_loss + spot_loss + kl_loss
    losses = jnp.stack([total_loss, gene_loss, spot_loss, kl_loss])
    gene_scale = 1.0 / (SLIDES * gene_count)
    coef_obs = jnp.dot(onehot, 1.0 / gene_root, precision=highest)
    coef_pred = jnp.dot(onehot, all_cross / (all_pred * gene_root), precision=highest)
    pred_grad = -gene_scale * (spot_expr * coef_obs - predicted * coef_pred)
    pred_grad = (
        pred_grad
        - (
            spot_expr / spot_root[:, None]
            - predicted * (spot_cross / (spot_pred * spot_root))[:, None]
        )
        / spot_total
    )
    mass_each = jnp.dot(onehot, slide_mass, precision=highest)
    bins_each = jnp.dot(onehot, slide_bins, precision=highest)
    mass_grad = (1.0 / mass_each - bin_values / (bins_each * mass)) / SLIDES
    grad_low = pred_grad.astype(jnp.bfloat16)
    mass_low = mass_grad.astype(jnp.bfloat16)
    grad_block = lax.all_gather(grad_low, "col", axis=0, tiled=True)
    mass_block = lax.all_gather(mass_low, "col", axis=0, tiled=True)
    back_map = lax.dot_general(
        grad_block, scaled_col, (((1,), (1,)), ((), ())), preferred_element_type=jnp.float32
    )
    back_map = back_map + mass_block.astype(jnp.float32)[:, None] * keep_col[None, :]
    back_low = back_map.astype(jnp.bfloat16)
    returned = lax.all_to_all(
        back_low.reshape(spot_dev * cols_count, rows_count, 1, cell_dev),
        "col",
        split_axis=0,
        concat_axis=2,
        tiled=True,
    ).reshape(spot_dev, cell_total)
    expr_part = lax.dot_general(
        mapped, grad_block, (((0,), (0,)), ((), ())), preferred_element_type=jnp.float32
    )
    mass_reach = lax.dot_general(
        mapped, mass_block, (((0,), (0,)), ((), ())), preferred_element_type=jnp.float32
    )
    expr_sum = lax.psum_scatter(expr_part, "row", scatter_dimension=0, tiled=True)
    mass_sum = lax.psum_scatter(mass_reach, "row", scatter_dimension=0, tiled=True)
    filter_grad = (
        keep_rate
        * (1.0 - keep_rate)
        * (jnp.sum(cell_expr.astype(jnp.float32) * expr_sum, axis=1) + mass_sum)
    )
    expr_grad = keep_rate[:, None] * expr_sum
    chance_grad = returned.astype(jnp.float32)
    inner_sum = jnp.sum(chances * chance_grad, axis=1, keepdims=True)
    map_grad = chances * (chance_grad - inner_sum)
    return (losses, predicted, map_grad, expr_grad, filter_grad)


def fused_kernel(
    total_spots, total_genes,
    logit_in, filt_hbm, cell_in, spot_in, cslide_hbm, sslide_hbm, bins_hbm,
    pred_out, map_out, expr_out, filt_out, loss_out,
    chance, own_low, plane_low, plane_turn, cell_v, hand, col, part, send1, early, send2, late,
    pred_h, spot_h, stat, st_sum, st1, st2, st3, spacc, spgot, ob_acc, ob_got, coef, grad,
    sums_up, sums_dn, pass_on, fin, back, back_got, back_low, back_ret, other, other_got,
    f_line, f_pair, f_all, keep_all, m_src, m_got, r_src, r_mate, r_plane_src, r_plane, r_line_src, r_line,
    l_src, l_mate, l_plane, l_line_src, l_line, filt_acc, hot_lie, hot_stand, mass_row, filt_in, cslide_in, sslide_in, bins_in,
    load_sem, own_sem, hand_s, hand_r, up_s, dn_s, col_r, low_s, low_r, send1_s, send2_s, early_r, late_r,
    pred_s, pred_r, spot_s, spot_r, st_s, st_r, spx_s, spx_r, ob_s, ob_r, g_s, g_r, rs_s, rs_r, fin_r, back_s, back_r,
    ret_s, ret_r, oth_s, oth_r, sm_s, sm_r, ready,
):
    f32, b16 = jnp.float32, jnp.bfloat16
    half = col.shape[2]
    chunks = half // WIDTH
    units = WIDTH // 128
    keep = {}
    z = lax.axis_index("row")
    c = lax.axis_index("col")
    j = lax.div(c, 2)
    k = lax.rem(c, 2)
    y = lax.div(j, 2)
    x = lax.rem(j, 2)
    mate = 1 - k

    def dev(zz, jj, kk):
        return (zz, jj * 2 + kk)

    jx = y * 2 + (1 - x)
    jy = (1 - y) * 2 + x
    jd = (1 - y) * 2 + (1 - x)
    dev_mate = dev(z, j, mate)
    dev_x = dev(z, jx, k)
    dev_y = dev(z, jy, k)
    dev_up = dev(lax.rem(z + 1, 4), j, k)
    dev_dn = dev(lax.rem(z + 3, 4), j, k)
    cross_up = dev(lax.rem(z + 1, 4), j, mate)
    cross_dn = dev(lax.rem(z + 3, 4), j, mate)
    plane_others = (jx, jy, jd)
    line_others = [lax.rem(z + i, 4) for i in (1, 2, 3)]

    def rc(src, dst, ss, rs, to):
        return pltpu.make_async_remote_copy(
            src_ref=src, dst_ref=dst, send_sem=ss, recv_sem=rs, device_id=to, device_id_type=MESH
        )

    def got(ref, sem):
        rc(ref, ref, sem, sem, dev_mate).wait_recv()

    def sent(ref, sem):
        rc(ref, ref, sem, sem, dev_mate).wait_send()

    def rows(i, size):
        return pl.ds(pl.multiple_of(i * size, size), size)

    def at_chunk(q):
        return pl.ds(q * WIDTH, WIDTH)

    def lanes(kk, q):
        return pl.ds(pl.multiple_of(kk * half + q * WIDTH, WIDTH), WIDTH)

    load_cell = pltpu.make_async_copy(cell_in, cell_v, load_sem.at[0])
    load_logit = pltpu.make_async_copy(logit_in, chance, load_sem.at[1])
    load_spot = pltpu.make_async_copy(
        spot_in.at[:, pl.ds(pl.multiple_of(k * half, half), half)], spot_h.at[rows(k, 128)], load_sem.at[2]
    )
    small_loads = [
        pltpu.make_async_copy(src, dst, load_sem.at[3 + i])
        for i, (src, dst) in enumerate((
            (filt_hbm, filt_in), (sslide_hbm, sslide_in), (bins_hbm, bins_in), (cslide_hbm, cslide_in),
        ))
    ]
    barrier = pltpu.get_barrier_semaphore()
    for to in (dev_mate, dev_x, dev_y, dev(z, jd, k)):
        pl.semaphore_signal(barrier, inc=1, device_id=to, device_id_type=MESH)
    for i, near in enumerate(((dev_up, cross_up), (dev_dn, cross_dn))):
        @pl.when((z < 3) if i == 0 else (z > 0))
        def _():
            for to in near:
                pl.semaphore_signal(barrier, inc=1, device_id=to, device_id_type=MESH)
    small_loads[0].start()
    load_cell.start()
    for load in small_loads[1:]:
        load.start()
    load_logit.start()
    load_spot.start()

    eye = lax.broadcasted_iota(jnp.int32, (128, 128), 0) == lax.broadcasted_iota(
        jnp.int32, (128, 128), 1
    )
    lane = lax.broadcasted_iota(jnp.int32, (128, 128), 1)

    def stand(row):
        return jnp.sum(jnp.where(eye, jnp.broadcast_to(row, (128, 128)), 0.0), 1, keepdims=True)

    def lie(column):
        return jnp.sum(jnp.where(eye, jnp.broadcast_to(column, (128, 128)), 0.0), 0, keepdims=True)

    for load in small_loads[:3]:
        load.wait()
    filt_row = filt_in[...].astype(f32)
    keep_col = stand(jax.nn.sigmoid(filt_row))
    slide_col = stand(sslide_in[...].astype(f32))
    bins_col = stand(bins_in[...].astype(f32))

    def hand_copy(q):
        return rc(hand.at[q], col.at[z, rows(k, 128), at_chunk(q)], hand_s, hand_r, dev_mate)

    def col_up(q, b):
        at = col.at[b, :, at_chunk(q)]
        return rc(at, at, up_s, col_r.at[q, b], dev_up)

    def col_dn(q, b):
        at = col.at[b, :, at_chunk(q)]
        return rc(at, at, dn_s, col_r.at[q, b], dev_dn)

    def scale_cells(q):
        hand[q] = (keep_col * cell_v[:, lanes(mate, q)].astype(f32)).astype(b16)
        col[z, rows(k, 128), at_chunk(q)] = (keep_col * cell_v[:, lanes(k, q)].astype(f32)).astype(b16)

    def col_own(q):
        own = col.at[z, rows(k, 128), at_chunk(q)]

        @pl.when(z < 3)
        def _():
            rc(own, own, up_s, col_r.at[q, z], dev_up).start()
            rc(hand.at[q], own, up_s, col_r.at[q, z], cross_up).start()

        @pl.when(z > 0)
        def _():
            rc(own, own, dn_s, col_r.at[q, z], dev_dn).start()
            rc(hand.at[q], own, dn_s, col_r.at[q, z], cross_dn).start()

    hops = [(q, s) for q in range(chunks) for s in range(3)]

    def hop():
        q, s = hops.pop(0)

        @pl.when(z - 1 - s >= 0)
        def _():
            b = z - 1 - s
            got(col.at[b, :, at_chunk(q)], col_r.at[q, b])

            @pl.when(z < 3)
            def _():
                col_up(q, b).start()

        @pl.when(z + 1 + s <= 3)
        def _():
            b = z + 1 + s
            got(col.at[b, :, at_chunk(q)], col_r.at[q, b])

            @pl.when(z > 0)
            def _():
                col_dn(q, b).start()

    load_cell.wait()
    scale_cells(0)
    pl.semaphore_wait(barrier, jnp.where((z == 0) | (z == 3), 6, 8))

    def far_ready(i):
        if i == 0:
            @pl.when(z == 1)
            def _():
                pl.semaphore_signal(ready, inc=1, device_id=dev_up, device_id_type=MESH)

            @pl.when(z == 2)
            def _():
                pl.semaphore_signal(ready, inc=1, device_id=dev_dn, device_id_type=MESH)
        else:
            pl.semaphore_wait(ready, 1)

            @pl.when(z == 1)
            def _():
                pl.semaphore_signal(ready, inc=1, device_id=dev_dn, device_id_type=MESH)

            @pl.when(z == 2)
            def _():
                pl.semaphore_signal(ready, inc=1, device_id=dev_up, device_id_type=MESH)


    def scale_more(q):
        if q:
            scale_cells(q)
        hand_copy(q).start()

    def spread(source, slots, which, i):
        for o in plane_others if which == "plane" else line_others:
            to = dev(z, o, k) if which == "plane" else dev(o, j, k)
            rc(source(o), slots.at[j if which == "plane" else z], sm_s.at[i], sm_r.at[i], to).start()

    def hand_over(source, slot, i):
        rc(source, slot, sm_s.at[i], sm_r.at[i], dev_mate).start()

    def filt_line():
        f_line[z] = filt_row
        spread(lambda o: f_line.at[z], f_line, "line", 0)

    def softmax_some(i):
        if not keep.get("logits"):
            small_loads[3].wait()
            load_logit.wait()
            keep["logits"] = True
        pl.loop(2 * i, 2 * i + 2)(softmax_rows)

    def softmax_rows(g):
        at = rows(g, 16)
        logits = chance[at, :]
        pick = lax.broadcasted_iota(jnp.int32, (16, 128), 0) + g * 16
        here = lax.broadcasted_iota(jnp.int32, (16, 128), 1)
        slide = jnp.sum(
            jnp.where(pick == here, jnp.broadcast_to(sslide_in[...].astype(f32), (16, 128)), 0.0),
            1, keepdims=True,
        )
        allowed = slide == cslide_in[...].astype(f32)
        shifted = jnp.where(allowed, logits, -1e30)
        raised = jnp.exp(shifted - jnp.max(shifted, axis=1, keepdims=True))
        value = raised / jnp.sum(raised, axis=1, keepdims=True)
        chance[at, :] = value
        low = value.astype(b16)
        for b in range(4):
            for jj in range(4):
                own_low[jj, at, b * 256 : b * 256 + 256] = low[
                    :, b * 1024 + jj * 256 : b * 1024 + jj * 256 + 256
                ]

    def low_copy(jj, i):
        at = pl.ds(i * 32, 32)
        return rc(own_low.at[jj, at], plane_low.at[k, j, at], low_s.at[0], low_r.at[j], dev(z, jj, k))

    def low_pass(jj):
        return rc(plane_low.at[k, jj], plane_low.at[k, jj], low_s.at[1], low_r.at[4], dev_mate)

    def low_give(i):
        for jj in (jd, jx, jy):
            low_copy(jj, i).start()

    spot_give = rc(
        spot_in.at[:, pl.ds(pl.multiple_of(mate * half, half), half)], spot_h.at[rows(k, 128)], spot_s, spot_r, dev_mate
    )

    def low_own():
        plane_low[k, j] = own_low[j]
        low_pass(j).start()
        spot_give.start()

    def filt_pair():
        got(f_line.at[pl.ds(0, 3)], sm_r.at[0])
        f_pair[k] = f_line[...]
        hand_over(f_line, f_pair.at[k], 1)

    def filt_plane():
        got(f_line, sm_r.at[1])
        f_all[j] = f_pair[...]
        spread(lambda o: f_pair, f_all, "plane", 2)

    def of_cells(jj, kk, b):
        return own_low[jj, :, pl.ds(pl.multiple_of(b * 256 + kk * 128, 128), 128)].astype(f32)

    def split(d):
        return lax.div(d, 8), lax.rem(lax.div(d, 4), 2), lax.rem(d, 4)

    kind = lax.div(lane, 8)
    of_slide = lax.rem(lane, 8) == slide_col.astype(jnp.int32)

    def mass_make():
        got(f_all.at[pl.ds(0, 3)], sm_r.at[2])
        keep_all[...] = jax.nn.sigmoid(f_all[...])

        def add_mass(d, acc):
            jj, kk, b = split(d)
            return acc + of_cells(jj, kk, b) * keep_all[jj, kk, b]

        mass = jnp.sum(lax.fori_loop(0, 32, add_mass, jnp.zeros((128, 128), f32)), axis=1, keepdims=True)
        keep["mass"] = mass
        log_term = bins_col * (jnp.log(bins_col) - jnp.log(mass))
        values = jnp.where(
            kind == 0, mass, jnp.where(kind == 1, bins_col, jnp.where(kind == 2, log_term, 0.0))
        )
        m_src[0] = jnp.sum(jnp.where(of_slide, values, 0.0), axis=0, keepdims=True)
        m_src[1] = sslide_in[...].astype(f32)
        hand_over(m_src, m_got, 3)

    lane2 = lax.broadcasted_iota(jnp.int32, (256, 128), 1)

    def mass_chip():
        got(m_src, sm_r.at[3])
        load_spot.wait()
        got(spot_h.at[rows(mate, 128)], spot_r)
        stat[...] = jnp.zeros_like(stat)
        chip_row = m_src[0] + m_got[0]
        for o in range(4):
            stat[0, o, 24:25, :] = chip_row
        first = jnp.where(k == 0, m_src[1], m_got[1])
        second = jnp.where(k == 0, m_got[1], m_src[1])
        hot_lie[...] = (
            lax.broadcasted_iota(jnp.int32, (8, 256), 0).astype(f32)
            == jnp.broadcast_to(jnp.concatenate([first, second], axis=1), (8, 256))
        ).astype(f32)
        slides_col = jnp.concatenate([stand(first), stand(second)], axis=0)
        hot_stand[...] = ((lax.rem(lane2, 8) == slides_col.astype(jnp.int32)) & (lane2 < 24)).astype(b16)
        coef[...] = jnp.zeros_like(coef)
        filt_acc[...] = jnp.zeros_like(filt_acc)

    def split_dot(a, v):
        high = v.astype(b16)
        rest = (v - high.astype(f32)).astype(b16)
        return jnp.dot(a, high, preferred_element_type=f32) + jnp.dot(a, rest, preferred_element_type=f32)

    def low_arrive(i):
        if i == 3:
            got(plane_low.at[mate], low_r.at[4])
            got(hand, hand_r)
        else:
            jj = (jx, jy, jd)[i]
            got(plane_low.at[k, jj], low_r.at[jj])
            low_pass(jj).start()

    def product(q, left, count):
        at = pl.ds(q * WIDTH, count * WIDTH)

        @pl.loop(0, 2)
        def _(h):
            if left is plane_low:
                whole = jnp.dot(left[h].reshape(512, 1024), col[:, :, at].reshape(1024, count * WIDTH), preferred_element_type=f32)
            else:
                whole = jnp.dot(left[rows(h, 512), :], grad[:, :, :, at].reshape(1024, count * WIDTH), preferred_element_type=f32)
            for i in range(count):
                part[q + i, h] = whole[:, i * WIDTH : i * WIDTH + WIDTH].reshape(4, 128, WIDTH)

    def reduce_first(q):
        for i, (core, owner, to, sem, slot) in enumerate((
            (0, jd, dev_x, early_r.at[q, 0], early.at[q, 0]),
            (1, jd, dev_y, early_r.at[q, 1], early.at[q, 1]),
            (0, jx, dev_x, late_r.at[q], late.at[q, 0]),
            (1, jy, dev_y, late_r.at[q], late.at[q, 1]),
        )):
            send1[q, i] = part[q, core, owner].astype(b16)
            rc(send1.at[q, i], slot, send1_s, sem, to).start()

    def reduce_second(q, i):
        owner, to = ((jy, dev_y), (jx, dev_x))[i]
        got(early.at[q, i], early_r.at[q, i])
        send2[q, i] = (part[q, i, owner] + early[q, i].astype(f32)).astype(b16)
        rc(send2.at[q, i], late.at[q, 2 + i], send2_s, late_r.at[q], to).start()

    def pred_give(q):
        return rc(
            pred_h.at[rows(mate, 128), pl.ds(q * WIDTH, WIDTH)], pred_out.at[:, lanes(k, q)], pred_s, pred_r, dev_mate
        )

    def pred_own(q):
        return pltpu.make_async_copy(
            pred_h.at[rows(k, 128), pl.ds(q * WIDTH, WIDTH)], pred_out.at[:, lanes(k, q)], own_sem
        )

    def reduce_last(q):
        got(late.at[q], late_r.at[q])
        for i in range(2):
            pred_h[i * 128 : i * 128 + 128, q * WIDTH : q * WIDTH + WIDTH] = part[q, i, j] + (
                late[q, i].astype(f32) + late[q, 2 + i].astype(f32)
            )

    def pred_move(q):
        pred_give(q).start()
        pred_own(q).start()

    def reduce_stat(q):
        pr = pred_h[:, q * WIDTH : q * WIDTH + WIDTH]
        sp = spot_h[:, q * WIDTH : q * WIDTH + WIDTH]
        for i, v in enumerate((pr * sp, pr * pr)):
            spacc[i] = v if q == 0 else spacc[i] + v

    def reduce_slides(q):
        pr = pred_h[:, q * WIDTH : q * WIDTH + WIDTH]
        sp = spot_h[:, q * WIDTH : q * WIDTH + WIDTH]
        for i, v in enumerate((pr * sp, pr * pr)):
            stat[q // 4, q % 4, i * 8 : i * 8 + 8] = split_dot(hot_lie[...].astype(b16), v)

    def obs_sums():
        for q in range(chunks):
            sp = spot_h[:, q * WIDTH : q * WIDTH + WIDTH]
            v = sp * sp
            ob_acc[...] = v if q == 0 else ob_acc[...] + v
            stat[q // 4, q % 4, 16:24] = split_dot(hot_lie[...].astype(b16), v)
        rc(ob_acc, ob_got, ob_s, ob_r, dev_mate).start()

    def st_send(g, i):
        slots = (st1, st2, st3)[i]
        if i == 0:
            st1[g, j] = stat[g, j]
        else:
            prior = (st1, st2)[i - 1]
            got(prior.at[g, pl.ds(0, 3)], st_r.at[g, i - 1])
            total = prior[g, 0] + prior[g, 1] + prior[g, 2] + prior[g, 3]
            st_sum[g, i - 1] = total
            if i == 1:
                st2[g, z] = total
            else:
                st3[g, j] = total
        for o in line_others if i == 1 else plane_others:
            src = stat.at[g, o] if i == 0 else st_sum.at[g, i - 1]
            to = dev(o, j, k) if i == 1 else dev(z, o, k)
            rc(src, slots.at[g, z if i == 1 else j], st_s.at[g, i], st_r.at[g, i], to).start()

    def st_finish(g):
        got(st3.at[g, pl.ds(0, 3)], st_r.at[g, 2])

    def turn(i):
        for kk in range(2):
            plane_turn[:, (kk * 4 + i) * 128 : (kk * 4 + i) * 128 + 128] = plane_low[kk, i].astype(f32).T.astype(b16)

    spx = rc(spacc, spgot, spx_s, spx_r, dev_mate)

    def spot_half():
        spx.start()

    slide8 = lax.broadcasted_iota(jnp.int32, (8, 128), 0)
    lane8 = lax.broadcasted_iota(jnp.int32, (8, 128), 1)

    def mass_end():
        sums_row = st_sum[0, 1, 24:25, :]
        each = jnp.broadcast_to(sums_row, (128, 128))
        mass_each = jnp.sum(jnp.where(of_slide & (kind == 0), each, 0.0), 1, keepdims=True)
        bins_each = jnp.sum(jnp.where(of_slide & (kind == 1), each, 0.0), 1, keepdims=True)
        mass_grad = (1.0 / mass_each - bins_col / (bins_each * keep["mass"])) / SLIDES
        keep["grad"] = mass_grad.astype(b16).astype(f32)

        def by_slide(begin):
            return jnp.sum(
                jnp.where(lane8 == slide8 + begin, jnp.broadcast_to(sums_row, (8, 128)), 0.0), 1, keepdims=True
            )

        mass_s, bins_s, log_s = by_slide(0), by_slide(8), by_slide(16)
        kl = jnp.sum(log_s / bins_s - jnp.log(bins_s) + jnp.log(mass_s), axis=0, keepdims=True)
        keep["kl"] = kl / SLIDES

    def reach_make():
        mass_grad = keep["grad"]

        @pl.loop(0, 32)
        def _(d):
            jj, kk, b = split(d)
            r_src[kk, jj, b] = jnp.sum(of_cells(jj, kk, b) * mass_grad, axis=0, keepdims=True)

        hand_over(r_src.at[mate], r_mate, 4)

    def reach_plane():
        got(r_mate, sm_r.at[4])
        r_plane_src[...] = r_src[k] + r_mate[...]
        r_plane[j] = r_plane_src[j]
        spread(lambda o: r_plane_src.at[o], r_plane, "plane", 5)

    def reach_line():
        got(r_plane.at[pl.ds(0, 3)], sm_r.at[5])
        r_line_src[...] = r_plane[0] + r_plane[1] + r_plane[2] + r_plane[3]
        r_line[z] = r_line_src[z]
        spread(lambda o: r_line_src.at[o], r_line, "line", 6)

    def obs_end():
        got(ob_got, ob_r)
        keep["obs_c"] = jnp.sum(ob_acc[...] + ob_got[...], axis=1, keepdims=True)

    def spot_sums():
        st_finish(0)
        got(spgot, spx_r)
        cross_c, pred_c = [jnp.sum(spacc[i] + spgot[i], axis=1, keepdims=True) for i in range(2)]
        obs_c = keep["obs_c"]
        root_c = jnp.sqrt(pred_c * obs_c)
        keep["cos"] = cross_c / root_c
        keep["obs"] = (1.0 / root_c) / total_spots
        keep["prd"] = (cross_c / (pred_c * root_c)) / total_spots

    def grad_make(q):
        scale = 1.0 / (SLIDES * total_genes)
        for e in range(units):
            g, o = divmod(q * units + e, 4)
            sums = st3[g, o]
            cross, prd, obs = sums[:8], sums[8:16], sums[16:24]
            root = jnp.sqrt(prd * obs)
            for i, v in enumerate((scale / root, scale * cross / (prd * root))):
                high = v.astype(b16).astype(f32)
                mid = (v - high).astype(b16).astype(f32)
                low = v - high - mid
                stack = jnp.concatenate([high, mid, low, jnp.zeros((8, 128), f32)], axis=0)
                coef[:32, (i * units + e) * 128 : (i * units + e) * 128 + 128] = stack.astype(b16)
        each_spot = jnp.dot(hot_stand[...], coef[...], preferred_element_type=f32)
        at = slice(q * WIDTH, q * WIDTH + WIDTH)
        value = pred_h[:, at] * (each_spot[:, WIDTH:] + keep["prd"]) - spot_h[:, at] * (each_spot[:, :WIDTH] + keep["obs"])
        value = value.astype(b16)
        grad[0, j, :, at] = value[:128]
        grad[1, j, :, at] = value[128:]

    def gene_cos():
        total = jnp.zeros((8, 128), f32)
        for g in range(2):
            for e in range(4):
                sums = st3[g, e]
                total = total + sums[:8] / jnp.sqrt(sums[8:16] * sums[16:24])
        return jnp.sum(jnp.sum(total, axis=0, keepdims=True), axis=1, keepdims=True)

    def grad_send(q):
        grad_make(q)
        at = grad.at[:, j, :, at_chunk(q)]
        rc(at, at, g_s.at[0], g_r.at[q, 0], dev_x).start()
        rc(at, at, g_s.at[1], g_r.at[q, 1], dev_y).start()

    def grad_direct(q):
        grad_make(q)
        at = grad.at[:, j, :, at_chunk(q)]
        rc(at, at, g_s.at[4], g_r.at[q, 2], dev(z, jd, k)).start()
        rc(at, at, g_s.at[0], g_r.at[q, 0], dev_x).start()
        rc(at, at, g_s.at[1], g_r.at[q, 1], dev_y).start()

    def grad_pass(q, i):
        owner, to = ((jx, dev_y), (jy, dev_x))[i]
        got(grad.at[:, owner, :, at_chunk(q)], g_r.at[q, i])
        at = grad.at[i, owner, :, at_chunk(q)]
        rc(at, at, g_s.at[2 + i], g_r.at[q, 2], to).start()

    def run_up(q, b):
        return rc(pass_on.at[q, b], sums_up.at[q, b], rs_s, rs_r.at[q, b], dev_up)

    def run_dn(q, b):
        return rc(pass_on.at[q, b], sums_dn.at[q, b], rs_s, rs_r.at[q, b], dev_dn)

    def block(q, b):
        return part[q, b // 2, pl.ds(2 * (b % 2), 2)].reshape(256, WIDTH)

    def run_last(q, b, up):
        i = 0 if up else 1
        to, cross = (dev_up, cross_up) if up else (dev_dn, cross_dn)
        rc(pass_on.at[q, b, rows(k, 128)], fin.at[q, i, k], rs_s, fin_r.at[q], to).start()
        rc(pass_on.at[q, b, rows(mate, 128)], fin.at[q, i, k], rs_s, fin_r.at[q], cross).start()

    def sums_half(q, h):
        whole = jnp.dot(
            plane_turn[rows(h, 512), :], grad[:, :, :, at_chunk(q)].reshape(1024, WIDTH), preferred_element_type=f32
        )
        part[q, h] = whole.reshape(4, 128, WIDTH)

    def sums_give(q, b):
        pass_on[q, b] = block(q, b).astype(b16)

    def grad_wait(q):
        if DIRECT == q:
            got(grad.at[:, jx, :, at_chunk(q)], g_r.at[q, 0])
            got(grad.at[:, jy, :, at_chunk(q)], g_r.at[q, 1])
        got(grad.at[:, jd, :, at_chunk(q)], g_r.at[q, 2])

    def sums_first(q, count):
        if count == 2:
            product(q, plane_turn, count)
        for step in range(2):
            if count == 1:
                sums_half(q, jnp.where(z < 2, 1 - step, step))

            @pl.when(z == 0)
            def _():
                for i in range(count):
                    for b in ((3, 2), (1,))[step]:
                        sums_give(q + i, b)
                        run_last(q + i, b, True) if b == 1 else run_up(q + i, b).start()

            @pl.when(z == 3)
            def _():
                for i in range(count):
                    for b in ((0, 1), (2,))[step]:
                        sums_give(q + i, b)
                        run_last(q + i, b, False) if b == 2 else run_dn(q + i, b).start()

    def pass_add(q, b, slots):
        got(slots.at[q, b], rs_r.at[q, b])
        pass_on[q, b] = (block(q, b) + slots[q, b].astype(f32)).astype(b16)

    def pass_far(q):
        @pl.when(z == 1)
        def _():
            pass_add(q, 3, sums_up)
            run_up(q, 3).start()

        @pl.when(z == 2)
        def _():
            pass_add(q, 0, sums_dn)
            run_dn(q, 0).start()

    def pass_middle(q):
        @pl.when(z == 1)
        def _():
            pass_add(q, 2, sums_up)
            run_last(q, 2, True)

        @pl.when(z == 2)
        def _():
            pass_add(q, 1, sums_dn)
            run_last(q, 1, False)

    def pass_near(q):
        @pl.when(z == 1)
        def _():
            pass_add(q, 0, sums_dn)
            run_last(q, 0, False)

        @pl.when(z == 2)
        def _():
            pass_add(q, 3, sums_up)
            run_last(q, 3, True)

    def other_give(q):
        return rc(other.at[q], other_got.at[q], oth_s, oth_r.at[q], dev_mate)

    def use_sums(q, kk, sums):
        at = lanes(kk, q)
        expr_out[:, at] = keep_col * sums
        weighed = cell_v[:, at].astype(f32) * sums
        for e in range(units):
            filt_acc[...] = filt_acc[...] + weighed[:, e * 128 : e * 128 + 128]

    def sums_other(q):
        other[q] = part[q, lax.div(z, 2), 2 * lax.rem(z, 2) + mate]
        other_give(q).start()

    def sums_last(q):
        @pl.when(z == 0)
        def _():
            got(fin.at[q, 1], fin_r.at[q])

        @pl.when(z == 3)
        def _():
            got(fin.at[q, 0], fin_r.at[q])

        @pl.when((z > 0) & (z < 3))
        def _():
            got(fin.at[q], fin_r.at[q])

        got(other_got.at[q], oth_r.at[q])
        own_at = (q, lax.div(z, 2), 2 * lax.rem(z, 2) + k)
        for kk, base in ((k, part[own_at]), (mate, other_got[q])):
            up = jnp.where(z > 0, fin[q, 0, kk].astype(f32), 0.0)
            dn = jnp.where(z < 3, fin[q, 1, kk].astype(f32), 0.0)
            use_sums(q, kk, base + (up + dn))

    def back_dot(b):
        @pl.loop(0, 2)
        def _(h):
            back[b, h] = lax.dot_general(
                grad[h].reshape(512, half), col[b], (((1,), (1,)), ((), ())), preferred_element_type=f32
            ).reshape(4, 128, 256)

        rc(back.at[b, mate], back_got.at[b], back_s, back_r.at[b], dev_mate).start()

    def back_add(b):
        got(back_got.at[b], back_r.at[b])
        for jj in range(4):
            back_low[jj, :, rows(b, 256)] = (back[b, k, jj] + back_got[b, jj]).astype(b16)

    def ret_send(b):
        at = rows(b, 256)
        for jj in (jd, jx, jy):
            rc(back_low.at[jj, :, at], back_ret.at[j, :, at], ret_s, ret_r, dev(z, jj, k)).start()
        back_ret[j, :, at] = back_low[j, :, at]

    loss_lane = lax.broadcasted_iota(jnp.int32, (1, 128), 1)

    def loss_mate():
        own_cos = jnp.sum(keep["cos"], axis=0, keepdims=True)
        l_src[...] = jnp.where(loss_lane == 0, own_cos, jnp.where(loss_lane == 1, gene_cos(), 0.0))
        hand_over(l_src, l_mate, 7)
        l_plane[j] = l_src[...]
        spread(lambda o: l_src, l_plane, "plane", 8)

    def loss_line():
        got(l_plane.at[pl.ds(0, 3)], sm_r.at[8])
        total = l_plane[0] + l_plane[1] + l_plane[2] + l_plane[3]
        l_line_src[...] = total
        l_line[z] = total
        spread(lambda o: l_line_src, l_line, "line", 9)

    def loss_end():
        got(l_line.at[pl.ds(0, 3)], sm_r.at[9])
        got(l_mate, sm_r.at[7])
        cos_row = l_line[0] + l_line[1] + l_line[2] + l_line[3]
        gene_row = l_src[...] + l_mate[...]
        cos_total = jnp.sum(jnp.where(loss_lane == 0, cos_row, 0.0), axis=1, keepdims=True)
        gene_total = jnp.sum(jnp.where(loss_lane == 1, gene_row, 0.0), axis=1, keepdims=True)
        gene_loss = 1.0 - gene_total / (SLIDES * total_genes)
        spot_loss = 1.0 - cos_total / total_spots
        kl_loss = keep["kl"]
        total_loss = gene_loss + spot_loss + kl_loss
        picked = jnp.where(loss_lane == 2, spot_loss, jnp.where(loss_lane == 3, kl_loss, 0.0))
        loss_out[...] = jnp.where(loss_lane == 0, total_loss, jnp.where(loss_lane == 1, gene_loss, picked))

    def map_rows(g):
        at = rows(g, 16)
        pick = lax.broadcasted_iota(jnp.int32, (16, 128), 0) + g * 16
        here = lax.broadcasted_iota(jnp.int32, (16, 128), 1)
        mg = jnp.sum(jnp.where(pick == here, jnp.broadcast_to(mass_row[...], (16, 128)), 0.0), 1, keepdims=True)
        inner = jnp.zeros((16, 128), f32)
        for d in range(32):
            b, jj, kk = d // 8, (d % 8) // 2, d % 2
            used = back_ret[jj, at, b * 256 + kk * 128 : b * 256 + kk * 128 + 128].astype(f32) + mg * keep_all[jj, kk, b]
            inner = inner + chance[at, d * 128 : d * 128 + 128] * used
            map_out[at, d * 128 : d * 128 + 128] = used
        inner = jnp.sum(inner, axis=1, keepdims=True)
        map_out[at, :] = chance[at, :] * (map_out[at, :] - inner)

    def map_some(i):
        if i == 0:
            got(back_ret.at[pl.ds(0, 3)], ret_r)
            mass_row[...] = lie(keep["grad"])
        pl.loop(2 * i, 2 * i + 2)(map_rows)

    steps = {
        "x": softmax_some, "H": scale_more, "F": lambda i: filt_line(), "N": far_ready, "Y": pred_move, "w": low_give, "v": lambda i: low_own(),
        "c": col_own, "h": lambda i: hop(), "i": lambda i: (filt_pair, filt_plane, mass_make, mass_chip)[i](),
        "a": low_arrive, "q": turn, "p": lambda q: product(q, plane_low, 1), "P": lambda q: product(q, plane_low, 2),
        "f": reduce_first, "s": lambda q: reduce_second(q, 0), "S": lambda q: reduce_second(q, 1),
        "l": reduce_last, "k": reduce_stat, "j": reduce_slides, "B": lambda i: (obs_sums, obs_end)[i](), "t": lambda i: st_send(0, i), "z": lambda i: (spot_half, mass_end, spot_sums)[i](),
        "g": grad_send, "G": grad_direct, "m": lambda q: grad_pass(q, 0), "n": lambda q: grad_pass(q, 1),
        "y": lambda i: st_send(1, i) if i < 3 else st_finish(1), "r": lambda q: sums_first(q, 1), "R": lambda q: sums_first(q, 2),
        "U": pass_far, "V": pass_middle, "D": pass_near,
        "L": sums_last, "O": sums_other, "b": back_dot, "A": back_add, "T": ret_send, "W": grad_wait, "M": map_some,
        "e": lambda i: (reach_make, reach_plane, reach_line)[i](), "o": lambda i: (loss_mate, loss_line, loss_end)[i](),
    }
    for group in ORDER:
        for word in group.split():
            steps[word[0]](int(word[1:]) if len(word) > 1 else 0)

    got(r_line.at[pl.ds(0, 3)], sm_r.at[6])
    reach_row = r_line[0] + r_line[1] + r_line[2] + r_line[3]
    filt_sum = jnp.sum(filt_acc[...], axis=1, keepdims=True)
    keep_row = jax.nn.sigmoid(filt_in[...].astype(f32))
    filt_out[...] = keep_row * (1.0 - keep_row) * (lie(filt_sum) + reach_row)

    sent(hand, hand_s)
    spot_give.wait_send()
    sent(send1, send1_s)
    sent(send2, send2_s)
    sent(pred_h.at[rows(mate, 128)], pred_s)
    got(pred_out.at[:, pl.ds(pl.multiple_of(mate * half, half), half)], pred_r)
    pltpu.make_async_copy(
        pred_h.at[rows(k, 128)], pred_out.at[:, pl.ds(pl.multiple_of(k * half, half), half)], own_sem
    ).wait()
    for i in range(2):
        sent(grad.at[:, j], g_s.at[i])
    others = [q for q in range(chunks) if q != DIRECT]
    sent(grad.at[0, jx, :, pl.ds(0, len(others) * WIDTH)], g_s.at[2])
    sent(grad.at[1, jy, :, pl.ds(0, len(others) * WIDTH)], g_s.at[3])
    if DIRECT is not None:
        sent(grad.at[:, j, :, at_chunk(DIRECT)], g_s.at[4])
    sent(ob_acc, ob_s)
    for i in range(3):
        @pl.when(z == i)
        def _():
            sent(col.at[pl.ds(0, i + 1)], up_s)

        @pl.when(z == 3 - i)
        def _():
            sent(col.at[pl.ds(3 - i, i + 1)], dn_s)
    sent(pass_on.at[:, pl.ds(0, 3)], rs_s)
    sent(plane_low.at[k, pl.ds(0, 3)], low_s.at[0])
    sent(plane_low.at[k], low_s.at[1])
    for g in range(2):
        for i in range(3):
            sent(st1.at[g, pl.ds(0, 3)], st_s.at[g, i])
    spx.wait_send()
    sent(back_got, back_s)
    sent(back_low.at[pl.ds(0, 3)], ret_s)
    sent(other, oth_s)
    for i, ref in enumerate((
        f_line.at[pl.ds(0, 3)], f_line, f_all.at[pl.ds(0, 3)], m_src, r_mate, r_plane.at[pl.ds(0, 3)],
        r_line.at[pl.ds(0, 3)], l_mate, l_plane.at[pl.ds(0, 3)], l_line.at[pl.ds(0, 3)],
    )):
        sent(ref, sm_s.at[i])


def hand_out(pred_in, map_in, expr_in, filt_in, loss_in, pred_out, map_out, expr_out, filt_out, loss_out, sems):
    pairs = ((map_in, map_out), (pred_in, pred_out), (expr_in, expr_out))
    size = 128 // 2
    copies = [
        pltpu.make_async_copy(src.at[pl.ds(p * size, size)], dst.at[pl.ds(p * size, size)], sems.at[i, p])
        for p in range(2)
        for i, (src, dst) in enumerate(pairs)
    ]
    for copy in copies:
        copy.start()
    filt_out[...] = filt_in[...]
    loss_out[...] = loss_in[:, :4]
    for copy in copies:
        copy.wait()


def fused_shards(map_logits, filter_logits, cell_expr, spot_expr, cell_slide, spot_slide, density_bins):
    f32, b16 = jnp.float32, jnp.bfloat16
    spots, cells = map_logits.shape
    genes = cell_expr.shape[1]
    n = genes // (2 * WIDTH)
    V, S = pltpu.VMEM, pltpu.SemaphoreType.DMA
    any_, vmem = pl.BlockSpec(memory_space=pl.ANY), pl.BlockSpec(memory_space=pltpu.VMEM)
    one = S(())
    scratch = [
        V((128, cells), f32),
        V((4, 128, 1024), b16),
        V((2, 4, 128, 1024), b16),
        V((1024, 1024), b16),
        V((128, genes), b16),
        V((n, 128, WIDTH), b16),
        V((4, 256, genes // 2), b16),
        V((n, 2, 4, 128, WIDTH), f32),
        V((n, 4, 128, WIDTH), b16),
        V((n, 2, 128, WIDTH), b16),
        V((n, 2, 128, WIDTH), b16),
        V((n, 4, 128, WIDTH), b16),
        V((256, genes // 2), f32),
        V((256, genes // 2), f32),
        V((2, 4, 32, 128), f32),
        V((2, 2, 32, 128), f32),
        V((2, 4, 32, 128), f32),
        V((2, 4, 32, 128), f32),
        V((2, 4, 32, 128), f32),
        V((2, 256, 128), f32),
        V((2, 256, 128), f32),
        V((256, 128), f32),
        V((256, 128), f32),
        V((128, 2 * WIDTH), b16),
        V((2, 4, 128, genes // 2), b16),
        V((n, 4, 256, WIDTH), b16),
        V((n, 4, 256, WIDTH), b16),
        V((n, 4, 256, WIDTH), b16),
        V((n, 2, 2, 128, WIDTH), b16),
        V((4, 2, 4, 128, 256), f32),
        V((4, 4, 128, 256), f32),
        V((4, 128, 1024), b16),
        V((4, 128, 1024), b16),
        V((n, 128, WIDTH), f32),
        V((n, 128, WIDTH), f32),
        V((4, 1, 128), f32),
        V((2, 4, 1, 128), f32),
        V((4, 2, 4, 1, 128), f32),
        V((4, 2, 4, 1, 128), f32),
        V((2, 1, 128), f32),
        V((2, 1, 128), f32),
        V((2, 4, 4, 1, 128), f32),
        V((4, 4, 1, 128), f32),
        V((4, 4, 1, 128), f32),
        V((4, 4, 1, 128), f32),
        V((4, 1, 128), f32),
        V((4, 1, 128), f32),
        V((1, 128), f32),
        V((1, 128), f32),
        V((4, 1, 128), f32),
        V((1, 128), f32),
        V((4, 1, 128), f32),
        V((128, 128), f32),
        V((8, 256), f32),
        V((256, 128), b16),
        V((1, 128), f32),
        V((1, 128), b16),
        V((1, cells), jnp.int32),
        V((1, 128), jnp.int32),
        V((1, 128), jnp.int32),
        S((7,)), one, one, one, one, one, S((n, 4)), S((2,)), S((5,)),
        one, one, S((n, 2)), S((n,)),
        one, one, one, one, S((2, 3)), S((2, 3)), one, one, one, one,
        S((5,)), S((n, 3)), one, S((n, 4)), S((n,)), one, S((4,)),
        one, one, one, S((n,)), S((10,)), S((10,)), pltpu.SemaphoreType.REGULAR,
    ]
    predicted, map_grad, expr_grad, filt, loss = pl.pallas_call(
        functools.partial(fused_kernel, float(spots * 32), float(genes)),
        out_shape=(
            pltpu.VMEM((spots, genes), f32),
            pltpu.VMEM((spots, cells), f32),
            pltpu.VMEM((spots, genes), f32),
            V((1, 128), f32),
            V((1, 128), f32),
        ),
        in_specs=[any_] * 7,
        out_specs=(vmem, vmem, vmem, vmem, vmem),
        scratch_shapes=scratch,
        compiler_params=pltpu.CompilerParams(
            collective_id=0, has_side_effects=True, vmem_limit_bytes=58 * 2**20
        ),
        name="mapping_step",
    )(
        map_logits,
        filter_logits.reshape(1, 128),
        cell_expr,
        spot_expr,
        cell_slide.reshape(1, cells),
        spot_slide.reshape(1, 128),
        density_bins.reshape(1, 128),
    )
    predicted, map_grad, expr_grad, filt, loss = pl.pallas_call(
        hand_out,
        out_shape=(
            jax.ShapeDtypeStruct((spots, genes), f32),
            jax.ShapeDtypeStruct((spots, cells), f32),
            jax.ShapeDtypeStruct((spots, genes), f32),
            jax.ShapeDtypeStruct((1, 128), f32),
            jax.ShapeDtypeStruct((1, 4), f32),
        ),
        in_specs=[vmem] * 5,
        out_specs=(any_, any_, any_, vmem, vmem),
        scratch_shapes=[S((3, 2))],
        compiler_params=pltpu.CompilerParams(vmem_limit_bytes=2**20),
        name="hand_out",
    )(*[pltpu.with_memory_space_constraint(v, pltpu.VMEM) for v in (predicted, map_grad, expr_grad, filt, loss)])
    return loss.reshape(4), predicted, map_grad, expr_grad, filt.reshape(128)


def solution(mesh):
    both = P(("row", "col"))
    rows = P(("row", "col"), None)
    in_specs = (rows, both, rows, rows, P(), both, both)
    out_specs = (P(), rows, rows, rows, both)
    step = fused_shards if (mesh.shape["row"], mesh.shape["col"]) == (4, 8) else shards
    return jax.shard_map(step, mesh=mesh, in_specs=in_specs, out_specs=out_specs, check_vma=False)
```
